32 devices in a mesh: dp: 8 (over y, x, core), ctx: 4 (over z).
Axes of the slice: x: 2, y: 2, z: 4, core: 2. Of those that a mesh axis runs over, the one named last changes fastest.
Arguments:
- tokens: bfloat16 [8, 2048, 1024], P('dp', 'ctx'), may hold values from -6 to 6
- first_values: bfloat16 [8, 2048, 1024], P('dp', 'ctx'), may hold values from -6 to 6
- v1_accum: float32 [8, 2048, 1024], P('dp', 'ctx'), may hold values from -6 to 6
- segment_ids: int32 [8, 2048], P('dp', 'ctx'), may hold values from 0 to 3, as said below
- positions: int32 [8, 2048], P('dp', 'ctx'), may hold values from 0 to 2047, as said below
- cotangent: bfloat16 [8, 2048, 1024], P('dp', 'ctx'), may hold values from -6 to 6
- attn_gain: bfloat16 [1024], P(('dp', 'ctx')), may hold values from 0.25 to 1.75
- w_query: bfloat16 [1024, 1024], P(('dp', 'ctx')), may hold values from -0.1875 to 0.1875
- w_key: bfloat16 [1024, 1024], P(('dp', 'ctx')), may hold values from -0.1875 to 0.1875
- w_value: bfloat16 [1024, 1024], P(('dp', 'ctx')), may hold values from -0.1875 to 0.1875
- w_out: bfloat16 [1024, 1024], P(('dp', 'ctx')), may hold values from -2 to 2
- mlp_gain: bfloat16 [1024], P(('dp', 'ctx')), may hold values from 0.25 to 1.75
- w_gate: bfloat16 [1024, 2816], P(('dp', 'ctx')), may hold values from -0.1875 to 0.1875
- w_up: bfloat16 [1024, 2816], P(('dp', 'ctx')), may hold values from -0.1875 to 0.1875
- w_down: bfloat16 [2816, 1024], P(('dp', 'ctx')), may hold values from -0.109375 to 0.109375
Outputs:
- output: bfloat16 [8, 2048, 1024], P('dp', 'ctx')
- input_grad: float32 [8, 2048, 1024], P('dp', 'ctx')
- v1_grad: float32 [8, 2048, 1024], P('dp', 'ctx')
- attn_gain_grad: float32 [1024], P(('dp', 'ctx'))
- w_query_grad: float32 [1024, 1024], P(('dp', 'ctx'))
- w_key_grad: float32 [1024, 1024], P(('dp', 'ctx'))
- w_value_grad: float32 [1024, 1024], P(('dp', 'ctx'))
- w_out_grad: float32 [1024, 1024], P(('dp', 'ctx'))
- mlp_gain_grad: float32 [1024], P(('dp', 'ctx'))
- w_gate_grad: float32 [1024, 2816], P(('dp', 'ctx'))
- w_up_grad: float32 [1024, 2816], P(('dp', 'ctx'))
- w_down_grad: float32 [2816, 1024], P(('dp', 'ctx'))
The draws below stay inside these ranges and needn't reach their ends.
Inputs may be any that keep to these rules, and one draw needn't show every extreme that they name: `segment_ids`: in each packed row the ids start at 0 and never fall; a row holds at most 4 documents, and one row of every draw holds a single one. `positions`: 0 at the start of a row or where the segment id changes, else one more than the token before; one row of every draw is a single document.
All inputs are finite; a program needn't handle non-finite values.
Results may differ from the reference program's by a relative error of at most 0.015.
Values may be sent and summed in bfloat16 or wider, within the bound.
A program may use at most 256 MiB of HBM per device.

```python
import jax
import jax.numpy as jnp
from jax import lax

D = 1024
HEADS = 16
HEAD_DIM = 64
FF = 2816
LENGTH = 2048
ROWS = 8


def document_cuts(key):
    cut_key = jax.random.fold_in(key, 11)
    cut_points = jax.random.randint(cut_key, (ROWS, 3), 1, LENGTH)
    lone_key = jax.random.fold_in(key, 12)
    lone_row = jax.random.randint(lone_key, (), 0, ROWS)
    row_idx = jnp.arange(ROWS, dtype=jnp.int32)
    cut_points = jnp.where(row_idx[:, None] == lone_row, LENGTH, cut_points).astype(jnp.int32)
    position_idx = jnp.arange(LENGTH, dtype=jnp.int32)
    boundary = jnp.any(position_idx[None, :, None] == cut_points[:, None, :], axis=2)
    return (boundary, position_idx)


def draw_segment_ids(key, part):
    boundary, position_idx = document_cuts(key)
    return jnp.cumsum(boundary.astype(jnp.int32), axis=1).astype(jnp.int32)


def draw_positions(key, part):
    boundary, position_idx = document_cuts(key)
    starts_at = jnp.where(boundary, position_idx[None, :], 0).astype(jnp.int32)
    latest = lax.cummax(starts_at, axis=1)
    return (position_idx[None, :] - latest).astype(jnp.int32)


def levels(key, dims, split, least, largest):
    gain, own = 1.0, jax.random.fold_in(key, 6)
    for axis_at, blocks in split:
        steps = jnp.exp(jax.random.uniform(jax.random.fold_in(own, axis_at), (blocks,), jnp.float32, least / len(split), largest / len(split)))
        gain = gain * jnp.repeat(steps, dims[axis_at] // blocks).reshape([-1 if axis == axis_at else 1 for axis in range(len(dims))])
    return gain


def scatter_about(stream_key, dims, scale, most, pieces=(), kind=jnp.bfloat16):
    values = jax.random.normal(stream_key, dims, jnp.float32) * scale
    if len(pieces) > 0:
        values = levels(stream_key, dims, pieces, -0.22, 0.18) * values
    return jnp.clip(values, min=-most, max=most).astype(kind)


def setup_inputs(seed: int = 0) -> dict:
    splits = jax.random.split(jax.random.key(seed), 16)
    tokens = scatter_about(splits[0], (ROWS, LENGTH, D), 1.0, 6.0, ((0, 8), (1, 4)))
    first_values = scatter_about(splits[1], (ROWS, LENGTH, D), 1.0, 6.0, ((0, 8), (1, 4)))
    v1_accum = scatter_about(splits[2], (ROWS, LENGTH, D), 1.0, 6.0, ((0, 8), (1, 4)), jnp.float32)
    segment_ids = draw_segment_ids(jax.random.fold_in(splits[15], 71), 0)
    positions = draw_positions(jax.random.fold_in(splits[15], 71), 0)
    cotangent = scatter_about(splits[5], (ROWS, LENGTH, D), 1.0, 6.0, ((0, 8), (1, 4)))
    attn_gain = jnp.clip(1.0 + 0.15 * jax.random.normal(splits[6], (D,), jnp.float32), 0.25, 1.75).astype(jnp.bfloat16)
    w_query = scatter_about(splits[7], (D, D), D ** -0.5, 0.1875, ((0, 32),))
    w_key = scatter_about(splits[8], (D, D), D ** -0.5, 0.1875, ((0, 32),))
    w_value = scatter_about(splits[9], (D, D), D ** -0.5, 0.1875, ((0, 32),))
    w_out = scatter_about(splits[10], (D, D), (D // 128) ** -0.5, 2.0, ((0, 32),))
    mlp_gain = jnp.clip(1.0 + 0.15 * jax.random.normal(splits[11], (D,), jnp.float32), 0.25, 1.75).astype(jnp.bfloat16)
    w_gate = scatter_about(splits[12], (D, FF), D ** -0.5, 0.1875, ((0, 32),))
    w_up = scatter_about(splits[13], (D, FF), D ** -0.5, 0.1875, ((0, 32),))
    w_down = scatter_about(splits[14], (FF, D), FF ** -0.5, 0.109375, ((0, 32),))
    return {"tokens": tokens, "first_values": first_values, "v1_accum": v1_accum, "segment_ids": segment_ids, "positions": positions, "cotangent": cotangent, "attn_gain": attn_gain, "w_query": w_query, "w_key": w_key, "w_value": w_value, "w_out": w_out, "mlp_gain": mlp_gain, "w_gate": w_gate, "w_up": w_up, "w_down": w_down}


epsilon = 1e-05

@jax.custom_vjp
def low(v):
    return lax.optimization_barrier(v.astype(jnp.bfloat16)).astype(jnp.float32)

@jax.custom_vjp
def low_back(v):
    return v

def low_keep(v):
    return (low(v), None)

def low_pass(kept, grad):
    return (grad,)

def back_keep(v):
    return (v, None)

def back_low(kept, grad):
    return (low(grad),)
low.defvjp(low_keep, low_pass)
low_back.defvjp(back_keep, back_low)

def rms_scale(values):
    return lax.rsqrt(lax.optimization_barrier(jnp.mean(values * values, axis=-1, keepdims=True)) + epsilon)

def matmul(left, right):
    return jnp.dot(left, right, precision=lax.Precision.HIGHEST)

def angle_tables(position_row):
    freqs = 10000.0 ** (-jnp.arange(HEAD_DIM // 2).astype(jnp.float32) * (2.0 / HEAD_DIM))
    angles = position_row.astype(jnp.float32)[..., None] * freqs
    return (jnp.cos(angles)[..., None, :], jnp.sin(angles)[..., None, :])

def rotate(heads_in, cosine_table, sine_table):
    half_dim = heads_in.shape[-1] // 2
    first_half = heads_in[..., :half_dim]
    second_half = heads_in[..., half_dim:]
    return jnp.concatenate([first_half * cosine_table - second_half * sine_table, second_half * cosine_table + first_half * sine_table], axis=-1)

def layer_row(members, params):
    tokens_row, first_row, segment_row, position_row = members
    attn_gain, w_query, w_key, w_value, w_out, mlp_gain, w_gate, w_up, w_down = params
    length = tokens_row.shape[0]
    normed = tokens_row * rms_scale(tokens_row)
    normed_in = low(normed * attn_gain)
    query_proj = low_back(matmul(normed_in, w_query))
    key_proj = low_back(matmul(normed_in, w_key))
    value_proj = low_back(matmul(normed_in, w_value))
    cosine_table, sine_table = angle_tables(position_row)
    query_rot = low(rotate(query_proj.reshape(length, HEADS, HEAD_DIM), cosine_table, sine_table))
    key_rot = low(rotate(key_proj.reshape(length, HEADS, HEAD_DIM), cosine_table, sine_table))
    value_mix = low(0.5 * value_proj + 0.5 * first_row).reshape(length, HEADS, HEAD_DIM)
    scores = low_back(jnp.einsum('qhd,khd->hqk', query_rot, key_rot, precision=lax.Precision.HIGHEST) * 0.125)
    order = jnp.arange(length)
    allowed = (segment_row[:, None] == segment_row[None, :]) & (order[:, None] >= order[None, :])
    scores = jnp.where(allowed[None], scores, -1e+30)
    highest = lax.optimization_barrier(jnp.max(scores, axis=-1, keepdims=True))
    exp_scores = jnp.exp(scores - highest)
    soft_low = low(exp_scores / lax.optimization_barrier(jnp.sum(exp_scores, axis=-1, keepdims=True)))
    attended = jnp.einsum('hqk,khd->qhd', soft_low, value_mix, precision=lax.Precision.HIGHEST)
    attended = low(low_back(attended.reshape(length, HEADS * HEAD_DIM)))
    middle = tokens_row + low_back(matmul(attended, w_out))
    normed_two = middle * rms_scale(middle)
    mlp_in = low(normed_two * mlp_gain)
    gate_proj = low_back(matmul(mlp_in, w_gate))
    up_proj = low_back(matmul(mlp_in, w_up))
    hidden = low(gate_proj * jax.nn.sigmoid(gate_proj) * up_proj)
    return middle + low_back(matmul(hidden, w_down))

def reference(tokens, first_values, v1_accum, segment_ids, positions, cotangent, attn_gain, w_query, w_key, w_value, w_out, mlp_gain, w_gate, w_up, w_down):
    params = tuple((weight.astype(jnp.float32) for weight in (attn_gain, w_query, w_key, w_value, w_out, mlp_gain, w_gate, w_up, w_down)))

    def forward(tokens_in, first_in, *params_in):

        def step_row(members):
            return layer_row(members, params_in)
        return lax.map(jax.checkpoint(step_row), (tokens_in, first_in, segment_ids, positions))
    output_full, pullback = jax.vjp(forward, tokens.astype(jnp.float32), first_values.astype(jnp.float32), *params)
    gradients = pullback(cotangent.astype(jnp.float32))
    return (output_full.astype(jnp.bfloat16), gradients[0], v1_accum + gradients[1], gradients[2], gradients[3], gradients[4], gradients[5], gradients[6], gradients[7], gradients[8], gradients[9], gradients[10])
```

```python
import functools

import jax
import jax.numpy as jnp
from jax import lax
from jax.experimental import pallas as pl
from jax.experimental.pallas import tpu as pltpu
from jax.sharding import PartitionSpec as P

HEADS = 16
HEAD_DIM = 64
LANES = 128
TOKEN_BLOCK = 512
FF_BLOCK = 256
NEG = -1e30
F32 = jnp.float32
LOW = jnp.bfloat16
BYTES = 60 * 2**20
epsilon = 1e-05


HEAD_BLOCK = 4


def rms_scale(values):
    return lax.rsqrt(jnp.mean(values * values, axis=-1, keepdims=True) + epsilon)


def angle_tables(position_rows):
    freqs = 10000.0 ** (-jnp.arange(HEAD_DIM // 2).astype(jnp.float32) * (2.0 / HEAD_DIM))
    angles = position_rows.astype(jnp.float32)[..., None] * freqs
    return (jnp.cos(angles)[..., None, :], jnp.sin(angles)[..., None, :])


def rotate(heads_in, cosine_table, sine_table):
    half_dim = heads_in.shape[-1] // 2
    first_half = heads_in[..., :half_dim]
    second_half = heads_in[..., half_dim:]
    return jnp.concatenate(
        [
            first_half * cosine_table - second_half * sine_table,
            second_half * cosine_table + first_half * sine_table,
        ],
        axis=-1,
    )


def norm_back(grad_normed, normed, inv_root, norm_gain):
    grad_scaled = grad_normed * norm_gain.astype(jnp.float32)
    grad_input = inv_root * (
        grad_scaled - normed * jnp.mean(grad_scaled * normed, axis=-1, keepdims=True)
    )
    return (grad_input, jnp.sum(grad_normed * normed, axis=0))


def attn_front(flat_tokens, first_flat, attn_set, cosine_table, sine_table, row_count, seq_piece):
    inv_root = rms_scale(flat_tokens)
    normed = flat_tokens * inv_root
    normed_in = (normed * attn_set[0].astype(jnp.float32)).astype(jnp.bfloat16)
    query_proj = jnp.dot(normed_in, attn_set[1], preferred_element_type=jnp.float32)
    key_proj = jnp.dot(normed_in, attn_set[2], preferred_element_type=jnp.float32)
    value_proj = jnp.dot(normed_in, attn_set[3], preferred_element_type=jnp.float32)
    query_rot = rotate(
        query_proj.reshape(row_count, seq_piece, HEADS, HEAD_DIM), cosine_table, sine_table
    )
    key_rot = rotate(
        key_proj.reshape(row_count, seq_piece, HEADS, HEAD_DIM), cosine_table, sine_table
    )
    query_rot = query_rot.astype(jnp.bfloat16).reshape(row_count, seq_piece, -1)
    key_rot = key_rot.astype(jnp.bfloat16).reshape(row_count, seq_piece, -1)
    value_mix = (
        (0.5 * value_proj + 0.5 * first_flat).astype(jnp.bfloat16).reshape(row_count, seq_piece, -1)
    )
    return (normed, inv_root, normed_in, query_rot, key_rot, value_mix)


def mlp_block(flat_tokens, attended_low, out_weight, mlp_set):
    middle = flat_tokens + jnp.dot(attended_low, out_weight, preferred_element_type=jnp.float32)
    inv_root_two = rms_scale(middle)
    normed_two = middle * inv_root_two
    mlp_in = (normed_two * mlp_set[0].astype(jnp.float32)).astype(jnp.bfloat16)
    gate_proj = jnp.dot(mlp_in, mlp_set[1], preferred_element_type=jnp.float32)
    up_proj = jnp.dot(mlp_in, mlp_set[2], preferred_element_type=jnp.float32)
    hidden = (gate_proj * jax.nn.sigmoid(gate_proj) * up_proj).astype(jnp.bfloat16)
    result = middle + jnp.dot(hidden, mlp_set[3], preferred_element_type=jnp.float32)
    return (normed_two, inv_root_two, mlp_in, gate_proj, up_proj, hidden, result)


def split_groups(row_block):
    tok_count = row_block.shape[0]
    return row_block.reshape(tok_count, HEADS // HEAD_BLOCK, HEAD_BLOCK * HEAD_DIM).transpose(
        1, 0, 2
    )


def join_groups(group_block):
    return group_block.transpose(1, 0, 2).reshape(group_block.shape[1], -1)


def as_heads(block):
    return block.reshape(block.shape[0], HEAD_BLOCK, HEAD_DIM)


def attend_row(members):
    query_row, key_row, value_row, allowed = members

    def per_group(pieces):
        query_block, key_block, value_block = pieces
        scores = (
            jnp.einsum(
                "qhd,khd->hqk",
                as_heads(query_block),
                as_heads(key_block),
                preferred_element_type=jnp.float32,
            )
            * 0.125
        )
        scores = jnp.where(allowed[None], scores, -1e30)
        highest = jnp.max(scores, axis=-1, keepdims=True)
        exp_scores = jnp.exp(scores - highest)
        denominator = jnp.sum(exp_scores, axis=-1, keepdims=True)
        soft_low = (exp_scores / denominator).astype(jnp.bfloat16)
        attended = jnp.einsum(
            "hqk,khd->qhd", soft_low, as_heads(value_block), preferred_element_type=jnp.float32
        )
        return (
            attended.reshape(query_block.shape[0], -1),
            (highest + jnp.log(denominator))[..., 0],
        )

    attended, log_total = lax.map(
        per_group, (split_groups(query_row), split_groups(key_row), split_groups(value_row))
    )
    return (join_groups(attended), log_total)


def attend_back(members):
    query_row, key_row, value_row, grad_row, log_total, allowed = members

    def per_group(pieces):
        query_block, key_block, value_block, grad_block, log_block = pieces
        query_heads = as_heads(query_block)
        key_heads = as_heads(key_block)
        grad_heads = as_heads(grad_block)
        scores = (
            jnp.einsum("qhd,khd->hqk", query_heads, key_heads, preferred_element_type=jnp.float32)
            * 0.125
        )
        soft_weights = jnp.where(allowed[None], jnp.exp(scores - log_block[..., None]), 0.0)
        soft_low = soft_weights.astype(jnp.bfloat16)
        grad_probs = jnp.einsum(
            "qhd,khd->hqk", grad_heads, as_heads(value_block), preferred_element_type=jnp.float32
        )
        row_delta = jnp.sum(soft_weights * grad_probs, axis=-1, keepdims=True)
        grad_scores = (soft_weights * (grad_probs - row_delta)).astype(jnp.bfloat16)
        grad_query = (
            jnp.einsum("hqk,khd->qhd", grad_scores, key_heads, preferred_element_type=jnp.float32)
            * 0.125
        )
        grad_key = (
            jnp.einsum("hqk,qhd->khd", grad_scores, query_heads, preferred_element_type=jnp.float32)
            * 0.125
        )
        grad_value = jnp.einsum(
            "hqk,qhd->khd", soft_low, grad_heads, preferred_element_type=jnp.float32
        )
        return (
            grad_query.reshape(query_block.shape[0], -1),
            grad_key.reshape(key_block.shape[0], -1),
            grad_value.reshape(key_block.shape[0], -1),
        )

    grad_query, grad_key, grad_value = lax.map(
        per_group,
        (
            split_groups(query_row),
            split_groups(key_row),
            split_groups(value_row),
            split_groups(grad_row),
            log_total,
        ),
    )
    return (join_groups(grad_query), join_groups(grad_key), join_groups(grad_value))


def plain_local(
    tokens,
    first_values,
    v1_accum,
    segment_ids,
    positions,
    cotangent,
    attn_gain,
    w_query,
    w_key,
    w_value,
    w_out,
    mlp_gain,
    w_gate,
    w_up,
    w_down,
):
    row_count, seq_piece, model_width = tokens.shape
    token_count = row_count * seq_piece
    flat_tokens = tokens.astype(jnp.float32).reshape(token_count, model_width)
    first_flat = first_values.astype(jnp.float32).reshape(token_count, model_width)
    cosine_table, sine_table = angle_tables(positions)
    segment_low = segment_ids.astype(jnp.bfloat16)
    attn_set = (
        lax.all_gather(attn_gain, ("dp", "ctx"), axis=0, tiled=True),
        lax.all_gather(w_query, ("dp", "ctx"), axis=0, tiled=True),
        lax.all_gather(w_key, ("dp", "ctx"), axis=0, tiled=True),
        lax.all_gather(w_value, ("dp", "ctx"), axis=0, tiled=True),
        lax.all_gather(w_out, ("dp", "ctx"), axis=0, tiled=True),
    )
    normed, inv_root, normed_in, query_rot, key_rot, value_mix = attn_front(
        flat_tokens, first_flat, attn_set, cosine_table, sine_table, row_count, seq_piece
    )
    key_full, value_full, segment_full = (
        lax.all_gather(key_rot, "ctx", axis=1, tiled=True),
        lax.all_gather(value_mix, "ctx", axis=1, tiled=True),
        lax.all_gather(segment_low, "ctx", axis=1, tiled=True),
    )
    query_order = lax.axis_index("ctx") * seq_piece + jnp.arange(seq_piece, dtype=jnp.int32)
    full_order = jnp.arange(key_full.shape[1], dtype=jnp.int32)
    segment_own = segment_ids.astype(jnp.float32)
    segment_all = segment_full.astype(jnp.float32)
    allowed = (segment_own[:, :, None] == segment_all[:, None, :]) & (
        query_order[None, :, None] >= full_order[None, None, :]
    )
    attended, log_total = lax.map(attend_row, (query_rot, key_full, value_full, allowed))
    attended_low = attended.reshape(token_count, model_width).astype(jnp.bfloat16)
    mlp_set = (
        lax.all_gather(mlp_gain, ("dp", "ctx"), axis=0, tiled=True),
        lax.all_gather(w_gate, ("dp", "ctx"), axis=0, tiled=True),
        lax.all_gather(w_up, ("dp", "ctx"), axis=0, tiled=True),
        lax.all_gather(w_down, ("dp", "ctx"), axis=0, tiled=True),
    )
    normed_two, inv_root_two, mlp_in, gate_proj, up_proj, hidden, output_flat = mlp_block(
        flat_tokens, attended_low, attn_set[4], mlp_set
    )
    output = output_flat.reshape(tokens.shape).astype(jnp.bfloat16)
    attn_set = (
        lax.all_gather(attn_gain, ("dp", "ctx"), axis=0, tiled=True),
        lax.all_gather(w_query, ("dp", "ctx"), axis=0, tiled=True),
        lax.all_gather(w_key, ("dp", "ctx"), axis=0, tiled=True),
        lax.all_gather(w_value, ("dp", "ctx"), axis=0, tiled=True),
        lax.all_gather(w_out, ("dp", "ctx"), axis=0, tiled=True),
    )
    mlp_set = (
        lax.all_gather(mlp_gain, ("dp", "ctx"), axis=0, tiled=True),
        lax.all_gather(w_gate, ("dp", "ctx"), axis=0, tiled=True),
        lax.all_gather(w_up, ("dp", "ctx"), axis=0, tiled=True),
        lax.all_gather(w_down, ("dp", "ctx"), axis=0, tiled=True),
    )
    normed, inv_root, normed_in, query_rot, key_rot, value_mix = attn_front(
        flat_tokens, first_flat, attn_set, cosine_table, sine_table, row_count, seq_piece
    )
    key_full, value_full = (
        lax.all_gather(key_rot, "ctx", axis=1, tiled=True),
        lax.all_gather(value_mix, "ctx", axis=1, tiled=True),
    )
    normed_two, inv_root_two, mlp_in, gate_proj, up_proj, hidden, output_flat = mlp_block(
        flat_tokens, attended_low, attn_set[4], mlp_set
    )
    cot_low = cotangent.reshape(token_count, model_width)
    cot_float = cot_low.astype(jnp.float32)
    grad_hidden = jnp.einsum("td,fd->tf", cot_low, mlp_set[3], preferred_element_type=jnp.float32)
    sigma = jax.nn.sigmoid(gate_proj)
    grad_gate_low = (grad_hidden * up_proj * sigma * (1.0 + gate_proj * (1.0 - sigma))).astype(
        jnp.bfloat16
    )
    grad_up_low = (grad_hidden * gate_proj * sigma).astype(jnp.bfloat16)
    grad_mlp_in = jnp.einsum(
        "tf,df->td", grad_gate_low, mlp_set[1], preferred_element_type=jnp.float32
    )
    grad_mlp_in = grad_mlp_in + jnp.einsum(
        "tf,df->td", grad_up_low, mlp_set[2], preferred_element_type=jnp.float32
    )
    grad_middle_norm, grad_gain_two = norm_back(grad_mlp_in, normed_two, inv_root_two, mlp_set[0])
    grad_middle = cot_float + grad_middle_norm
    grad_branch_low = grad_middle.astype(jnp.bfloat16)
    grad_attended = jnp.einsum(
        "te,de->td", grad_branch_low, attn_set[4], preferred_element_type=jnp.float32
    )
    grad_attended = grad_attended.astype(jnp.bfloat16).reshape(row_count, seq_piece, model_width)
    grad_query_rot, grad_key_full, grad_value_full = lax.map(
        attend_back, (query_rot, key_full, value_full, grad_attended, log_total, allowed)
    )
    grad_key_rot, grad_value_mix = (
        lax.psum_scatter(
            grad_key_full.astype(jnp.bfloat16), "ctx", scatter_dimension=1, tiled=True
        ).astype(jnp.float32),
        lax.psum_scatter(
            grad_value_full.astype(jnp.bfloat16), "ctx", scatter_dimension=1, tiled=True
        ).astype(jnp.float32),
    )
    v1_grad = v1_accum + 0.5 * grad_value_mix
    grad_query_low = rotate(
        grad_query_rot.reshape(row_count, seq_piece, HEADS, HEAD_DIM), cosine_table, -sine_table
    )
    grad_query_low = grad_query_low.astype(jnp.bfloat16).reshape(token_count, model_width)
    grad_key_low = rotate(
        grad_key_rot.reshape(row_count, seq_piece, HEADS, HEAD_DIM), cosine_table, -sine_table
    )
    grad_key_low = grad_key_low.astype(jnp.bfloat16).reshape(token_count, model_width)
    grad_value_low = (0.5 * grad_value_mix).astype(jnp.bfloat16).reshape(token_count, model_width)
    grad_normed_in = jnp.einsum(
        "te,de->td", grad_query_low, attn_set[1], preferred_element_type=jnp.float32
    )
    grad_normed_in = grad_normed_in + jnp.einsum(
        "te,de->td", grad_key_low, attn_set[2], preferred_element_type=jnp.float32
    )
    grad_normed_in = grad_normed_in + jnp.einsum(
        "te,de->td", grad_value_low, attn_set[3], preferred_element_type=jnp.float32
    )
    grad_input_norm, grad_gain_one = norm_back(grad_normed_in, normed, inv_root, attn_set[0])
    input_grad = (grad_middle + grad_input_norm).reshape(tokens.shape)
    attn_right = jnp.concatenate([grad_query_low, grad_key_low, grad_value_low], axis=1)
    left_in = normed_in
    projections = jnp.einsum("td,te->de", left_in, attn_right, preferred_element_type=jnp.float32)
    out_part = jnp.einsum(
        "td,te->de", attended_low, grad_branch_low, preferred_element_type=jnp.float32
    )
    attn_matrix = lax.psum_scatter(
        jnp.concatenate([projections, out_part], axis=1),
        ("dp", "ctx"),
        scatter_dimension=0,
        tiled=True,
    )
    mlp_right = jnp.concatenate([grad_gate_low, grad_up_low], axis=1)
    left_in = mlp_in
    gate_up_matrix = lax.psum_scatter(
        jnp.einsum("td,tf->df", left_in, mlp_right, preferred_element_type=jnp.float32),
        ("dp", "ctx"),
        scatter_dimension=0,
        tiled=True,
    )
    down_matrix = lax.psum_scatter(
        jnp.einsum("tf,td->fd", hidden, cot_low, preferred_element_type=jnp.float32),
        ("dp", "ctx"),
        scatter_dimension=0,
        tiled=True,
    )
    gain_one, gain_two = (
        lax.psum_scatter(grad_gain_one, ("dp", "ctx"), scatter_dimension=0, tiled=True),
        lax.psum_scatter(grad_gain_two, ("dp", "ctx"), scatter_dimension=0, tiled=True),
    )
    ff_width = w_gate.shape[1]
    return (
        output,
        input_grad,
        v1_grad,
        gain_one,
        attn_matrix[:, 0:model_width],
        attn_matrix[:, model_width : 2 * model_width],
        attn_matrix[:, 2 * model_width : 3 * model_width],
        attn_matrix[:, 3 * model_width : 4 * model_width],
        gain_two,
        gate_up_matrix[:, 0:ff_width],
        gate_up_matrix[:, ff_width : 2 * ff_width],
        down_matrix,
    )


def params(**kw):
    return pltpu.CompilerParams(vmem_limit_bytes=BYTES, **kw)


def dot(a, b, da, db):
    return lax.dot_general(a, b, (((da,), (db,)), ((), ())), preferred_element_type=F32)


def lane_block(index):
    return pl.ds(pl.multiple_of(index * LANES, LANES), LANES)


def half_swap(x):
    lane = lax.broadcasted_iota(jnp.int32, x.shape, 1)
    left = pltpu.roll(x, LANES - HEAD_DIM // 2, 1)
    right = pltpu.roll(x, HEAD_DIM // 2, 1)
    return jnp.where(lane % HEAD_DIM < HEAD_DIM // 2, left, right)


def head_lanes(x, head):
    lane = lax.broadcasted_iota(jnp.int32, x.shape, 1)
    return jnp.where(lane // HEAD_DIM == head, x, jnp.zeros_like(x))


def qkv_kernel(blocks, x_ref, w_ref, gain_ref, fv_ref, cos_ref, sin_ref, xn_ref, q_ref, k_ref, v_ref, rel):
    dp = lax.axis_index("dp")
    for d in range(blocks):
        rel[:, d * LANES : (d + 1) * LANES] = x_ref[:, lane_block(dp ^ d)].astype(F32)
    x = rel[...]
    inv = lax.rsqrt(jnp.mean(x * x, axis=-1, keepdims=True) + epsilon)
    xn = (x * inv * gain_ref[...]).astype(LOW)
    xn_ref[...] = xn
    width = q_ref.shape[1]
    proj = dot(xn, w_ref[...], 1, 0)
    cos, sin = cos_ref[...], sin_ref[...]
    for b in range(width // LANES):
        at = slice(b * LANES, (b + 1) * LANES)
        qb = proj[:, b * LANES : (b + 1) * LANES]
        q_ref[:, at] = ((qb * cos + half_swap(qb) * sin) * 0.125).astype(LOW)
        kb = proj[:, width + b * LANES : width + (b + 1) * LANES]
        k_ref[:, at] = (kb * cos + half_swap(kb) * sin).astype(LOW)
    v_ref[...] = (0.5 * proj[:, 2 * width :] + 0.5 * fv_ref[...].astype(F32)).astype(LOW)


def qkv_call(x, w, gain, fv, cos, sin):
    length, model = x.shape
    width = fv.shape[1]
    tb = TOKEN_BLOCK
    row = lambda cols: pl.BlockSpec((tb, cols), lambda i: (i, 0))
    whole = lambda a: pl.BlockSpec(a.shape, lambda i: (0, 0))
    return pl.pallas_call(
        functools.partial(qkv_kernel, model // LANES),
        grid=(length // tb,),
        in_specs=[row(model), whole(w), whole(gain), row(width), row(LANES), row(LANES)],
        out_specs=[row(model), row(width), row(width), row(width)],
        out_shape=[jax.ShapeDtypeStruct((length, model), LOW)]
        + [jax.ShapeDtypeStruct((length, width), LOW)] * 3,
        scratch_shapes=[pltpu.VMEM((tb, model), F32)],
        compiler_params=params(),
        cost_estimate=pl.CostEstimate(
            flops=2 * length * model * 3 * width, bytes_accessed=10 * 2**20, transcendentals=0
        ),
        name="qkv",
    )(x, w, gain, fv, cos, sin)


def attend_kernel(q_ref, k_ref, v_ref, sq_ref, sk_ref, o_ref, of_ref, lse_ref, s_ref, m_ref, l_ref, acc_ref):
    i = pl.program_id(0)
    tb = q_ref.shape[0]
    q = q_ref[...]
    seg_q = sq_ref[:, 0:1]
    lane = lax.broadcasted_iota(jnp.int32, (tb, LANES), 1)

    def fold(x, op):
        r = x[:, 0:LANES]
        for b in range(1, tb // LANES):
            r = op(r, x[:, b * LANES : (b + 1) * LANES])
        return r

    for head in range(2):
        qm = head_lanes(q, head)
        m_ref[...] = jnp.full_like(m_ref, NEG)

        def score(j, causal):
            at = pl.ds(pl.multiple_of(j * tb, tb), tb)
            s = dot(qm, k_ref[at, :], 1, 1)
            ok = seg_q == sk_ref[0:1, at]
            if causal:
                r = lax.broadcasted_iota(jnp.int32, (tb, tb), 0)
                c = lax.broadcasted_iota(jnp.int32, (tb, tb), 1)
                ok = ok & (r >= c)
            s = jnp.where(ok, s, NEG)
            s_ref[:, at] = s
            m_ref[...] = jnp.maximum(m_ref[...], fold(s, jnp.maximum))

        def score_step(j, carry):
            score(j, False)
            return carry

        lax.fori_loop(0, i, score_step, 0)
        score(i, True)
        top = jnp.max(m_ref[...], axis=1, keepdims=True)
        l_ref[...] = jnp.zeros_like(l_ref)
        acc_ref[...] = jnp.zeros_like(acc_ref)

        def value_step(j, carry):
            at = pl.ds(pl.multiple_of(j * tb, tb), tb)
            p = jnp.exp(s_ref[:, at] - top)
            l_ref[...] += fold(p, jnp.add)
            acc_ref[...] += dot(p.astype(LOW), v_ref[at, :], 1, 0)
            return carry

        lax.fori_loop(0, i + 1, value_step, 0)
        total = jnp.sum(l_ref[...], axis=1, keepdims=True)
        out = acc_ref[...] / total
        lse = jnp.broadcast_to(top + jnp.log(total), (tb, LANES))
        if head == 0:
            of_ref[...] = out
            lse_ref[...] = lse
        else:
            of_ref[...] = jnp.where(lane < HEAD_DIM, of_ref[...], out)
            lse_ref[...] = jnp.where(lane < HEAD_DIM, lse_ref[...], lse)
    o_ref[...] = of_ref[...].astype(LOW)


def attend_call(pair, q, k, v, seg_col, seg_row):
    length = q.shape[0]
    tb = TOKEN_BLOCK
    rows = pl.BlockSpec((tb, LANES), lambda i: (i, 0))
    full = pl.BlockSpec((length, LANES), lambda i: (0, pair))
    return pl.pallas_call(
        attend_kernel,
        grid=(length // tb,),
        in_specs=[
            pl.BlockSpec((tb, LANES), lambda i: (i, pair)),
            full,
            full,
            rows,
            pl.BlockSpec((8, length), lambda i: (0, 0)),
        ],
        out_specs=[rows, rows, rows],
        out_shape=[
            jax.ShapeDtypeStruct((length, LANES), LOW),
            jax.ShapeDtypeStruct((length, LANES), F32),
            jax.ShapeDtypeStruct((length, LANES), F32),
        ],
        scratch_shapes=[
            pltpu.VMEM((tb, length), F32),
            pltpu.VMEM((tb, LANES), F32),
            pltpu.VMEM((tb, LANES), F32),
            pltpu.VMEM((tb, LANES), F32),
        ],
        compiler_params=params(),
        cost_estimate=pl.CostEstimate(
            flops=8 * 10**9, bytes_accessed=6 * 2**20, transcendentals=length * length
        ),
        name="attend",
    )(q, k, v, seg_col, seg_row)


def attend_back_kernel(
    q_ref, k_ref, v_ref, g_ref, of_ref, lse_ref, sc_ref, sr_ref, cos_ref, sin_ref, out_ref,
    lse_row, delta_row, dq_acc, dk_acc, dv_acc,
):
    j = pl.program_id(0)
    steps = pl.num_programs(0)
    tb = dk_acc.shape[0]

    @pl.when(j == 0)
    def _():
        dq_acc[...] = jnp.zeros_like(dq_acc)
        r = lax.broadcasted_iota(jnp.int32, (8, LANES), 0)
        lane = lax.broadcasted_iota(jnp.int32, (8, LANES), 1)
        first = jnp.where(lane == r * HEAD_DIM, 1.0, 0.0)
        group = jnp.where(lane // HEAD_DIM == r, 1.0, 0.0)
        exact = lax.Precision.HIGHEST
        for b in range(lse_ref.shape[0] // tb):
            at = slice(b * tb, (b + 1) * tb)
            dims = (((1,), (1,)), ((), ()))
            lse_row[:, at] = lax.dot_general(first, lse_ref[at, :], dims, precision=exact, preferred_element_type=F32)
            prod = g_ref[at, :].astype(F32) * of_ref[at, :]
            delta_row[:, at] = lax.dot_general(group, prod, dims, precision=exact, preferred_element_type=F32)

    dk_acc[...] = jnp.zeros_like(dk_acc)
    dv_acc[...] = jnp.zeros_like(dv_acc)
    mine = pl.ds(pl.multiple_of(j * tb, tb), tb)
    k = k_ref[mine, :]
    v = v_ref[mine, :]
    seg_k = sc_ref[mine, 0:1]

    def block(i, causal):
        at = pl.ds(pl.multiple_of(i * tb, tb), tb)
        q = q_ref[at, :]
        g = g_ref[at, :]
        ok = seg_k == sr_ref[0:1, at]
        if causal:
            r = lax.broadcasted_iota(jnp.int32, (tb, tb), 0)
            c = lax.broadcasted_iota(jnp.int32, (tb, tb), 1)
            ok = ok & (r <= c)
        for head in range(2):
            qm = head_lanes(q, head)
            gm = head_lanes(g, head)
            s = dot(k, qm, 1, 1)
            p = jnp.where(ok, jnp.exp(s - lse_row[head : head + 1, at]), 0.0)
            dp = dot(v, gm, 1, 1)
            ds = (p * (dp - delta_row[head : head + 1, at])).astype(LOW)
            dv_acc[...] += dot(p.astype(LOW), gm, 1, 0)
            dk_acc[...] += dot(ds, qm, 1, 0)
            dq_acc[at, :] += dot(ds, head_lanes(k, head), 0, 0)

    block(j, True)

    def step(i, carry):
        block(i, False)
        return carry

    lax.fori_loop(j + 1, steps, step, 0)
    dk = dk_acc[...]
    dk = dk * cos_ref[mine, :] - half_swap(dk) * sin_ref[mine, :]
    out_ref[mine, LANES : 2 * LANES] = dk.astype(LOW)
    out_ref[mine, 2 * LANES : 3 * LANES] = dv_acc[...].astype(LOW)

    @pl.when(j == steps - 1)
    def _():
        for b in range(dq_acc.shape[0] // tb):
            at = slice(b * tb, (b + 1) * tb)
            dq = dq_acc[at, :] * 0.125
            dq = dq * cos_ref[at, :] - half_swap(dq) * sin_ref[at, :]
            out_ref[at, 0:LANES] = dq.astype(LOW)


def attend_back_call(pair, q, k, v, g, of, lse, seg_col, seg_row, cos, sin):
    length = q.shape[0]
    tb = TOKEN_BLOCK
    full = pl.BlockSpec((length, LANES), lambda j: (0, pair))
    own = pl.BlockSpec((length, LANES), lambda j: (0, 0))
    return pl.pallas_call(
        attend_back_kernel,
        grid=(length // tb,),
        in_specs=[full] * 4 + [own] * 3 + [pl.BlockSpec((8, length), lambda j: (0, 0))] + [own] * 2,
        out_specs=pl.BlockSpec((length, 3 * LANES), lambda j: (0, 0)),
        out_shape=jax.ShapeDtypeStruct((length, 3 * LANES), LOW),
        scratch_shapes=[
            pltpu.VMEM((8, length), F32),
            pltpu.VMEM((8, length), F32),
            pltpu.VMEM((length, LANES), F32),
            pltpu.VMEM((tb, LANES), F32),
            pltpu.VMEM((tb, LANES), F32),
        ],
        compiler_params=params(),
        cost_estimate=pl.CostEstimate(
            flops=20 * 10**9, bytes_accessed=8 * 2**20, transcendentals=length * length
        ),
        name="attend_back",
    )(q, k, v, g, of, lse, seg_col, seg_row, cos, sin)


def mlp_kernel(blocks, tok_ref, att_ref, cot_ref, gain_ref, *refs):
    pieces, refs = refs[: 3 * blocks], refs[3 * blocks :]
    go_in, up_in, dn_in = pieces[:blocks], pieces[blocks : 2 * blocks], pieces[2 * blocks :]
    out_ref, gm_ref, ga_ref, gk, gs, uk, us, ok, os, dk, ds = refs[:11]
    wo, wg, wu, wd, att, nat, n2, mi, mit, inv_ref, oacc, dacc, dwd, sem, osem = refs[11:]
    dp = lax.axis_index("dp")
    u = pl.program_id(0)
    last = pl.num_programs(0) - 1
    ff = wu.shape[1]
    down = dn_in[0].shape[0]

    def copies():
        made = []
        for d in range(blocks):
            at = pl.ds(d * LANES, LANES)
            made.append(pltpu.make_async_copy(go_in[d].at[:, pl.ds(ff, wo.shape[1])], wo.at[at, :], sem.at[0, d]))
        for d in range(blocks):
            at = pl.ds(d * LANES, LANES)
            made.append(pltpu.make_async_copy(go_in[d].at[:, pl.ds(0, ff)], wg.at[at, :], sem.at[1, d]))
            made.append(pltpu.make_async_copy(up_in[d], wu.at[at, :], sem.at[2, d]))
            rows = pl.ds(pl.multiple_of((dp ^ d) * down, 32), down)
            made.append(pltpu.make_async_copy(dn_in[d], wd.at[rows, :], sem.at[3, d]))
        return made

    def out_copies():
        made = []
        for d in range(blocks):
            rows = pl.ds(pl.multiple_of((dp ^ d) * down, 32), down)
            made.append(pltpu.make_async_copy(dwd.at[rows, :], (ds if d % 2 else dk).at[d // 2], osem.at[d]))
        return made

    @pl.when(u == 0)
    def _():
        made = copies()
        for c in made:
            c.start()
        for d in range(blocks):
            att[:, d * LANES : (d + 1) * LANES] = att_ref[:, lane_block(dp ^ d)]
        for c in made[:blocks]:
            c.wait()
        mid = tok_ref[...].astype(F32) + dot(att[...], wo[...], 1, 0)
        inv = lax.rsqrt(jnp.mean(mid * mid, axis=-1, keepdims=True) + epsilon)
        oacc[...] = mid
        nat[...] = mid * inv
        inv_ref[...] = jnp.broadcast_to(inv, inv_ref.shape)
        for d in range(blocks):
            n2[:, d * LANES : (d + 1) * LANES] = nat[:, lane_block(dp ^ d)]
        mi[...] = (n2[...] * gain_ref[...]).astype(LOW)
        mit[...] = mi[...].T
        dacc[...] = jnp.zeros_like(dacc)
        for c in made[blocks:]:
            c.wait()

    cols = pl.ds(pl.multiple_of(u * FF_BLOCK, FF_BLOCK), FF_BLOCK)
    x = mi[...]
    cot = cot_ref[...]
    wgu, wuu, wdu = wg[:, cols], wu[:, cols], wd[cols, :]
    gate = dot(x, wgu, 1, 0)
    up = dot(x, wuu, 1, 0)
    grad_hidden = dot(cot, wdu, 1, 1)
    sig = jax.nn.sigmoid(gate)
    hidden = (gate * sig * up).astype(LOW)
    dg = (grad_hidden * up * sig * (1.0 + gate * (1.0 - sig))).astype(LOW)
    du = (grad_hidden * gate * sig).astype(LOW)
    oacc[...] += dot(hidden, wdu, 1, 0)
    dacc[...] += dot(dg, wgu, 1, 1) + dot(du, wuu, 1, 1)
    xt = mit[...]
    dwg = dot(xt, dg, 1, 0).astype(LOW)
    dwu = dot(xt, du, 1, 0).astype(LOW)
    for d in range(blocks):
        (gs if d % 2 else gk)[d // 2] = dwg[d * LANES : (d + 1) * LANES]
        (us if d % 2 else uk)[d // 2] = dwu[d * LANES : (d + 1) * LANES]
    dwd[cols, :] = dot(hidden, cot, 0, 0).astype(LOW)

    @pl.when(u == last)
    def _():
        made = out_copies()
        for c in made:
            c.start()
        out_ref[...] = oacc[...].astype(LOW)
        scaled = dacc[...] * gain_ref[...]
        norm = n2[...]
        mean = jnp.mean(scaled * norm, axis=-1, keepdims=True)
        n2[...] = inv_ref[:, 0:1] * (scaled - norm * mean)
        for d in range(blocks):
            nat[:, lane_block(dp ^ d)] = n2[:, d * LANES : (d + 1) * LANES]
        gm = cot.astype(F32) + nat[...]
        gm_ref[...] = gm
        gb = gm.astype(LOW)
        n2[...] = dot(gb, wo[...], 1, 1)
        for d in range(blocks):
            ga_ref[:, lane_block(dp ^ d)] = n2[:, d * LANES : (d + 1) * LANES].astype(LOW)
        dwo = dot(att[...], gb, 0, 0).astype(LOW)
        for d in range(blocks):
            (os if d % 2 else ok)[d // 2] = dwo[d * LANES : (d + 1) * LANES]
        for c in made:
            c.wait()


def mlp_call(tok, att, cot, gain, go, up, dn):
    tb, model = tok.shape
    blocks = len(go)
    ff = up[0].shape[1]
    half = blocks // 2
    down = dn[0].shape[0]
    whole = lambda a: pl.BlockSpec(a.shape, lambda u: (0, 0))
    anyspace = pl.BlockSpec(memory_space=pl.ANY)
    half_cols = pl.BlockSpec((half, LANES, FF_BLOCK), lambda u: (0, 0, u))
    half_out = pl.BlockSpec((half, LANES, model), lambda u: (0, 0, 0))
    tokens = pl.BlockSpec((tb, model), lambda u: (0, 0))
    shape = jax.ShapeDtypeStruct
    return pl.pallas_call(
        functools.partial(mlp_kernel, blocks),
        grid=(ff // FF_BLOCK,),
        in_specs=[whole(tok), whole(att), whole(cot), whole(gain)] + [anyspace] * (3 * blocks),
        out_specs=[tokens, tokens, tokens] + [half_cols] * 4 + [half_out] * 2 + [anyspace] * 2,
        out_shape=[shape((tb, model), LOW), shape((tb, model), F32), shape((tb, model), LOW)]
        + [shape((half, LANES, ff), LOW)] * 4
        + [shape((half, LANES, model), LOW)] * 2
        + [shape((half, down, model), LOW)] * 2,
        scratch_shapes=[
            pltpu.VMEM((model, model), LOW),
            pltpu.VMEM((model, ff), LOW),
            pltpu.VMEM((model, ff), LOW),
            pltpu.VMEM((ff, model), LOW),
            pltpu.VMEM((tb, model), LOW),
            pltpu.VMEM((tb, model), F32),
            pltpu.VMEM((tb, model), F32),
            pltpu.VMEM((tb, model), LOW),
            pltpu.VMEM((model, tb), LOW),
            pltpu.VMEM((tb, LANES), F32),
            pltpu.VMEM((tb, model), F32),
            pltpu.VMEM((tb, model), F32),
            pltpu.VMEM((ff, model), LOW),
            pltpu.SemaphoreType.DMA((4, blocks)),
            pltpu.SemaphoreType.DMA((blocks,)),
        ],
        compiler_params=params(),
        cost_estimate=pl.CostEstimate(
            flops=2 * tb * model * (8 * ff + 3 * model), bytes_accessed=50 * 2**20, transcendentals=0
        ),
        name="mlp",
    )(tok, att, cot, gain, *go, *up, *dn)


def input_kernel(blocks, parts, tok_ref, gm_ref, v1_ref, gain_ref, *refs):
    w_in, refs = refs[:blocks], refs[blocks:]
    g_in, refs = refs[: 2 * parts], refs[2 * parts :]
    ig_ref, vg_ref, w, g, rel, nat, sem = refs
    dp = lax.axis_index("dp")
    c = lax.axis_index("ctx")
    model = tok_ref.shape[1]
    made = [pltpu.make_async_copy(w_in[d], w.at[pl.ds(d * LANES, LANES), :], sem.at[d]) for d in range(blocks)]
    for m in made:
        m.start()
    for d in range(blocks):
        rel[:, d * LANES : (d + 1) * LANES] = tok_ref[:, lane_block(dp ^ d)].astype(F32)
    for k in range(parts):
        source = lax.rem(c + parts - k, parts)
        for pair in range(2):
            for t in range(3):
                block = g_in[2 * k + pair][:, t * LANES : (t + 1) * LANES]
                g[:, pl.ds(pl.multiple_of(t * model + source * 2 * LANES + pair * LANES, LANES), LANES)] = block
    gv = g[:, 2 * model :].astype(F32)
    vg_ref[...] = v1_ref[...] + 0.5 * gv
    x = rel[...]
    inv = lax.rsqrt(jnp.mean(x * x, axis=-1, keepdims=True) + epsilon)
    norm = x * inv
    for m in made:
        m.wait()
    grad = dot(g[:, : 2 * model], w[:, : 2 * model], 1, 1)
    grad = grad + 0.5 * dot(g[:, 2 * model :], w[:, 2 * model :], 1, 1)
    scaled = grad * gain_ref[...]
    mean = jnp.mean(scaled * norm, axis=-1, keepdims=True)
    rel[...] = inv * (scaled - norm * mean)
    for d in range(blocks):
        nat[:, lane_block(dp ^ d)] = rel[:, d * LANES : (d + 1) * LANES]
    ig_ref[...] = gm_ref[...] + nat[...]


def input_call(tok, gm, v1, gain, ws, gs):
    tb, model = tok.shape
    blocks = len(ws)
    parts = len(gs) // 2
    vmem = pl.BlockSpec(memory_space=pltpu.VMEM)
    shape = jax.ShapeDtypeStruct
    return pl.pallas_call(
        functools.partial(input_kernel, blocks, parts),
        in_specs=[vmem] * 4 + [pl.BlockSpec(memory_space=pl.ANY)] * blocks + [vmem] * len(gs),
        out_specs=[vmem, vmem],
        out_shape=[shape((tb, model), F32)] * 2,
        scratch_shapes=[
            pltpu.VMEM((model, 3 * model), LOW),
            pltpu.VMEM((tb, 3 * model), LOW),
            pltpu.VMEM((tb, model), F32),
            pltpu.VMEM((tb, model), F32),
            pltpu.SemaphoreType.DMA((blocks,)),
        ],
        compiler_params=params(),
        cost_estimate=pl.CostEstimate(
            flops=2 * tb * model * 3 * model, bytes_accessed=20 * 2**20, transcendentals=0
        ),
        name="input_grad",
    )(tok, gm, v1, gain, *ws, *gs)


def fast_local(
    n_dp, n_ctx, tokens, first_values, v1_accum, segment_ids, positions, cotangent,
    attn_gain, w_query, w_key, w_value, w_out, mlp_gain, w_gate, w_up, w_down,
):
    c = lax.axis_index("ctx")
    seq, model = tokens.shape[1:]
    width = model // n_ctx
    length = seq * n_ctx
    ff = w_gate.shape[1]
    own_rows = w_query.shape[0]
    down_rows = w_down.shape[0]
    bits = [1 << b for b in range(n_dp.bit_length() - 1)]
    plane = bits[1:]

    def shift(x, k):
        return lax.ppermute(x, "ctx", [(i, (i + k) % n_ctx) for i in range(n_ctx)])

    def flip(x, bit):
        return lax.ppermute(x, "dp", [(i, i ^ bit) for i in range(n_dp)])

    def cut(x, index, size, axis):
        return lax.dynamic_slice_in_dim(x, index * size, size, axis)

    def swap_ctx(x, axis):
        size = x.shape[axis] // n_ctx
        return [cut(x, c, size, axis)] + [shift(cut(x, (c + k) % n_ctx, size, axis), k) for k in range(1, n_ctx)]

    def place(slots, axis):
        size = slots[0].shape[axis]
        dims = list(slots[0].shape)
        dims[axis] = size * n_ctx
        out = jnp.zeros(dims, slots[0].dtype)
        for k, slot in enumerate(slots):
            out = lax.dynamic_update_slice_in_dim(out, slot, ((c + n_ctx - k) % n_ctx) * size, axis)
        return out

    def gather_dp(x, order):
        got = {0: x}
        for bit in order:
            for d in sorted(got):
                got[d ^ bit] = flip(got[d], bit)
        return [got[d] for d in range(n_dp)]

    def gather_ctx(x):
        return lax.all_gather(x, "ctx", axis=0, tiled=True)

    tok = tokens[0]
    row_tokens = gather_ctx(tok)
    marks = jnp.concatenate([segment_ids, positions], axis=0)
    marks = place([marks] + [shift(marks, k) for k in range(1, n_ctx)], 1)
    head_first = place(swap_ctx(first_values[0], 1), 0)

    gains = jnp.stack([attn_gain, mlp_gain], axis=1)
    gains = jnp.tile(jnp.pad(gains, ((0, 0), (0, width - 2))), (1, n_ctx))
    packed = jnp.stack([w_query, w_key, w_value, gains])
    slots = jnp.stack(swap_ctx(packed, 2))
    slots = place([slots[k : k + 1] for k in range(n_ctx)], 0)
    slots = jnp.stack(gather_dp(slots, plane + bits[:1]))
    packed_all = slots.reshape(n_dp * n_ctx, 4, own_rows, width)
    head_weights = packed_all[:, :3].transpose(0, 2, 1, 3).reshape(model, 3 * width)
    gain_rel = packed_all[:, 3, :, 0].reshape(1, model).astype(F32)
    gain_two_rel = packed_all[:, 3, :, 1].reshape(1, model).astype(F32)

    go = gather_ctx(jnp.concatenate([w_gate, w_out], axis=1))
    up = gather_ctx(w_up)
    dn = gather_ctx(w_down)
    go = gather_dp(go, plane + bits[:1])
    up = gather_dp(up, plane[::-1] + bits[:1])
    dn = gather_dp(dn, plane[::-1] + bits[:1])

    seg_row = jnp.broadcast_to(marks[0:1], (8, length))
    seg_col = jnp.broadcast_to(marks[0][:, None], (length, LANES))
    freqs = 10000.0 ** (-jnp.arange(HEAD_DIM // 2).astype(F32) * (2.0 / HEAD_DIM))
    angles = marks[1].astype(F32)[:, None] * freqs
    cos, sin = jnp.cos(angles), jnp.sin(angles)
    cos = jnp.concatenate([cos] * 4, axis=1)
    sin = jnp.concatenate([-sin, sin] * 2, axis=1)
    xn, q, k, v = qkv_call(row_tokens, head_weights, gain_rel, head_first, cos, sin)
    pairs = width // LANES
    outs = [attend_call(p, q, k, v, seg_col, seg_row) for p in range(pairs)]
    attended = jnp.zeros((seq, model), LOW)
    for p in range(pairs):
        for s, slot in enumerate(swap_ctx(outs[p][0], 0)):
            at = ((c + n_ctx - s) % n_ctx) * width + p * LANES
            attended = lax.dynamic_update_slice_in_dim(attended, slot, at, 1)
    cot = cotangent[0]
    (output, grad_middle, grad_attended, gate_keep, gate_send, up_keep, up_send, out_keep, out_send,
     down_keep, down_send) = mlp_call(tok, attended, cot, gain_two_rel, go, up, dn)

    head_grad = place(swap_ctx(grad_attended, 1), 0)

    qkv_all = gather_dp(gather_ctx(jnp.concatenate([w_query, w_key, w_value], axis=1)), plane + bits[:1])

    back = [
        attend_back_call(p, q, k, v, head_grad, outs[p][1], outs[p][2], seg_col, seg_row, cos, sin)
        for p in range(pairs)
    ]

    def scatter_dp(keep, send, order):
        terms = [keep, flip(send, bits[0])]
        count = keep.shape[0]
        names = list(range(count))
        for bit in order:
            near = bit >> 1
            stay = [n for n in names if not n & near]
            leave = [n for n in names if n & near]

            def pick(which):
                return sum(
                    jnp.stack([t[names.index(n)] for n in which]).astype(F32) for t in terms
                )

            got = flip(pick(leave).astype(LOW), bit)
            terms = [jnp.stack([t[names.index(n)] for n in stay]) for t in terms] + [got]
            names = stay
        return sum(t[0].astype(F32) for t in terms)

    def scatter_ctx(x):
        size = x.shape[0] // n_ctx
        got = cut(x, c, size, 0)
        for k in range(1, n_ctx):
            got = got + shift(cut(x, (c + k) % n_ctx, size, 0).astype(LOW), k).astype(F32)
        return got

    gate_grad = scatter_ctx(scatter_dp(gate_keep, gate_send, plane))
    up_grad = scatter_ctx(scatter_dp(up_keep, up_send, plane[::-1]))
    down_grad = scatter_ctx(scatter_dp(down_keep, down_send, plane))
    out_grad = scatter_ctx(scatter_dp(out_keep, out_send, plane[::-1]))

    grads = [swap_ctx(b, 0) for b in back]
    qkv_grad = jnp.zeros((3, own_rows, model), F32)
    for p in range(pairs):
        product = lax.dot_general(
            xn, back[p], (((0,), (0,)), ((), ())), preferred_element_type=F32
        ).astype(LOW).reshape(n_dp // 2, 2, model // n_dp, 3 * LANES)
        total = scatter_dp(product[:, 0], product[:, 1], plane)
        for s, slot in enumerate(swap_ctx(total.astype(LOW), 0)):
            block = slot.astype(F32).reshape(own_rows, 3, LANES).transpose(1, 0, 2)
            at = ((c + n_ctx - s) % n_ctx) * width + p * LANES
            qkv_grad = lax.dynamic_update_slice_in_dim(qkv_grad, block, at, 2)
    query_grad, key_grad, value_grad = qkv_grad[0], qkv_grad[1], 0.5 * qkv_grad[2]

    input_grad, v1_grad = input_call(
        tok, grad_middle, v1_accum[0], gain_rel, qkv_all, [grads[p][s] for s in range(n_ctx) for p in range(pairs)]
    )

    def row_dot(a, w):
        return jnp.sum(a * w.astype(F32), axis=1)

    gain_one = (
        row_dot(query_grad, w_query) + row_dot(key_grad, w_key) + row_dot(value_grad, w_value)
    ) / attn_gain.astype(F32)
    gain_two = (row_dot(gate_grad, w_gate) + row_dot(up_grad, w_up)) / mlp_gain.astype(F32)
    return (
        output[None], input_grad[None], v1_grad[None], gain_one, query_grad, key_grad, value_grad,
        out_grad, gain_two, gate_grad, up_grad, down_grad,
    )


def solution(mesh):
    placed = (
        P("dp", "ctx", None),
        P("dp", "ctx", None),
        P("dp", "ctx", None),
        P("dp", "ctx"),
        P("dp", "ctx"),
        P("dp", "ctx", None),
        P(("dp", "ctx")),
        P(("dp", "ctx"), None),
        P(("dp", "ctx"), None),
        P(("dp", "ctx"), None),
        P(("dp", "ctx"), None),
        P(("dp", "ctx")),
        P(("dp", "ctx"), None),
        P(("dp", "ctx"), None),
        P(("dp", "ctx"), None),
    )
    n_dp, n_ctx = mesh.shape["dp"], mesh.shape["ctx"]

    def local(*args):
        rows, seq, model = args[0].shape
        fits = (
            rows == 1
            and seq == TOKEN_BLOCK
            and model == n_dp * LANES
            and model == 2 * LANES * n_ctx
            and args[12].shape[1] % FF_BLOCK == 0
        )
        return fast_local(n_dp, n_ctx, *args) if fits else plain_local(*args)

    return jax.shard_map(
        local,
        mesh=mesh,
        in_specs=placed,
        out_specs=(
            P("dp", "ctx", None),
            P("dp", "ctx", None),
            P("dp", "ctx", None),
            P(("dp", "ctx")),
            P(("dp", "ctx"), None),
            P(("dp", "ctx"), None),
            P(("dp", "ctx"), None),
            P(("dp", "ctx"), None),
            P(("dp", "ctx")),
            P(("dp", "ctx"), None),
            P(("dp", "ctx"), None),
            P(("dp", "ctx"), None),
        ),
        check_vma=False,
    )
```

```python
import functools

import jax
import jax.numpy as jnp
from jax import lax
from jax.experimental import pallas as pl
from jax.experimental.pallas import tpu as pltpu
from jax.sharding import PartitionSpec as P

HEADS = 16
HEAD_DIM = 64
LANES = 128
TOKEN_BLOCK = 512
FF_BLOCK = 256
NEG = -1e30
MESH = pl.DeviceIdType.MESH
F32 = jnp.float32
LOW = jnp.bfloat16
BYTES = 60 * 2**20
epsilon = 1e-05


HEAD_BLOCK = 4


def rms_scale(values):
    return lax.rsqrt(jnp.mean(values * values, axis=-1, keepdims=True) + epsilon)


def angle_tables(position_rows):
    freqs = 10000.0 ** (-jnp.arange(HEAD_DIM // 2).astype(jnp.float32) * (2.0 / HEAD_DIM))
    angles = position_rows.astype(jnp.float32)[..., None] * freqs
    return (jnp.cos(angles)[..., None, :], jnp.sin(angles)[..., None, :])


def rotate(heads_in, cosine_table, sine_table):
    half_dim = heads_in.shape[-1] // 2
    first_half = heads_in[..., :half_dim]
    second_half = heads_in[..., half_dim:]
    return jnp.concatenate(
        [
            first_half * cosine_table - second_half * sine_table,
            second_half * cosine_table + first_half * sine_table,
        ],
        axis=-1,
    )


def norm_back(grad_normed, normed, inv_root, norm_gain):
    grad_scaled = grad_normed * norm_gain.astype(jnp.float32)
    grad_input = inv_root * (
        grad_scaled - normed * jnp.mean(grad_scaled * normed, axis=-1, keepdims=True)
    )
    return (grad_input, jnp.sum(grad_normed * normed, axis=0))


def attn_front(flat_tokens, first_flat, attn_set, cosine_table, sine_table, row_count, seq_piece):
    inv_root = rms_scale(flat_tokens)
    normed = flat_tokens * inv_root
    normed_in = (normed * attn_set[0].astype(jnp.float32)).astype(jnp.bfloat16)
    query_proj = jnp.dot(normed_in, attn_set[1], preferred_element_type=jnp.float32)
    key_proj = jnp.dot(normed_in, attn_set[2], preferred_element_type=jnp.float32)
    value_proj = jnp.dot(normed_in, attn_set[3], preferred_element_type=jnp.float32)
    query_rot = rotate(
        query_proj.reshape(row_count, seq_piece, HEADS, HEAD_DIM), cosine_table, sine_table
    )
    key_rot = rotate(
        key_proj.reshape(row_count, seq_piece, HEADS, HEAD_DIM), cosine_table, sine_table
    )
    query_rot = query_rot.astype(jnp.bfloat16).reshape(row_count, seq_piece, -1)
    key_rot = key_rot.astype(jnp.bfloat16).reshape(row_count, seq_piece, -1)
    value_mix = (
        (0.5 * value_proj + 0.5 * first_flat).astype(jnp.bfloat16).reshape(row_count, seq_piece, -1)
    )
    return (normed, inv_root, normed_in, query_rot, key_rot, value_mix)


def mlp_block(flat_tokens, attended_low, out_weight, mlp_set):
    middle = flat_tokens + jnp.dot(attended_low, out_weight, preferred_element_type=jnp.float32)
    inv_root_two = rms_scale(middle)
    normed_two = middle * inv_root_two
    mlp_in = (normed_two * mlp_set[0].astype(jnp.float32)).astype(jnp.bfloat16)
    gate_proj = jnp.dot(mlp_in, mlp_set[1], preferred_element_type=jnp.float32)
    up_proj = jnp.dot(mlp_in, mlp_set[2], preferred_element_type=jnp.float32)
    hidden = (gate_proj * jax.nn.sigmoid(gate_proj) * up_proj).astype(jnp.bfloat16)
    result = middle + jnp.dot(hidden, mlp_set[3], preferred_element_type=jnp.float32)
    return (normed_two, inv_root_two, mlp_in, gate_proj, up_proj, hidden, result)


def split_groups(row_block):
    tok_count = row_block.shape[0]
    return row_block.reshape(tok_count, HEADS // HEAD_BLOCK, HEAD_BLOCK * HEAD_DIM).transpose(
        1, 0, 2
    )


def join_groups(group_block):
    return group_block.transpose(1, 0, 2).reshape(group_block.shape[1], -1)


def as_heads(block):
    return block.reshape(block.shape[0], HEAD_BLOCK, HEAD_DIM)


def attend_row(members):
    query_row, key_row, value_row, allowed = members

    def per_group(pieces):
        query_block, key_block, value_block = pieces
        scores = (
            jnp.einsum(
                "qhd,khd->hqk",
                as_heads(query_block),
                as_heads(key_block),
                preferred_element_type=jnp.float32,
            )
            * 0.125
        )
        scores = jnp.where(allowed[None], scores, -1e30)
        highest = jnp.max(scores, axis=-1, keepdims=True)
        exp_scores = jnp.exp(scores - highest)
        denominator = jnp.sum(exp_scores, axis=-1, keepdims=True)
        soft_low = (exp_scores / denominator).astype(jnp.bfloat16)
        attended = jnp.einsum(
            "hqk,khd->qhd", soft_low, as_heads(value_block), preferred_element_type=jnp.float32
        )
        return (
            attended.reshape(query_block.shape[0], -1),
            (highest + jnp.log(denominator))[..., 0],
        )

    attended, log_total = lax.map(
        per_group, (split_groups(query_row), split_groups(key_row), split_groups(value_row))
    )
    return (join_groups(attended), log_total)


def attend_back(members):
    query_row, key_row, value_row, grad_row, log_total, allowed = members

    def per_group(pieces):
        query_block, key_block, value_block, grad_block, log_block = pieces
        query_heads = as_heads(query_block)
        key_heads = as_heads(key_block)
        grad_heads = as_heads(grad_block)
        scores = (
            jnp.einsum("qhd,khd->hqk", query_heads, key_heads, preferred_element_type=jnp.float32)
            * 0.125
        )
        soft_weights = jnp.where(allowed[None], jnp.exp(scores - log_block[..., None]), 0.0)
        soft_low = soft_weights.astype(jnp.bfloat16)
        grad_probs = jnp.einsum(
            "qhd,khd->hqk", grad_heads, as_heads(value_block), preferred_element_type=jnp.float32
        )
        row_delta = jnp.sum(soft_weights * grad_probs, axis=-1, keepdims=True)
        grad_scores = (soft_weights * (grad_probs - row_delta)).astype(jnp.bfloat16)
        grad_query = (
            jnp.einsum("hqk,khd->qhd", grad_scores, key_heads, preferred_element_type=jnp.float32)
            * 0.125
        )
        grad_key = (
            jnp.einsum("hqk,qhd->khd", grad_scores, query_heads, preferred_element_type=jnp.float32)
            * 0.125
        )
        grad_value = jnp.einsum(
            "hqk,qhd->khd", soft_low, grad_heads, preferred_element_type=jnp.float32
        )
        return (
            grad_query.reshape(query_block.shape[0], -1),
            grad_key.reshape(key_block.shape[0], -1),
            grad_value.reshape(key_block.shape[0], -1),
        )

    grad_query, grad_key, grad_value = lax.map(
        per_group,
        (
            split_groups(query_row),
            split_groups(key_row),
            split_groups(value_row),
            split_groups(grad_row),
            log_total,
        ),
    )
    return (join_groups(grad_query), join_groups(grad_key), join_groups(grad_value))


def plain_local(
    tokens,
    first_values,
    v1_accum,
    segment_ids,
    positions,
    cotangent,
    attn_gain,
    w_query,
    w_key,
    w_value,
    w_out,
    mlp_gain,
    w_gate,
    w_up,
    w_down,
):
    row_count, seq_piece, model_width = tokens.shape
    token_count = row_count * seq_piece
    flat_tokens = tokens.astype(jnp.float32).reshape(token_count, model_width)
    first_flat = first_values.astype(jnp.float32).reshape(token_count, model_width)
    cosine_table, sine_table = angle_tables(positions)
    segment_low = segment_ids.astype(jnp.bfloat16)
    attn_set = (
        lax.all_gather(attn_gain, ("dp", "ctx"), axis=0, tiled=True),
        lax.all_gather(w_query, ("dp", "ctx"), axis=0, tiled=True),
        lax.all_gather(w_key, ("dp", "ctx"), axis=0, tiled=True),
        lax.all_gather(w_value, ("dp", "ctx"), axis=0, tiled=True),
        lax.all_gather(w_out, ("dp", "ctx"), axis=0, tiled=True),
    )
    normed, inv_root, normed_in, query_rot, key_rot, value_mix = attn_front(
        flat_tokens, first_flat, attn_set, cosine_table, sine_table, row_count, seq_piece
    )
    key_full, value_full, segment_full = (
        lax.all_gather(key_rot, "ctx", axis=1, tiled=True),
        lax.all_gather(value_mix, "ctx", axis=1, tiled=True),
        lax.all_gather(segment_low, "ctx", axis=1, tiled=True),
    )
    query_order = lax.axis_index("ctx") * seq_piece + jnp.arange(seq_piece, dtype=jnp.int32)
    full_order = jnp.arange(key_full.shape[1], dtype=jnp.int32)
    segment_own = segment_ids.astype(jnp.float32)
    segment_all = segment_full.astype(jnp.float32)
    allowed = (segment_own[:, :, None] == segment_all[:, None, :]) & (
        query_order[None, :, None] >= full_order[None, None, :]
    )
    attended, log_total = lax.map(attend_row, (query_rot, key_full, value_full, allowed))
    attended_low = attended.reshape(token_count, model_width).astype(jnp.bfloat16)
    mlp_set = (
        lax.all_gather(mlp_gain, ("dp", "ctx"), axis=0, tiled=True),
        lax.all_gather(w_gate, ("dp", "ctx"), axis=0, tiled=True),
        lax.all_gather(w_up, ("dp", "ctx"), axis=0, tiled=True),
        lax.all_gather(w_down, ("dp", "ctx"), axis=0, tiled=True),
    )
    normed_two, inv_root_two, mlp_in, gate_proj, up_proj, hidden, output_flat = mlp_block(
        flat_tokens, attended_low, attn_set[4], mlp_set
    )
    output = output_flat.reshape(tokens.shape).astype(jnp.bfloat16)
    attn_set = (
        lax.all_gather(attn_gain, ("dp", "ctx"), axis=0, tiled=True),
        lax.all_gather(w_query, ("dp", "ctx"), axis=0, tiled=True),
        lax.all_gather(w_key, ("dp", "ctx"), axis=0, tiled=True),
        lax.all_gather(w_value, ("dp", "ctx"), axis=0, tiled=True),
        lax.all_gather(w_out, ("dp", "ctx"), axis=0, tiled=True),
    )
    mlp_set = (
        lax.all_gather(mlp_gain, ("dp", "ctx"), axis=0, tiled=True),
        lax.all_gather(w_gate, ("dp", "ctx"), axis=0, tiled=True),
        lax.all_gather(w_up, ("dp", "ctx"), axis=0, tiled=True),
        lax.all_gather(w_down, ("dp", "ctx"), axis=0, tiled=True),
    )
    normed, inv_root, normed_in, query_rot, key_rot, value_mix = attn_front(
        flat_tokens, first_flat, attn_set, cosine_table, sine_table, row_count, seq_piece
    )
    key_full, value_full = (
        lax.all_gather(key_rot, "ctx", axis=1, tiled=True),
        lax.all_gather(value_mix, "ctx", axis=1, tiled=True),
    )
    normed_two, inv_root_two, mlp_in, gate_proj, up_proj, hidden, output_flat = mlp_block(
        flat_tokens, attended_low, attn_set[4], mlp_set
    )
    cot_low = cotangent.reshape(token_count, model_width)
    cot_float = cot_low.astype(jnp.float32)
    grad_hidden = jnp.einsum("td,fd->tf", cot_low, mlp_set[3], preferred_element_type=jnp.float32)
    sigma = jax.nn.sigmoid(gate_proj)
    grad_gate_low = (grad_hidden * up_proj * sigma * (1.0 + gate_proj * (1.0 - sigma))).astype(
        jnp.bfloat16
    )
    grad_up_low = (grad_hidden * gate_proj * sigma).astype(jnp.bfloat16)
    grad_mlp_in = jnp.einsum(
        "tf,df->td", grad_gate_low, mlp_set[1], preferred_element_type=jnp.float32
    )
    grad_mlp_in = grad_mlp_in + jnp.einsum(
        "tf,df->td", grad_up_low, mlp_set[2], preferred_element_type=jnp.float32
    )
    grad_middle_norm, grad_gain_two = norm_back(grad_mlp_in, normed_two, inv_root_two, mlp_set[0])
    grad_middle = cot_float + grad_middle_norm
    grad_branch_low = grad_middle.astype(jnp.bfloat16)
    grad_attended = jnp.einsum(
        "te,de->td", grad_branch_low, attn_set[4], preferred_element_type=jnp.float32
    )
    grad_attended = grad_attended.astype(jnp.bfloat16).reshape(row_count, seq_piece, model_width)
    grad_query_rot, grad_key_full, grad_value_full = lax.map(
        attend_back, (query_rot, key_full, value_full, grad_attended, log_total, allowed)
    )
    grad_key_rot, grad_value_mix = (
        lax.psum_scatter(
            grad_key_full.astype(jnp.bfloat16), "ctx", scatter_dimension=1, tiled=True
        ).astype(jnp.float32),
        lax.psum_scatter(
            grad_value_full.astype(jnp.bfloat16), "ctx", scatter_dimension=1, tiled=True
        ).astype(jnp.float32),
    )
    v1_grad = v1_accum + 0.5 * grad_value_mix
    grad_query_low = rotate(
        grad_query_rot.reshape(row_count, seq_piece, HEADS, HEAD_DIM), cosine_table, -sine_table
    )
    grad_query_low = grad_query_low.astype(jnp.bfloat16).reshape(token_count, model_width)
    grad_key_low = rotate(
        grad_key_rot.reshape(row_count, seq_piece, HEADS, HEAD_DIM), cosine_table, -sine_table
    )
    grad_key_low = grad_key_low.astype(jnp.bfloat16).reshape(token_count, model_width)
    grad_value_low = (0.5 * grad_value_mix).astype(jnp.bfloat16).reshape(token_count, model_width)
    grad_normed_in = jnp.einsum(
        "te,de->td", grad_query_low, attn_set[1], preferred_element_type=jnp.float32
    )
    grad_normed_in = grad_normed_in + jnp.einsum(
        "te,de->td", grad_key_low, attn_set[2], preferred_element_type=jnp.float32
    )
    grad_normed_in = grad_normed_in + jnp.einsum(
        "te,de->td", grad_value_low, attn_set[3], preferred_element_type=jnp.float32
    )
    grad_input_norm, grad_gain_one = norm_back(grad_normed_in, normed, inv_root, attn_set[0])
    input_grad = (grad_middle + grad_input_norm).reshape(tokens.shape)
    attn_right = jnp.concatenate([grad_query_low, grad_key_low, grad_value_low], axis=1)
    left_in = normed_in
    projections = jnp.einsum("td,te->de", left_in, attn_right, preferred_element_type=jnp.float32)
    out_part = jnp.einsum(
        "td,te->de", attended_low, grad_branch_low, preferred_element_type=jnp.float32
    )
    attn_matrix = lax.psum_scatter(
        jnp.concatenate([projections, out_part], axis=1),
        ("dp", "ctx"),
        scatter_dimension=0,
        tiled=True,
    )
    mlp_right = jnp.concatenate([grad_gate_low, grad_up_low], axis=1)
    left_in = mlp_in
    gate_up_matrix = lax.psum_scatter(
        jnp.einsum("td,tf->df", left_in, mlp_right, preferred_element_type=jnp.float32),
        ("dp", "ctx"),
        scatter_dimension=0,
        tiled=True,
    )
    down_matrix = lax.psum_scatter(
        jnp.einsum("tf,td->fd", hidden, cot_low, preferred_element_type=jnp.float32),
        ("dp", "ctx"),
        scatter_dimension=0,
        tiled=True,
    )
    gain_one, gain_two = (
        lax.psum_scatter(grad_gain_one, ("dp", "ctx"), scatter_dimension=0, tiled=True),
        lax.psum_scatter(grad_gain_two, ("dp", "ctx"), scatter_dimension=0, tiled=True),
    )
    ff_width = w_gate.shape[1]
    return (
        output,
        input_grad,
        v1_grad,
        gain_one,
        attn_matrix[:, 0:model_width],
        attn_matrix[:, model_width : 2 * model_width],
        attn_matrix[:, 2 * model_width : 3 * model_width],
        attn_matrix[:, 3 * model_width : 4 * model_width],
        gain_two,
        gate_up_matrix[:, 0:ff_width],
        gate_up_matrix[:, ff_width : 2 * ff_width],
        down_matrix,
    )


def params(**kw):
    return pltpu.CompilerParams(vmem_limit_bytes=BYTES, **kw)


def dot(a, b, da, db):
    return lax.dot_general(a, b, (((da,), (db,)), ((), ())), preferred_element_type=F32)


def lane_block(index):
    return pl.ds(pl.multiple_of(index * LANES, LANES), LANES)


def half_swap(x):
    lane = lax.broadcasted_iota(jnp.int32, x.shape, 1)
    left = pltpu.roll(x, LANES - HEAD_DIM // 2, 1)
    right = pltpu.roll(x, HEAD_DIM // 2, 1)
    return jnp.where(lane % HEAD_DIM < HEAD_DIM // 2, left, right)


def head_lanes(x, head):
    lane = lax.broadcasted_iota(jnp.int32, x.shape, 1)
    return jnp.where(lane // HEAD_DIM == head, x, jnp.zeros_like(x))


def qkv_kernel(blocks, x_ref, w_ref, gain_ref, fv_ref, cos_ref, sin_ref, xn_ref, q_ref, k_ref, v_ref, rel):
    dp = lax.axis_index("dp")
    for d in range(blocks):
        rel[:, d * LANES : (d + 1) * LANES] = x_ref[:, lane_block(dp ^ d)].astype(F32)
    x = rel[...]
    inv = lax.rsqrt(jnp.mean(x * x, axis=-1, keepdims=True) + epsilon)
    xn = (x * inv * gain_ref[...]).astype(LOW)
    xn_ref[...] = xn
    width = q_ref.shape[1]
    proj = dot(xn, w_ref[...], 1, 0)
    cos, sin = cos_ref[...], sin_ref[...]
    for b in range(width // LANES):
        at = slice(b * LANES, (b + 1) * LANES)
        qb = proj[:, b * LANES : (b + 1) * LANES]
        q_ref[:, at] = ((qb * cos + half_swap(qb) * sin) * 0.125).astype(LOW)
        kb = proj[:, width + b * LANES : width + (b + 1) * LANES]
        k_ref[:, at] = (kb * cos + half_swap(kb) * sin).astype(LOW)
    v_ref[...] = (0.5 * proj[:, 2 * width :] + 0.5 * fv_ref[...].astype(F32)).astype(LOW)


def qkv_call(x, w, gain, fv, cos, sin):
    length, model = x.shape
    width = fv.shape[1]
    tb = TOKEN_BLOCK
    row = lambda cols: pl.BlockSpec((tb, cols), lambda i: (i, 0))
    whole = lambda a: pl.BlockSpec(a.shape, lambda i: (0, 0))
    return pl.pallas_call(
        functools.partial(qkv_kernel, model // LANES),
        grid=(length // tb,),
        in_specs=[row(model), whole(w), whole(gain), row(width), row(LANES), row(LANES)],
        out_specs=[row(model), row(width), row(width), row(width)],
        out_shape=[jax.ShapeDtypeStruct((length, model), LOW)]
        + [jax.ShapeDtypeStruct((length, width), LOW)] * 3,
        scratch_shapes=[pltpu.VMEM((tb, model), F32)],
        compiler_params=params(),
        cost_estimate=pl.CostEstimate(
            flops=2 * length * model * 3 * width, bytes_accessed=10 * 2**20, transcendentals=0
        ),
        name="qkv",
    )(x, w, gain, fv, cos, sin)


def meet_ctx(n_ctx):
    c = lax.axis_index("ctx")
    barrier = pltpu.get_barrier_semaphore()
    for k in range(1, n_ctx):
        pl.semaphore_signal(barrier, inc=1, device_id={"ctx": lax.rem(c + k, n_ctx)}, device_id_type=MESH)
    pl.semaphore_wait(barrier, n_ctx - 1)


def ctx_copy(src, dst, send, recv, to):
    return pltpu.make_async_remote_copy(
        src_ref=src, dst_ref=dst, send_sem=send, recv_sem=recv, device_id={"ctx": to}, device_id_type=MESH
    )


def attend_kernel(n_ctx, q_ref, k_ref, v_ref, sq_ref, sk_ref, att_ref, of_ref, lse_ref,
                  o_ref, s_ref, m_ref, l_ref, acc_ref, send, recv, own):
    c = lax.axis_index("ctx")
    tb = m_ref.shape[0]
    width = q_ref.shape[1]
    lane = lax.broadcasted_iota(jnp.int32, (tb, LANES), 1)
    meet_ctx(n_ctx)

    def fold(x, op):
        r = x[:, 0:LANES]
        for b in range(1, tb // LANES):
            r = op(r, x[:, b * LANES : (b + 1) * LANES])
        return r

    def home(pair):
        return att_ref.at[:, pl.ds(pl.multiple_of(c * width + pair * LANES, LANES), LANES)]

    for pair in range(width // LANES):
        cols = slice(pair * LANES, (pair + 1) * LANES)

        def query_block(i, carry):
            mine = pl.ds(pl.multiple_of(i * tb, tb), tb)
            q = q_ref[mine, cols]
            seg_q = sq_ref[mine, 0:1]
            for head in range(2):
                qm = head_lanes(q, head)
                m_ref[...] = jnp.full_like(m_ref, NEG)

                def score(j, causal):
                    at = pl.ds(pl.multiple_of(j * tb, tb), tb)
                    s = dot(qm, k_ref[at, cols], 1, 1)
                    ok = seg_q == sk_ref[0:1, at]
                    if causal:
                        r = lax.broadcasted_iota(jnp.int32, (tb, tb), 0)
                        t = lax.broadcasted_iota(jnp.int32, (tb, tb), 1)
                        ok = ok & (r >= t)
                    s = jnp.where(ok, s, NEG)
                    s_ref[:, at] = s
                    m_ref[...] = jnp.maximum(m_ref[...], fold(s, jnp.maximum))

                def score_step(j, carry):
                    score(j, False)
                    return carry

                lax.fori_loop(0, i, score_step, 0)
                score(i, True)
                top = jnp.max(m_ref[...], axis=1, keepdims=True)
                l_ref[...] = jnp.zeros_like(l_ref)
                acc_ref[...] = jnp.zeros_like(acc_ref)

                def value_step(j, carry):
                    at = pl.ds(pl.multiple_of(j * tb, tb), tb)
                    p = jnp.exp(s_ref[:, at] - top)
                    l_ref[...] += fold(p, jnp.add)
                    acc_ref[...] += dot(p.astype(LOW), v_ref[at, cols], 1, 0)
                    return carry

                lax.fori_loop(0, i + 1, value_step, 0)
                total = jnp.sum(l_ref[...], axis=1, keepdims=True)
                out = acc_ref[...] / total
                lse = jnp.broadcast_to(top + jnp.log(total), (tb, LANES))
                if head == 0:
                    of_ref[mine, cols] = out
                    lse_ref[mine, cols] = lse
                else:
                    of_ref[mine, cols] = jnp.where(lane < HEAD_DIM, of_ref[mine, cols], out)
                    lse_ref[mine, cols] = jnp.where(lane < HEAD_DIM, lse_ref[mine, cols], lse)
            o_ref[mine, cols] = of_ref[mine, cols].astype(LOW)

            @pl.when(i == c)
            def _():
                pltpu.make_async_copy(o_ref.at[mine, cols], home(pair), own.at[pair]).start()

            @pl.when(i != c)
            def _():
                k = lax.rem(i + n_ctx - c, n_ctx) - 1
                ctx_copy(o_ref.at[mine, cols], home(pair), send.at[k, pair], recv.at[k, pair], i).start()

            return carry

        lax.fori_loop(0, n_ctx, query_block, 0)
    for pair in range(width // LANES):
        cols = slice(pair * LANES, (pair + 1) * LANES)
        pltpu.make_async_copy(o_ref.at[0:tb, cols], home(pair), own.at[pair]).wait()
        for k in range(n_ctx - 1):
            ctx_copy(o_ref.at[0:tb, cols], home(pair), send.at[k, pair], recv.at[k, pair], c).wait()


def attend_call(n_ctx, q, k, v, seg_col, seg_row):
    length, width = q.shape
    tb = TOKEN_BLOCK
    pairs = width // LANES
    vmem = pl.BlockSpec(memory_space=pltpu.VMEM)
    return pl.pallas_call(
        functools.partial(attend_kernel, n_ctx),
        in_specs=[vmem] * 5,
        out_specs=[pl.BlockSpec(memory_space=pl.ANY), vmem, vmem],
        out_shape=[
            jax.ShapeDtypeStruct((tb, n_ctx * width), LOW),
            jax.ShapeDtypeStruct((length, width), F32),
            jax.ShapeDtypeStruct((length, width), F32),
        ],
        scratch_shapes=[
            pltpu.VMEM((length, width), LOW),
            pltpu.VMEM((tb, length), F32),
            pltpu.VMEM((tb, LANES), F32),
            pltpu.VMEM((tb, LANES), F32),
            pltpu.VMEM((tb, LANES), F32),
            pltpu.SemaphoreType.DMA((n_ctx - 1, pairs)),
            pltpu.SemaphoreType.DMA((n_ctx - 1, pairs)),
            pltpu.SemaphoreType.DMA((pairs,)),
        ],
        compiler_params=params(collective_id=1, has_side_effects=True),
        cost_estimate=pl.CostEstimate(
            flops=16 * 10**9, bytes_accessed=12 * 2**20, transcendentals=2 * length * length
        ),
        name="attend",
    )(q, k, v, seg_col, seg_row)


def attend_back_kernel(
    n_ctx, ga_ref, q_ref, k_ref, v_ref, of_ref, lse_ref, sc_ref, sr_ref, cos_ref, sin_ref, out_ref, home_ref,
    g_ref, lse_row, delta_row, dq_acc, dk_acc, dv_acc, gsend, grecv, send, recv, own,
):
    c = lax.axis_index("ctx")
    tb = dk_acc.shape[0]
    length, width = q_ref.shape
    model = n_ctx * width
    meet_ctx(n_ctx)

    def grad_copy(k, to):
        rows = pl.ds(pl.multiple_of(c * tb, tb), tb)
        cols = pl.ds(pl.multiple_of(to * width, width), width)
        return ctx_copy(ga_ref.at[:, cols], g_ref.at[rows, :], gsend.at[k - 1], grecv.at[k - 1], to)

    def home(pair, t):
        return home_ref.at[:, pl.ds(pl.multiple_of(t * model + c * width + pair * LANES, LANES), LANES)]

    def part(pair, t, chunk):
        rows = pl.ds(pl.multiple_of(chunk * tb, tb), tb)
        return out_ref.at[pair, rows, t * LANES : (t + 1) * LANES]

    def part_copy(pair, t, k):
        to = lax.rem(c + k, n_ctx)
        return ctx_copy(part(pair, t, to), home(pair, t), send.at[k - 1, pair, t], recv.at[k - 1, pair, t], to)

    first = [grad_copy(k, lax.rem(c + k, n_ctx)) for k in range(1, n_ctx)]
    for f in first:
        f.start()
    keep = pltpu.make_async_copy(
        ga_ref.at[:, pl.ds(pl.multiple_of(c * width, width), width)],
        g_ref.at[pl.ds(pl.multiple_of(c * tb, tb), tb), :],
        own.at[0, 0],
    )
    keep.start()
    keep.wait()
    for f in first:
        f.wait()

    r8 = lax.broadcasted_iota(jnp.int32, (8, LANES), 0)
    l8 = lax.broadcasted_iota(jnp.int32, (8, LANES), 1)
    pick = jnp.where(l8 == r8 * HEAD_DIM, 1.0, 0.0)
    group = jnp.where(l8 // HEAD_DIM == r8, 1.0, 0.0)
    exact = lax.Precision.HIGHEST
    dims = (((1,), (1,)), ((), ()))
    for pair in range(width // LANES):
        cols = slice(pair * LANES, (pair + 1) * LANES)

        def stats(b, carry):
            at = pl.ds(pl.multiple_of(b * tb, tb), tb)
            lse_row[:, at] = lax.dot_general(pick, lse_ref[at, cols], dims, precision=exact, preferred_element_type=F32)
            prod = g_ref[at, cols].astype(F32) * of_ref[at, cols]
            delta_row[:, at] = lax.dot_general(group, prod, dims, precision=exact, preferred_element_type=F32)
            dq_acc[at, :] = jnp.zeros((tb, LANES), F32)
            return carry

        lax.fori_loop(0, n_ctx, stats, 0)

        def key_block(j, carry):
            dk_acc[...] = jnp.zeros_like(dk_acc)
            dv_acc[...] = jnp.zeros_like(dv_acc)
            mine = pl.ds(pl.multiple_of(j * tb, tb), tb)
            k = k_ref[mine, cols]
            v = v_ref[mine, cols]
            seg_k = sc_ref[mine, 0:1]

            def block(i, causal):
                at = pl.ds(pl.multiple_of(i * tb, tb), tb)
                q = q_ref[at, cols]
                g = g_ref[at, cols]
                ok = seg_k == sr_ref[0:1, at]
                if causal:
                    r = lax.broadcasted_iota(jnp.int32, (tb, tb), 0)
                    t = lax.broadcasted_iota(jnp.int32, (tb, tb), 1)
                    ok = ok & (r <= t)
                for head in range(2):
                    qm = head_lanes(q, head)
                    gm = head_lanes(g, head)
                    s = dot(k, qm, 1, 1)
                    p = jnp.where(ok, jnp.exp(s - lse_row[head : head + 1, at]), 0.0)
                    dp = dot(v, gm, 1, 1)
                    ds = (p * (dp - delta_row[head : head + 1, at])).astype(LOW)
                    dv_acc[...] += dot(p.astype(LOW), gm, 1, 0)
                    dk_acc[...] += dot(ds, qm, 1, 0)
                    dq_acc[at, :] += dot(ds, head_lanes(k, head), 0, 0)

            block(j, True)

            def step(i, carry):
                block(i, False)
                return carry

            lax.fori_loop(j + 1, n_ctx, step, 0)
            dk = dk_acc[...]
            dk = dk * cos_ref[mine, :] - half_swap(dk) * sin_ref[mine, :]
            out_ref[pair, mine, LANES : 2 * LANES] = dk.astype(LOW)
            out_ref[pair, mine, 2 * LANES : 3 * LANES] = dv_acc[...].astype(LOW)
            return carry

        lax.fori_loop(0, n_ctx, key_block, 0)

        def query_done(b, carry):
            at = pl.ds(pl.multiple_of(b * tb, tb), tb)
            dq = dq_acc[at, :] * 0.125
            dq = dq * cos_ref[at, :] - half_swap(dq) * sin_ref[at, :]
            out_ref[pair, at, 0:LANES] = dq.astype(LOW)
            return carry

        lax.fori_loop(0, n_ctx, query_done, 0)
        for t in range(3):
            pltpu.make_async_copy(part(pair, t, c), home(pair, t), own.at[pair, t]).start()
            for k in range(1, n_ctx):
                part_copy(pair, t, k).start()
    for pair in range(width // LANES):
        for t in range(3):
            pltpu.make_async_copy(part(pair, t, c), home(pair, t), own.at[pair, t]).wait()
            for k in range(1, n_ctx):
                part_copy(pair, t, k).wait()


def attend_back_call(n_ctx, ga, q, k, v, of, lse, seg_col, seg_row, cos, sin):
    length, width = q.shape
    tb = TOKEN_BLOCK
    pairs = width // LANES
    vmem = pl.BlockSpec(memory_space=pltpu.VMEM)
    return pl.pallas_call(
        functools.partial(attend_back_kernel, n_ctx),
        in_specs=[pl.BlockSpec(memory_space=pl.ANY)] + [vmem] * 9,
        out_specs=[vmem, pl.BlockSpec(memory_space=pl.ANY)],
        out_shape=[
            jax.ShapeDtypeStruct((pairs, length, 3 * LANES), LOW),
            jax.ShapeDtypeStruct((tb, 3 * n_ctx * width), LOW),
        ],
        scratch_shapes=[
            pltpu.VMEM((length, width), LOW),
            pltpu.VMEM((8, length), F32),
            pltpu.VMEM((8, length), F32),
            pltpu.VMEM((length, LANES), F32),
            pltpu.VMEM((tb, LANES), F32),
            pltpu.VMEM((tb, LANES), F32),
            pltpu.SemaphoreType.DMA((n_ctx - 1,)),
            pltpu.SemaphoreType.DMA((n_ctx - 1,)),
            pltpu.SemaphoreType.DMA((n_ctx - 1, pairs, 3)),
            pltpu.SemaphoreType.DMA((n_ctx - 1, pairs, 3)),
            pltpu.SemaphoreType.DMA((pairs, 3)),
        ],
        compiler_params=params(collective_id=2, has_side_effects=True),
        cost_estimate=pl.CostEstimate(
            flops=40 * 10**9, bytes_accessed=16 * 2**20, transcendentals=2 * length * length
        ),
        name="attend_back",
    )(ga, q, k, v, of, lse, seg_col, seg_row, cos, sin)


def mlp_kernel(blocks, tok_ref, att_ref, cot_ref, gain_ref, *refs):
    pieces, refs = refs[: 3 * blocks], refs[3 * blocks :]
    go_in, up_in, dn_in = pieces[:blocks], pieces[blocks : 2 * blocks], pieces[2 * blocks :]
    out_ref, gm_ref, ga_ref, gk, gs, uk, us, ok, os, dk, ds = refs[:11]
    wo, wg, wu, wd, att, nat, n2, mi, mit, inv_ref, oacc, dacc, dwd, sem, osem = refs[11:]
    dp = lax.axis_index("dp")
    u = pl.program_id(0)
    last = pl.num_programs(0) - 1
    ff = wu.shape[1]
    down = dn_in[0].shape[0]

    def copies():
        made = []
        for d in range(blocks):
            at = pl.ds(d * LANES, LANES)
            made.append(pltpu.make_async_copy(go_in[d].at[:, pl.ds(ff, wo.shape[1])], wo.at[at, :], sem.at[0, d]))
        for d in range(blocks):
            at = pl.ds(d * LANES, LANES)
            made.append(pltpu.make_async_copy(go_in[d].at[:, pl.ds(0, ff)], wg.at[at, :], sem.at[1, d]))
            made.append(pltpu.make_async_copy(up_in[d], wu.at[at, :], sem.at[2, d]))
            rows = pl.ds(pl.multiple_of((dp ^ d) * down, 32), down)
            made.append(pltpu.make_async_copy(dn_in[d], wd.at[rows, :], sem.at[3, d]))
        return made

    def out_copies():
        made = []
        for d in range(blocks):
            rows = pl.ds(pl.multiple_of((dp ^ d) * down, 32), down)
            made.append(pltpu.make_async_copy(dwd.at[rows, :], (ds if d % 2 else dk).at[d // 2], osem.at[d]))
        return made

    @pl.when(u == 0)
    def _():
        made = copies()
        for c in made:
            c.start()
        for d in range(blocks):
            att[:, d * LANES : (d + 1) * LANES] = att_ref[:, lane_block(dp ^ d)]
        for c in made[:blocks]:
            c.wait()
        mid = tok_ref[...].astype(F32) + dot(att[...], wo[...], 1, 0)
        inv = lax.rsqrt(jnp.mean(mid * mid, axis=-1, keepdims=True) + epsilon)
        oacc[...] = mid
        nat[...] = mid * inv
        inv_ref[...] = jnp.broadcast_to(inv, inv_ref.shape)
        for d in range(blocks):
            n2[:, d * LANES : (d + 1) * LANES] = nat[:, lane_block(dp ^ d)]
        mi[...] = (n2[...] * gain_ref[...]).astype(LOW)
        mit[...] = mi[...].T
        dacc[...] = jnp.zeros_like(dacc)
        for c in made[blocks:]:
            c.wait()

    cols = pl.ds(pl.multiple_of(u * FF_BLOCK, FF_BLOCK), FF_BLOCK)
    x = mi[...]
    cot = cot_ref[...]
    wgu, wuu, wdu = wg[:, cols], wu[:, cols], wd[cols, :]
    gate = dot(x, wgu, 1, 0)
    up = dot(x, wuu, 1, 0)
    grad_hidden = dot(cot, wdu, 1, 1)
    sig = jax.nn.sigmoid(gate)
    hidden = (gate * sig * up).astype(LOW)
    dg = (grad_hidden * up * sig * (1.0 + gate * (1.0 - sig))).astype(LOW)
    du = (grad_hidden * gate * sig).astype(LOW)
    oacc[...] += dot(hidden, wdu, 1, 0)
    dacc[...] += dot(dg, wgu, 1, 1) + dot(du, wuu, 1, 1)
    xt = mit[...]
    dwg = dot(xt, dg, 1, 0).astype(LOW)
    dwu = dot(xt, du, 1, 0).astype(LOW)
    for d in range(blocks):
        (gs if d % 2 else gk)[d // 2] = dwg[d * LANES : (d + 1) * LANES]
        (us if d % 2 else uk)[d // 2] = dwu[d * LANES : (d + 1) * LANES]
    dwd[cols, :] = dot(hidden, cot, 0, 0).astype(LOW)

    @pl.when(u == last)
    def _():
        made = out_copies()
        for c in made:
            c.start()
        out_ref[...] = oacc[...].astype(LOW)
        scaled = dacc[...] * gain_ref[...]
        norm = n2[...]
        mean = jnp.mean(scaled * norm, axis=-1, keepdims=True)
        n2[...] = inv_ref[:, 0:1] * (scaled - norm * mean)
        for d in range(blocks):
            nat[:, lane_block(dp ^ d)] = n2[:, d * LANES : (d + 1) * LANES]
        gm = cot.astype(F32) + nat[...]
        gm_ref[...] = gm
        gb = gm.astype(LOW)
        n2[...] = dot(gb, wo[...], 1, 1)
        for d in range(blocks):
            ga_ref[:, lane_block(dp ^ d)] = n2[:, d * LANES : (d + 1) * LANES].astype(LOW)
        dwo = dot(att[...], gb, 0, 0).astype(LOW)
        for d in range(blocks):
            (os if d % 2 else ok)[d // 2] = dwo[d * LANES : (d + 1) * LANES]
        for c in made:
            c.wait()


def mlp_call(tok, att, cot, gain, go, up, dn):
    tb, model = tok.shape
    blocks = len(go)
    ff = up[0].shape[1]
    half = blocks // 2
    down = dn[0].shape[0]
    whole = lambda a: pl.BlockSpec(a.shape, lambda u: (0, 0))
    anyspace = pl.BlockSpec(memory_space=pl.ANY)
    half_cols = pl.BlockSpec((half, LANES, FF_BLOCK), lambda u: (0, 0, u))
    half_out = pl.BlockSpec((half, LANES, model), lambda u: (0, 0, 0))
    tokens = pl.BlockSpec((tb, model), lambda u: (0, 0))
    shape = jax.ShapeDtypeStruct
    return pl.pallas_call(
        functools.partial(mlp_kernel, blocks),
        grid=(ff // FF_BLOCK,),
        in_specs=[whole(tok), whole(att), whole(cot), whole(gain)] + [anyspace] * (3 * blocks),
        out_specs=[tokens, tokens, tokens] + [half_cols] * 4 + [half_out] * 2 + [anyspace] * 2,
        out_shape=[shape((tb, model), LOW), shape((tb, model), F32), shape((tb, model), LOW)]
        + [shape((half, LANES, ff), LOW)] * 4
        + [shape((half, LANES, model), LOW)] * 2
        + [shape((half, down, model), LOW)] * 2,
        scratch_shapes=[
            pltpu.VMEM((model, model), LOW),
            pltpu.VMEM((model, ff), LOW),
            pltpu.VMEM((model, ff), LOW),
            pltpu.VMEM((ff, model), LOW),
            pltpu.VMEM((tb, model), LOW),
            pltpu.VMEM((tb, model), F32),
            pltpu.VMEM((tb, model), F32),
            pltpu.VMEM((tb, model), LOW),
            pltpu.VMEM((model, tb), LOW),
            pltpu.VMEM((tb, LANES), F32),
            pltpu.VMEM((tb, model), F32),
            pltpu.VMEM((tb, model), F32),
            pltpu.VMEM((ff, model), LOW),
            pltpu.SemaphoreType.DMA((4, blocks)),
            pltpu.SemaphoreType.DMA((blocks,)),
        ],
        compiler_params=params(),
        cost_estimate=pl.CostEstimate(
            flops=2 * tb * model * (8 * ff + 3 * model), bytes_accessed=50 * 2**20, transcendentals=0
        ),
        name="mlp",
    )(tok, att, cot, gain, *go, *up, *dn)


def input_kernel(blocks, tok_ref, gm_ref, v1_ref, gain_ref, g, *refs):
    w_in, refs = refs[:blocks], refs[blocks:]
    ig_ref, vg_ref, w, rel, nat, sem = refs
    dp = lax.axis_index("dp")
    model = tok_ref.shape[1]
    made = [pltpu.make_async_copy(w_in[d], w.at[pl.ds(d * LANES, LANES), :], sem.at[d]) for d in range(blocks)]
    for m in made:
        m.start()
    for d in range(blocks):
        rel[:, d * LANES : (d + 1) * LANES] = tok_ref[:, lane_block(dp ^ d)].astype(F32)
    gv = g[:, 2 * model :].astype(F32)
    vg_ref[...] = v1_ref[...] + 0.5 * gv
    x = rel[...]
    inv = lax.rsqrt(jnp.mean(x * x, axis=-1, keepdims=True) + epsilon)
    norm = x * inv
    for m in made:
        m.wait()
    grad = dot(g[:, : 2 * model], w[:, : 2 * model], 1, 1)
    grad = grad + 0.5 * dot(g[:, 2 * model :], w[:, 2 * model :], 1, 1)
    scaled = grad * gain_ref[...]
    mean = jnp.mean(scaled * norm, axis=-1, keepdims=True)
    rel[...] = inv * (scaled - norm * mean)
    for d in range(blocks):
        nat[:, lane_block(dp ^ d)] = rel[:, d * LANES : (d + 1) * LANES]
    ig_ref[...] = gm_ref[...] + nat[...]


def input_call(tok, gm, v1, gain, g, ws):
    tb, model = tok.shape
    blocks = len(ws)
    vmem = pl.BlockSpec(memory_space=pltpu.VMEM)
    shape = jax.ShapeDtypeStruct
    return pl.pallas_call(
        functools.partial(input_kernel, blocks),
        in_specs=[vmem] * 5 + [pl.BlockSpec(memory_space=pl.ANY)] * blocks,
        out_specs=[vmem, vmem],
        out_shape=[shape((tb, model), F32)] * 2,
        scratch_shapes=[
            pltpu.VMEM((model, 3 * model), LOW),
            pltpu.VMEM((tb, model), F32),
            pltpu.VMEM((tb, model), F32),
            pltpu.SemaphoreType.DMA((blocks,)),
        ],
        compiler_params=params(),
        cost_estimate=pl.CostEstimate(
            flops=2 * tb * model * 3 * model, bytes_accessed=20 * 2**20, transcendentals=0
        ),
        name="input_grad",
    )(tok, gm, v1, gain, g, *ws)


def fast_local(
    n_dp, n_ctx, tokens, first_values, v1_accum, segment_ids, positions, cotangent,
    attn_gain, w_query, w_key, w_value, w_out, mlp_gain, w_gate, w_up, w_down,
):
    c = lax.axis_index("ctx")
    seq, model = tokens.shape[1:]
    width = model // n_ctx
    length = seq * n_ctx
    ff = w_gate.shape[1]
    own_rows = w_query.shape[0]
    down_rows = w_down.shape[0]
    bits = [1 << b for b in range(n_dp.bit_length() - 1)]
    plane = bits[1:]

    def shift(x, k):
        return lax.ppermute(x, "ctx", [(i, (i + k) % n_ctx) for i in range(n_ctx)])

    def flip(x, bit):
        return lax.ppermute(x, "dp", [(i, i ^ bit) for i in range(n_dp)])

    def cut(x, index, size, axis):
        return lax.dynamic_slice_in_dim(x, index * size, size, axis)

    def swap_ctx(x, axis):
        size = x.shape[axis] // n_ctx
        return [cut(x, c, size, axis)] + [shift(cut(x, (c + k) % n_ctx, size, axis), k) for k in range(1, n_ctx)]

    def place(slots, axis):
        size = slots[0].shape[axis]
        dims = list(slots[0].shape)
        dims[axis] = size * n_ctx
        out = jnp.zeros(dims, slots[0].dtype)
        for k, slot in enumerate(slots):
            out = lax.dynamic_update_slice_in_dim(out, slot, ((c + n_ctx - k) % n_ctx) * size, axis)
        return out

    def gather_dp(x, order):
        got = {0: x}
        for bit in order:
            for d in sorted(got):
                got[d ^ bit] = flip(got[d], bit)
        return [got[d] for d in range(n_dp)]

    def gather_ctx(x):
        return lax.all_gather(x, "ctx", axis=0, tiled=True)

    tok = tokens[0]
    row_tokens = gather_ctx(tok)
    marks = jnp.concatenate([segment_ids, positions], axis=0)
    marks = place([marks] + [shift(marks, k) for k in range(1, n_ctx)], 1)
    head_first = place(swap_ctx(first_values[0], 1), 0)

    gains = jnp.stack([attn_gain, mlp_gain], axis=1)
    gains = jnp.tile(jnp.pad(gains, ((0, 0), (0, width - 2))), (1, n_ctx))
    packed = jnp.stack([w_query, w_key, w_value, gains])
    slots = jnp.stack(swap_ctx(packed, 2))
    slots = place([slots[k : k + 1] for k in range(n_ctx)], 0)
    slots = jnp.stack(gather_dp(slots, plane + bits[:1]))
    packed_all = slots.reshape(n_dp * n_ctx, 4, own_rows, width)
    head_weights = packed_all[:, :3].transpose(0, 2, 1, 3).reshape(model, 3 * width)
    gain_rel = packed_all[:, 3, :, 0].reshape(1, model).astype(F32)
    gain_two_rel = packed_all[:, 3, :, 1].reshape(1, model).astype(F32)

    go = gather_ctx(jnp.concatenate([w_gate, w_out], axis=1))
    up = gather_ctx(w_up)
    dn = gather_ctx(w_down)
    go = gather_dp(go, plane + bits[:1])
    up = gather_dp(up, plane[::-1] + bits[:1])
    dn = gather_dp(dn, plane[::-1] + bits[:1])

    seg_row = jnp.broadcast_to(marks[0:1], (8, length))
    seg_col = jnp.broadcast_to(marks[0][:, None], (length, LANES))
    freqs = 10000.0 ** (-jnp.arange(HEAD_DIM // 2).astype(F32) * (2.0 / HEAD_DIM))
    angles = marks[1].astype(F32)[:, None] * freqs
    cos, sin = jnp.cos(angles), jnp.sin(angles)
    cos = jnp.concatenate([cos] * 4, axis=1)
    sin = jnp.concatenate([-sin, sin] * 2, axis=1)
    xn, q, k, v = qkv_call(row_tokens, head_weights, gain_rel, head_first, cos, sin)
    pairs = width // LANES
    attended, out_full, log_total = attend_call(n_ctx, q, k, v, seg_col, seg_row)
    cot = cotangent[0]
    (output, grad_middle, grad_attended, gate_keep, gate_send, up_keep, up_send, out_keep, out_send,
     down_keep, down_send) = mlp_call(tok, attended, cot, gain_two_rel, go, up, dn)

    qkv_all = gather_dp(gather_ctx(jnp.concatenate([w_query, w_key, w_value], axis=1)), plane + bits[:1])

    back, home_grad = attend_back_call(
        n_ctx, grad_attended, q, k, v, out_full, log_total, seg_col, seg_row, cos, sin
    )

    def scatter_dp(keep, send, order):
        terms = [keep, flip(send, bits[0])]
        count = keep.shape[0]
        names = list(range(count))
        for bit in order:
            near = bit >> 1
            stay = [n for n in names if not n & near]
            leave = [n for n in names if n & near]

            def pick(which):
                return sum(
                    jnp.stack([t[names.index(n)] for n in which]).astype(F32) for t in terms
                )

            got = flip(pick(leave).astype(LOW), bit)
            terms = [jnp.stack([t[names.index(n)] for n in stay]) for t in terms] + [got]
            names = stay
        return sum(t[0].astype(F32) for t in terms)

    def scatter_ctx(x):
        size = x.shape[0] // n_ctx
        got = cut(x, c, size, 0)
        for k in range(1, n_ctx):
            got = got + shift(cut(x, (c + k) % n_ctx, size, 0).astype(LOW), k).astype(F32)
        return got

    gate_grad = scatter_ctx(scatter_dp(gate_keep, gate_send, plane))
    up_grad = scatter_ctx(scatter_dp(up_keep, up_send, plane[::-1]))
    down_grad = scatter_ctx(scatter_dp(down_keep, down_send, plane))
    out_grad = scatter_ctx(scatter_dp(out_keep, out_send, plane[::-1]))

    qkv_grad = jnp.zeros((3, own_rows, model), F32)
    for p in range(pairs):
        product = lax.dot_general(
            xn, back[p], (((0,), (0,)), ((), ())), preferred_element_type=F32
        ).astype(LOW).reshape(n_dp // 2, 2, model // n_dp, 3 * LANES)
        total = scatter_dp(product[:, 0], product[:, 1], plane)
        for s, slot in enumerate(swap_ctx(total.astype(LOW), 0)):
            block = slot.astype(F32).reshape(own_rows, 3, LANES).transpose(1, 0, 2)
            at = ((c + n_ctx - s) % n_ctx) * width + p * LANES
            qkv_grad = lax.dynamic_update_slice_in_dim(qkv_grad, block, at, 2)
    query_grad, key_grad, value_grad = qkv_grad[0], qkv_grad[1], 0.5 * qkv_grad[2]

    input_grad, v1_grad = input_call(tok, grad_middle, v1_accum[0], gain_rel, home_grad, qkv_all)

    def row_dot(a, w):
        return jnp.sum(a * w.astype(F32), axis=1)

    gain_one = (
        row_dot(query_grad, w_query) + row_dot(key_grad, w_key) + row_dot(value_grad, w_value)
    ) / attn_gain.astype(F32)
    gain_two = (row_dot(gate_grad, w_gate) + row_dot(up_grad, w_up)) / mlp_gain.astype(F32)
    return (
        output[None], input_grad[None], v1_grad[None], gain_one, query_grad, key_grad, value_grad,
        out_grad, gain_two, gate_grad, up_grad, down_grad,
    )


def solution(mesh):
    placed = (
        P("dp", "ctx", None),
        P("dp", "ctx", None),
        P("dp", "ctx", None),
        P("dp", "ctx"),
        P("dp", "ctx"),
        P("dp", "ctx", None),
        P(("dp", "ctx")),
        P(("dp", "ctx"), None),
        P(("dp", "ctx"), None),
        P(("dp", "ctx"), None),
        P(("dp", "ctx"), None),
        P(("dp", "ctx")),
        P(("dp", "ctx"), None),
        P(("dp", "ctx"), None),
        P(("dp", "ctx"), None),
    )
    n_dp, n_ctx = mesh.shape["dp"], mesh.shape["ctx"]

    def local(*args):
        rows, seq, model = args[0].shape
        fits = (
            rows == 1
            and seq == TOKEN_BLOCK
            and model == n_dp * LANES
            and model == 2 * LANES * n_ctx
            and args[12].shape[1] % FF_BLOCK == 0
        )
        return fast_local(n_dp, n_ctx, *args) if fits else plain_local(*args)

    return jax.shard_map(
        local,
        mesh=mesh,
        in_specs=placed,
        out_specs=(
            P("dp", "ctx", None),
            P("dp", "ctx", None),
            P("dp", "ctx", None),
            P(("dp", "ctx")),
            P(("dp", "ctx"), None),
            P(("dp", "ctx"), None),
            P(("dp", "ctx"), None),
            P(("dp", "ctx"), None),
            P(("dp", "ctx")),
            P(("dp", "ctx"), None),
            P(("dp", "ctx"), None),
            P(("dp", "ctx"), None),
        ),
        check_vma=False,
    )
```

```python
import functools

import jax
import jax.numpy as jnp
from jax import lax
from jax.experimental import pallas as pl
from jax.experimental.pallas import tpu as pltpu
from jax.sharding import PartitionSpec as P

HEADS = 16
HEAD_DIM = 64
LANES = 128
TOKEN_BLOCK = 512
FF_BLOCK = 256
NEG = -1e30
MESH = pl.DeviceIdType.MESH
F32 = jnp.float32
LOW = jnp.bfloat16
BYTES = 60 * 2**20
epsilon = 1e-05


HEAD_BLOCK = 4


def rms_scale(values):
    return lax.rsqrt(jnp.mean(values * values, axis=-1, keepdims=True) + epsilon)


def angle_tables(position_rows):
    freqs = 10000.0 ** (-jnp.arange(HEAD_DIM // 2).astype(jnp.float32) * (2.0 / HEAD_DIM))
    angles = position_rows.astype(jnp.float32)[..., None] * freqs
    return (jnp.cos(angles)[..., None, :], jnp.sin(angles)[..., None, :])


def rotate(heads_in, cosine_table, sine_table):
    half_dim = heads_in.shape[-1] // 2
    first_half = heads_in[..., :half_dim]
    second_half = heads_in[..., half_dim:]
    return jnp.concatenate(
        [
            first_half * cosine_table - second_half * sine_table,
            second_half * cosine_table + first_half * sine_table,
        ],
        axis=-1,
    )


def norm_back(grad_normed, normed, inv_root, norm_gain):
    grad_scaled = grad_normed * norm_gain.astype(jnp.float32)
    grad_input = inv_root * (
        grad_scaled - normed * jnp.mean(grad_scaled * normed, axis=-1, keepdims=True)
    )
    return (grad_input, jnp.sum(grad_normed * normed, axis=0))


def attn_front(flat_tokens, first_flat, attn_set, cosine_table, sine_table, row_count, seq_piece):
    inv_root = rms_scale(flat_tokens)
    normed = flat_tokens * inv_root
    normed_in = (normed * attn_set[0].astype(jnp.float32)).astype(jnp.bfloat16)
    query_proj = jnp.dot(normed_in, attn_set[1], preferred_element_type=jnp.float32)
    key_proj = jnp.dot(normed_in, attn_set[2], preferred_element_type=jnp.float32)
    value_proj = jnp.dot(normed_in, attn_set[3], preferred_element_type=jnp.float32)
    query_rot = rotate(
        query_proj.reshape(row_count, seq_piece, HEADS, HEAD_DIM), cosine_table, sine_table
    )
    key_rot = rotate(
        key_proj.reshape(row_count, seq_piece, HEADS, HEAD_DIM), cosine_table, sine_table
    )
    query_rot = query_rot.astype(jnp.bfloat16).reshape(row_count, seq_piece, -1)
    key_rot = key_rot.astype(jnp.bfloat16).reshape(row_count, seq_piece, -1)
    value_mix = (
        (0.5 * value_proj + 0.5 * first_flat).astype(jnp.bfloat16).reshape(row_count, seq_piece, -1)
    )
    return (normed, inv_root, normed_in, query_rot, key_rot, value_mix)


def mlp_block(flat_tokens, attended_low, out_weight, mlp_set):
    middle = flat_tokens + jnp.dot(attended_low, out_weight, preferred_element_type=jnp.float32)
    inv_root_two = rms_scale(middle)
    normed_two = middle * inv_root_two
    mlp_in = (normed_two * mlp_set[0].astype(jnp.float32)).astype(jnp.bfloat16)
    gate_proj = jnp.dot(mlp_in, mlp_set[1], preferred_element_type=jnp.float32)
    up_proj = jnp.dot(mlp_in, mlp_set[2], preferred_element_type=jnp.float32)
    hidden = (gate_proj * jax.nn.sigmoid(gate_proj) * up_proj).astype(jnp.bfloat16)
    result = middle + jnp.dot(hidden, mlp_set[3], preferred_element_type=jnp.float32)
    return (normed_two, inv_root_two, mlp_in, gate_proj, up_proj, hidden, result)


def split_groups(row_block):
    tok_count = row_block.shape[0]
    return row_block.reshape(tok_count, HEADS // HEAD_BLOCK, HEAD_BLOCK * HEAD_DIM).transpose(
        1, 0, 2
    )


def join_groups(group_block):
    return group_block.transpose(1, 0, 2).reshape(group_block.shape[1], -1)


def as_heads(block):
    return block.reshape(block.shape[0], HEAD_BLOCK, HEAD_DIM)


def attend_row(members):
    query_row, key_row, value_row, allowed = members

    def per_group(pieces):
        query_block, key_block, value_block = pieces
        scores = (
            jnp.einsum(
                "qhd,khd->hqk",
                as_heads(query_block),
                as_heads(key_block),
                preferred_element_type=jnp.float32,
            )
            * 0.125
        )
        scores = jnp.where(allowed[None], scores, -1e30)
        highest = jnp.max(scores, axis=-1, keepdims=True)
        exp_scores = jnp.exp(scores - highest)
        denominator = jnp.sum(exp_scores, axis=-1, keepdims=True)
        soft_low = (exp_scores / denominator).astype(jnp.bfloat16)
        attended = jnp.einsum(
            "hqk,khd->qhd", soft_low, as_heads(value_block), preferred_element_type=jnp.float32
        )
        return (
            attended.reshape(query_block.shape[0], -1),
            (highest + jnp.log(denominator))[..., 0],
        )

    attended, log_total = lax.map(
        per_group, (split_groups(query_row), split_groups(key_row), split_groups(value_row))
    )
    return (join_groups(attended), log_total)


def attend_back(members):
    query_row, key_row, value_row, grad_row, log_total, allowed = members

    def per_group(pieces):
        query_block, key_block, value_block, grad_block, log_block = pieces
        query_heads = as_heads(query_block)
        key_heads = as_heads(key_block)
        grad_heads = as_heads(grad_block)
        scores = (
            jnp.einsum("qhd,khd->hqk", query_heads, key_heads, preferred_element_type=jnp.float32)
            * 0.125
        )
        soft_weights = jnp.where(allowed[None], jnp.exp(scores - log_block[..., None]), 0.0)
        soft_low = soft_weights.astype(jnp.bfloat16)
        grad_probs = jnp.einsum(
            "qhd,khd->hqk", grad_heads, as_heads(value_block), preferred_element_type=jnp.float32
        )
        row_delta = jnp.sum(soft_weights * grad_probs, axis=-1, keepdims=True)
        grad_scores = (soft_weights * (grad_probs - row_delta)).astype(jnp.bfloat16)
        grad_query = (
            jnp.einsum("hqk,khd->qhd", grad_scores, key_heads, preferred_element_type=jnp.float32)
            * 0.125
        )
        grad_key = (
            jnp.einsum("hqk,qhd->khd", grad_scores, query_heads, preferred_element_type=jnp.float32)
            * 0.125
        )
        grad_value = jnp.einsum(
            "hqk,qhd->khd", soft_low, grad_heads, preferred_element_type=jnp.float32
        )
        return (
            grad_query.reshape(query_block.shape[0], -1),
            grad_key.reshape(key_block.shape[0], -1),
            grad_value.reshape(key_block.shape[0], -1),
        )

    grad_query, grad_key, grad_value = lax.map(
        per_group,
        (
            split_groups(query_row),
            split_groups(key_row),
            split_groups(value_row),
            split_groups(grad_row),
            log_total,
        ),
    )
    return (join_groups(grad_query), join_groups(grad_key), join_groups(grad_value))


def plain_local(
    tokens,
    first_values,
    v1_accum,
    segment_ids,
    positions,
    cotangent,
    attn_gain,
    w_query,
    w_key,
    w_value,
    w_out,
    mlp_gain,
    w_gate,
    w_up,
    w_down,
):
    row_count, seq_piece, model_width = tokens.shape
    token_count = row_count * seq_piece
    flat_tokens = tokens.astype(jnp.float32).reshape(token_count, model_width)
    first_flat = first_values.astype(jnp.float32).reshape(token_count, model_width)
    cosine_table, sine_table = angle_tables(positions)
    segment_low = segment_ids.astype(jnp.bfloat16)
    attn_set = (
        lax.all_gather(attn_gain, ("dp", "ctx"), axis=0, tiled=True),
        lax.all_gather(w_query, ("dp", "ctx"), axis=0, tiled=True),
        lax.all_gather(w_key, ("dp", "ctx"), axis=0, tiled=True),
        lax.all_gather(w_value, ("dp", "ctx"), axis=0, tiled=True),
        lax.all_gather(w_out, ("dp", "ctx"), axis=0, tiled=True),
    )
    normed, inv_root, normed_in, query_rot, key_rot, value_mix = attn_front(
        flat_tokens, first_flat, attn_set, cosine_table, sine_table, row_count, seq_piece
    )
    key_full, value_full, segment_full = (
        lax.all_gather(key_rot, "ctx", axis=1, tiled=True),
        lax.all_gather(value_mix, "ctx", axis=1, tiled=True),
        lax.all_gather(segment_low, "ctx", axis=1, tiled=True),
    )
    query_order = lax.axis_index("ctx") * seq_piece + jnp.arange(seq_piece, dtype=jnp.int32)
    full_order = jnp.arange(key_full.shape[1], dtype=jnp.int32)
    segment_own = segment_ids.astype(jnp.float32)
    segment_all = segment_full.astype(jnp.float32)
    allowed = (segment_own[:, :, None] == segment_all[:, None, :]) & (
        query_order[None, :, None] >= full_order[None, None, :]
    )
    attended, log_total = lax.map(attend_row, (query_rot, key_full, value_full, allowed))
    attended_low = attended.reshape(token_count, model_width).astype(jnp.bfloat16)
    mlp_set = (
        lax.all_gather(mlp_gain, ("dp", "ctx"), axis=0, tiled=True),
        lax.all_gather(w_gate, ("dp", "ctx"), axis=0, tiled=True),
        lax.all_gather(w_up, ("dp", "ctx"), axis=0, tiled=True),
        lax.all_gather(w_down, ("dp", "ctx"), axis=0, tiled=True),
    )
    normed_two, inv_root_two, mlp_in, gate_proj, up_proj, hidden, output_flat = mlp_block(
        flat_tokens, attended_low, attn_set[4], mlp_set
    )
    output = output_flat.reshape(tokens.shape).astype(jnp.bfloat16)
    attn_set = (
        lax.all_gather(attn_gain, ("dp", "ctx"), axis=0, tiled=True),
        lax.all_gather(w_query, ("dp", "ctx"), axis=0, tiled=True),
        lax.all_gather(w_key, ("dp", "ctx"), axis=0, tiled=True),
        lax.all_gather(w_value, ("dp", "ctx"), axis=0, tiled=True),
        lax.all_gather(w_out, ("dp", "ctx"), axis=0, tiled=True),
    )
    mlp_set = (
        lax.all_gather(mlp_gain, ("dp", "ctx"), axis=0, tiled=True),
        lax.all_gather(w_gate, ("dp", "ctx"), axis=0, tiled=True),
        lax.all_gather(w_up, ("dp", "ctx"), axis=0, tiled=True),
        lax.all_gather(w_down, ("dp", "ctx"), axis=0, tiled=True),
    )
    normed, inv_root, normed_in, query_rot, key_rot, value_mix = attn_front(
        flat_tokens, first_flat, attn_set, cosine_table, sine_table, row_count, seq_piece
    )
    key_full, value_full = (
        lax.all_gather(key_rot, "ctx", axis=1, tiled=True),
        lax.all_gather(value_mix, "ctx", axis=1, tiled=True),
    )
    normed_two, inv_root_two, mlp_in, gate_proj, up_proj, hidden, output_flat = mlp_block(
        flat_tokens, attended_low, attn_set[4], mlp_set
    )
    cot_low = cotangent.reshape(token_count, model_width)
    cot_float = cot_low.astype(jnp.float32)
    grad_hidden = jnp.einsum("td,fd->tf", cot_low, mlp_set[3], preferred_element_type=jnp.float32)
    sigma = jax.nn.sigmoid(gate_proj)
    grad_gate_low = (grad_hidden * up_proj * sigma * (1.0 + gate_proj * (1.0 - sigma))).astype(
        jnp.bfloat16
    )
    grad_up_low = (grad_hidden * gate_proj * sigma).astype(jnp.bfloat16)
    grad_mlp_in = jnp.einsum(
        "tf,df->td", grad_gate_low, mlp_set[1], preferred_element_type=jnp.float32
    )
    grad_mlp_in = grad_mlp_in + jnp.einsum(
        "tf,df->td", grad_up_low, mlp_set[2], preferred_element_type=jnp.float32
    )
    grad_middle_norm, grad_gain_two = norm_back(grad_mlp_in, normed_two, inv_root_two, mlp_set[0])
    grad_middle = cot_float + grad_middle_norm
    grad_branch_low = grad_middle.astype(jnp.bfloat16)
    grad_attended = jnp.einsum(
        "te,de->td", grad_branch_low, attn_set[4], preferred_element_type=jnp.float32
    )
    grad_attended = grad_attended.astype(jnp.bfloat16).reshape(row_count, seq_piece, model_width)
    grad_query_rot, grad_key_full, grad_value_full = lax.map(
        attend_back, (query_rot, key_full, value_full, grad_attended, log_total, allowed)
    )
    grad_key_rot, grad_value_mix = (
        lax.psum_scatter(
            grad_key_full.astype(jnp.bfloat16), "ctx", scatter_dimension=1, tiled=True
        ).astype(jnp.float32),
        lax.psum_scatter(
            grad_value_full.astype(jnp.bfloat16), "ctx", scatter_dimension=1, tiled=True
        ).astype(jnp.float32),
    )
    v1_grad = v1_accum + 0.5 * grad_value_mix
    grad_query_low = rotate(
        grad_query_rot.reshape(row_count, seq_piece, HEADS, HEAD_DIM), cosine_table, -sine_table
    )
    grad_query_low = grad_query_low.astype(jnp.bfloat16).reshape(token_count, model_width)
    grad_key_low = rotate(
        grad_key_rot.reshape(row_count, seq_piece, HEADS, HEAD_DIM), cosine_table, -sine_table
    )
    grad_key_low = grad_key_low.astype(jnp.bfloat16).reshape(token_count, model_width)
    grad_value_low = (0.5 * grad_value_mix).astype(jnp.bfloat16).reshape(token_count, model_width)
    grad_normed_in = jnp.einsum(
        "te,de->td", grad_query_low, attn_set[1], preferred_element_type=jnp.float32
    )
    grad_normed_in = grad_normed_in + jnp.einsum(
        "te,de->td", grad_key_low, attn_set[2], preferred_element_type=jnp.float32
    )
    grad_normed_in = grad_normed_in + jnp.einsum(
        "te,de->td", grad_value_low, attn_set[3], preferred_element_type=jnp.float32
    )
    grad_input_norm, grad_gain_one = norm_back(grad_normed_in, normed, inv_root, attn_set[0])
    input_grad = (grad_middle + grad_input_norm).reshape(tokens.shape)
    attn_right = jnp.concatenate([grad_query_low, grad_key_low, grad_value_low], axis=1)
    left_in = normed_in
    projections = jnp.einsum("td,te->de", left_in, attn_right, preferred_element_type=jnp.float32)
    out_part = jnp.einsum(
        "td,te->de", attended_low, grad_branch_low, preferred_element_type=jnp.float32
    )
    attn_matrix = lax.psum_scatter(
        jnp.concatenate([projections, out_part], axis=1),
        ("dp", "ctx"),
        scatter_dimension=0,
        tiled=True,
    )
    mlp_right = jnp.concatenate([grad_gate_low, grad_up_low], axis=1)
    left_in = mlp_in
    gate_up_matrix = lax.psum_scatter(
        jnp.einsum("td,tf->df", left_in, mlp_right, preferred_element_type=jnp.float32),
        ("dp", "ctx"),
        scatter_dimension=0,
        tiled=True,
    )
    down_matrix = lax.psum_scatter(
        jnp.einsum("tf,td->fd", hidden, cot_low, preferred_element_type=jnp.float32),
        ("dp", "ctx"),
        scatter_dimension=0,
        tiled=True,
    )
    gain_one, gain_two = (
        lax.psum_scatter(grad_gain_one, ("dp", "ctx"), scatter_dimension=0, tiled=True),
        lax.psum_scatter(grad_gain_two, ("dp", "ctx"), scatter_dimension=0, tiled=True),
    )
    ff_width = w_gate.shape[1]
    return (
        output,
        input_grad,
        v1_grad,
        gain_one,
        attn_matrix[:, 0:model_width],
        attn_matrix[:, model_width : 2 * model_width],
        attn_matrix[:, 2 * model_width : 3 * model_width],
        attn_matrix[:, 3 * model_width : 4 * model_width],
        gain_two,
        gate_up_matrix[:, 0:ff_width],
        gate_up_matrix[:, ff_width : 2 * ff_width],
        down_matrix,
    )


def params(**kw):
    return pltpu.CompilerParams(vmem_limit_bytes=BYTES, **kw)


def dot(a, b, da, db):
    return lax.dot_general(a, b, (((da,), (db,)), ((), ())), preferred_element_type=F32)


def lane_block(index):
    return pl.ds(pl.multiple_of(index * LANES, LANES), LANES)


def half_swap(x):
    lane = lax.broadcasted_iota(jnp.int32, x.shape, 1)
    left = pltpu.roll(x, LANES - HEAD_DIM // 2, 1)
    right = pltpu.roll(x, HEAD_DIM // 2, 1)
    return jnp.where(lane % HEAD_DIM < HEAD_DIM // 2, left, right)


def head_lanes(x, head):
    lane = lax.broadcasted_iota(jnp.int32, x.shape, 1)
    return jnp.where(lane // HEAD_DIM == head, x, jnp.zeros_like(x))


def meet(n_ctx, bits):
    c, dp = lax.axis_index("ctx"), lax.axis_index("dp")
    barrier = pltpu.get_barrier_semaphore()
    for k in range(1, n_ctx):
        pl.semaphore_signal(barrier, inc=1, device_id={"ctx": lax.rem(c + k, n_ctx)}, device_id_type=MESH)
    for bit in bits:
        pl.semaphore_signal(barrier, inc=1, device_id={"dp": dp ^ bit}, device_id_type=MESH)
    pl.semaphore_wait(barrier, n_ctx - 1 + len(bits))


def ctx_copy(src, dst, send, recv, to):
    return pltpu.make_async_remote_copy(
        src_ref=src, dst_ref=dst, send_sem=send, recv_sem=recv, device_id={"ctx": to}, device_id_type=MESH
    )


def dp_copy(src, dst, send, recv, bit):
    to = lax.axis_index("dp") ^ bit
    return pltpu.make_async_remote_copy(
        src_ref=src, dst_ref=dst, send_sem=send, recv_sem=recv, device_id={"dp": to}, device_id_type=MESH
    )


def rows_of(index, size):
    return pl.ds(pl.multiple_of(index * size, size), size)


CORE, NEAR, FAR = 1, 2, 4


class Gather:
    def __init__(self, n_ctx, src, dst, send, recv, order):
        self.n, self.src, self.dst, self.send, self.recv = n_ctx, src, dst, send, recv
        self.first, self.second = order
        self.rows = src.shape[0]

    def along(self, k):
        c = lax.axis_index("ctx")
        to = lax.rem(c + k, self.n)
        return ctx_copy(self.src, self.dst.at[0, pl.ds(c * self.rows, self.rows), :], self.send.at[k - 1], self.recv.at[k - 1], to)

    def plane(self, slot, bit, at):
        return dp_copy(self.dst.at[slot], self.dst.at[slot ^ bit], self.send.at[at], self.recv.at[at], bit)

    def own(self):
        c = lax.axis_index("ctx")
        return pltpu.make_async_copy(self.src, self.dst.at[0, pl.ds(c * self.rows, self.rows), :], self.send.at[10])

    def hop(self, at):
        one, two = self.first, self.second
        slot, bit = [(0, one), (0, two), (one, two), (0, CORE), (one, CORE), (two, CORE), (one | two, CORE)][at]
        return self.plane(slot, bit, 3 + at)

    def start(self):
        self.own().start()
        for k in range(1, self.n):
            self.along(k).start()

    def spread(self):
        self.own().wait()
        for k in range(1, self.n):
            self.along(k).wait_recv()
        for at in (0, 1, 3):
            self.hop(at).start()

    def forward(self):
        self.hop(0).wait_recv()
        self.hop(2).start()
        self.hop(4).start()

    def cross(self):
        self.hop(1).wait_recv()
        self.hop(5).start()
        self.hop(2).wait_recv()
        self.hop(6).start()

    def finish(self):
        for k in range(1, self.n):
            self.along(k).wait_send()
        for at in range(7):
            self.hop(at).wait_send()
        for at in range(3, 7):
            self.hop(at).wait_recv()


def front_kernel(
    n_ctx, tok_ref, fv_ref, mark_ref, pack_ref, freq_ref, wg_ref, wu_ref, wo_ref, wd_ref,
    xn_ref, q_ref, k_ref, v_ref, of_ref, lse_ref, cos_ref, sin_ref, seg_ref, marks, gain_ref,
    att_ref, wg_all, wu_all, wo_all, wd_all,
    x_all, fvs, packs, whead, rel, o_ref, s_ref, m_ref, l_ref, acc_ref,
    mark_send, mark_recv, pack_send, pack_recv, tok_send, tok_recv, fv_send, fv_recv, w_send, w_recv,
    o_send, o_recv, own, own_o,
):
    c, dp = lax.axis_index("ctx"), lax.axis_index("dp")
    tb = m_ref.shape[0]
    half = tb // 2
    model = tok_ref.shape[1]
    blocks = model // LANES
    width = q_ref.shape[1]
    own_rows = wg_ref.shape[0]
    lane = lax.broadcasted_iota(jnp.int32, (tb, LANES), 1)
    right, left = lax.rem(c + 1, n_ctx), lax.rem(c + n_ctx - 1, n_ctx)
    exact = lax.Precision.HIGHEST

    weights = [
        Gather(n_ctx, src, dst, w_send.at[i], w_recv.at[i], order)
        for i, (src, dst, order) in enumerate(
            [
                (wg_ref, wg_all, (NEAR, FAR)),
                (wo_ref, wo_all, (FAR, NEAR)),
                (wu_ref, wu_all, (FAR, NEAR)),
                (wd_ref, wd_all, (NEAR, FAR)),
            ]
        )
    ]
    early, late = weights[:2], weights[2:]

    def mark_copy(k):
        at = rows_of(c, tb)
        return ctx_copy(mark_ref, marks.at[:, at], mark_send.at[k - 1], mark_recv.at[k - 1], lax.rem(c + k, n_ctx))

    def pack_copy(k):
        to = lax.rem(c + k, n_ctx)
        return ctx_copy(pack_ref.at[to], packs.at[0, c], pack_send.at[k - 1], pack_recv.at[k - 1], to)

    def pack_hop(slot, bit, at):
        return dp_copy(packs.at[slot], packs.at[slot ^ bit], pack_send.at[at], pack_recv.at[at], bit)

    def fv_copy(k):
        to = lax.rem(c + k, n_ctx)
        return ctx_copy(fv_ref.at[:, rows_of(to, width)], fvs.at[rows_of(c, tb), :], fv_send.at[k - 1], fv_recv.at[k - 1], to)

    def tok_copy(way, step):
        block = lax.rem(c + n_ctx - step, n_ctx) if way == 0 else lax.rem(c + step, n_ctx)
        at = pl.ds(pl.multiple_of(block * tb + way * half, half), half)
        src = tok_ref.at[pl.ds(way * half, half), :] if step == 0 else x_all.at[at, :]
        return ctx_copy(src, x_all.at[at, :], tok_send.at[way, step], tok_recv.at[way, step], left if way else right)

    locals_ = [
        pltpu.make_async_copy(tok_ref, x_all.at[rows_of(c, tb), :], own.at[0]),
        pltpu.make_async_copy(fv_ref.at[:, rows_of(c, width)], fvs.at[rows_of(c, tb), :], own.at[1]),
        pltpu.make_async_copy(pack_ref.at[c], packs.at[0, c], own.at[2]),
        pltpu.make_async_copy(mark_ref, marks.at[:, rows_of(c, tb)], own.at[3]),
    ]

    meet(n_ctx, (CORE, NEAR, FAR))
    for k in range(1, n_ctx):
        mark_copy(k).start()
        pack_copy(k).start()
    for way in range(2):
        tok_copy(way, 0).start()
    for w in early:
        w.start()
    for m in locals_:
        m.start()
    for k in range(1, n_ctx):
        fv_copy(k).start()

    locals_[3].wait()
    for k in range(1, n_ctx):
        mark_copy(k).wait_recv()
    row8 = lax.broadcasted_iota(jnp.int32, (8, LANES), 0)
    pick_seg = jnp.where(row8 == 0, 1.0, 0.0)
    pick_pos = jnp.where(row8 == 1, 1.0, 0.0)

    def table(b, carry):
        at = rows_of(b, tb)
        m = marks[:, at].astype(F32)
        dims = (((0,), (0,)), ((), ()))
        seg_ref[at, :] = lax.dot_general(m, pick_seg, dims, precision=exact, preferred_element_type=F32)
        pos = lax.dot_general(m, pick_pos, dims, precision=exact, preferred_element_type=F32)
        angle = pos * freq_ref[0:1, :]
        cos_ref[at, :] = jnp.cos(angle)
        sin_ref[at, :] = jnp.sin(angle) * freq_ref[1:2, :]
        return carry

    locals_[2].wait()
    for k in range(1, n_ctx):
        pack_copy(k).wait_recv()
    pack_hop(0, NEAR, 3).start()
    lax.fori_loop(0, n_ctx, table, 0)
    pack_hop(0, NEAR, 3).wait_recv()
    pack_hop(0, FAR, 4).start()
    pack_hop(NEAR, FAR, 5).start()
    pack_hop(0, CORE, 6).start()
    pack_hop(NEAR, CORE, 7).start()

    for way in range(2):
        tok_copy(way, 0).wait_recv()
        tok_copy(way, 1).start()
    pack_hop(0, FAR, 4).wait_recv()
    pack_hop(FAR, CORE, 8).start()
    pack_hop(NEAR, FAR, 5).wait_recv()
    pack_hop(NEAR | FAR, CORE, 9).start()
    for w in early:
        w.spread()
    for at, (slot, bit) in enumerate([(0, CORE), (NEAR, CORE), (FAR, CORE), (NEAR | FAR, CORE)]):
        pack_hop(slot, bit, 6 + at).wait_recv()
    count = packs.shape[0]
    for t in range(3):
        block = packs[:, :, t * own_rows : (t + 1) * own_rows, :]
        whead[:, t * width : (t + 1) * width] = block.reshape(model, width)
    gains = packs[:, :, 3 * own_rows : 4 * own_rows, 0:LANES].reshape(model, LANES).astype(F32)
    gain_ref[...] = gains.T[0:8, :]
    locals_[0].wait()
    locals_[1].wait()

    def project(chunk, part):
        at = pl.ds(pl.multiple_of(chunk * tb + part * half, half), half)
        for d in range(blocks):
            rel[:, d * LANES : (d + 1) * LANES] = x_all[at, lane_block(dp ^ d)].astype(F32)
        x = rel[...]
        inv = lax.rsqrt(jnp.mean(x * x, axis=-1, keepdims=True) + epsilon)
        xn = (x * inv * gain_ref[0:1, :]).astype(LOW)
        xn_ref[at, :] = xn
        proj = dot(xn, whead[...], 1, 0)
        cos, sin = cos_ref[at, :], sin_ref[at, :]
        for b in range(width // LANES):
            cols = slice(b * LANES, (b + 1) * LANES)
            qb = proj[:, b * LANES : (b + 1) * LANES]
            q_ref[at, cols] = ((qb * cos + half_swap(qb) * sin) * 0.125).astype(LOW)
            kb = proj[:, width + b * LANES : width + (b + 1) * LANES]
            k_ref[at, cols] = (kb * cos + half_swap(kb) * sin).astype(LOW)
        v_ref[at, :] = (0.5 * proj[:, 2 * width :] + 0.5 * fvs[at, :].astype(F32)).astype(LOW)

    def project_pair(step):
        def one(part, carry):
            project(lax.rem(c + (2 * part - 1) * step + n_ctx, n_ctx), part)
            return carry

        lax.fori_loop(0, 2, one, 0)

    project_pair(0)
    for w in early:
        w.forward()
    for way in range(2):
        tok_copy(way, 1).wait_recv()
        tok_copy(way, 2).start()
    for k in range(1, n_ctx):
        fv_copy(k).wait_recv()
    project_pair(1)
    project_pair(2)
    for w in early:
        w.cross()
    for way in range(2):
        tok_copy(way, 2).wait_recv()
    for w in late:
        w.start()
    project_pair(3)

    def fold(x, op):
        r = x[:, 0:LANES]
        for b in range(1, tb // LANES):
            r = op(r, x[:, b * LANES : (b + 1) * LANES])
        return r

    def home(pair):
        return att_ref.at[:, pl.ds(pl.multiple_of(c * width + pair * LANES, LANES), LANES)]

    def query_block(pair, i):
        cols = slice(pair * LANES, (pair + 1) * LANES)
        mine = rows_of(i, tb)
        q = q_ref[mine, cols]
        seg_q = seg_ref[mine, 0:1]
        for head in range(2):
            qm = head_lanes(q, head)
            m_ref[...] = jnp.full_like(m_ref, NEG)

            def score(j, causal):
                at = rows_of(j, tb)
                s = dot(qm, k_ref[at, cols], 1, 1)
                ok = seg_q == marks[0:1, at].astype(F32)
                if causal:
                    r = lax.broadcasted_iota(jnp.int32, (tb, tb), 0)
                    t = lax.broadcasted_iota(jnp.int32, (tb, tb), 1)
                    ok = ok & (r >= t)
                s = jnp.where(ok, s, NEG)
                s_ref[:, at] = s
                m_ref[...] = jnp.maximum(m_ref[...], fold(s, jnp.maximum))

            def score_step(j, carry):
                score(j, False)
                return carry

            lax.fori_loop(0, i, score_step, 0)
            score(i, True)
            top = jnp.max(m_ref[...], axis=1, keepdims=True)
            l_ref[...] = jnp.zeros_like(l_ref)
            acc_ref[...] = jnp.zeros_like(acc_ref)

            def value_step(j, carry):
                at = rows_of(j, tb)
                p = jnp.exp(s_ref[:, at] - top)
                l_ref[...] += fold(p, jnp.add)
                acc_ref[...] += dot(p.astype(LOW), v_ref[at, cols], 1, 0)
                return carry

            lax.fori_loop(0, i + 1, value_step, 0)
            total = jnp.sum(l_ref[...], axis=1, keepdims=True)
            out = acc_ref[...] / total
            lse = jnp.broadcast_to(top + jnp.log(total), (tb, LANES))
            if head == 0:
                of_ref[mine, cols] = out
                lse_ref[mine, cols] = lse
            else:
                of_ref[mine, cols] = jnp.where(lane < HEAD_DIM, of_ref[mine, cols], out)
                lse_ref[mine, cols] = jnp.where(lane < HEAD_DIM, lse_ref[mine, cols], lse)
        o_ref[mine, cols] = of_ref[mine, cols].astype(LOW)

        @pl.when(i == c)
        def _():
            pltpu.make_async_copy(o_ref.at[mine, cols], home(pair), own_o.at[pair]).start()

        @pl.when(i != c)
        def _():
            k = lax.rem(i + n_ctx - c, n_ctx) - 1
            ctx_copy(o_ref.at[mine, cols], home(pair), o_send.at[k, pair], o_recv.at[k, pair], i).start()

    def query_blocks(pair, lo, hi):
        def one(i, carry):
            query_block(pair, i)
            return carry

        lax.fori_loop(lo, hi, one, 0)

    query_blocks(0, 0, n_ctx)
    for w in late:
        w.spread()
    query_blocks(1, 0, n_ctx)
    for w in late:
        w.forward()
    for pair in range(width // LANES):
        cols = slice(pair * LANES, (pair + 1) * LANES)
        pltpu.make_async_copy(o_ref.at[0:tb, cols], home(pair), own_o.at[pair]).wait()
        for k in range(n_ctx - 1):
            ctx_copy(o_ref.at[0:tb, cols], home(pair), o_send.at[k, pair], o_recv.at[k, pair], c).wait()
    for w in late:
        w.cross()
    for k in range(1, n_ctx):
        mark_copy(k).wait_send()
        pack_copy(k).wait_send()
        fv_copy(k).wait_send()
    for at, (slot, bit) in enumerate(
        [(0, NEAR), (0, FAR), (NEAR, FAR), (0, CORE), (NEAR, CORE), (FAR, CORE), (NEAR | FAR, CORE)]
    ):
        pack_hop(slot, bit, 3 + at).wait_send()
    for way in range(2):
        for step in range(3):
            tok_copy(way, step).wait_send()
    for w in weights:
        w.finish()


def front_call(n_dp, n_ctx, tok, fv, mark, pack, freq, wg, wu, wo, wd):
    tb, model = tok.shape
    width = model // n_ctx
    length = n_ctx * tb
    pairs = width // LANES
    vmem = pl.BlockSpec(memory_space=pltpu.VMEM)
    anyspace = pl.BlockSpec(memory_space=pl.ANY)
    shape = jax.ShapeDtypeStruct
    dma = pltpu.SemaphoreType.DMA
    return pl.pallas_call(
        functools.partial(front_kernel, n_ctx),
        in_specs=[anyspace] * 4 + [vmem] + [anyspace] * 4,
        out_specs=[vmem] * 11 + [anyspace] * 5,
        out_shape=[shape((length, model), LOW)]
        + [shape((length, width), LOW)] * 3
        + [shape((length, width), F32)] * 2
        + [shape((length, LANES), F32)] * 3
        + [shape((8, length), jnp.int32), shape((8, model), F32)]
        + [shape((tb, model), LOW)]
        + [shape((n_dp, n_ctx * w.shape[0], w.shape[1]), LOW) for w in (wg, wu, wo, wd)],
        scratch_shapes=[
            pltpu.VMEM((length, model), LOW),
            pltpu.VMEM((length, width), LOW),
            pltpu.VMEM((n_dp,) + pack.shape, LOW),
            pltpu.VMEM((model, 3 * width), LOW),
            pltpu.VMEM((tb // 2, model), F32),
            pltpu.VMEM((length, width), LOW),
            pltpu.VMEM((tb, length), F32),
            pltpu.VMEM((tb, LANES), F32),
            pltpu.VMEM((tb, LANES), F32),
            pltpu.VMEM((tb, LANES), F32),
            dma((n_ctx - 1,)), dma((n_ctx - 1,)),
            dma((n_ctx + 6,)), dma((n_ctx + 6,)),
            dma((2, n_ctx - 1)), dma((2, n_ctx - 1)),
            dma((n_ctx - 1,)), dma((n_ctx - 1,)),
            dma((4, 11)), dma((4, 11)),
            dma((n_ctx - 1, pairs)), dma((n_ctx - 1, pairs)),
            dma((4,)), dma((pairs,)),
        ],
        compiler_params=params(collective_id=1, has_side_effects=True),
        cost_estimate=pl.CostEstimate(
            flops=24 * 10**9, bytes_accessed=60 * 2**20, transcendentals=2 * length * length
        ),
        name="front",
    )(tok, fv, mark, pack, freq, wg, wu, wo, wd)


def attend_back_kernel(
    n_ctx, ga_ref, q_ref, k_ref, v_ref, of_ref, lse_ref, sc_ref, sr_ref, cos_ref, sin_ref, out_ref, home_ref,
    g_ref, lse_row, delta_row, dq_acc, dk_acc, dv_acc, gsend, grecv, send, recv, own,
):
    c = lax.axis_index("ctx")
    tb = dk_acc.shape[0]
    length, width = q_ref.shape
    model = n_ctx * width
    meet(n_ctx, ())

    def grad_copy(k, to):
        rows = pl.ds(pl.multiple_of(c * tb, tb), tb)
        cols = pl.ds(pl.multiple_of(to * width, width), width)
        return ctx_copy(ga_ref.at[:, cols], g_ref.at[rows, :], gsend.at[k - 1], grecv.at[k - 1], to)

    def home(pair, t):
        return home_ref.at[:, pl.ds(pl.multiple_of(t * model + c * width + pair * LANES, LANES), LANES)]

    def part(pair, t, chunk):
        rows = pl.ds(pl.multiple_of(chunk * tb, tb), tb)
        return out_ref.at[pair, rows, t * LANES : (t + 1) * LANES]

    def part_copy(pair, t, k):
        to = lax.rem(c + k, n_ctx)
        return ctx_copy(part(pair, t, to), home(pair, t), send.at[k - 1, pair, t], recv.at[k - 1, pair, t], to)

    first = [grad_copy(k, lax.rem(c + k, n_ctx)) for k in range(1, n_ctx)]
    for f in first:
        f.start()
    keep = pltpu.make_async_copy(
        ga_ref.at[:, pl.ds(pl.multiple_of(c * width, width), width)],
        g_ref.at[pl.ds(pl.multiple_of(c * tb, tb), tb), :],
        own.at[0, 0],
    )
    keep.start()
    keep.wait()
    for f in first:
        f.wait()

    r8 = lax.broadcasted_iota(jnp.int32, (8, LANES), 0)
    l8 = lax.broadcasted_iota(jnp.int32, (8, LANES), 1)
    pick = jnp.where(l8 == r8 * HEAD_DIM, 1.0, 0.0)
    group = jnp.where(l8 // HEAD_DIM == r8, 1.0, 0.0)
    exact = lax.Precision.HIGHEST
    dims = (((1,), (1,)), ((), ()))
    for pair in range(width // LANES):
        cols = slice(pair * LANES, (pair + 1) * LANES)

        def stats(b, carry):
            at = pl.ds(pl.multiple_of(b * tb, tb), tb)
            lse_row[:, at] = lax.dot_general(pick, lse_ref[at, cols], dims, precision=exact, preferred_element_type=F32)
            prod = g_ref[at, cols].astype(F32) * of_ref[at, cols]
            delta_row[:, at] = lax.dot_general(group, prod, dims, precision=exact, preferred_element_type=F32)
            dq_acc[at, :] = jnp.zeros((tb, LANES), F32)
            return carry

        lax.fori_loop(0, n_ctx, stats, 0)

        def key_block(j, carry):
            dk_acc[...] = jnp.zeros_like(dk_acc)
            dv_acc[...] = jnp.zeros_like(dv_acc)
            mine = pl.ds(pl.multiple_of(j * tb, tb), tb)
            k = k_ref[mine, cols]
            v = v_ref[mine, cols]
            seg_k = sc_ref[mine, 0:1]

            def block(i, causal):
                at = pl.ds(pl.multiple_of(i * tb, tb), tb)
                q = q_ref[at, cols]
                g = g_ref[at, cols]
                ok = seg_k == sr_ref[0:1, at].astype(F32)
                if causal:
                    r = lax.broadcasted_iota(jnp.int32, (tb, tb), 0)
                    t = lax.broadcasted_iota(jnp.int32, (tb, tb), 1)
                    ok = ok & (r <= t)
                for head in range(2):
                    qm = head_lanes(q, head)
                    gm = head_lanes(g, head)
                    s = dot(k, qm, 1, 1)
                    p = jnp.where(ok, jnp.exp(s - lse_row[head : head + 1, at]), 0.0)
                    dp = dot(v, gm, 1, 1)
                    ds = (p * (dp - delta_row[head : head + 1, at])).astype(LOW)
                    dv_acc[...] += dot(p.astype(LOW), gm, 1, 0)
                    dk_acc[...] += dot(ds, qm, 1, 0)
                    dq_acc[at, :] += dot(ds, head_lanes(k, head), 0, 0)

            block(j, True)

            def step(i, carry):
                block(i, False)
                return carry

            lax.fori_loop(j + 1, n_ctx, step, 0)
            dk = dk_acc[...]
            dk = dk * cos_ref[mine, :] - half_swap(dk) * sin_ref[mine, :]
            out_ref[pair, mine, LANES : 2 * LANES] = dk.astype(LOW)
            out_ref[pair, mine, 2 * LANES : 3 * LANES] = dv_acc[...].astype(LOW)
            return carry

        lax.fori_loop(0, n_ctx, key_block, 0)

        def query_done(b, carry):
            at = pl.ds(pl.multiple_of(b * tb, tb), tb)
            dq = dq_acc[at, :] * 0.125
            dq = dq * cos_ref[at, :] - half_swap(dq) * sin_ref[at, :]
            out_ref[pair, at, 0:LANES] = dq.astype(LOW)
            return carry

        lax.fori_loop(0, n_ctx, query_done, 0)
        for t in range(3):
            pltpu.make_async_copy(part(pair, t, c), home(pair, t), own.at[pair, t]).start()
            for k in range(1, n_ctx):
                part_copy(pair, t, k).start()
    for pair in range(width // LANES):
        for t in range(3):
            pltpu.make_async_copy(part(pair, t, c), home(pair, t), own.at[pair, t]).wait()
            for k in range(1, n_ctx):
                part_copy(pair, t, k).wait()


def attend_back_call(n_ctx, ga, q, k, v, of, lse, seg_col, seg_row, cos, sin):
    length, width = q.shape
    tb = TOKEN_BLOCK
    pairs = width // LANES
    vmem = pl.BlockSpec(memory_space=pltpu.VMEM)
    return pl.pallas_call(
        functools.partial(attend_back_kernel, n_ctx),
        in_specs=[pl.BlockSpec(memory_space=pl.ANY)] + [vmem] * 9,
        out_specs=[vmem, pl.BlockSpec(memory_space=pl.ANY)],
        out_shape=[
            jax.ShapeDtypeStruct((pairs, length, 3 * LANES), LOW),
            jax.ShapeDtypeStruct((tb, 3 * n_ctx * width), LOW),
        ],
        scratch_shapes=[
            pltpu.VMEM((length, width), LOW),
            pltpu.VMEM((8, length), F32),
            pltpu.VMEM((8, length), F32),
            pltpu.VMEM((length, LANES), F32),
            pltpu.VMEM((tb, LANES), F32),
            pltpu.VMEM((tb, LANES), F32),
            pltpu.SemaphoreType.DMA((n_ctx - 1,)),
            pltpu.SemaphoreType.DMA((n_ctx - 1,)),
            pltpu.SemaphoreType.DMA((n_ctx - 1, pairs, 3)),
            pltpu.SemaphoreType.DMA((n_ctx - 1, pairs, 3)),
            pltpu.SemaphoreType.DMA((pairs, 3)),
        ],
        compiler_params=params(collective_id=2, has_side_effects=True),
        cost_estimate=pl.CostEstimate(
            flops=40 * 10**9, bytes_accessed=16 * 2**20, transcendentals=2 * length * length
        ),
        name="attend_back",
    )(ga, q, k, v, of, lse, seg_col, seg_row, cos, sin)


def mlp_kernel(blocks, tok_ref, att_ref, cot_ref, gain_ref, *refs):
    (wo_in, wg_in, wu_in, wd_in), refs = refs[:4], refs[4:]
    out_ref, gm_ref, ga_ref, gk, gs, uk, us, ok, os, dk, ds = refs[:11]
    wo, wg, wu, wd, att, nat, n2, mi, mit, inv_ref, oacc, dacc, dwd, sem, osem = refs[11:]
    dp = lax.axis_index("dp")
    u = pl.program_id(0)
    last = pl.num_programs(0) - 1
    down = wd_in.shape[1]

    def copies():
        made = []
        for d in range(blocks):
            at = pl.ds(d * LANES, LANES)
            made.append(pltpu.make_async_copy(wo_in.at[d], wo.at[at, :], sem.at[0, d]))
        for d in range(blocks):
            at = pl.ds(d * LANES, LANES)
            made.append(pltpu.make_async_copy(wg_in.at[d], wg.at[at, :], sem.at[1, d]))
            made.append(pltpu.make_async_copy(wu_in.at[d], wu.at[at, :], sem.at[2, d]))
            rows = pl.ds(pl.multiple_of((dp ^ d) * down, 32), down)
            made.append(pltpu.make_async_copy(wd_in.at[d], wd.at[rows, :], sem.at[3, d]))
        return made

    def out_copies():
        made = []
        for d in range(blocks):
            rows = pl.ds(pl.multiple_of((dp ^ d) * down, 32), down)
            made.append(pltpu.make_async_copy(dwd.at[rows, :], (ds if d % 2 else dk).at[d // 2], osem.at[d]))
        return made

    @pl.when(u == 0)
    def _():
        made = copies()
        for c in made:
            c.start()
        for d in range(blocks):
            att[:, d * LANES : (d + 1) * LANES] = att_ref[:, lane_block(dp ^ d)]
        for c in made[:blocks]:
            c.wait()
        mid = tok_ref[...].astype(F32) + dot(att[...], wo[...], 1, 0)
        inv = lax.rsqrt(jnp.mean(mid * mid, axis=-1, keepdims=True) + epsilon)
        oacc[...] = mid
        nat[...] = mid * inv
        inv_ref[...] = jnp.broadcast_to(inv, inv_ref.shape)
        for d in range(blocks):
            n2[:, d * LANES : (d + 1) * LANES] = nat[:, lane_block(dp ^ d)]
        mi[...] = (n2[...] * gain_ref[...]).astype(LOW)
        mit[...] = mi[...].T
        dacc[...] = jnp.zeros_like(dacc)
        for c in made[blocks:]:
            c.wait()

    cols = pl.ds(pl.multiple_of(u * FF_BLOCK, FF_BLOCK), FF_BLOCK)
    x = mi[...]
    cot = cot_ref[...]
    wgu, wuu, wdu = wg[:, cols], wu[:, cols], wd[cols, :]
    gate = dot(x, wgu, 1, 0)
    up = dot(x, wuu, 1, 0)
    grad_hidden = dot(cot, wdu, 1, 1)
    sig = jax.nn.sigmoid(gate)
    hidden = (gate * sig * up).astype(LOW)
    dg = (grad_hidden * up * sig * (1.0 + gate * (1.0 - sig))).astype(LOW)
    du = (grad_hidden * gate * sig).astype(LOW)
    oacc[...] += dot(hidden, wdu, 1, 0)
    dacc[...] += dot(dg, wgu, 1, 1) + dot(du, wuu, 1, 1)
    xt = mit[...]
    dwg = dot(xt, dg, 1, 0).astype(LOW)
    dwu = dot(xt, du, 1, 0).astype(LOW)
    for d in range(blocks):
        (gs if d % 2 else gk)[d // 2] = dwg[d * LANES : (d + 1) * LANES]
        (us if d % 2 else uk)[d // 2] = dwu[d * LANES : (d + 1) * LANES]
    dwd[cols, :] = dot(hidden, cot, 0, 0).astype(LOW)

    @pl.when(u == last)
    def _():
        made = out_copies()
        for c in made:
            c.start()
        out_ref[...] = oacc[...].astype(LOW)
        scaled = dacc[...] * gain_ref[...]
        norm = n2[...]
        mean = jnp.mean(scaled * norm, axis=-1, keepdims=True)
        n2[...] = inv_ref[:, 0:1] * (scaled - norm * mean)
        for d in range(blocks):
            nat[:, lane_block(dp ^ d)] = n2[:, d * LANES : (d + 1) * LANES]
        gm = cot.astype(F32) + nat[...]
        gm_ref[...] = gm
        gb = gm.astype(LOW)
        n2[...] = dot(gb, wo[...], 1, 1)
        for d in range(blocks):
            ga_ref[:, lane_block(dp ^ d)] = n2[:, d * LANES : (d + 1) * LANES].astype(LOW)
        dwo = dot(att[...], gb, 0, 0).astype(LOW)
        for d in range(blocks):
            (os if d % 2 else ok)[d // 2] = dwo[d * LANES : (d + 1) * LANES]
        for c in made:
            c.wait()


def mlp_call(tok, att, cot, gain, wo, wg, wu, wd):
    tb, model = tok.shape
    blocks, _, ff = wg.shape
    half = blocks // 2
    down = wd.shape[1]
    whole = lambda a: pl.BlockSpec(a.shape, lambda u: (0, 0))
    anyspace = pl.BlockSpec(memory_space=pl.ANY)
    half_cols = pl.BlockSpec((half, LANES, FF_BLOCK), lambda u: (0, 0, u))
    half_out = pl.BlockSpec((half, LANES, model), lambda u: (0, 0, 0))
    tokens = pl.BlockSpec((tb, model), lambda u: (0, 0))
    shape = jax.ShapeDtypeStruct
    return pl.pallas_call(
        functools.partial(mlp_kernel, blocks),
        grid=(ff // FF_BLOCK,),
        in_specs=[whole(tok), whole(att), whole(cot), whole(gain)] + [anyspace] * 4,
        out_specs=[tokens, tokens, tokens] + [half_cols] * 4 + [half_out] * 2 + [anyspace] * 2,
        out_shape=[shape((tb, model), LOW), shape((tb, model), F32), shape((tb, model), LOW)]
        + [shape((half, LANES, ff), LOW)] * 4
        + [shape((half, LANES, model), LOW)] * 2
        + [shape((half, down, model), LOW)] * 2,
        scratch_shapes=[
            pltpu.VMEM((model, model), LOW),
            pltpu.VMEM((model, ff), LOW),
            pltpu.VMEM((model, ff), LOW),
            pltpu.VMEM((ff, model), LOW),
            pltpu.VMEM((tb, model), LOW),
            pltpu.VMEM((tb, model), F32),
            pltpu.VMEM((tb, model), F32),
            pltpu.VMEM((tb, model), LOW),
            pltpu.VMEM((model, tb), LOW),
            pltpu.VMEM((tb, LANES), F32),
            pltpu.VMEM((tb, model), F32),
            pltpu.VMEM((tb, model), F32),
            pltpu.VMEM((ff, model), LOW),
            pltpu.SemaphoreType.DMA((4, blocks)),
            pltpu.SemaphoreType.DMA((blocks,)),
        ],
        compiler_params=params(),
        cost_estimate=pl.CostEstimate(
            flops=2 * tb * model * (8 * ff + 3 * model), bytes_accessed=50 * 2**20, transcendentals=0
        ),
        name="mlp",
    )(tok, att, cot, gain, wo, wg, wu, wd)


def input_kernel(blocks, tok_ref, gm_ref, v1_ref, gain_ref, g, *refs):
    w_in, refs = refs[:blocks], refs[blocks:]
    ig_ref, vg_ref, w, rel, nat, sem = refs
    dp = lax.axis_index("dp")
    model = tok_ref.shape[1]
    made = [pltpu.make_async_copy(w_in[d], w.at[pl.ds(d * LANES, LANES), :], sem.at[d]) for d in range(blocks)]
    for m in made:
        m.start()
    for d in range(blocks):
        rel[:, d * LANES : (d + 1) * LANES] = tok_ref[:, lane_block(dp ^ d)].astype(F32)
    gv = g[:, 2 * model :].astype(F32)
    vg_ref[...] = v1_ref[...] + 0.5 * gv
    x = rel[...]
    inv = lax.rsqrt(jnp.mean(x * x, axis=-1, keepdims=True) + epsilon)
    norm = x * inv
    for m in made:
        m.wait()
    grad = dot(g[:, : 2 * model], w[:, : 2 * model], 1, 1)
    grad = grad + 0.5 * dot(g[:, 2 * model :], w[:, 2 * model :], 1, 1)
    scaled = grad * gain_ref[...]
    mean = jnp.mean(scaled * norm, axis=-1, keepdims=True)
    rel[...] = inv * (scaled - norm * mean)
    for d in range(blocks):
        nat[:, lane_block(dp ^ d)] = rel[:, d * LANES : (d + 1) * LANES]
    ig_ref[...] = gm_ref[...] + nat[...]


def input_call(tok, gm, v1, gain, g, ws):
    tb, model = tok.shape
    blocks = len(ws)
    vmem = pl.BlockSpec(memory_space=pltpu.VMEM)
    shape = jax.ShapeDtypeStruct
    return pl.pallas_call(
        functools.partial(input_kernel, blocks),
        in_specs=[vmem] * 5 + [pl.BlockSpec(memory_space=pl.ANY)] * blocks,
        out_specs=[vmem, vmem],
        out_shape=[shape((tb, model), F32)] * 2,
        scratch_shapes=[
            pltpu.VMEM((model, 3 * model), LOW),
            pltpu.VMEM((tb, model), F32),
            pltpu.VMEM((tb, model), F32),
            pltpu.SemaphoreType.DMA((blocks,)),
        ],
        compiler_params=params(),
        cost_estimate=pl.CostEstimate(
            flops=2 * tb * model * 3 * model, bytes_accessed=20 * 2**20, transcendentals=0
        ),
        name="input_grad",
    )(tok, gm, v1, gain, g, *ws)


def fast_local(
    n_dp, n_ctx, tokens, first_values, v1_accum, segment_ids, positions, cotangent,
    attn_gain, w_query, w_key, w_value, w_out, mlp_gain, w_gate, w_up, w_down,
):
    c = lax.axis_index("ctx")
    seq, model = tokens.shape[1:]
    width = model // n_ctx
    length = seq * n_ctx
    ff = w_gate.shape[1]
    own_rows = w_query.shape[0]
    down_rows = w_down.shape[0]
    bits = [1 << b for b in range(n_dp.bit_length() - 1)]
    plane = bits[1:]

    def shift(x, k):
        return lax.ppermute(x, "ctx", [(i, (i + k) % n_ctx) for i in range(n_ctx)])

    def flip(x, bit):
        return lax.ppermute(x, "dp", [(i, i ^ bit) for i in range(n_dp)])

    def cut(x, index, size, axis):
        return lax.dynamic_slice_in_dim(x, index * size, size, axis)

    def swap_ctx(x, axis):
        size = x.shape[axis] // n_ctx
        return [cut(x, c, size, axis)] + [shift(cut(x, (c + k) % n_ctx, size, axis), k) for k in range(1, n_ctx)]

    def place(slots, axis):
        size = slots[0].shape[axis]
        dims = list(slots[0].shape)
        dims[axis] = size * n_ctx
        out = jnp.zeros(dims, slots[0].dtype)
        for k, slot in enumerate(slots):
            out = lax.dynamic_update_slice_in_dim(out, slot, ((c + n_ctx - k) % n_ctx) * size, axis)
        return out

    def gather_dp(x, order):
        got = {0: x}
        for bit in order:
            for d in sorted(got):
                got[d ^ bit] = flip(got[d], bit)
        return [got[d] for d in range(n_dp)]

    def gather_ctx(x):
        return lax.all_gather(x, "ctx", axis=0, tiled=True)

    pairs = width // LANES
    tok = tokens[0]
    mark = jnp.concatenate([segment_ids, positions, jnp.zeros((6, seq), jnp.int32)], axis=0)
    gains = jnp.stack([attn_gain, mlp_gain], axis=1)
    gains = jnp.tile(jnp.pad(gains, ((0, 0), (0, width - 2))), (1, n_ctx))
    pack = jnp.concatenate([w_query, w_key, w_value, gains], axis=0)
    pack = pack.reshape(4 * own_rows, n_ctx, width).transpose(1, 0, 2)
    freqs = 10000.0 ** (-jnp.arange(HEAD_DIM // 2).astype(F32) * (2.0 / HEAD_DIM))
    turn = jnp.ones((HEAD_DIM // 2,), F32)
    freq = jnp.stack([jnp.tile(freqs, 4), jnp.tile(jnp.concatenate([-turn, turn]), 2)])
    freq = jnp.pad(freq, ((0, 6), (0, 0)))
    (xn, q, k, v, out_full, log_total, cos, sin, seg_col, seg_row, gain_rows, attended,
     gate_all, up_all, out_all, down_all) = front_call(
        n_dp, n_ctx, tok, first_values[0], mark, pack, freq, w_gate, w_up, w_out, w_down
    )
    gain_rel, gain_two_rel = gain_rows[0:1], gain_rows[1:2]
    cot = cotangent[0]
    (output, grad_middle, grad_attended, gate_keep, gate_send, up_keep, up_send, out_keep, out_send,
     down_keep, down_send) = mlp_call(tok, attended, cot, gain_two_rel, out_all, gate_all, up_all, down_all)

    qkv_all = gather_dp(gather_ctx(jnp.concatenate([w_query, w_key, w_value], axis=1)), plane + bits[:1])

    back, home_grad = attend_back_call(
        n_ctx, grad_attended, q, k, v, out_full, log_total, seg_col, seg_row, cos, sin
    )

    def scatter_dp(keep, send, order):
        terms = [keep, flip(send, bits[0])]
        count = keep.shape[0]
        names = list(range(count))
        for bit in order:
            near = bit >> 1
            stay = [n for n in names if not n & near]
            leave = [n for n in names if n & near]

            def pick(which):
                return sum(
                    jnp.stack([t[names.index(n)] for n in which]).astype(F32) for t in terms
                )

            got = flip(pick(leave).astype(LOW), bit)
            terms = [jnp.stack([t[names.index(n)] for n in stay]) for t in terms] + [got]
            names = stay
        return sum(t[0].astype(F32) for t in terms)

    def scatter_ctx(x):
        size = x.shape[0] // n_ctx
        got = cut(x, c, size, 0)
        for k in range(1, n_ctx):
            got = got + shift(cut(x, (c + k) % n_ctx, size, 0).astype(LOW), k).astype(F32)
        return got

    gate_grad = scatter_ctx(scatter_dp(gate_keep, gate_send, plane))
    up_grad = scatter_ctx(scatter_dp(up_keep, up_send, plane[::-1]))
    down_grad = scatter_ctx(scatter_dp(down_keep, down_send, plane))
    out_grad = scatter_ctx(scatter_dp(out_keep, out_send, plane[::-1]))

    qkv_grad = jnp.zeros((3, own_rows, model), F32)
    for p in range(pairs):
        product = lax.dot_general(
            xn, back[p], (((0,), (0,)), ((), ())), preferred_element_type=F32
        ).astype(LOW).reshape(n_dp // 2, 2, model // n_dp, 3 * LANES)
        total = scatter_dp(product[:, 0], product[:, 1], plane)
        for s, slot in enumerate(swap_ctx(total.astype(LOW), 0)):
            block = slot.astype(F32).reshape(own_rows, 3, LANES).transpose(1, 0, 2)
            at = ((c + n_ctx - s) % n_ctx) * width + p * LANES
            qkv_grad = lax.dynamic_update_slice_in_dim(qkv_grad, block, at, 2)
    query_grad, key_grad, value_grad = qkv_grad[0], qkv_grad[1], 0.5 * qkv_grad[2]

    input_grad, v1_grad = input_call(tok, grad_middle, v1_accum[0], gain_rel, home_grad, qkv_all)

    def row_dot(a, w):
        return jnp.sum(a * w.astype(F32), axis=1)

    gain_one = (
        row_dot(query_grad, w_query) + row_dot(key_grad, w_key) + row_dot(value_grad, w_value)
    ) / attn_gain.astype(F32)
    gain_two = (row_dot(gate_grad, w_gate) + row_dot(up_grad, w_up)) / mlp_gain.astype(F32)
    return (
        output[None], input_grad[None], v1_grad[None], gain_one, query_grad, key_grad, value_grad,
        out_grad, gain_two, gate_grad, up_grad, down_grad,
    )


def solution(mesh):
    placed = (
        P("dp", "ctx", None),
        P("dp", "ctx", None),
        P("dp", "ctx", None),
        P("dp", "ctx"),
        P("dp", "ctx"),
        P("dp", "ctx", None),
        P(("dp", "ctx")),
        P(("dp", "ctx"), None),
        P(("dp", "ctx"), None),
        P(("dp", "ctx"), None),
        P(("dp", "ctx"), None),
        P(("dp", "ctx")),
        P(("dp", "ctx"), None),
        P(("dp", "ctx"), None),
        P(("dp", "ctx"), None),
    )
    n_dp, n_ctx = mesh.shape["dp"], mesh.shape["ctx"]

    def local(*args):
        rows, seq, model = args[0].shape
        fits = (
            rows == 1
            and seq == TOKEN_BLOCK
            and model == n_dp * LANES
            and model == 2 * LANES * n_ctx
            and args[12].shape[1] % FF_BLOCK == 0
        )
        return fast_local(n_dp, n_ctx, *args) if fits else plain_local(*args)

    return jax.shard_map(
        local,
        mesh=mesh,
        in_specs=placed,
        out_specs=(
            P("dp", "ctx", None),
            P("dp", "ctx", None),
            P("dp", "ctx", None),
            P(("dp", "ctx")),
            P(("dp", "ctx"), None),
            P(("dp", "ctx"), None),
            P(("dp", "ctx"), None),
            P(("dp", "ctx"), None),
            P(("dp", "ctx")),
            P(("dp", "ctx"), None),
            P(("dp", "ctx"), None),
            P(("dp", "ctx"), None),
        ),
        check_vma=False,
    )
```

```python
import functools

import jax
import jax.numpy as jnp
from jax import lax
from jax.experimental import pallas as pl
from jax.experimental.pallas import tpu as pltpu
from jax.sharding import PartitionSpec as P

HEADS = 16
HEAD_DIM = 64
LANES = 128
TOKEN_BLOCK = 512
FF_BLOCK = 256
NEG = -1e30
MESH = pl.DeviceIdType.MESH
F32 = jnp.float32
LOW = jnp.bfloat16
BYTES = 63 * 2**20
epsilon = 1e-05


HEAD_BLOCK = 4


def rms_scale(values):
    return lax.rsqrt(jnp.mean(values * values, axis=-1, keepdims=True) + epsilon)


def angle_tables(position_rows):
    freqs = 10000.0 ** (-jnp.arange(HEAD_DIM // 2).astype(jnp.float32) * (2.0 / HEAD_DIM))
    angles = position_rows.astype(jnp.float32)[..., None] * freqs
    return (jnp.cos(angles)[..., None, :], jnp.sin(angles)[..., None, :])


def rotate(heads_in, cosine_table, sine_table):
    half_dim = heads_in.shape[-1] // 2
    first_half = heads_in[..., :half_dim]
    second_half = heads_in[..., half_dim:]
    return jnp.concatenate(
        [
            first_half * cosine_table - second_half * sine_table,
            second_half * cosine_table + first_half * sine_table,
        ],
        axis=-1,
    )


def norm_back(grad_normed, normed, inv_root, norm_gain):
    grad_scaled = grad_normed * norm_gain.astype(jnp.float32)
    grad_input = inv_root * (
        grad_scaled - normed * jnp.mean(grad_scaled * normed, axis=-1, keepdims=True)
    )
    return (grad_input, jnp.sum(grad_normed * normed, axis=0))


def attn_front(flat_tokens, first_flat, attn_set, cosine_table, sine_table, row_count, seq_piece):
    inv_root = rms_scale(flat_tokens)
    normed = flat_tokens * inv_root
    normed_in = (normed * attn_set[0].astype(jnp.float32)).astype(jnp.bfloat16)
    query_proj = jnp.dot(normed_in, attn_set[1], preferred_element_type=jnp.float32)
    key_proj = jnp.dot(normed_in, attn_set[2], preferred_element_type=jnp.float32)
    value_proj = jnp.dot(normed_in, attn_set[3], preferred_element_type=jnp.float32)
    query_rot = rotate(
        query_proj.reshape(row_count, seq_piece, HEADS, HEAD_DIM), cosine_table, sine_table
    )
    key_rot = rotate(
        key_proj.reshape(row_count, seq_piece, HEADS, HEAD_DIM), cosine_table, sine_table
    )
    query_rot = query_rot.astype(jnp.bfloat16).reshape(row_count, seq_piece, -1)
    key_rot = key_rot.astype(jnp.bfloat16).reshape(row_count, seq_piece, -1)
    value_mix = (
        (0.5 * value_proj + 0.5 * first_flat).astype(jnp.bfloat16).reshape(row_count, seq_piece, -1)
    )
    return (normed, inv_root, normed_in, query_rot, key_rot, value_mix)


def mlp_block(flat_tokens, attended_low, out_weight, mlp_set):
    middle = flat_tokens + jnp.dot(attended_low, out_weight, preferred_element_type=jnp.float32)
    inv_root_two = rms_scale(middle)
    normed_two = middle * inv_root_two
    mlp_in = (normed_two * mlp_set[0].astype(jnp.float32)).astype(jnp.bfloat16)
    gate_proj = jnp.dot(mlp_in, mlp_set[1], preferred_element_type=jnp.float32)
    up_proj = jnp.dot(mlp_in, mlp_set[2], preferred_element_type=jnp.float32)
    hidden = (gate_proj * jax.nn.sigmoid(gate_proj) * up_proj).astype(jnp.bfloat16)
    result = middle + jnp.dot(hidden, mlp_set[3], preferred_element_type=jnp.float32)
    return (normed_two, inv_root_two, mlp_in, gate_proj, up_proj, hidden, result)


def split_groups(row_block):
    tok_count = row_block.shape[0]
    return row_block.reshape(tok_count, HEADS // HEAD_BLOCK, HEAD_BLOCK * HEAD_DIM).transpose(
        1, 0, 2
    )


def join_groups(group_block):
    return group_block.transpose(1, 0, 2).reshape(group_block.shape[1], -1)


def as_heads(block):
    return block.reshape(block.shape[0], HEAD_BLOCK, HEAD_DIM)


def attend_row(members):
    query_row, key_row, value_row, allowed = members

    def per_group(pieces):
        query_block, key_block, value_block = pieces
        scores = (
            jnp.einsum(
                "qhd,khd->hqk",
                as_heads(query_block),
                as_heads(key_block),
                preferred_element_type=jnp.float32,
            )
            * 0.125
        )
        scores = jnp.where(allowed[None], scores, -1e30)
        highest = jnp.max(scores, axis=-1, keepdims=True)
        exp_scores = jnp.exp(scores - highest)
        denominator = jnp.sum(exp_scores, axis=-1, keepdims=True)
        soft_low = (exp_scores / denominator).astype(jnp.bfloat16)
        attended = jnp.einsum(
            "hqk,khd->qhd", soft_low, as_heads(value_block), preferred_element_type=jnp.float32
        )
        return (
            attended.reshape(query_block.shape[0], -1),
            (highest + jnp.log(denominator))[..., 0],
        )

    attended, log_total = lax.map(
        per_group, (split_groups(query_row), split_groups(key_row), split_groups(value_row))
    )
    return (join_groups(attended), log_total)


def attend_back(members):
    query_row, key_row, value_row, grad_row, log_total, allowed = members

    def per_group(pieces):
        query_block, key_block, value_block, grad_block, log_block = pieces
        query_heads = as_heads(query_block)
        key_heads = as_heads(key_block)
        grad_heads = as_heads(grad_block)
        scores = (
            jnp.einsum("qhd,khd->hqk", query_heads, key_heads, preferred_element_type=jnp.float32)
            * 0.125
        )
        soft_weights = jnp.where(allowed[None], jnp.exp(scores - log_block[..., None]), 0.0)
        soft_low = soft_weights.astype(jnp.bfloat16)
        grad_probs = jnp.einsum(
            "qhd,khd->hqk", grad_heads, as_heads(value_block), preferred_element_type=jnp.float32
        )
        row_delta = jnp.sum(soft_weights * grad_probs, axis=-1, keepdims=True)
        grad_scores = (soft_weights * (grad_probs - row_delta)).astype(jnp.bfloat16)
        grad_query = (
            jnp.einsum("hqk,khd->qhd", grad_scores, key_heads, preferred_element_type=jnp.float32)
            * 0.125
        )
        grad_key = (
            jnp.einsum("hqk,qhd->khd", grad_scores, query_heads, preferred_element_type=jnp.float32)
            * 0.125
        )
        grad_value = jnp.einsum(
            "hqk,qhd->khd", soft_low, grad_heads, preferred_element_type=jnp.float32
        )
        return (
            grad_query.reshape(query_block.shape[0], -1),
            grad_key.reshape(key_block.shape[0], -1),
            grad_value.reshape(key_block.shape[0], -1),
        )

    grad_query, grad_key, grad_value = lax.map(
        per_group,
        (
            split_groups(query_row),
            split_groups(key_row),
            split_groups(value_row),
            split_groups(grad_row),
            log_total,
        ),
    )
    return (join_groups(grad_query), join_groups(grad_key), join_groups(grad_value))


def plain_local(
    tokens,
    first_values,
    v1_accum,
    segment_ids,
    positions,
    cotangent,
    attn_gain,
    w_query,
    w_key,
    w_value,
    w_out,
    mlp_gain,
    w_gate,
    w_up,
    w_down,
):
    row_count, seq_piece, model_width = tokens.shape
    token_count = row_count * seq_piece
    flat_tokens = tokens.astype(jnp.float32).reshape(token_count, model_width)
    first_flat = first_values.astype(jnp.float32).reshape(token_count, model_width)
    cosine_table, sine_table = angle_tables(positions)
    segment_low = segment_ids.astype(jnp.bfloat16)
    attn_set = (
        lax.all_gather(attn_gain, ("dp", "ctx"), axis=0, tiled=True),
        lax.all_gather(w_query, ("dp", "ctx"), axis=0, tiled=True),
        lax.all_gather(w_key, ("dp", "ctx"), axis=0, tiled=True),
        lax.all_gather(w_value, ("dp", "ctx"), axis=0, tiled=True),
        lax.all_gather(w_out, ("dp", "ctx"), axis=0, tiled=True),
    )
    normed, inv_root, normed_in, query_rot, key_rot, value_mix = attn_front(
        flat_tokens, first_flat, attn_set, cosine_table, sine_table, row_count, seq_piece
    )
    key_full, value_full, segment_full = (
        lax.all_gather(key_rot, "ctx", axis=1, tiled=True),
        lax.all_gather(value_mix, "ctx", axis=1, tiled=True),
        lax.all_gather(segment_low, "ctx", axis=1, tiled=True),
    )
    query_order = lax.axis_index("ctx") * seq_piece + jnp.arange(seq_piece, dtype=jnp.int32)
    full_order = jnp.arange(key_full.shape[1], dtype=jnp.int32)
    segment_own = segment_ids.astype(jnp.float32)
    segment_all = segment_full.astype(jnp.float32)
    allowed = (segment_own[:, :, None] == segment_all[:, None, :]) & (
        query_order[None, :, None] >= full_order[None, None, :]
    )
    attended, log_total = lax.map(attend_row, (query_rot, key_full, value_full, allowed))
    attended_low = attended.reshape(token_count, model_width).astype(jnp.bfloat16)
    mlp_set = (
        lax.all_gather(mlp_gain, ("dp", "ctx"), axis=0, tiled=True),
        lax.all_gather(w_gate, ("dp", "ctx"), axis=0, tiled=True),
        lax.all_gather(w_up, ("dp", "ctx"), axis=0, tiled=True),
        lax.all_gather(w_down, ("dp", "ctx"), axis=0, tiled=True),
    )
    normed_two, inv_root_two, mlp_in, gate_proj, up_proj, hidden, output_flat = mlp_block(
        flat_tokens, attended_low, attn_set[4], mlp_set
    )
    output = output_flat.reshape(tokens.shape).astype(jnp.bfloat16)
    attn_set = (
        lax.all_gather(attn_gain, ("dp", "ctx"), axis=0, tiled=True),
        lax.all_gather(w_query, ("dp", "ctx"), axis=0, tiled=True),
        lax.all_gather(w_key, ("dp", "ctx"), axis=0, tiled=True),
        lax.all_gather(w_value, ("dp", "ctx"), axis=0, tiled=True),
        lax.all_gather(w_out, ("dp", "ctx"), axis=0, tiled=True),
    )
    mlp_set = (
        lax.all_gather(mlp_gain, ("dp", "ctx"), axis=0, tiled=True),
        lax.all_gather(w_gate, ("dp", "ctx"), axis=0, tiled=True),
        lax.all_gather(w_up, ("dp", "ctx"), axis=0, tiled=True),
        lax.all_gather(w_down, ("dp", "ctx"), axis=0, tiled=True),
    )
    normed, inv_root, normed_in, query_rot, key_rot, value_mix = attn_front(
        flat_tokens, first_flat, attn_set, cosine_table, sine_table, row_count, seq_piece
    )
    key_full, value_full = (
        lax.all_gather(key_rot, "ctx", axis=1, tiled=True),
        lax.all_gather(value_mix, "ctx", axis=1, tiled=True),
    )
    normed_two, inv_root_two, mlp_in, gate_proj, up_proj, hidden, output_flat = mlp_block(
        flat_tokens, attended_low, attn_set[4], mlp_set
    )
    cot_low = cotangent.reshape(token_count, model_width)
    cot_float = cot_low.astype(jnp.float32)
    grad_hidden = jnp.einsum("td,fd->tf", cot_low, mlp_set[3], preferred_element_type=jnp.float32)
    sigma = jax.nn.sigmoid(gate_proj)
    grad_gate_low = (grad_hidden * up_proj * sigma * (1.0 + gate_proj * (1.0 - sigma))).astype(
        jnp.bfloat16
    )
    grad_up_low = (grad_hidden * gate_proj * sigma).astype(jnp.bfloat16)
    grad_mlp_in = jnp.einsum(
        "tf,df->td", grad_gate_low, mlp_set[1], preferred_element_type=jnp.float32
    )
    grad_mlp_in = grad_mlp_in + jnp.einsum(
        "tf,df->td", grad_up_low, mlp_set[2], preferred_element_type=jnp.float32
    )
    grad_middle_norm, grad_gain_two = norm_back(grad_mlp_in, normed_two, inv_root_two, mlp_set[0])
    grad_middle = cot_float + grad_middle_norm
    grad_branch_low = grad_middle.astype(jnp.bfloat16)
    grad_attended = jnp.einsum(
        "te,de->td", grad_branch_low, attn_set[4], preferred_element_type=jnp.float32
    )
    grad_attended = grad_attended.astype(jnp.bfloat16).reshape(row_count, seq_piece, model_width)
    grad_query_rot, grad_key_full, grad_value_full = lax.map(
        attend_back, (query_rot, key_full, value_full, grad_attended, log_total, allowed)
    )
    grad_key_rot, grad_value_mix = (
        lax.psum_scatter(
            grad_key_full.astype(jnp.bfloat16), "ctx", scatter_dimension=1, tiled=True
        ).astype(jnp.float32),
        lax.psum_scatter(
            grad_value_full.astype(jnp.bfloat16), "ctx", scatter_dimension=1, tiled=True
        ).astype(jnp.float32),
    )
    v1_grad = v1_accum + 0.5 * grad_value_mix
    grad_query_low = rotate(
        grad_query_rot.reshape(row_count, seq_piece, HEADS, HEAD_DIM), cosine_table, -sine_table
    )
    grad_query_low = grad_query_low.astype(jnp.bfloat16).reshape(token_count, model_width)
    grad_key_low = rotate(
        grad_key_rot.reshape(row_count, seq_piece, HEADS, HEAD_DIM), cosine_table, -sine_table
    )
    grad_key_low = grad_key_low.astype(jnp.bfloat16).reshape(token_count, model_width)
    grad_value_low = (0.5 * grad_value_mix).astype(jnp.bfloat16).reshape(token_count, model_width)
    grad_normed_in = jnp.einsum(
        "te,de->td", grad_query_low, attn_set[1], preferred_element_type=jnp.float32
    )
    grad_normed_in = grad_normed_in + jnp.einsum(
        "te,de->td", grad_key_low, attn_set[2], preferred_element_type=jnp.float32
    )
    grad_normed_in = grad_normed_in + jnp.einsum(
        "te,de->td", grad_value_low, attn_set[3], preferred_element_type=jnp.float32
    )
    grad_input_norm, grad_gain_one = norm_back(grad_normed_in, normed, inv_root, attn_set[0])
    input_grad = (grad_middle + grad_input_norm).reshape(tokens.shape)
    attn_right = jnp.concatenate([grad_query_low, grad_key_low, grad_value_low], axis=1)
    left_in = normed_in
    projections = jnp.einsum("td,te->de", left_in, attn_right, preferred_element_type=jnp.float32)
    out_part = jnp.einsum(
        "td,te->de", attended_low, grad_branch_low, preferred_element_type=jnp.float32
    )
    attn_matrix = lax.psum_scatter(
        jnp.concatenate([projections, out_part], axis=1),
        ("dp", "ctx"),
        scatter_dimension=0,
        tiled=True,
    )
    mlp_right = jnp.concatenate([grad_gate_low, grad_up_low], axis=1)
    left_in = mlp_in
    gate_up_matrix = lax.psum_scatter(
        jnp.einsum("td,tf->df", left_in, mlp_right, preferred_element_type=jnp.float32),
        ("dp", "ctx"),
        scatter_dimension=0,
        tiled=True,
    )
    down_matrix = lax.psum_scatter(
        jnp.einsum("tf,td->fd", hidden, cot_low, preferred_element_type=jnp.float32),
        ("dp", "ctx"),
        scatter_dimension=0,
        tiled=True,
    )
    gain_one, gain_two = (
        lax.psum_scatter(grad_gain_one, ("dp", "ctx"), scatter_dimension=0, tiled=True),
        lax.psum_scatter(grad_gain_two, ("dp", "ctx"), scatter_dimension=0, tiled=True),
    )
    ff_width = w_gate.shape[1]
    return (
        output,
        input_grad,
        v1_grad,
        gain_one,
        attn_matrix[:, 0:model_width],
        attn_matrix[:, model_width : 2 * model_width],
        attn_matrix[:, 2 * model_width : 3 * model_width],
        attn_matrix[:, 3 * model_width : 4 * model_width],
        gain_two,
        gate_up_matrix[:, 0:ff_width],
        gate_up_matrix[:, ff_width : 2 * ff_width],
        down_matrix,
    )


def params(**kw):
    return pltpu.CompilerParams(vmem_limit_bytes=BYTES, **kw)


def dot(a, b, da, db):
    return lax.dot_general(a, b, (((da,), (db,)), ((), ())), preferred_element_type=F32)


def lane_block(index):
    return pl.ds(pl.multiple_of(index * LANES, LANES), LANES)


def half_swap(x):
    lane = lax.broadcasted_iota(jnp.int32, x.shape, 1)
    left = pltpu.roll(x, LANES - HEAD_DIM // 2, 1)
    right = pltpu.roll(x, HEAD_DIM // 2, 1)
    return jnp.where(lane % HEAD_DIM < HEAD_DIM // 2, left, right)


def head_lanes(x, head):
    lane = lax.broadcasted_iota(jnp.int32, x.shape, 1)
    return jnp.where(lane // HEAD_DIM == head, x, jnp.zeros_like(x))


def meet(n_ctx, bits):
    c, dp = lax.axis_index("ctx"), lax.axis_index("dp")
    barrier = pltpu.get_barrier_semaphore()
    for k in range(1, n_ctx):
        pl.semaphore_signal(barrier, inc=1, device_id={"ctx": lax.rem(c + k, n_ctx)}, device_id_type=MESH)
    for bit in bits:
        pl.semaphore_signal(barrier, inc=1, device_id={"dp": dp ^ bit}, device_id_type=MESH)
    pl.semaphore_wait(barrier, n_ctx - 1 + len(bits))


def ctx_copy(src, dst, send, recv, to):
    return pltpu.make_async_remote_copy(
        src_ref=src, dst_ref=dst, send_sem=send, recv_sem=recv, device_id={"ctx": to}, device_id_type=MESH
    )


def dp_copy(src, dst, send, recv, bit):
    to = lax.axis_index("dp") ^ bit
    return pltpu.make_async_remote_copy(
        src_ref=src, dst_ref=dst, send_sem=send, recv_sem=recv, device_id={"dp": to}, device_id_type=MESH
    )


def rows_of(index, size):
    return pl.ds(pl.multiple_of(index * size, size), size)


CORE, NEAR, FAR = 1, 2, 4


class Gather:
    def __init__(self, n_ctx, src, dst, send, recv, order):
        self.n, self.src, self.dst, self.send, self.recv = n_ctx, src, dst, send, recv
        self.first, self.second = order
        self.rows = src.shape[0]

    def along(self, k):
        c = lax.axis_index("ctx")
        to = lax.rem(c + k, self.n)
        return ctx_copy(self.src, self.dst.at[0, pl.ds(c * self.rows, self.rows), :], self.send.at[k - 1], self.recv.at[k - 1], to)

    def plane(self, slot, bit, at):
        return dp_copy(self.dst.at[slot], self.dst.at[slot ^ bit], self.send.at[at], self.recv.at[at], bit)

    def own(self):
        c = lax.axis_index("ctx")
        return pltpu.make_async_copy(self.src, self.dst.at[0, pl.ds(c * self.rows, self.rows), :], self.send.at[10])

    def hop(self, at):
        one, two = self.first, self.second
        slot, bit = [(0, one), (0, two), (one, two), (0, CORE), (one, CORE), (two, CORE), (one | two, CORE)][at]
        return self.plane(slot, bit, 3 + at)

    def start(self):
        self.own().start()
        for k in range(1, self.n):
            self.along(k).start()

    def spread(self):
        self.own().wait()
        for k in range(1, self.n):
            self.along(k).wait_recv()
        for at in (0, 1, 3):
            self.hop(at).start()

    def forward(self):
        self.hop(0).wait_recv()
        self.hop(2).start()
        self.hop(4).start()

    def cross(self):
        self.hop(1).wait_recv()
        self.hop(5).start()
        self.hop(2).wait_recv()
        self.hop(6).start()

    def finish(self):
        for k in range(1, self.n):
            self.along(k).wait_send()
        for at in range(7):
            self.hop(at).wait_send()
        for at in range(3, 7):
            self.hop(at).wait_recv()


def front_kernel(
    n_ctx, tok_ref, fv_ref, mark_ref, pack_ref, freq_ref, wg_ref, wu_ref, wo_ref, wd_ref,
    xn_ref, q_ref, k_ref, v_ref, of_ref, lse_ref, cos_ref, sin_ref, seg_ref, marks, gain_ref,
    att_ref, wg_all, wu_all, wo_all, wd_all,
    x_all, fvs, packs, whead, rel, o_ref, s_ref, m_ref, l_ref, acc_ref,
    mark_send, mark_recv, pack_send, pack_recv, tok_send, tok_recv, fv_send, fv_recv, w_send, w_recv,
    o_send, o_recv, own, own_o,
):
    c, dp = lax.axis_index("ctx"), lax.axis_index("dp")
    tb = m_ref.shape[0]
    half = tb // 2
    model = tok_ref.shape[1]
    blocks = model // LANES
    width = q_ref.shape[1]
    own_rows = wg_ref.shape[0]
    lane = lax.broadcasted_iota(jnp.int32, (tb, LANES), 1)
    right, left = lax.rem(c + 1, n_ctx), lax.rem(c + n_ctx - 1, n_ctx)
    exact = lax.Precision.HIGHEST

    weights = [
        Gather(n_ctx, src, dst, w_send.at[i], w_recv.at[i], order)
        for i, (src, dst, order) in enumerate(
            [
                (wg_ref, wg_all, (NEAR, FAR)),
                (wo_ref, wo_all, (FAR, NEAR)),
                (wu_ref, wu_all, (FAR, NEAR)),
                (wd_ref, wd_all, (NEAR, FAR)),
            ]
        )
    ]
    early, late = weights[:2], weights[2:]

    def mark_copy(k):
        at = rows_of(c, tb)
        return ctx_copy(mark_ref, marks.at[:, at], mark_send.at[k - 1], mark_recv.at[k - 1], lax.rem(c + k, n_ctx))

    def pack_copy(k):
        to = lax.rem(c + k, n_ctx)
        return ctx_copy(pack_ref.at[to], packs.at[0, c], pack_send.at[k - 1], pack_recv.at[k - 1], to)

    def pack_hop(slot, bit, at):
        return dp_copy(packs.at[slot], packs.at[slot ^ bit], pack_send.at[at], pack_recv.at[at], bit)

    def fv_copy(k):
        to = lax.rem(c + k, n_ctx)
        return ctx_copy(fv_ref.at[:, rows_of(to, width)], fvs.at[rows_of(c, tb), :], fv_send.at[k - 1], fv_recv.at[k - 1], to)

    def tok_copy(way, step):
        block = lax.rem(c + n_ctx - step, n_ctx) if way == 0 else lax.rem(c + step, n_ctx)
        at = pl.ds(pl.multiple_of(block * tb + way * half, half), half)
        src = tok_ref.at[pl.ds(way * half, half), :] if step == 0 else x_all.at[at, :]
        return ctx_copy(src, x_all.at[at, :], tok_send.at[way, step], tok_recv.at[way, step], left if way else right)

    locals_ = [
        pltpu.make_async_copy(tok_ref, x_all.at[rows_of(c, tb), :], own.at[0]),
        pltpu.make_async_copy(fv_ref.at[:, rows_of(c, width)], fvs.at[rows_of(c, tb), :], own.at[1]),
        pltpu.make_async_copy(pack_ref.at[c], packs.at[0, c], own.at[2]),
        pltpu.make_async_copy(mark_ref, marks.at[:, rows_of(c, tb)], own.at[3]),
    ]

    meet(n_ctx, (CORE, NEAR, FAR))
    for k in range(1, n_ctx):
        mark_copy(k).start()
        pack_copy(k).start()
    for way in range(2):
        tok_copy(way, 0).start()
    for w in early:
        w.start()
    for m in locals_:
        m.start()
    for k in range(1, n_ctx):
        fv_copy(k).start()

    locals_[3].wait()
    for k in range(1, n_ctx):
        mark_copy(k).wait_recv()
    row8 = lax.broadcasted_iota(jnp.int32, (8, LANES), 0)
    pick_seg = jnp.where(row8 == 0, 1.0, 0.0)
    pick_pos = jnp.where(row8 == 1, 1.0, 0.0)

    def table(b, carry):
        at = rows_of(b, tb)
        m = marks[:, at].astype(F32)
        dims = (((0,), (0,)), ((), ()))
        seg_ref[at, :] = lax.dot_general(m, pick_seg, dims, precision=exact, preferred_element_type=F32)
        pos = lax.dot_general(m, pick_pos, dims, precision=exact, preferred_element_type=F32)
        angle = pos * freq_ref[0:1, :]
        cos_ref[at, :] = jnp.cos(angle)
        sin_ref[at, :] = jnp.sin(angle) * freq_ref[1:2, :]
        return carry

    locals_[2].wait()
    for k in range(1, n_ctx):
        pack_copy(k).wait_recv()
    pack_hop(0, NEAR, 3).start()
    lax.fori_loop(0, n_ctx, table, 0)
    pack_hop(0, NEAR, 3).wait_recv()
    pack_hop(0, FAR, 4).start()
    pack_hop(NEAR, FAR, 5).start()
    pack_hop(0, CORE, 6).start()
    pack_hop(NEAR, CORE, 7).start()

    for way in range(2):
        tok_copy(way, 0).wait_recv()
        tok_copy(way, 1).start()
    pack_hop(0, FAR, 4).wait_recv()
    pack_hop(FAR, CORE, 8).start()
    pack_hop(NEAR, FAR, 5).wait_recv()
    pack_hop(NEAR | FAR, CORE, 9).start()
    for w in early:
        w.spread()
    for at, (slot, bit) in enumerate([(0, CORE), (NEAR, CORE), (FAR, CORE), (NEAR | FAR, CORE)]):
        pack_hop(slot, bit, 6 + at).wait_recv()
    count = packs.shape[0]
    for t in range(3):
        block = packs[:, :, t * own_rows : (t + 1) * own_rows, :]
        whead[:, t * width : (t + 1) * width] = block.reshape(model, width)
    gains = packs[:, :, 3 * own_rows : 4 * own_rows, 0:LANES].reshape(model, LANES).astype(F32)
    gain_ref[...] = gains.T[0:8, :]
    locals_[0].wait()
    locals_[1].wait()

    def project(chunk, part):
        at = pl.ds(pl.multiple_of(chunk * tb + part * half, half), half)
        for d in range(blocks):
            rel[:, d * LANES : (d + 1) * LANES] = x_all[at, lane_block(dp ^ d)].astype(F32)
        x = rel[...]
        inv = lax.rsqrt(jnp.mean(x * x, axis=-1, keepdims=True) + epsilon)
        xn = (x * inv * gain_ref[0:1, :]).astype(LOW)
        xn_ref[at, :] = xn
        proj = dot(xn, whead[...], 1, 0)
        cos, sin = cos_ref[at, :], sin_ref[at, :]
        for b in range(width // LANES):
            cols = slice(b * LANES, (b + 1) * LANES)
            qb = proj[:, b * LANES : (b + 1) * LANES]
            q_ref[at, cols] = ((qb * cos + half_swap(qb) * sin) * 0.125).astype(LOW)
            kb = proj[:, width + b * LANES : width + (b + 1) * LANES]
            k_ref[at, cols] = (kb * cos + half_swap(kb) * sin).astype(LOW)
        v_ref[at, :] = (0.5 * proj[:, 2 * width :] + 0.5 * fvs[at, :].astype(F32)).astype(LOW)

    def project_pair(step):
        def one(part, carry):
            project(lax.rem(c + (2 * part - 1) * step + n_ctx, n_ctx), part)
            return carry

        lax.fori_loop(0, 2, one, 0)

    project_pair(0)
    for w in early:
        w.forward()
    for way in range(2):
        tok_copy(way, 1).wait_recv()
        tok_copy(way, 2).start()
    for k in range(1, n_ctx):
        fv_copy(k).wait_recv()
    project_pair(1)
    project_pair(2)
    for w in early:
        w.cross()
    for way in range(2):
        tok_copy(way, 2).wait_recv()
    for w in late:
        w.start()
    project_pair(3)

    def fold(x, op):
        r = x[:, 0:LANES]
        for b in range(1, tb // LANES):
            r = op(r, x[:, b * LANES : (b + 1) * LANES])
        return r

    def home(pair):
        return att_ref.at[:, pl.ds(pl.multiple_of(c * width + pair * LANES, LANES), LANES)]

    def query_block(pair, i):
        cols = slice(pair * LANES, (pair + 1) * LANES)
        mine = rows_of(i, tb)
        q = q_ref[mine, cols]
        seg_q = seg_ref[mine, 0:1]
        for head in range(2):
            qm = head_lanes(q, head)
            m_ref[...] = jnp.full_like(m_ref, NEG)

            def score(j, causal):
                at = rows_of(j, tb)
                s = dot(qm, k_ref[at, cols], 1, 1)
                ok = seg_q == marks[0:1, at].astype(F32)
                if causal:
                    r = lax.broadcasted_iota(jnp.int32, (tb, tb), 0)
                    t = lax.broadcasted_iota(jnp.int32, (tb, tb), 1)
                    ok = ok & (r >= t)
                s = jnp.where(ok, s, NEG)
                s_ref[:, at] = s
                m_ref[...] = jnp.maximum(m_ref[...], fold(s, jnp.maximum))

            def score_step(j, carry):
                score(j, False)
                return carry

            lax.fori_loop(0, i, score_step, 0)
            score(i, True)
            top = jnp.max(m_ref[...], axis=1, keepdims=True)
            l_ref[...] = jnp.zeros_like(l_ref)
            acc_ref[...] = jnp.zeros_like(acc_ref)

            def value_step(j, carry):
                at = rows_of(j, tb)
                p = jnp.exp(s_ref[:, at] - top)
                l_ref[...] += fold(p, jnp.add)
                acc_ref[...] += dot(p.astype(LOW), v_ref[at, cols], 1, 0)
                return carry

            lax.fori_loop(0, i + 1, value_step, 0)
            total = jnp.sum(l_ref[...], axis=1, keepdims=True)
            out = acc_ref[...] / total
            lse = jnp.broadcast_to(top + jnp.log(total), (tb, LANES))
            if head == 0:
                of_ref[mine, cols] = out
                lse_ref[mine, cols] = lse
            else:
                of_ref[mine, cols] = jnp.where(lane < HEAD_DIM, of_ref[mine, cols], out)
                lse_ref[mine, cols] = jnp.where(lane < HEAD_DIM, lse_ref[mine, cols], lse)
        o_ref[mine, cols] = of_ref[mine, cols].astype(LOW)

        @pl.when(i == c)
        def _():
            pltpu.make_async_copy(o_ref.at[mine, cols], home(pair), own_o.at[pair]).start()

        @pl.when(i != c)
        def _():
            k = lax.rem(i + n_ctx - c, n_ctx) - 1
            ctx_copy(o_ref.at[mine, cols], home(pair), o_send.at[k, pair], o_recv.at[k, pair], i).start()

    def query_blocks(pair, lo, hi):
        def one(i, carry):
            query_block(pair, i)
            return carry

        lax.fori_loop(lo, hi, one, 0)

    query_blocks(0, 0, n_ctx)
    for w in late:
        w.spread()
    query_blocks(1, 0, n_ctx)
    for w in late:
        w.forward()
    for pair in range(width // LANES):
        cols = slice(pair * LANES, (pair + 1) * LANES)
        pltpu.make_async_copy(o_ref.at[0:tb, cols], home(pair), own_o.at[pair]).wait()
        for k in range(n_ctx - 1):
            ctx_copy(o_ref.at[0:tb, cols], home(pair), o_send.at[k, pair], o_recv.at[k, pair], c).wait()
    for w in late:
        w.cross()
    for k in range(1, n_ctx):
        mark_copy(k).wait_send()
        pack_copy(k).wait_send()
        fv_copy(k).wait_send()
    for at, (slot, bit) in enumerate(
        [(0, NEAR), (0, FAR), (NEAR, FAR), (0, CORE), (NEAR, CORE), (FAR, CORE), (NEAR | FAR, CORE)]
    ):
        pack_hop(slot, bit, 3 + at).wait_send()
    for way in range(2):
        for step in range(3):
            tok_copy(way, step).wait_send()
    for w in weights:
        w.finish()


def front_call(n_dp, n_ctx, tok, fv, mark, pack, freq, wg, wu, wo, wd):
    tb, model = tok.shape
    width = model // n_ctx
    length = n_ctx * tb
    pairs = width // LANES
    vmem = pl.BlockSpec(memory_space=pltpu.VMEM)
    anyspace = pl.BlockSpec(memory_space=pl.ANY)
    shape = jax.ShapeDtypeStruct
    dma = pltpu.SemaphoreType.DMA
    return pl.pallas_call(
        functools.partial(front_kernel, n_ctx),
        in_specs=[anyspace] * 4 + [vmem] + [anyspace] * 4,
        out_specs=[vmem] * 11 + [anyspace] * 5,
        out_shape=[shape((length, model), LOW)]
        + [shape((length, width), LOW)] * 3
        + [shape((length, width), F32)] * 2
        + [shape((length, LANES), F32)] * 3
        + [shape((8, length), jnp.int32), shape((8, model), F32)]
        + [shape((tb, model), LOW)]
        + [shape((n_dp, n_ctx * w.shape[0], w.shape[1]), LOW) for w in (wg, wu, wo, wd)],
        scratch_shapes=[
            pltpu.VMEM((length, model), LOW),
            pltpu.VMEM((length, width), LOW),
            pltpu.VMEM((n_dp,) + pack.shape, LOW),
            pltpu.VMEM((model, 3 * width), LOW),
            pltpu.VMEM((tb // 2, model), F32),
            pltpu.VMEM((length, width), LOW),
            pltpu.VMEM((tb, length), F32),
            pltpu.VMEM((tb, LANES), F32),
            pltpu.VMEM((tb, LANES), F32),
            pltpu.VMEM((tb, LANES), F32),
            dma((n_ctx - 1,)), dma((n_ctx - 1,)),
            dma((n_ctx + 6,)), dma((n_ctx + 6,)),
            dma((2, n_ctx - 1)), dma((2, n_ctx - 1)),
            dma((n_ctx - 1,)), dma((n_ctx - 1,)),
            dma((4, 11)), dma((4, 11)),
            dma((n_ctx - 1, pairs)), dma((n_ctx - 1, pairs)),
            dma((4,)), dma((pairs,)),
        ],
        compiler_params=params(collective_id=1, has_side_effects=True),
        cost_estimate=pl.CostEstimate(
            flops=24 * 10**9, bytes_accessed=60 * 2**20, transcendentals=2 * length * length
        ),
        name="front",
    )(tok, fv, mark, pack, freq, wg, wu, wo, wd)


class Reduce:
    def __init__(self, n_ctx, keep, gone, acc, rc, rx, ry, rz, out, send, recv, order):
        self.n, self.keep, self.gone, self.acc, self.rc, self.rx, self.ry, self.rz = n_ctx, keep, gone, acc, rc, rx, ry, rz
        self.out, self.send, self.recv = out, send, recv
        self.one, self.two = order
        self.leave = (self.one >> 1, 3)
        self.stay = self.two >> 1

    def hop(self, at):
        src, dst, bit = [
            (self.gone, self.rc, CORE),
            (self.acc.at[self.leave[0]], self.rx.at[0], self.one),
            (self.acc.at[self.leave[1]], self.rx.at[1], self.one),
            (self.acc.at[self.stay], self.ry, self.two),
        ][at]
        return dp_copy(src, dst, self.send.at[at], self.recv.at[at], bit)

    def held(self):
        return pltpu.make_async_copy(self.keep, self.acc, self.send.at[7])

    def along(self, k):
        to = lax.rem(lax.axis_index("ctx") + k, self.n)
        return ctx_copy(self.acc.at[0, to], self.rz.at[k - 1], self.send.at[3 + k], self.recv.at[3 + k], to)

    def begin(self):
        self.hop(0).start()
        self.held().start()

    def add(self, block, terms):
        def one(j, carry):
            total = self.acc[block, j].astype(F32)
            for t in terms:
                total = total + t(j).astype(F32)
            self.acc[block, j] = total.astype(LOW)
            return carry

        lax.fori_loop(0, self.acc.shape[1], one, 0)

    def step_one(self):
        self.held().wait()
        self.hop(0).wait_recv()
        for at in (1, 0):
            block = self.leave[at]
            self.add(block, [lambda j, block=block: self.rc[block, j]])
            self.hop(1 + at).start()

    def step_two(self):
        self.hop(2).wait_recv()
        self.add(self.stay, [lambda j: self.rc[self.stay, j], lambda j: self.rx[1, j]])
        self.hop(3).start()

    def step_ctx(self):
        c = lax.axis_index("ctx")
        self.hop(1).wait_recv()
        self.hop(3).wait_recv()
        self.out[...] = (
            self.acc[0, c].astype(F32) + self.rc[0, c].astype(F32) + self.rx[0, c].astype(F32) + self.ry[c].astype(F32)
        )
        self.add(0, [lambda j: self.rc[0, j], lambda j: self.rx[0, j], lambda j: self.ry[j]])
        for k in range(1, self.n):
            self.along(k).start()

    def finish(self):
        for k in range(1, self.n):
            self.along(k).wait_recv()
            self.out[...] += self.rz[k - 1].astype(F32)
        for at in range(4):
            self.hop(at).wait_send()
        for k in range(1, self.n):
            self.along(k).wait_send()


def back_kernel(n_ctx, *refs):
    ga_ref, q_ref, k_ref, v_ref, of_ref, lse_ref, sc_ref, sr_ref, cos_ref, sin_ref, xn_ref = refs[:11]
    sides = refs[11:19]
    home_ref, qkv_out = refs[19:21]
    outs = refs[21:25]
    (g_ref, part_ref, lse_row, delta_row, dq_acc, dk_acc, dv_acc, prod) = refs[25:33]
    rest = refs[33:]
    buffers, rest = rest[:20], rest[20:]
    (pk, ps, prc, prx, pry, pz, qz) = rest[:7]
    (gsend, grecv, send, recv, own, r_send, r_recv, p_send, p_recv, z_send, z_recv) = rest[7:]
    c = lax.axis_index("ctx")
    tb = dk_acc.shape[0]
    length, width = q_ref.shape
    model = n_ctx * width
    pairs = width // LANES
    blocks = model // LANES
    near_first, far_first = (NEAR, FAR), (FAR, NEAR)
    gate, up, out, down = [
        Reduce(n_ctx, sides[2 * i], sides[2 * i + 1], *buffers[5 * i : 5 * i + 5], outs[i], r_send.at[i], r_recv.at[i], order)
        for i, order in enumerate([near_first, far_first, near_first, far_first])
    ]

    def grad_copy(k):
        to = lax.rem(c + k, n_ctx)
        return ctx_copy(ga_ref.at[:, rows_of(to, width)], g_ref.at[rows_of(c, tb), :], gsend.at[k - 1], grecv.at[k - 1], to)

    def home(pair, t):
        return home_ref.at[:, pl.ds(pl.multiple_of(t * model + c * width + pair * LANES, LANES), LANES)]

    def part(pair, t, chunk):
        return part_ref.at[pair, rows_of(chunk, tb), pl.ds(t * LANES, LANES)]

    def part_copy(pair, t, k):
        to = lax.rem(c + k, n_ctx)
        return ctx_copy(part(pair, t, to), home(pair, t), send.at[k - 1, pair, t], recv.at[k - 1, pair, t], to)

    def part_own(pair, t):
        return pltpu.make_async_copy(part(pair, t, c), home(pair, t), own.at[pair, t])

    meet(n_ctx, (CORE, NEAR, FAR))
    for k in range(1, n_ctx):
        grad_copy(k).start()
    keep = pltpu.make_async_copy(ga_ref.at[:, rows_of(c, width)], g_ref.at[rows_of(c, tb), :], own.at[0, 0])
    keep.start()
    for r in (gate, up, out, down):
        r.begin()
    for r in (gate, up, out, down):
        r.step_one()
    keep.wait()
    for k in range(1, n_ctx):
        grad_copy(k).wait_recv()

    r8 = lax.broadcasted_iota(jnp.int32, (8, LANES), 0)
    l8 = lax.broadcasted_iota(jnp.int32, (8, LANES), 1)
    pick = jnp.where(l8 == r8 * HEAD_DIM, 1.0, 0.0)
    group = jnp.where(l8 // HEAD_DIM == r8, 1.0, 0.0)
    exact = lax.Precision.HIGHEST
    dims = (((1,), (1,)), ((), ()))

    def stats(pair):
        cols = slice(pair * LANES, (pair + 1) * LANES)

        def one(b, carry):
            at = rows_of(b, tb)
            lse_row[:, at] = lax.dot_general(pick, lse_ref[at, cols], dims, precision=exact, preferred_element_type=F32)
            mixed = g_ref[at, cols].astype(F32) * of_ref[at, cols]
            delta_row[:, at] = lax.dot_general(group, mixed, dims, precision=exact, preferred_element_type=F32)
            dq_acc[at, :] = jnp.zeros((tb, LANES), F32)
            return carry

        lax.fori_loop(0, n_ctx, one, 0)

    def key_blocks(pair, lo, hi):
        cols = slice(pair * LANES, (pair + 1) * LANES)

        def key_block(j, carry):
            dk_acc[...] = jnp.zeros_like(dk_acc)
            dv_acc[...] = jnp.zeros_like(dv_acc)
            mine = rows_of(j, tb)
            k = k_ref[mine, cols]
            v = v_ref[mine, cols]
            seg_k = sc_ref[mine, 0:1]

            def block(i, causal):
                at = rows_of(i, tb)
                q = q_ref[at, cols]
                g = g_ref[at, cols]
                ok = seg_k == sr_ref[0:1, at].astype(F32)
                if causal:
                    r = lax.broadcasted_iota(jnp.int32, (tb, tb), 0)
                    t = lax.broadcasted_iota(jnp.int32, (tb, tb), 1)
                    ok = ok & (r <= t)
                for head in range(2):
                    qm = head_lanes(q, head)
                    gm = head_lanes(g, head)
                    s = dot(k, qm, 1, 1)
                    p = jnp.where(ok, jnp.exp(s - lse_row[head : head + 1, at]), 0.0)
                    dp = dot(v, gm, 1, 1)
                    ds = (p * (dp - delta_row[head : head + 1, at])).astype(LOW)
                    dv_acc[...] += dot(p.astype(LOW), gm, 1, 0)
                    dk_acc[...] += dot(ds, qm, 1, 0)
                    dq_acc[at, :] += dot(ds, head_lanes(k, head), 0, 0)

            block(j, True)

            def step(i, carry):
                block(i, False)
                return carry

            lax.fori_loop(j + 1, n_ctx, step, 0)
            dk = dk_acc[...]
            dk = dk * cos_ref[mine, :] - half_swap(dk) * sin_ref[mine, :]
            part_ref[pair, mine, LANES : 2 * LANES] = dk.astype(LOW)
            part_ref[pair, mine, 2 * LANES : 3 * LANES] = dv_acc[...].astype(LOW)
            return carry

        lax.fori_loop(lo, hi, key_block, 0)

    def send_home(pair):
        def query_done(b, carry):
            at = rows_of(b, tb)
            dq = dq_acc[at, :] * 0.125
            dq = dq * cos_ref[at, :] - half_swap(dq) * sin_ref[at, :]
            part_ref[pair, at, 0:LANES] = dq.astype(LOW)
            return carry

        lax.fori_loop(0, n_ctx, query_done, 0)
        for t in range(3):
            part_own(pair, t).start()
            for k in range(1, n_ctx):
                part_copy(pair, t, k).start()

    def pair_hop(pair, at):
        src, dst, bit = [
            (ps.at[pair], prc.at[pair], CORE),
            (pk.at[pair, 1], prx.at[pair, 0], NEAR),
            (pk.at[pair, 3], prx.at[pair, 1], NEAR),
            (pk.at[pair, 2], pry.at[pair], FAR),
        ][at]
        return dp_copy(src, dst, p_send.at[pair, at], p_recv.at[pair, at], bit)

    def pair_ctx(pair, k):
        to = lax.rem(c + k, n_ctx)
        return ctx_copy(pz.at[pair, to], qz.at[c, pair], z_send.at[pair, k - 1], z_recv.at[pair, k - 1], to)

    def pair_product(pair):
        prod[...] = jnp.zeros_like(prod)

        def one(b, carry):
            at = rows_of(b, tb)
            prod[...] += dot(part_ref[pair, at, :], xn_ref[at, :], 0, 0)
            return carry

        lax.fori_loop(0, n_ctx, one, 0)
        for d in range(blocks):
            (ps if d % 2 else pk)[pair, d // 2] = prod[:, d * LANES : (d + 1) * LANES].astype(LOW)
        pair_hop(pair, 0).start()

    def pair_one(pair):
        pair_hop(pair, 0).wait_recv()
        for i in (3, 1):
            pk[pair, i] = (pk[pair, i].astype(F32) + prc[pair, i].astype(F32)).astype(LOW)
            pair_hop(pair, 1 + i // 2).start()

    def pair_two(pair):
        pair_hop(pair, 2).wait_recv()
        total = pk[pair, 2].astype(F32) + prc[pair, 2].astype(F32) + prx[pair, 1].astype(F32)
        pk[pair, 2] = total.astype(LOW)
        pair_hop(pair, 3).start()

    def pair_three(pair):
        pair_hop(pair, 1).wait_recv()
        pair_hop(pair, 3).wait_recv()
        total = pk[pair, 0].astype(F32) + prc[pair, 0].astype(F32) + prx[pair, 0].astype(F32) + pry[pair].astype(F32)
        pz[pair] = total.T.reshape(pz.shape[1:]).astype(LOW)
        qz[c, pair] = pz[pair, c]
        for k in range(1, n_ctx):
            pair_ctx(pair, k).start()

    def pair_finish(pair):
        for k in range(1, n_ctx):
            pair_ctx(pair, k).wait()
        for at in range(4):
            pair_hop(pair, at).wait_send()

    stats(0)
    key_blocks(0, 0, n_ctx)
    send_home(0)
    pair_product(0)
    stats(1)
    key_blocks(1, 0, n_ctx // 2)
    pair_one(0)
    gate.step_two()
    out.step_two()
    key_blocks(1, n_ctx // 2, n_ctx)
    send_home(1)
    pair_product(1)
    pair_two(0)
    up.step_two()
    down.step_two()
    pair_one(1)
    pair_three(0)
    gate.step_ctx()
    out.step_ctx()
    pair_two(1)
    up.step_ctx()
    down.step_ctx()
    pair_three(1)
    for pair in range(pairs):
        pair_finish(pair)
        for s in range(n_ctx):
            for t in range(3):
                at = t * model + s * width + pair * LANES
                qkv_out[:, at : at + LANES] = qz[s, pair, :, t * LANES : (t + 1) * LANES].astype(F32)
    for k in range(1, n_ctx):
        grad_copy(k).wait_send()
    for r in (gate, out, up, down):
        r.finish()
    for pair in range(pairs):
        for t in range(3):
            part_own(pair, t).wait()
            for k in range(1, n_ctx):
                part_copy(pair, t, k).wait()


def back_call(n_ctx, ga, q, k, v, of, lse, seg_col, seg_row, cos, sin, xn, sides):
    length, width = q.shape
    model = n_ctx * width
    tb = TOKEN_BLOCK
    pairs = width // LANES
    own_rows = model // (model // LANES) // n_ctx
    vmem = pl.BlockSpec(memory_space=pltpu.VMEM)
    anyspace = pl.BlockSpec(memory_space=pl.ANY)
    shape = jax.ShapeDtypeStruct
    dma = pltpu.SemaphoreType.DMA
    buffers = []
    for keep in sides[::2]:
        four, parts, rows, cols = keep.shape
        buffers += [
            pltpu.VMEM((four, parts, rows, cols), LOW),
            pltpu.VMEM((four, parts, rows, cols), LOW),
            pltpu.VMEM((2, parts, rows, cols), LOW),
            pltpu.VMEM((parts, rows, cols), LOW),
            pltpu.VMEM((parts - 1, rows, cols), LOW),
        ]
    wide = 3 * LANES
    return pl.pallas_call(
        functools.partial(back_kernel, n_ctx),
        in_specs=[anyspace] + [vmem] * 10 + [anyspace] * 8,
        out_specs=[anyspace] + [vmem] * 5,
        out_shape=[shape((tb, 3 * model), LOW), shape((own_rows, 3 * model), F32)]
        + [shape(keep.shape[2:], F32) for keep in sides[::2]],
        scratch_shapes=[
            pltpu.VMEM((length, width), LOW),
            pltpu.VMEM((pairs, length, wide), LOW),
            pltpu.VMEM((8, length), F32),
            pltpu.VMEM((8, length), F32),
            pltpu.VMEM((length, LANES), F32),
            pltpu.VMEM((tb, LANES), F32),
            pltpu.VMEM((tb, LANES), F32),
            pltpu.VMEM((wide, model), F32),
        ]
        + buffers
        + [
            pltpu.VMEM((pairs, 4, wide, LANES), LOW),
            pltpu.VMEM((pairs, 4, wide, LANES), LOW),
            pltpu.VMEM((pairs, 4, wide, LANES), LOW),
            pltpu.VMEM((pairs, 2, wide, LANES), LOW),
            pltpu.VMEM((pairs, wide, LANES), LOW),
            pltpu.VMEM((pairs, n_ctx, own_rows, wide), LOW),
            pltpu.VMEM((n_ctx, pairs, own_rows, wide), LOW),
            dma((n_ctx - 1,)), dma((n_ctx - 1,)),
            dma((n_ctx - 1, pairs, 3)), dma((n_ctx - 1, pairs, 3)),
            dma((pairs, 3)),
            dma((4, 8)), dma((4, 8)),
            dma((pairs, 4)), dma((pairs, 4)),
            dma((pairs, n_ctx - 1)), dma((pairs, n_ctx - 1)),
        ],
        compiler_params=params(collective_id=3, has_side_effects=True),
        cost_estimate=pl.CostEstimate(
            flops=40 * 10**9, bytes_accessed=60 * 2**20, transcendentals=2 * length * length
        ),
        name="back",
    )(ga, q, k, v, of, lse, seg_col, seg_row, cos, sin, xn, *sides)


def mlp_kernel(blocks, n_ctx, tok_ref, att_ref, cot_ref, gain_ref, *refs):
    (wo_in, wg_in, wu_in, wd_in, wq_ref), refs = refs[:5], refs[5:]
    out_ref, gm_ref, ga_ref, gk, gs, uk, us, ok, os, dk, ds, wq_all = refs[:12]
    wo, wg, wu, wd, att, nat, n2, mi, mit, inv_ref, oacc, dacc, dwd, sem, osem, q_send, q_recv = refs[12:]
    dp = lax.axis_index("dp")
    u = pl.program_id(0)
    last = pl.num_programs(0) - 1
    down = wd_in.shape[1]

    def copies():
        made = []
        for d in range(blocks):
            at = pl.ds(d * LANES, LANES)
            made.append(pltpu.make_async_copy(wo_in.at[d], wo.at[at, :], sem.at[0, d]))
        for d in range(blocks):
            at = pl.ds(d * LANES, LANES)
            made.append(pltpu.make_async_copy(wg_in.at[d], wg.at[at, :], sem.at[1, d]))
            made.append(pltpu.make_async_copy(wu_in.at[d], wu.at[at, :], sem.at[2, d]))
            rows = pl.ds(pl.multiple_of((dp ^ d) * down, 32), down)
            made.append(pltpu.make_async_copy(wd_in.at[d], wd.at[rows, :], sem.at[3, d]))
        return made

    def out_copies():
        made = []
        for d in range(blocks):
            rows = pl.ds(pl.multiple_of((dp ^ d) * down, 32), down)
            made.append(pltpu.make_async_copy(dwd.at[rows, :], (ds if d % 2 else dk).at[d // 2], osem.at[d]))
        return made

    attn = Gather(n_ctx, wq_ref, wq_all, q_send, q_recv, (NEAR, FAR))

    @pl.when(u == 0)
    def _():
        meet(n_ctx, (CORE, NEAR, FAR))
        attn.start()
        made = copies()
        for c in made:
            c.start()
        for d in range(blocks):
            att[:, d * LANES : (d + 1) * LANES] = att_ref[:, lane_block(dp ^ d)]
        for c in made[:blocks]:
            c.wait()
        mid = tok_ref[...].astype(F32) + dot(att[...], wo[...], 1, 0)
        inv = lax.rsqrt(jnp.mean(mid * mid, axis=-1, keepdims=True) + epsilon)
        oacc[...] = mid
        nat[...] = mid * inv
        inv_ref[...] = jnp.broadcast_to(inv, inv_ref.shape)
        for d in range(blocks):
            n2[:, d * LANES : (d + 1) * LANES] = nat[:, lane_block(dp ^ d)]
        mi[...] = (n2[...] * gain_ref[...]).astype(LOW)
        mit[...] = mi[...].T
        dacc[...] = jnp.zeros_like(dacc)
        for c in made[blocks:]:
            c.wait()

    cols = pl.ds(pl.multiple_of(u * FF_BLOCK, FF_BLOCK), FF_BLOCK)
    x = mi[...]
    cot = cot_ref[...]
    wgu, wuu, wdu = wg[:, cols], wu[:, cols], wd[cols, :]
    gate = dot(x, wgu, 1, 0)
    up = dot(x, wuu, 1, 0)
    grad_hidden = dot(cot, wdu, 1, 1)
    sig = jax.nn.sigmoid(gate)
    hidden = (gate * sig * up).astype(LOW)
    dg = (grad_hidden * up * sig * (1.0 + gate * (1.0 - sig))).astype(LOW)
    du = (grad_hidden * gate * sig).astype(LOW)
    oacc[...] += dot(hidden, wdu, 1, 0)
    dacc[...] += dot(dg, wgu, 1, 1) + dot(du, wuu, 1, 1)
    xt = mit[...]
    dwg = dot(xt, dg, 1, 0).astype(LOW)
    dwu = dot(xt, du, 1, 0).astype(LOW)
    for d in range(blocks):
        (gs if d % 2 else gk)[d // 2] = dwg[d * LANES : (d + 1) * LANES]
        (us if d % 2 else uk)[d // 2] = dwu[d * LANES : (d + 1) * LANES]
    dwd[cols, :] = dot(hidden, cot, 0, 0).astype(LOW)

    for at, move in ((3, attn.spread), (5, attn.forward), (8, attn.cross)):
        pl.when(u == at)(move)

    @pl.when(u == last)
    def _():
        made = out_copies()
        for c in made:
            c.start()
        out_ref[...] = oacc[...].astype(LOW)
        scaled = dacc[...] * gain_ref[...]
        norm = n2[...]
        mean = jnp.mean(scaled * norm, axis=-1, keepdims=True)
        n2[...] = inv_ref[:, 0:1] * (scaled - norm * mean)
        for d in range(blocks):
            nat[:, lane_block(dp ^ d)] = n2[:, d * LANES : (d + 1) * LANES]
        gm = cot.astype(F32) + nat[...]
        gm_ref[...] = gm
        gb = gm.astype(LOW)
        n2[...] = dot(gb, wo[...], 1, 1)
        for d in range(blocks):
            ga_ref[:, lane_block(dp ^ d)] = n2[:, d * LANES : (d + 1) * LANES].astype(LOW)
        attn.finish()
        dwo = dot(att[...], gb, 0, 0).astype(LOW)
        for d in range(blocks):
            (os if d % 2 else ok)[d // 2] = dwo[d * LANES : (d + 1) * LANES]
        for c in made:
            c.wait()


def mlp_call(n_ctx, tok, att, cot, gain, wo, wg, wu, wd, wq):
    tb, model = tok.shape
    blocks, _, ff = wg.shape
    half = blocks // 2
    down = wd.shape[1]
    whole = lambda a: pl.BlockSpec(a.shape, lambda u: (0, 0))
    anyspace = pl.BlockSpec(memory_space=pl.ANY)
    half_cols = pl.BlockSpec((half, LANES, FF_BLOCK), lambda u: (0, 0, u))
    half_out = pl.BlockSpec((half, LANES, model), lambda u: (0, 0, 0))
    tokens = pl.BlockSpec((tb, model), lambda u: (0, 0))
    shape = jax.ShapeDtypeStruct
    return pl.pallas_call(
        functools.partial(mlp_kernel, blocks, n_ctx),
        grid=(ff // FF_BLOCK,),
        in_specs=[whole(tok), whole(att), whole(cot), whole(gain)] + [anyspace] * 5,
        out_specs=[tokens, tokens, tokens] + [half_cols] * 4 + [half_out] * 2 + [anyspace] * 3,
        out_shape=[shape((tb, model), LOW), shape((tb, model), F32), shape((tb, model), LOW)]
        + [shape((half, LANES, ff), LOW)] * 4
        + [shape((half, LANES, model), LOW)] * 2
        + [shape((half, down, model), LOW)] * 2
        + [shape((blocks, n_ctx * wq.shape[0], wq.shape[1]), LOW)],
        scratch_shapes=[
            pltpu.VMEM((model, model), LOW),
            pltpu.VMEM((model, ff), LOW),
            pltpu.VMEM((model, ff), LOW),
            pltpu.VMEM((ff, model), LOW),
            pltpu.VMEM((tb, model), LOW),
            pltpu.VMEM((tb, model), F32),
            pltpu.VMEM((tb, model), F32),
            pltpu.VMEM((tb, model), LOW),
            pltpu.VMEM((model, tb), LOW),
            pltpu.VMEM((tb, LANES), F32),
            pltpu.VMEM((tb, model), F32),
            pltpu.VMEM((tb, model), F32),
            pltpu.VMEM((ff, model), LOW),
            pltpu.SemaphoreType.DMA((4, blocks)),
            pltpu.SemaphoreType.DMA((blocks,)),
            pltpu.SemaphoreType.DMA((11,)),
            pltpu.SemaphoreType.DMA((11,)),
        ],
        compiler_params=params(collective_id=2, has_side_effects=True),
        cost_estimate=pl.CostEstimate(
            flops=2 * tb * model * (8 * ff + 3 * model), bytes_accessed=50 * 2**20, transcendentals=0
        ),
        name="mlp",
    )(tok, att, cot, gain, wo, wg, wu, wd, wq)


def input_kernel(blocks, tok_ref, gm_ref, v1_ref, gain_ref, g, w_in, ig_ref, vg_ref, w, rel, nat, sem):
    dp = lax.axis_index("dp")
    model = tok_ref.shape[1]
    made = [pltpu.make_async_copy(w_in.at[d], w.at[pl.ds(d * LANES, LANES), :], sem.at[d]) for d in range(blocks)]
    for m in made:
        m.start()
    for d in range(blocks):
        rel[:, d * LANES : (d + 1) * LANES] = tok_ref[:, lane_block(dp ^ d)].astype(F32)
    gv = g[:, 2 * model :].astype(F32)
    vg_ref[...] = v1_ref[...] + 0.5 * gv
    x = rel[...]
    inv = lax.rsqrt(jnp.mean(x * x, axis=-1, keepdims=True) + epsilon)
    norm = x * inv
    for m in made:
        m.wait()
    grad = dot(g[:, : 2 * model], w[:, : 2 * model], 1, 1)
    grad = grad + 0.5 * dot(g[:, 2 * model :], w[:, 2 * model :], 1, 1)
    scaled = grad * gain_ref[...]
    mean = jnp.mean(scaled * norm, axis=-1, keepdims=True)
    rel[...] = inv * (scaled - norm * mean)
    for d in range(blocks):
        nat[:, lane_block(dp ^ d)] = rel[:, d * LANES : (d + 1) * LANES]
    ig_ref[...] = gm_ref[...] + nat[...]


def input_call(tok, gm, v1, gain, g, ws):
    tb, model = tok.shape
    blocks = ws.shape[0]
    vmem = pl.BlockSpec(memory_space=pltpu.VMEM)
    shape = jax.ShapeDtypeStruct
    return pl.pallas_call(
        functools.partial(input_kernel, blocks),
        in_specs=[vmem] * 5 + [pl.BlockSpec(memory_space=pl.ANY)],
        out_specs=[vmem, vmem],
        out_shape=[shape((tb, model), F32)] * 2,
        scratch_shapes=[
            pltpu.VMEM((model, 3 * model), LOW),
            pltpu.VMEM((tb, model), F32),
            pltpu.VMEM((tb, model), F32),
            pltpu.SemaphoreType.DMA((blocks,)),
        ],
        compiler_params=params(),
        cost_estimate=pl.CostEstimate(
            flops=2 * tb * model * 3 * model, bytes_accessed=20 * 2**20, transcendentals=0
        ),
        name="input_grad",
    )(tok, gm, v1, gain, g, ws)


def fast_local(
    n_dp, n_ctx, tokens, first_values, v1_accum, segment_ids, positions, cotangent,
    attn_gain, w_query, w_key, w_value, w_out, mlp_gain, w_gate, w_up, w_down,
):
    seq, model = tokens.shape[1:]
    width = model // n_ctx
    own_rows = w_query.shape[0]
    tok = tokens[0]
    mark = jnp.concatenate([segment_ids, positions, jnp.zeros((6, seq), jnp.int32)], axis=0)
    gains = jnp.stack([attn_gain, mlp_gain], axis=1)
    gains = jnp.tile(jnp.pad(gains, ((0, 0), (0, width - 2))), (1, n_ctx))
    pack = jnp.concatenate([w_query, w_key, w_value, gains], axis=0)
    pack = pack.reshape(4 * own_rows, n_ctx, width).transpose(1, 0, 2)
    freqs = 10000.0 ** (-jnp.arange(HEAD_DIM // 2).astype(F32) * (2.0 / HEAD_DIM))
    turn = jnp.ones((HEAD_DIM // 2,), F32)
    freq = jnp.stack([jnp.tile(freqs, 4), jnp.tile(jnp.concatenate([-turn, turn]), 2)])
    freq = jnp.pad(freq, ((0, 6), (0, 0)))
    (xn, q, k, v, out_full, log_total, cos, sin, seg_col, seg_row, gain_rows, attended,
     gate_all, up_all, out_all, down_all) = front_call(
        n_dp, n_ctx, tok, first_values[0], mark, pack, freq, w_gate, w_up, w_out, w_down
    )
    qkv = jnp.concatenate([w_query, w_key, w_value], axis=1)
    (output, grad_middle, grad_attended, gate_keep, gate_send, up_keep, up_send, out_keep, out_send,
     down_keep, down_send, qkv_all) = mlp_call(
        n_ctx, tok, attended, cotangent[0], gain_rows[1:2], out_all, gate_all, up_all, down_all, qkv
    )
    sides = [
        x.reshape(x.shape[0], n_ctx, x.shape[1] // n_ctx, x.shape[2])
        for x in (gate_keep, gate_send, up_keep, up_send, out_keep, out_send, down_keep, down_send)
    ]
    home_grad, qkv_grad, gate_grad, up_grad, out_grad, down_grad = back_call(
        n_ctx, grad_attended, q, k, v, out_full, log_total, seg_col, seg_row, cos, sin, xn, sides
    )
    query_grad, key_grad = qkv_grad[:, :model], qkv_grad[:, model : 2 * model]
    value_grad = 0.5 * qkv_grad[:, 2 * model :]
    input_grad, v1_grad = input_call(tok, grad_middle, v1_accum[0], gain_rows[0:1], home_grad, qkv_all)

    def row_dot(a, w):
        return jnp.sum(a * w.astype(F32), axis=1)

    gain_one = (
        row_dot(query_grad, w_query) + row_dot(key_grad, w_key) + row_dot(value_grad, w_value)
    ) / attn_gain.astype(F32)
    gain_two = (row_dot(gate_grad, w_gate) + row_dot(up_grad, w_up)) / mlp_gain.astype(F32)
    return (
        output[None], input_grad[None], v1_grad[None], gain_one, query_grad, key_grad, value_grad,
        out_grad, gain_two, gate_grad, up_grad, down_grad,
    )


def solution(mesh):
    placed = (
        P("dp", "ctx", None),
        P("dp", "ctx", None),
        P("dp", "ctx", None),
        P("dp", "ctx"),
        P("dp", "ctx"),
        P("dp", "ctx", None),
        P(("dp", "ctx")),
        P(("dp", "ctx"), None),
        P(("dp", "ctx"), None),
        P(("dp", "ctx"), None),
        P(("dp", "ctx"), None),
        P(("dp", "ctx")),
        P(("dp", "ctx"), None),
        P(("dp", "ctx"), None),
        P(("dp", "ctx"), None),
    )
    n_dp, n_ctx = mesh.shape["dp"], mesh.shape["ctx"]

    def local(*args):
        rows, seq, model = args[0].shape
        fits = (
            rows == 1
            and seq == TOKEN_BLOCK
            and model == n_dp * LANES
            and model == 2 * LANES * n_ctx
            and args[12].shape[1] % FF_BLOCK == 0
        )
        return fast_local(n_dp, n_ctx, *args) if fits else plain_local(*args)

    return jax.shard_map(
        local,
        mesh=mesh,
        in_specs=placed,
        out_specs=(
            P("dp", "ctx", None),
            P("dp", "ctx", None),
            P("dp", "ctx", None),
            P(("dp", "ctx")),
            P(("dp", "ctx"), None),
            P(("dp", "ctx"), None),
            P(("dp", "ctx"), None),
            P(("dp", "ctx"), None),
            P(("dp", "ctx")),
            P(("dp", "ctx"), None),
            P(("dp", "ctx"), None),
            P(("dp", "ctx"), None),
        ),
        check_vma=False,
    )
```

```python
import functools

import jax
import jax.numpy as jnp
from jax import lax
from jax.experimental import pallas as pl
from jax.experimental.pallas import tpu as pltpu
from jax.sharding import PartitionSpec as P

HEADS = 16
HEAD_DIM = 64
LANES = 128
TOKEN_BLOCK = 512
FF_BLOCK = 256
NEG = -1e30
MESH = pl.DeviceIdType.MESH
F32 = jnp.float32
LOW = jnp.bfloat16
BYTES = 63 * 2**20
epsilon = 1e-05


HEAD_BLOCK = 4


def rms_scale(values):
    return lax.rsqrt(jnp.mean(values * values, axis=-1, keepdims=True) + epsilon)


def angle_tables(position_rows):
    freqs = 10000.0 ** (-jnp.arange(HEAD_DIM // 2).astype(jnp.float32) * (2.0 / HEAD_DIM))
    angles = position_rows.astype(jnp.float32)[..., None] * freqs
    return (jnp.cos(angles)[..., None, :], jnp.sin(angles)[..., None, :])


def rotate(heads_in, cosine_table, sine_table):
    half_dim = heads_in.shape[-1] // 2
    first_half = heads_in[..., :half_dim]
    second_half = heads_in[..., half_dim:]
    return jnp.concatenate(
        [
            first_half * cosine_table - second_half * sine_table,
            second_half * cosine_table + first_half * sine_table,
        ],
        axis=-1,
    )


def norm_back(grad_normed, normed, inv_root, norm_gain):
    grad_scaled = grad_normed * norm_gain.astype(jnp.float32)
    grad_input = inv_root * (
        grad_scaled - normed * jnp.mean(grad_scaled * normed, axis=-1, keepdims=True)
    )
    return (grad_input, jnp.sum(grad_normed * normed, axis=0))


def attn_front(flat_tokens, first_flat, attn_set, cosine_table, sine_table, row_count, seq_piece):
    inv_root = rms_scale(flat_tokens)
    normed = flat_tokens * inv_root
    normed_in = (normed * attn_set[0].astype(jnp.float32)).astype(jnp.bfloat16)
    query_proj = jnp.dot(normed_in, attn_set[1], preferred_element_type=jnp.float32)
    key_proj = jnp.dot(normed_in, attn_set[2], preferred_element_type=jnp.float32)
    value_proj = jnp.dot(normed_in, attn_set[3], preferred_element_type=jnp.float32)
    query_rot = rotate(
        query_proj.reshape(row_count, seq_piece, HEADS, HEAD_DIM), cosine_table, sine_table
    )
    key_rot = rotate(
        key_proj.reshape(row_count, seq_piece, HEADS, HEAD_DIM), cosine_table, sine_table
    )
    query_rot = query_rot.astype(jnp.bfloat16).reshape(row_count, seq_piece, -1)
    key_rot = key_rot.astype(jnp.bfloat16).reshape(row_count, seq_piece, -1)
    value_mix = (
        (0.5 * value_proj + 0.5 * first_flat).astype(jnp.bfloat16).reshape(row_count, seq_piece, -1)
    )
    return (normed, inv_root, normed_in, query_rot, key_rot, value_mix)


def mlp_block(flat_tokens, attended_low, out_weight, mlp_set):
    middle = flat_tokens + jnp.dot(attended_low, out_weight, preferred_element_type=jnp.float32)
    inv_root_two = rms_scale(middle)
    normed_two = middle * inv_root_two
    mlp_in = (normed_two * mlp_set[0].astype(jnp.float32)).astype(jnp.bfloat16)
    gate_proj = jnp.dot(mlp_in, mlp_set[1], preferred_element_type=jnp.float32)
    up_proj = jnp.dot(mlp_in, mlp_set[2], preferred_element_type=jnp.float32)
    hidden = (gate_proj * jax.nn.sigmoid(gate_proj) * up_proj).astype(jnp.bfloat16)
    result = middle + jnp.dot(hidden, mlp_set[3], preferred_element_type=jnp.float32)
    return (normed_two, inv_root_two, mlp_in, gate_proj, up_proj, hidden, result)


def split_groups(row_block):
    tok_count = row_block.shape[0]
    return row_block.reshape(tok_count, HEADS // HEAD_BLOCK, HEAD_BLOCK * HEAD_DIM).transpose(
        1, 0, 2
    )


def join_groups(group_block):
    return group_block.transpose(1, 0, 2).reshape(group_block.shape[1], -1)


def as_heads(block):
    return block.reshape(block.shape[0], HEAD_BLOCK, HEAD_DIM)


def attend_row(members):
    query_row, key_row, value_row, allowed = members

    def per_group(pieces):
        query_block, key_block, value_block = pieces
        scores = (
            jnp.einsum(
                "qhd,khd->hqk",
                as_heads(query_block),
                as_heads(key_block),
                preferred_element_type=jnp.float32,
            )
            * 0.125
        )
        scores = jnp.where(allowed[None], scores, -1e30)
        highest = jnp.max(scores, axis=-1, keepdims=True)
        exp_scores = jnp.exp(scores - highest)
        denominator = jnp.sum(exp_scores, axis=-1, keepdims=True)
        soft_low = (exp_scores / denominator).astype(jnp.bfloat16)
        attended = jnp.einsum(
            "hqk,khd->qhd", soft_low, as_heads(value_block), preferred_element_type=jnp.float32
        )
        return (
            attended.reshape(query_block.shape[0], -1),
            (highest + jnp.log(denominator))[..., 0],
        )

    attended, log_total = lax.map(
        per_group, (split_groups(query_row), split_groups(key_row), split_groups(value_row))
    )
    return (join_groups(attended), log_total)


def attend_back(members):
    query_row, key_row, value_row, grad_row, log_total, allowed = members

    def per_group(pieces):
        query_block, key_block, value_block, grad_block, log_block = pieces
        query_heads = as_heads(query_block)
        key_heads = as_heads(key_block)
        grad_heads = as_heads(grad_block)
        scores = (
            jnp.einsum("qhd,khd->hqk", query_heads, key_heads, preferred_element_type=jnp.float32)
            * 0.125
        )
        soft_weights = jnp.where(allowed[None], jnp.exp(scores - log_block[..., None]), 0.0)
        soft_low = soft_weights.astype(jnp.bfloat16)
        grad_probs = jnp.einsum(
            "qhd,khd->hqk", grad_heads, as_heads(value_block), preferred_element_type=jnp.float32
        )
        row_delta = jnp.sum(soft_weights * grad_probs, axis=-1, keepdims=True)
        grad_scores = (soft_weights * (grad_probs - row_delta)).astype(jnp.bfloat16)
        grad_query = (
            jnp.einsum("hqk,khd->qhd", grad_scores, key_heads, preferred_element_type=jnp.float32)
            * 0.125
        )
        grad_key = (
            jnp.einsum("hqk,qhd->khd", grad_scores, query_heads, preferred_element_type=jnp.float32)
            * 0.125
        )
        grad_value = jnp.einsum(
            "hqk,qhd->khd", soft_low, grad_heads, preferred_element_type=jnp.float32
        )
        return (
            grad_query.reshape(query_block.shape[0], -1),
            grad_key.reshape(key_block.shape[0], -1),
            grad_value.reshape(key_block.shape[0], -1),
        )

    grad_query, grad_key, grad_value = lax.map(
        per_group,
        (
            split_groups(query_row),
            split_groups(key_row),
            split_groups(value_row),
            split_groups(grad_row),
            log_total,
        ),
    )
    return (join_groups(grad_query), join_groups(grad_key), join_groups(grad_value))


def plain_local(
    tokens,
    first_values,
    v1_accum,
    segment_ids,
    positions,
    cotangent,
    attn_gain,
    w_query,
    w_key,
    w_value,
    w_out,
    mlp_gain,
    w_gate,
    w_up,
    w_down,
):
    row_count, seq_piece, model_width = tokens.shape
    token_count = row_count * seq_piece
    flat_tokens = tokens.astype(jnp.float32).reshape(token_count, model_width)
    first_flat = first_values.astype(jnp.float32).reshape(token_count, model_width)
    cosine_table, sine_table = angle_tables(positions)
    segment_low = segment_ids.astype(jnp.bfloat16)
    attn_set = (
        lax.all_gather(attn_gain, ("dp", "ctx"), axis=0, tiled=True),
        lax.all_gather(w_query, ("dp", "ctx"), axis=0, tiled=True),
        lax.all_gather(w_key, ("dp", "ctx"), axis=0, tiled=True),
        lax.all_gather(w_value, ("dp", "ctx"), axis=0, tiled=True),
        lax.all_gather(w_out, ("dp", "ctx"), axis=0, tiled=True),
    )
    normed, inv_root, normed_in, query_rot, key_rot, value_mix = attn_front(
        flat_tokens, first_flat, attn_set, cosine_table, sine_table, row_count, seq_piece
    )
    key_full, value_full, segment_full = (
        lax.all_gather(key_rot, "ctx", axis=1, tiled=True),
        lax.all_gather(value_mix, "ctx", axis=1, tiled=True),
        lax.all_gather(segment_low, "ctx", axis=1, tiled=True),
    )
    query_order = lax.axis_index("ctx") * seq_piece + jnp.arange(seq_piece, dtype=jnp.int32)
    full_order = jnp.arange(key_full.shape[1], dtype=jnp.int32)
    segment_own = segment_ids.astype(jnp.float32)
    segment_all = segment_full.astype(jnp.float32)
    allowed = (segment_own[:, :, None] == segment_all[:, None, :]) & (
        query_order[None, :, None] >= full_order[None, None, :]
    )
    attended, log_total = lax.map(attend_row, (query_rot, key_full, value_full, allowed))
    attended_low = attended.reshape(token_count, model_width).astype(jnp.bfloat16)
    mlp_set = (
        lax.all_gather(mlp_gain, ("dp", "ctx"), axis=0, tiled=True),
        lax.all_gather(w_gate, ("dp", "ctx"), axis=0, tiled=True),
        lax.all_gather(w_up, ("dp", "ctx"), axis=0, tiled=True),
        lax.all_gather(w_down, ("dp", "ctx"), axis=0, tiled=True),
    )
    normed_two, inv_root_two, mlp_in, gate_proj, up_proj, hidden, output_flat = mlp_block(
        flat_tokens, attended_low, attn_set[4], mlp_set
    )
    output = output_flat.reshape(tokens.shape).astype(jnp.bfloat16)
    attn_set = (
        lax.all_gather(attn_gain, ("dp", "ctx"), axis=0, tiled=True),
        lax.all_gather(w_query, ("dp", "ctx"), axis=0, tiled=True),
        lax.all_gather(w_key, ("dp", "ctx"), axis=0, tiled=True),
        lax.all_gather(w_value, ("dp", "ctx"), axis=0, tiled=True),
        lax.all_gather(w_out, ("dp", "ctx"), axis=0, tiled=True),
    )
    mlp_set = (
        lax.all_gather(mlp_gain, ("dp", "ctx"), axis=0, tiled=True),
        lax.all_gather(w_gate, ("dp", "ctx"), axis=0, tiled=True),
        lax.all_gather(w_up, ("dp", "ctx"), axis=0, tiled=True),
        lax.all_gather(w_down, ("dp", "ctx"), axis=0, tiled=True),
    )
    normed, inv_root, normed_in, query_rot, key_rot, value_mix = attn_front(
        flat_tokens, first_flat, attn_set, cosine_table, sine_table, row_count, seq_piece
    )
    key_full, value_full = (
        lax.all_gather(key_rot, "ctx", axis=1, tiled=True),
        lax.all_gather(value_mix, "ctx", axis=1, tiled=True),
    )
    normed_two, inv_root_two, mlp_in, gate_proj, up_proj, hidden, output_flat = mlp_block(
        flat_tokens, attended_low, attn_set[4], mlp_set
    )
    cot_low = cotangent.reshape(token_count, model_width)
    cot_float = cot_low.astype(jnp.float32)
    grad_hidden = jnp.einsum("td,fd->tf", cot_low, mlp_set[3], preferred_element_type=jnp.float32)
    sigma = jax.nn.sigmoid(gate_proj)
    grad_gate_low = (grad_hidden * up_proj * sigma * (1.0 + gate_proj * (1.0 - sigma))).astype(
        jnp.bfloat16
    )
    grad_up_low = (grad_hidden * gate_proj * sigma).astype(jnp.bfloat16)
    grad_mlp_in = jnp.einsum(
        "tf,df->td", grad_gate_low, mlp_set[1], preferred_element_type=jnp.float32
    )
    grad_mlp_in = grad_mlp_in + jnp.einsum(
        "tf,df->td", grad_up_low, mlp_set[2], preferred_element_type=jnp.float32
    )
    grad_middle_norm, grad_gain_two = norm_back(grad_mlp_in, normed_two, inv_root_two, mlp_set[0])
    grad_middle = cot_float + grad_middle_norm
    grad_branch_low = grad_middle.astype(jnp.bfloat16)
    grad_attended = jnp.einsum(
        "te,de->td", grad_branch_low, attn_set[4], preferred_element_type=jnp.float32
    )
    grad_attended = grad_attended.astype(jnp.bfloat16).reshape(row_count, seq_piece, model_width)
    grad_query_rot, grad_key_full, grad_value_full = lax.map(
        attend_back, (query_rot, key_full, value_full, grad_attended, log_total, allowed)
    )
    grad_key_rot, grad_value_mix = (
        lax.psum_scatter(
            grad_key_full.astype(jnp.bfloat16), "ctx", scatter_dimension=1, tiled=True
        ).astype(jnp.float32),
        lax.psum_scatter(
            grad_value_full.astype(jnp.bfloat16), "ctx", scatter_dimension=1, tiled=True
        ).astype(jnp.float32),
    )
    v1_grad = v1_accum + 0.5 * grad_value_mix
    grad_query_low = rotate(
        grad_query_rot.reshape(row_count, seq_piece, HEADS, HEAD_DIM), cosine_table, -sine_table
    )
    grad_query_low = grad_query_low.astype(jnp.bfloat16).reshape(token_count, model_width)
    grad_key_low = rotate(
        grad_key_rot.reshape(row_count, seq_piece, HEADS, HEAD_DIM), cosine_table, -sine_table
    )
    grad_key_low = grad_key_low.astype(jnp.bfloat16).reshape(token_count, model_width)
    grad_value_low = (0.5 * grad_value_mix).astype(jnp.bfloat16).reshape(token_count, model_width)
    grad_normed_in = jnp.einsum(
        "te,de->td", grad_query_low, attn_set[1], preferred_element_type=jnp.float32
    )
    grad_normed_in = grad_normed_in + jnp.einsum(
        "te,de->td", grad_key_low, attn_set[2], preferred_element_type=jnp.float32
    )
    grad_normed_in = grad_normed_in + jnp.einsum(
        "te,de->td", grad_value_low, attn_set[3], preferred_element_type=jnp.float32
    )
    grad_input_norm, grad_gain_one = norm_back(grad_normed_in, normed, inv_root, attn_set[0])
    input_grad = (grad_middle + grad_input_norm).reshape(tokens.shape)
    attn_right = jnp.concatenate([grad_query_low, grad_key_low, grad_value_low], axis=1)
    left_in = normed_in
    projections = jnp.einsum("td,te->de", left_in, attn_right, preferred_element_type=jnp.float32)
    out_part = jnp.einsum(
        "td,te->de", attended_low, grad_branch_low, preferred_element_type=jnp.float32
    )
    attn_matrix = lax.psum_scatter(
        jnp.concatenate([projections, out_part], axis=1),
        ("dp", "ctx"),
        scatter_dimension=0,
        tiled=True,
    )
    mlp_right = jnp.concatenate([grad_gate_low, grad_up_low], axis=1)
    left_in = mlp_in
    gate_up_matrix = lax.psum_scatter(
        jnp.einsum("td,tf->df", left_in, mlp_right, preferred_element_type=jnp.float32),
        ("dp", "ctx"),
        scatter_dimension=0,
        tiled=True,
    )
    down_matrix = lax.psum_scatter(
        jnp.einsum("tf,td->fd", hidden, cot_low, preferred_element_type=jnp.float32),
        ("dp", "ctx"),
        scatter_dimension=0,
        tiled=True,
    )
    gain_one, gain_two = (
        lax.psum_scatter(grad_gain_one, ("dp", "ctx"), scatter_dimension=0, tiled=True),
        lax.psum_scatter(grad_gain_two, ("dp", "ctx"), scatter_dimension=0, tiled=True),
    )
    ff_width = w_gate.shape[1]
    return (
        output,
        input_grad,
        v1_grad,
        gain_one,
        attn_matrix[:, 0:model_width],
        attn_matrix[:, model_width : 2 * model_width],
        attn_matrix[:, 2 * model_width : 3 * model_width],
        attn_matrix[:, 3 * model_width : 4 * model_width],
        gain_two,
        gate_up_matrix[:, 0:ff_width],
        gate_up_matrix[:, ff_width : 2 * ff_width],
        down_matrix,
    )


def params(**kw):
    return pltpu.CompilerParams(vmem_limit_bytes=BYTES, **kw)


def dot(a, b, da, db):
    return lax.dot_general(a, b, (((da,), (db,)), ((), ())), preferred_element_type=F32)


def lane_block(index):
    return pl.ds(pl.multiple_of(index * LANES, LANES), LANES)


def half_swap(x):
    lane = lax.broadcasted_iota(jnp.int32, x.shape, 1)
    left = pltpu.roll(x, LANES - HEAD_DIM // 2, 1)
    right = pltpu.roll(x, HEAD_DIM // 2, 1)
    return jnp.where(lane % HEAD_DIM < HEAD_DIM // 2, left, right)


def head_lanes(x, head):
    lane = lax.broadcasted_iota(jnp.int32, x.shape, 1)
    return jnp.where(lane // HEAD_DIM == head, x, jnp.zeros_like(x))


def meet(n_ctx, bits):
    c, dp = lax.axis_index("ctx"), lax.axis_index("dp")
    barrier = pltpu.get_barrier_semaphore()
    for k in range(1, n_ctx):
        pl.semaphore_signal(barrier, inc=1, device_id={"ctx": lax.rem(c + k, n_ctx)}, device_id_type=MESH)
    for bit in bits:
        pl.semaphore_signal(barrier, inc=1, device_id={"dp": dp ^ bit}, device_id_type=MESH)
    pl.semaphore_wait(barrier, n_ctx - 1 + len(bits))


def ctx_copy(src, dst, send, recv, to):
    return pltpu.make_async_remote_copy(
        src_ref=src, dst_ref=dst, send_sem=send, recv_sem=recv, device_id={"ctx": to}, device_id_type=MESH
    )


def dp_copy(src, dst, send, recv, bit):
    to = lax.axis_index("dp") ^ bit
    return pltpu.make_async_remote_copy(
        src_ref=src, dst_ref=dst, send_sem=send, recv_sem=recv, device_id={"dp": to}, device_id_type=MESH
    )


def rows_of(index, size):
    return pl.ds(pl.multiple_of(index * size, size), size)


CORE, NEAR, FAR = 1, 2, 4


class Gather:
    def __init__(self, n_ctx, src, dst, send, recv, order):
        self.n, self.src, self.dst, self.send, self.recv = n_ctx, src, dst, send, recv
        self.first, self.second = order
        self.rows = src.shape[0]

    def place(self, c):
        return self.dst.at[0, pl.ds(c * self.rows, self.rows), :]

    def along(self, bit):
        c = lax.axis_index("ctx")
        return ctx_copy(self.src, self.place(c), self.send.at[bit - 1], self.recv.at[bit - 1], c ^ bit)

    def pass_on(self):
        c = lax.axis_index("ctx")
        return ctx_copy(self.place(c ^ 2), self.place(c ^ 2), self.send.at[2], self.recv.at[2], c ^ 1)

    def plane(self, slot, bit, at):
        return dp_copy(self.dst.at[slot], self.dst.at[slot ^ bit], self.send.at[at], self.recv.at[at], bit)

    def own(self):
        c = lax.axis_index("ctx")
        return pltpu.make_async_copy(self.src, self.dst.at[0, pl.ds(c * self.rows, self.rows), :], self.send.at[10])

    def hop(self, at):
        one, two = self.first, self.second
        slot, bit = [(0, one), (0, two), (one, two), (0, CORE), (one, CORE), (two, CORE), (one | two, CORE)][at]
        return self.plane(slot, bit, 3 + at)

    def start(self):
        self.own().start()
        self.along(2).start()
        self.along(1).start()

    def relay(self):
        self.along(2).wait_recv()
        self.pass_on().start()

    def spread(self):
        self.own().wait()
        self.along(1).wait_recv()
        self.pass_on().wait_recv()
        for at in (0, 1, 3):
            self.hop(at).start()

    def forward(self):
        self.hop(0).wait_recv()
        self.hop(2).start()
        self.hop(4).start()

    def cross(self):
        self.hop(1).wait_recv()
        self.hop(5).start()
        self.hop(2).wait_recv()
        self.hop(6).start()

    def finish(self):
        self.along(1).wait_send()
        self.along(2).wait_send()
        self.pass_on().wait_send()
        for at in range(7):
            self.hop(at).wait_send()
        for at in range(3, 7):
            self.hop(at).wait_recv()


def front_kernel(
    n_ctx, tok_ref, fv_ref, mark_ref, pack_ref, freq_ref, wg_ref, wu_ref, wo_ref, wd_ref,
    xn_ref, q_ref, k_ref, v_ref, of_ref, lse_ref, cos_ref, sin_ref, seg_ref, marks, gain_ref,
    att_ref, wg_all, wu_all, wo_all, wd_all,
    x_all, fvs, packs, whead, rel, o_ref, s_ref, m_ref, l_ref, acc_ref,
    mark_send, mark_recv, pack_send, pack_recv, tok_send, tok_recv, fv_send, fv_recv, w_send, w_recv,
    o_send, o_recv, own, own_o,
):
    c, dp = lax.axis_index("ctx"), lax.axis_index("dp")
    tb = m_ref.shape[0]
    half = tb // 2
    model = tok_ref.shape[1]
    blocks = model // LANES
    width = q_ref.shape[1]
    own_rows = wg_ref.shape[0]
    lane = lax.broadcasted_iota(jnp.int32, (tb, LANES), 1)
    exact = lax.Precision.HIGHEST

    weights = [
        Gather(n_ctx, src, dst, w_send.at[i], w_recv.at[i], order)
        for i, (src, dst, order) in enumerate(
            [
                (wg_ref, wg_all, (NEAR, FAR)),
                (wo_ref, wo_all, (FAR, NEAR)),
                (wu_ref, wu_all, (FAR, NEAR)),
                (wd_ref, wd_all, (NEAR, FAR)),
            ]
        )
    ]
    early, late = weights[:3], weights[3:]

    def mark_copy(k):
        at = rows_of(c, tb)
        return ctx_copy(mark_ref, marks.at[:, at], mark_send.at[k - 1], mark_recv.at[k - 1], lax.rem(c + k, n_ctx))

    def pack_copy(k):
        to = lax.rem(c + k, n_ctx)
        return ctx_copy(pack_ref.at[to], packs.at[0, c], pack_send.at[k - 1], pack_recv.at[k - 1], to)

    def pack_hop(slot, bit, at):
        return dp_copy(packs.at[slot], packs.at[slot ^ bit], pack_send.at[at], pack_recv.at[at], bit)

    def fv_copy(k):
        to = lax.rem(c + k, n_ctx)
        return ctx_copy(fv_ref.at[:, rows_of(to, width)], fvs.at[rows_of(c, tb), :], fv_send.at[k - 1], fv_recv.at[k - 1], to)

    def tok_copy(bit):
        return ctx_copy(tok_ref, x_all.at[rows_of(c, tb), :], tok_send.at[bit - 1], tok_recv.at[bit - 1], c ^ bit)

    def tok_pass():
        at = rows_of(c ^ 2, tb)
        return ctx_copy(x_all.at[at, :], x_all.at[at, :], tok_send.at[2], tok_recv.at[2], c ^ 1)

    locals_ = [
        pltpu.make_async_copy(tok_ref, x_all.at[rows_of(c, tb), :], own.at[0]),
        pltpu.make_async_copy(fv_ref.at[:, rows_of(c, width)], fvs.at[rows_of(c, tb), :], own.at[1]),
        pltpu.make_async_copy(pack_ref.at[c], packs.at[0, c], own.at[2]),
        pltpu.make_async_copy(mark_ref, marks.at[:, rows_of(c, tb)], own.at[3]),
    ]

    meet(n_ctx, (CORE, NEAR, FAR))
    for k in range(1, n_ctx):
        mark_copy(k).start()
        pack_copy(k).start()
    for w in early:
        w.start()
    for m in locals_:
        m.start()

    locals_[3].wait()
    for k in range(1, n_ctx):
        mark_copy(k).wait_recv()
    row8 = lax.broadcasted_iota(jnp.int32, (8, LANES), 0)
    pick_seg = jnp.where(row8 == 0, 1.0, 0.0)
    pick_pos = jnp.where(row8 == 1, 1.0, 0.0)

    def table(b, carry):
        at = rows_of(b, tb)
        m = marks[:, at].astype(F32)
        dims = (((0,), (0,)), ((), ()))
        seg_ref[at, :] = lax.dot_general(m, pick_seg, dims, precision=exact, preferred_element_type=F32)
        pos = lax.dot_general(m, pick_pos, dims, precision=exact, preferred_element_type=F32)
        angle = pos * freq_ref[0:1, :]
        cos_ref[at, :] = jnp.cos(angle)
        sin_ref[at, :] = jnp.sin(angle) * freq_ref[1:2, :]
        return carry

    locals_[2].wait()
    for k in range(1, n_ctx):
        pack_copy(k).wait_recv()
    pack_hop(0, NEAR, 3).start()
    lax.fori_loop(0, n_ctx, table, 0)
    pack_hop(0, NEAR, 3).wait_recv()
    pack_hop(0, FAR, 4).start()
    pack_hop(NEAR, FAR, 5).start()
    pack_hop(0, CORE, 6).start()
    pack_hop(NEAR, CORE, 7).start()

    for w in early:
        w.relay()
    tok_copy(2).start()
    tok_copy(1).start()
    pack_hop(0, FAR, 4).wait_recv()
    pack_hop(FAR, CORE, 8).start()
    pack_hop(NEAR, FAR, 5).wait_recv()
    pack_hop(NEAR | FAR, CORE, 9).start()
    for at, (slot, bit) in enumerate([(0, CORE), (NEAR, CORE), (FAR, CORE), (NEAR | FAR, CORE)]):
        pack_hop(slot, bit, 6 + at).wait_recv()
    count = packs.shape[0]
    for t in range(3):
        block = packs[:, :, t * own_rows : (t + 1) * own_rows, :]
        whead[:, t * width : (t + 1) * width] = block.reshape(model, width)
    gains = packs[:, :, 3 * own_rows : 4 * own_rows, 0:LANES].reshape(model, LANES).astype(F32)
    gain_ref[...] = gains.T[0:8, :]
    locals_[0].wait()
    locals_[1].wait()

    def project(chunk, part):
        at = pl.ds(pl.multiple_of(chunk * tb + part * half, half), half)
        for d in range(blocks):
            rel[:, d * LANES : (d + 1) * LANES] = x_all[at, lane_block(dp ^ d)].astype(F32)
        x = rel[...]
        inv = lax.rsqrt(jnp.mean(x * x, axis=-1, keepdims=True) + epsilon)
        xn = (x * inv * gain_ref[0:1, :]).astype(LOW)
        xn_ref[at, :] = xn
        proj = dot(xn, whead[...], 1, 0)
        cos, sin = cos_ref[at, :], sin_ref[at, :]
        for b in range(width // LANES):
            cols = slice(b * LANES, (b + 1) * LANES)
            qb = proj[:, b * LANES : (b + 1) * LANES]
            q_ref[at, cols] = ((qb * cos + half_swap(qb) * sin) * 0.125).astype(LOW)
            kb = proj[:, width + b * LANES : width + (b + 1) * LANES]
            k_ref[at, cols] = (kb * cos + half_swap(kb) * sin).astype(LOW)
        v_ref[at, :] = (0.5 * proj[:, 2 * width :] + 0.5 * fvs[at, :].astype(F32)).astype(LOW)

    def project_chunk(bit):
        def one(part, carry):
            project(c ^ bit, part)
            return carry

        lax.fori_loop(0, 2, one, 0)

    for w in early:
        w.spread()
    project_chunk(0)
    tok_copy(2).wait_recv()
    tok_pass().start()
    for k in range(1, n_ctx):
        fv_copy(k).start()
    for w in early:
        w.forward()
    tok_copy(1).wait_recv()
    for k in range(1, n_ctx):
        fv_copy(k).wait_recv()
    project_chunk(1)
    project_chunk(2)
    tok_pass().wait_recv()
    for w in late:
        w.start()
    project_chunk(3)
    for w in early:
        w.cross()

    def fold(x, op):
        r = x[:, 0:LANES]
        for b in range(1, tb // LANES):
            r = op(r, x[:, b * LANES : (b + 1) * LANES])
        return r

    def home(pair):
        return att_ref.at[:, pl.ds(pl.multiple_of(c * width + pair * LANES, LANES), LANES)]

    def query_block(pair, i):
        cols = slice(pair * LANES, (pair + 1) * LANES)
        mine = rows_of(i, tb)
        q = q_ref[mine, cols]
        seg_q = seg_ref[mine, 0:1]
        for head in range(2):
            qm = head_lanes(q, head)
            m_ref[...] = jnp.full_like(m_ref, NEG)

            def score(j, causal):
                at = rows_of(j, tb)
                s = dot(qm, k_ref[at, cols], 1, 1)
                ok = seg_q == marks[0:1, at].astype(F32)
                if causal:
                    r = lax.broadcasted_iota(jnp.int32, (tb, tb), 0)
                    t = lax.broadcasted_iota(jnp.int32, (tb, tb), 1)
                    ok = ok & (r >= t)
                s = jnp.where(ok, s, NEG)
                s_ref[:, at] = s
                m_ref[...] = jnp.maximum(m_ref[...], fold(s, jnp.maximum))

            def score_step(j, carry):
                score(j, False)
                return carry

            lax.fori_loop(0, i, score_step, 0)
            score(i, True)
            top = jnp.max(m_ref[...], axis=1, keepdims=True)
            l_ref[...] = jnp.zeros_like(l_ref)
            acc_ref[...] = jnp.zeros_like(acc_ref)

            def value_step(j, carry):
                at = rows_of(j, tb)
                p = jnp.exp(s_ref[:, at] - top)
                l_ref[...] += fold(p, jnp.add)
                acc_ref[...] += dot(p.astype(LOW), v_ref[at, cols], 1, 0)
                return carry

            lax.fori_loop(0, i + 1, value_step, 0)
            total = jnp.sum(l_ref[...], axis=1, keepdims=True)
            out = acc_ref[...] / total
            lse = jnp.broadcast_to(top + jnp.log(total), (tb, LANES))
            if head == 0:
                of_ref[mine, cols] = out
                lse_ref[mine, cols] = lse
            else:
                of_ref[mine, cols] = jnp.where(lane < HEAD_DIM, of_ref[mine, cols], out)
                lse_ref[mine, cols] = jnp.where(lane < HEAD_DIM, lse_ref[mine, cols], lse)
        o_ref[mine, cols] = of_ref[mine, cols].astype(LOW)

        @pl.when(i == c)
        def _():
            pltpu.make_async_copy(o_ref.at[mine, cols], home(pair), own_o.at[pair]).start()

        @pl.when(i != c)
        def _():
            k = lax.rem(i + n_ctx - c, n_ctx) - 1
            ctx_copy(o_ref.at[mine, cols], home(pair), o_send.at[k, pair], o_recv.at[k, pair], i).start()

    def query_blocks(pair, lo, hi):
        def one(i, carry):
            query_block(pair, i)
            return carry

        lax.fori_loop(lo, hi, one, 0)

    query_blocks(0, 0, 3)
    for w in late:
        w.relay()
    query_blocks(0, 3, n_ctx)
    for w in late:
        w.spread()
    query_blocks(1, 0, n_ctx)
    for w in late:
        w.forward()
    for pair in range(width // LANES):
        cols = slice(pair * LANES, (pair + 1) * LANES)
        pltpu.make_async_copy(o_ref.at[0:tb, cols], home(pair), own_o.at[pair]).wait()
        for k in range(n_ctx - 1):
            ctx_copy(o_ref.at[0:tb, cols], home(pair), o_send.at[k, pair], o_recv.at[k, pair], c).wait()
    for w in late:
        w.cross()
    for k in range(1, n_ctx):
        mark_copy(k).wait_send()
        pack_copy(k).wait_send()
        fv_copy(k).wait_send()
    for at, (slot, bit) in enumerate(
        [(0, NEAR), (0, FAR), (NEAR, FAR), (0, CORE), (NEAR, CORE), (FAR, CORE), (NEAR | FAR, CORE)]
    ):
        pack_hop(slot, bit, 3 + at).wait_send()
    tok_copy(1).wait_send()
    tok_copy(2).wait_send()
    tok_pass().wait_send()
    for w in weights:
        w.finish()


def front_call(n_dp, n_ctx, tok, fv, mark, pack, freq, wg, wu, wo, wd):
    tb, model = tok.shape
    width = model // n_ctx
    length = n_ctx * tb
    pairs = width // LANES
    vmem = pl.BlockSpec(memory_space=pltpu.VMEM)
    anyspace = pl.BlockSpec(memory_space=pl.ANY)
    shape = jax.ShapeDtypeStruct
    dma = pltpu.SemaphoreType.DMA
    return pl.pallas_call(
        functools.partial(front_kernel, n_ctx),
        in_specs=[anyspace] * 4 + [vmem] + [anyspace] * 4,
        out_specs=[vmem] * 11 + [anyspace] * 5,
        out_shape=[shape((length, model), LOW)]
        + [shape((length, width), LOW)] * 3
        + [shape((length, width), F32)] * 2
        + [shape((length, LANES), F32)] * 3
        + [shape((8, length), jnp.int32), shape((8, model), F32)]
        + [shape((tb, model), LOW)]
        + [shape((n_dp, n_ctx * w.shape[0], w.shape[1]), LOW) for w in (wg, wu, wo, wd)],
        scratch_shapes=[
            pltpu.VMEM((length, model), LOW),
            pltpu.VMEM((length, width), LOW),
            pltpu.VMEM((n_dp,) + pack.shape, LOW),
            pltpu.VMEM((model, 3 * width), LOW),
            pltpu.VMEM((tb // 2, model), F32),
            pltpu.VMEM((length, width), LOW),
            pltpu.VMEM((tb, length), F32),
            pltpu.VMEM((tb, LANES), F32),
            pltpu.VMEM((tb, LANES), F32),
            pltpu.VMEM((tb, LANES), F32),
            dma((n_ctx - 1,)), dma((n_ctx - 1,)),
            dma((n_ctx + 6,)), dma((n_ctx + 6,)),
            dma((3,)), dma((3,)),
            dma((n_ctx - 1,)), dma((n_ctx - 1,)),
            dma((4, 11)), dma((4, 11)),
            dma((n_ctx - 1, pairs)), dma((n_ctx - 1, pairs)),
            dma((4,)), dma((pairs,)),
        ],
        compiler_params=params(collective_id=1, has_side_effects=True),
        cost_estimate=pl.CostEstimate(
            flops=24 * 10**9, bytes_accessed=60 * 2**20, transcendentals=2 * length * length
        ),
        name="front",
    )(tok, fv, mark, pack, freq, wg, wu, wo, wd)


class Reduce:
    def __init__(self, n_ctx, keep, came, acc, rc, rx, ry, rz, out, send, recv, order):
        self.n, self.keep, self.came, self.acc, self.rc, self.rx, self.ry, self.rz = n_ctx, keep, came, acc, rc, rx, ry, rz
        self.out, self.send, self.recv = out, send, recv
        self.one, self.two = order
        self.leave = (self.one >> 1, 3)
        self.stay = self.two >> 1

    def hop(self, at):
        src, dst, bit = [
            (self.acc.at[self.leave[0]], self.rx.at[0], self.one),
            (self.acc.at[self.leave[1]], self.rx.at[1], self.one),
            (self.acc.at[self.stay], self.ry, self.two),
        ][at - 1]
        return dp_copy(src, dst, self.send.at[at], self.recv.at[at], bit)

    def held(self):
        return pltpu.make_async_copy(self.keep, self.acc, self.send.at[7])

    def partner(self):
        return pltpu.make_async_copy(self.came, self.rc, self.send.at[0])

    def along(self, at):
        c = lax.axis_index("ctx")
        block, to = ((c ^ 1, c ^ 1), (c ^ 3, c ^ 1), (c ^ 2, c ^ 2))[at]
        return ctx_copy(self.acc.at[0, block], self.rz.at[at], self.send.at[4 + at], self.recv.at[4 + at], to)

    def begin(self):
        self.partner().start()
        self.held().start()

    def add(self, block, terms):
        def one(j, carry):
            total = self.acc[block, j].astype(F32)
            for t in terms:
                total = total + t(j).astype(F32)
            self.acc[block, j] = total.astype(LOW)
            return carry

        lax.fori_loop(0, self.acc.shape[1], one, 0)

    def step_one(self):
        self.held().wait()
        self.partner().wait()
        for at in (1, 0):
            block = self.leave[at]
            self.add(block, [lambda j, block=block: self.rc[block, j]])
            self.hop(1 + at).start()

    def step_two(self):
        self.hop(2).wait_recv()
        self.add(self.stay, [lambda j: self.rc[self.stay, j], lambda j: self.rx[1, j]])
        self.hop(3).start()

    def step_ctx(self):
        c = lax.axis_index("ctx")
        self.hop(1).wait_recv()
        self.hop(3).wait_recv()
        self.out[...] = (
            self.acc[0, c].astype(F32) + self.rc[0, c].astype(F32) + self.rx[0, c].astype(F32) + self.ry[c].astype(F32)
        )
        self.add(0, [lambda j: self.rc[0, j], lambda j: self.rx[0, j], lambda j: self.ry[j]])
        self.along(1).start()
        self.along(0).start()

    def step_far(self):
        block = lax.axis_index("ctx") ^ 2
        self.along(1).wait_recv()
        self.acc[0, block] = (self.acc[0, block].astype(F32) + self.rz[1].astype(F32)).astype(LOW)
        self.along(2).start()

    def finish(self):
        self.along(0).wait_recv()
        self.along(2).wait_recv()
        self.out[...] += self.rz[0].astype(F32) + self.rz[2].astype(F32)
        for at in range(1, 4):
            self.hop(at).wait_send()
        for at in range(3):
            self.along(at).wait_send()


def back_kernel(n_ctx, *refs):
    g_ref, q_ref, k_ref, v_ref, of_ref, lse_ref, sc_ref, sr_ref, cos_ref, sin_ref, xn_ref = refs[:11]
    sides = refs[11:19]
    home_ref, qkv_out = refs[19:21]
    outs = refs[21:25]
    (part_ref, lse_row, delta_row, dq_acc, dk_acc, dv_acc, prod) = refs[25:32]
    rest = refs[32:]
    buffers, rest = rest[:40], rest[40:]
    (pk, ps, prc, prx, pry, pz, qz) = rest[:7]
    (send, recv, own, r_send, r_recv, p_send, p_recv, z_send, z_recv) = rest[7:]
    c = lax.axis_index("ctx")
    tb = dk_acc.shape[0]
    length, width = q_ref.shape
    model = n_ctx * width
    pairs = width // LANES
    blocks = model // LANES
    orders = ((NEAR, FAR), (FAR, NEAR))
    groups = []
    for i in range(4):
        keep, came = sides[2 * i], sides[2 * i + 1]
        wide = keep.shape[3] // 2
        groups.append([])
        for h, order in enumerate(orders):
            cols = pl.ds(h * wide, wide)
            unit = 2 * i + h
            groups[i].append(
                Reduce(
                    n_ctx, keep.at[:, :, :, cols], came.at[:, :, :, cols], *buffers[5 * unit : 5 * unit + 5],
                    outs[i].at[:, cols], r_send.at[unit], r_recv.at[unit], order,
                )
            )

    def each(i, what):
        for unit in groups[i]:
            getattr(unit, what)()

    def home(pair, t):
        return home_ref.at[:, pl.ds(pl.multiple_of(t * model + c * width + pair * LANES, LANES), LANES)]

    def part(pair, t, chunk):
        return part_ref.at[pair, rows_of(chunk, tb), pl.ds(t * LANES, LANES)]

    def part_copy(pair, t, k):
        to = lax.rem(c + k, n_ctx)
        return ctx_copy(part(pair, t, to), home(pair, t), send.at[k - 1, pair, t], recv.at[k - 1, pair, t], to)

    def part_own(pair, t):
        return pltpu.make_async_copy(part(pair, t, c), home(pair, t), own.at[pair, t])

    meet(n_ctx, (CORE, NEAR, FAR))
    for i in range(4):
        each(i, "begin")
    each(0, "step_one")

    r8 = lax.broadcasted_iota(jnp.int32, (8, LANES), 0)
    l8 = lax.broadcasted_iota(jnp.int32, (8, LANES), 1)
    pick = jnp.where(l8 == r8 * HEAD_DIM, 1.0, 0.0)
    group = jnp.where(l8 // HEAD_DIM == r8, 1.0, 0.0)
    exact = lax.Precision.HIGHEST
    dims = (((1,), (1,)), ((), ()))

    def stats(pair):
        cols = slice(pair * LANES, (pair + 1) * LANES)

        def one(b, carry):
            at = rows_of(b, tb)
            lse_row[:, at] = lax.dot_general(pick, lse_ref[at, cols], dims, precision=exact, preferred_element_type=F32)
            mixed = g_ref[at, cols].astype(F32) * of_ref[at, cols]
            delta_row[:, at] = lax.dot_general(group, mixed, dims, precision=exact, preferred_element_type=F32)
            dq_acc[at, :] = jnp.zeros((tb, LANES), F32)
            return carry

        lax.fori_loop(0, n_ctx, one, 0)

    def key_blocks(pair, lo, hi):
        cols = slice(pair * LANES, (pair + 1) * LANES)

        def key_block(j, carry):
            dk_acc[...] = jnp.zeros_like(dk_acc)
            dv_acc[...] = jnp.zeros_like(dv_acc)
            mine = rows_of(j, tb)
            k = k_ref[mine, cols]
            v = v_ref[mine, cols]
            seg_k = sc_ref[mine, 0:1]

            def block(i, causal):
                at = rows_of(i, tb)
                q = q_ref[at, cols]
                g = g_ref[at, cols]
                ok = seg_k == sr_ref[0:1, at].astype(F32)
                if causal:
                    r = lax.broadcasted_iota(jnp.int32, (tb, tb), 0)
                    t = lax.broadcasted_iota(jnp.int32, (tb, tb), 1)
                    ok = ok & (r <= t)
                for head in range(2):
                    qm = head_lanes(q, head)
                    gm = head_lanes(g, head)
                    s = dot(k, qm, 1, 1)
                    p = jnp.where(ok, jnp.exp(s - lse_row[head : head + 1, at]), 0.0)
                    dp = dot(v, gm, 1, 1)
                    ds = (p * (dp - delta_row[head : head + 1, at])).astype(LOW)
                    dv_acc[...] += dot(p.astype(LOW), gm, 1, 0)
                    dk_acc[...] += dot(ds, qm, 1, 0)
                    dq_acc[at, :] += dot(ds, head_lanes(k, head), 0, 0)

            block(j, True)

            def step(i, carry):
                block(i, False)
                return carry

            lax.fori_loop(j + 1, n_ctx, step, 0)
            dk = dk_acc[...]
            dk = dk * cos_ref[mine, :] - half_swap(dk) * sin_ref[mine, :]
            part_ref[pair, mine, LANES : 2 * LANES] = dk.astype(LOW)
            part_ref[pair, mine, 2 * LANES : 3 * LANES] = dv_acc[...].astype(LOW)
            return carry

        lax.fori_loop(lo, hi, key_block, 0)

    def send_home(pair):
        def query_done(b, carry):
            at = rows_of(b, tb)
            dq = dq_acc[at, :] * 0.125
            dq = dq * cos_ref[at, :] - half_swap(dq) * sin_ref[at, :]
            part_ref[pair, at, 0:LANES] = dq.astype(LOW)
            return carry

        lax.fori_loop(0, n_ctx, query_done, 0)
        for t in range(3):
            part_own(pair, t).start()
            for k in range(1, n_ctx):
                part_copy(pair, t, k).start()

    def pair_hop(pair, at):
        src, dst, bit = [
            (ps.at[pair], prc.at[pair], CORE),
            (pk.at[pair, 1], prx.at[pair, 0], NEAR),
            (pk.at[pair, 3], prx.at[pair, 1], NEAR),
            (pk.at[pair, 2], pry.at[pair], FAR),
        ][at]
        return dp_copy(src, dst, p_send.at[pair, at], p_recv.at[pair, at], bit)

    def pair_ctx(pair, k):
        to = lax.rem(c + k, n_ctx)
        return ctx_copy(pz.at[pair, to], qz.at[c, pair], z_send.at[pair, k - 1], z_recv.at[pair, k - 1], to)

    def pair_product(pair):
        prod[...] = jnp.zeros_like(prod)

        def one(b, carry):
            at = rows_of(b, tb)
            prod[...] += dot(part_ref[pair, at, :], xn_ref[at, :], 0, 0)
            return carry

        lax.fori_loop(0, n_ctx, one, 0)
        for d in range(blocks):
            (ps if d % 2 else pk)[pair, d // 2] = prod[:, d * LANES : (d + 1) * LANES].astype(LOW)
        pair_hop(pair, 0).start()

    def pair_one(pair):
        pair_hop(pair, 0).wait_recv()
        for i in (3, 1):
            pk[pair, i] = (pk[pair, i].astype(F32) + prc[pair, i].astype(F32)).astype(LOW)
            pair_hop(pair, 1 + i // 2).start()

    def pair_two(pair):
        pair_hop(pair, 2).wait_recv()
        total = pk[pair, 2].astype(F32) + prc[pair, 2].astype(F32) + prx[pair, 1].astype(F32)
        pk[pair, 2] = total.astype(LOW)
        pair_hop(pair, 3).start()

    def pair_three(pair):
        pair_hop(pair, 1).wait_recv()
        pair_hop(pair, 3).wait_recv()
        total = pk[pair, 0].astype(F32) + prc[pair, 0].astype(F32) + prx[pair, 0].astype(F32) + pry[pair].astype(F32)
        pz[pair] = total.T.reshape(pz.shape[1:]).astype(LOW)
        qz[c, pair] = pz[pair, c]
        for k in range(1, n_ctx):
            pair_ctx(pair, k).start()

    def pair_finish(pair):
        for k in range(1, n_ctx):
            pair_ctx(pair, k).wait()
        for at in range(4):
            pair_hop(pair, at).wait_send()

    middle = n_ctx // 2
    stats(0)
    key_blocks(0, 0, middle)
    each(0, "step_two")
    each(1, "step_one")
    key_blocks(0, middle, n_ctx)
    send_home(0)
    pair_product(0)
    each(0, "step_ctx")
    stats(1)
    key_blocks(1, 0, middle)
    each(1, "step_two")
    each(2, "step_one")
    pair_one(0)
    each(0, "step_far")
    key_blocks(1, middle, n_ctx)
    send_home(1)
    each(1, "step_ctx")
    pair_product(1)
    pair_two(0)
    each(2, "step_two")
    each(3, "step_one")
    pair_one(1)
    pair_three(0)
    each(1, "step_far")
    each(2, "step_ctx")
    pair_two(1)
    each(3, "step_two")
    each(2, "step_far")
    pair_three(1)
    each(3, "step_ctx")
    each(3, "step_far")
    for pair in range(pairs):
        pair_finish(pair)
        for s in range(n_ctx):
            for t in range(3):
                at = t * model + s * width + pair * LANES
                qkv_out[:, at : at + LANES] = qz[s, pair, :, t * LANES : (t + 1) * LANES].astype(F32)
    for i in range(4):
        each(i, "finish")
    for pair in range(pairs):
        for t in range(3):
            part_own(pair, t).wait()
            for k in range(1, n_ctx):
                part_copy(pair, t, k).wait()


def back_call(n_ctx, g, q, k, v, of, lse, seg_col, seg_row, cos, sin, xn, sides):
    length, width = q.shape
    model = n_ctx * width
    tb = TOKEN_BLOCK
    pairs = width // LANES
    own_rows = model // (model // LANES) // n_ctx
    vmem = pl.BlockSpec(memory_space=pltpu.VMEM)
    anyspace = pl.BlockSpec(memory_space=pl.ANY)
    shape = jax.ShapeDtypeStruct
    dma = pltpu.SemaphoreType.DMA
    buffers = []
    for keep in sides[::2]:
        four, parts, rows, cols = keep.shape
        for lead in ((four, parts), (four, parts), (2, parts), (parts,), (3,)) * 2:
            buffers.append(pltpu.VMEM(lead + (rows, cols // 2), LOW))
    wide = 3 * LANES
    return pl.pallas_call(
        functools.partial(back_kernel, n_ctx),
        in_specs=[vmem] * 11 + [anyspace] * 8,
        out_specs=[anyspace] + [vmem] * 5,
        out_shape=[shape((tb, 3 * model), LOW), shape((own_rows, 3 * model), F32)]
        + [shape(keep.shape[2:], F32) for keep in sides[::2]],
        scratch_shapes=[
            pltpu.VMEM((pairs, length, wide), LOW),
            pltpu.VMEM((8, length), F32),
            pltpu.VMEM((8, length), F32),
            pltpu.VMEM((length, LANES), F32),
            pltpu.VMEM((tb, LANES), F32),
            pltpu.VMEM((tb, LANES), F32),
            pltpu.VMEM((wide, model), F32),
        ]
        + buffers
        + [
            pltpu.VMEM((pairs, 4, wide, LANES), LOW),
            pltpu.VMEM((pairs, 4, wide, LANES), LOW),
            pltpu.VMEM((pairs, 4, wide, LANES), LOW),
            pltpu.VMEM((pairs, 2, wide, LANES), LOW),
            pltpu.VMEM((pairs, wide, LANES), LOW),
            pltpu.VMEM((pairs, n_ctx, own_rows, wide), LOW),
            pltpu.VMEM((n_ctx, pairs, own_rows, wide), LOW),
            dma((n_ctx - 1, pairs, 3)), dma((n_ctx - 1, pairs, 3)),
            dma((pairs, 3)),
            dma((8, 8)), dma((8, 8)),
            dma((pairs, 4)), dma((pairs, 4)),
            dma((pairs, n_ctx - 1)), dma((pairs, n_ctx - 1)),
        ],
        compiler_params=params(collective_id=3, has_side_effects=True),
        cost_estimate=pl.CostEstimate(
            flops=40 * 10**9, bytes_accessed=60 * 2**20, transcendentals=2 * length * length
        ),
        name="back",
    )(g, q, k, v, of, lse, seg_col, seg_row, cos, sin, xn, *sides)


def mlp_kernel(
    blocks, n_ctx, tok_ref, att_ref, cot_ref, gain_ref, wo_in, wg_in, wu_in, wd_in, wq_ref, wr_ref,
    out_ref, gm_ref, gh_ref, gk, gc, uk, uc, ok, oc, dk, dc, wq_all, wr_all,
    wo, wg, wu, wd, att, nat, n2, mi, mit, oacc, dacc, hid_all, dg_all, du_all, stage, ostage,
    sem, hop_send, hop_recv, st_own, st_send, st_recv, o_sem, d_own, d_send, d_recv, g_send, g_recv,
):
    c, dp = lax.axis_index("ctx"), lax.axis_index("dp")
    tb, model = tok_ref.shape
    width = model // n_ctx
    ff = wu.shape[1]
    steps = ff // FF_BLOCK
    down = wd_in.shape[1]
    half = blocks // 2
    attn = [
        Gather(n_ctx, wq_ref, wq_all, hop_send.at[0], hop_recv.at[0], (NEAR, FAR)),
        Gather(n_ctx, wr_ref, wr_all, hop_send.at[1], hop_recv.at[1], (FAR, NEAR)),
    ]

    loads = []
    for d in range(blocks):
        at = pl.ds(d * LANES, LANES)
        loads.append(pltpu.make_async_copy(wo_in.at[d], wo.at[at, :], sem.at[0, d]))
    for d in range(blocks):
        at = pl.ds(d * LANES, LANES)
        rows = pl.ds(pl.multiple_of((dp ^ d) * down, 32), down)
        loads.append(pltpu.make_async_copy(wg_in.at[d], wg.at[at, :], sem.at[1, d]))
        loads.append(pltpu.make_async_copy(wu_in.at[d], wu.at[at, :], sem.at[2, d]))
        loads.append(pltpu.make_async_copy(wd_in.at[d], wd.at[rows, :], sem.at[3, d]))
    for m in loads:
        m.start()
    for d in range(blocks):
        att[:, d * LANES : (d + 1) * LANES] = att_ref[:, lane_block(dp ^ d)]
    meet(n_ctx, (CORE, NEAR, FAR))
    for w in attn:
        w.start()
    for m in loads[:blocks]:
        m.wait()
    mid = tok_ref[...].astype(F32) + dot(att[...], wo[...], 1, 0)
    inv = lax.rsqrt(jnp.mean(mid * mid, axis=-1, keepdims=True) + epsilon)
    oacc[...] = mid
    nat[...] = mid * inv
    for d in range(blocks):
        n2[:, d * LANES : (d + 1) * LANES] = nat[:, lane_block(dp ^ d)]
    mi[...] = (n2[...] * gain_ref[...]).astype(LOW)
    mit[...] = mi[...].T
    dacc[...] = jnp.zeros_like(dacc)
    for m in loads[blocks:]:
        m.wait()

    def columns(u):
        return pl.ds(pl.multiple_of(u * FF_BLOCK, FF_BLOCK), FF_BLOCK)

    def data_step(u, carry):
        cols = columns(u)
        x = mi[...]
        cot = cot_ref[...]
        wgu, wuu, wdu = wg[:, cols], wu[:, cols], wd[cols, :]
        gate = dot(x, wgu, 1, 0)
        up = dot(x, wuu, 1, 0)
        grad_hidden = dot(cot, wdu, 1, 1)
        sig = jax.nn.sigmoid(gate)
        hidden = (gate * sig * up).astype(LOW)
        dg = (grad_hidden * up * sig * (1.0 + gate * (1.0 - sig))).astype(LOW)
        du = (grad_hidden * gate * sig).astype(LOW)
        hid_all[:, cols] = hidden
        dg_all[:, cols] = dg
        du_all[:, cols] = du
        oacc[...] += dot(hidden, wdu, 1, 0)
        dacc[...] += dot(dg, wgu, 1, 1) + dot(du, wuu, 1, 1)
        return carry

    lax.fori_loop(0, 3, data_step, 0)
    for w in attn:
        w.relay()
    lax.fori_loop(3, 6, data_step, 0)
    for w in attn:
        w.spread()
    lax.fori_loop(6, steps, data_step, 0)

    out_ref[...] = oacc[...].astype(LOW)
    scaled = dacc[...] * gain_ref[...]
    norm = n2[...]
    mean = jnp.mean(scaled * norm, axis=-1, keepdims=True)
    n2[...] = inv * (scaled - norm * mean)
    for d in range(blocks):
        nat[:, lane_block(dp ^ d)] = n2[:, d * LANES : (d + 1) * LANES]
    gm = cot_ref[...].astype(F32) + nat[...]
    gm_ref[...] = gm
    gb = gm.astype(LOW)
    n2[...] = dot(gb, wo[...], 1, 1)
    for d in range(blocks):
        mi[:, lane_block(dp ^ d)] = n2[:, d * LANES : (d + 1) * LANES].astype(LOW)

    def grad_copy(k):
        to = lax.rem(c + k, n_ctx)
        return ctx_copy(mi.at[:, rows_of(to, width)], gh_ref.at[rows_of(c, tb), :], g_send.at[k - 1], g_recv.at[k - 1], to)

    grad_own = pltpu.make_async_copy(mi.at[:, rows_of(c, width)], gh_ref.at[rows_of(c, tb), :], o_sem.at[2])
    for k in range(1, n_ctx):
        grad_copy(k).start()
    grad_own.start()
    for w in attn:
        w.forward()

    def down_step(u, carry):
        cols = columns(u)
        wd[cols, :] = dot(hid_all[:, cols], cot_ref[...], 0, 0).astype(LOW)
        return carry

    lax.fori_loop(0, steps, down_step, 0)

    def down_copy(d):
        rows = pl.ds(pl.multiple_of((dp ^ d) * down, 32), down)
        if d % 2:
            return dp_copy(wd.at[rows, :], dc.at[d // 2], d_send.at[d // 2], d_recv.at[d // 2], CORE)
        return pltpu.make_async_copy(wd.at[rows, :], dk.at[d // 2], d_own.at[d // 2])

    for d in range(blocks):
        down_copy(d).start()

    dwo = dot(att[...], gb, 0, 0).astype(LOW)
    for d in range(blocks):
        ostage[d % 2, d // 2] = dwo[d * LANES : (d + 1) * LANES]
    out_own = pltpu.make_async_copy(ostage.at[0], ok, o_sem.at[0])
    out_gone = dp_copy(ostage.at[1], oc, o_sem.at[1], o_sem.at[3], CORE)
    out_own.start()
    out_gone.start()

    def side(u, t, which):
        slot = lax.rem(u, 2)
        cols = columns(u)
        keep, came = ((gk, gc), (uk, uc))[t]
        if which == 0:
            return pltpu.make_async_copy(stage.at[slot, t, 0], keep.at[:, :, cols], st_own.at[slot, t])
        return dp_copy(stage.at[slot, t, 1], came.at[:, :, cols], st_send.at[slot, t], st_recv.at[t, u], CORE)

    def weight_step(u, carry):
        cols = columns(u)

        @pl.when(u >= 2)
        def _():
            for t in range(2):
                side(u - 2, t, 0).wait()
                side(u - 2, t, 1).wait_send()

        slot = lax.rem(u, 2)
        for t, grad in enumerate((dg_all, du_all)):
            dw = dot(mit[...], grad[:, cols], 1, 0).astype(LOW)
            for d in range(blocks):
                stage[slot, t, d % 2, d // 2] = dw[d * LANES : (d + 1) * LANES]
            side(u, t, 0).start()
            side(u, t, 1).start()
        return carry

    lax.fori_loop(0, 5, weight_step, 0)
    for w in attn:
        w.cross()
    lax.fori_loop(5, steps, weight_step, 0)

    for u in (steps - 2, steps - 1):
        for t in range(2):
            side(u, t, 0).wait()
            side(u, t, 1).wait_send()

    def arrived(u, carry):
        for t in range(2):
            side(u, t, 1).wait_recv()
        return carry

    lax.fori_loop(0, steps, arrived, 0)
    out_own.wait()
    out_gone.wait()
    for d in range(blocks):
        down_copy(d).wait()
    grad_own.wait()
    for k in range(1, n_ctx):
        grad_copy(k).wait()
    for w in attn:
        w.finish()


def mlp_call(n_ctx, tok, att, cot, gain, wo, wg, wu, wd, wq, wr):
    tb, model = tok.shape
    blocks, _, ff = wg.shape
    half = blocks // 2
    down = wd.shape[1]
    width = model // n_ctx
    vmem = pl.BlockSpec(memory_space=pltpu.VMEM)
    anyspace = pl.BlockSpec(memory_space=pl.ANY)
    shape = jax.ShapeDtypeStruct
    dma = pltpu.SemaphoreType.DMA
    return pl.pallas_call(
        functools.partial(mlp_kernel, blocks, n_ctx),
        in_specs=[vmem] * 4 + [anyspace] * 6,
        out_specs=[vmem] * 2 + [anyspace] * 11,
        out_shape=[shape((tb, model), LOW), shape((tb, model), F32), shape((n_ctx * tb, width), LOW)]
        + [shape((half, LANES, ff), LOW)] * 4
        + [shape((half, LANES, model), LOW)] * 2
        + [shape((half, down, model), LOW)] * 2
        + [shape((blocks, n_ctx * w.shape[0], w.shape[1]), LOW) for w in (wq, wr)],
        scratch_shapes=[
            pltpu.VMEM((model, model), LOW),
            pltpu.VMEM((model, ff), LOW),
            pltpu.VMEM((model, ff), LOW),
            pltpu.VMEM((ff, model), LOW),
            pltpu.VMEM((tb, model), LOW),
            pltpu.VMEM((tb, model), F32),
            pltpu.VMEM((tb, model), F32),
            pltpu.VMEM((tb, model), LOW),
            pltpu.VMEM((model, tb), LOW),
            pltpu.VMEM((tb, model), F32),
            pltpu.VMEM((tb, model), F32),
            pltpu.VMEM((tb, ff), LOW),
            pltpu.VMEM((tb, ff), LOW),
            pltpu.VMEM((tb, ff), LOW),
            pltpu.VMEM((2, 2, 2, half, LANES, FF_BLOCK), LOW),
            pltpu.VMEM((2, half, LANES, model), LOW),
            dma((4, blocks)),
            dma((2, 11)), dma((2, 11)),
            dma((2, 2)), dma((2, 2)), dma((2, ff // FF_BLOCK)),
            dma((4,)),
            dma((half,)), dma((half,)), dma((half,)),
            dma((n_ctx - 1,)), dma((n_ctx - 1,)),
        ],
        compiler_params=params(collective_id=2, has_side_effects=True),
        cost_estimate=pl.CostEstimate(
            flops=2 * tb * model * (8 * ff + 3 * model), bytes_accessed=50 * 2**20, transcendentals=0
        ),
        name="mlp",
    )(tok, att, cot, gain, wo, wg, wu, wd, wq, wr)


def input_kernel(
    blocks, tok_ref, gm_ref, v1_ref, gain_ref, g, own_gain, qkv_ref, gate_ref, up_ref, out_ref, down_ref,
    wq_ref, wr_ref, wgate_ref, wup_ref, wq_all, wr_all,
    ig_ref, vg_ref, gq_ref, gk_ref, gv_ref, go_ref, gg_ref, gu_ref, gd_ref, gains_ref, w, rel, nat, sem,
):
    dp = lax.axis_index("dp")
    model = tok_ref.shape[1]
    cut = wq_ref.shape[1]
    made = []
    for d in range(blocks):
        at = pl.ds(d * LANES, LANES)
        made.append(pltpu.make_async_copy(wq_all.at[d], w.at[at, pl.ds(0, cut)], sem.at[0, d]))
        made.append(pltpu.make_async_copy(wr_all.at[d], w.at[at, pl.ds(cut, 3 * model - cut)], sem.at[1, d]))
    for m in made:
        m.start()
    for d in range(blocks):
        rel[:, d * LANES : (d + 1) * LANES] = tok_ref[:, lane_block(dp ^ d)].astype(F32)
    gv = g[:, 2 * model :].astype(F32)
    vg_ref[...] = v1_ref[...] + 0.5 * gv

    def row_dot(a, b):
        return jnp.sum(a * b.astype(F32), axis=1, keepdims=True)

    gq_ref[...] = qkv_ref[:, :model]
    gk_ref[...] = qkv_ref[:, model : 2 * model]
    gv_ref[...] = 0.5 * qkv_ref[:, 2 * model :]
    go_ref[...] = out_ref[...]
    gg_ref[...] = gate_ref[...]
    gu_ref[...] = up_ref[...]
    gd_ref[...] = down_ref[...]
    both = 2 * model - cut
    one = row_dot(qkv_ref[:, :cut], wq_ref[...]) + row_dot(qkv_ref[:, cut : 2 * model], wr_ref[:, :both])
    one = one + row_dot(gv_ref[...], wr_ref[:, both:])
    two = row_dot(gate_ref[...], wgate_ref[...]) + row_dot(up_ref[...], wup_ref[...])
    lane = lax.broadcasted_iota(jnp.int32, gains_ref.shape, 1)
    gains_ref[...] = jnp.where(lane == 0, one, two) / own_gain[...]

    x = rel[...]
    inv = lax.rsqrt(jnp.mean(x * x, axis=-1, keepdims=True) + epsilon)
    norm = x * inv
    for m in made:
        m.wait()
    grad = dot(g[:, : 2 * model], w[:, : 2 * model], 1, 1)
    grad = grad + 0.5 * dot(g[:, 2 * model :], w[:, 2 * model :], 1, 1)
    scaled = grad * gain_ref[...]
    mean = jnp.mean(scaled * norm, axis=-1, keepdims=True)
    rel[...] = inv * (scaled - norm * mean)
    for d in range(blocks):
        nat[:, lane_block(dp ^ d)] = rel[:, d * LANES : (d + 1) * LANES]
    ig_ref[...] = gm_ref[...] + nat[...]


def input_call(tok, gm, v1, gain, g, own_gain, qkv, grads, wq, wr, wgate, wup, wq_all, wr_all):
    tb, model = tok.shape
    blocks = wq_all.shape[0]
    rows = qkv.shape[0]
    vmem = pl.BlockSpec(memory_space=pltpu.VMEM)
    shape = jax.ShapeDtypeStruct
    return pl.pallas_call(
        functools.partial(input_kernel, blocks),
        in_specs=[vmem] * 15 + [pl.BlockSpec(memory_space=pl.ANY)] * 2,
        out_specs=[vmem] * 10,
        out_shape=[shape((tb, model), F32)] * 2
        + [shape((rows, model), F32)] * 4
        + [shape(x.shape, F32) for x in (grads[0], grads[1], grads[3])]
        + [shape((rows, LANES), F32)],
        scratch_shapes=[
            pltpu.VMEM((model, 3 * model), LOW),
            pltpu.VMEM((tb, model), F32),
            pltpu.VMEM((tb, model), F32),
            pltpu.SemaphoreType.DMA((2, blocks)),
        ],
        compiler_params=params(),
        cost_estimate=pl.CostEstimate(
            flops=2 * tb * model * 3 * model, bytes_accessed=20 * 2**20, transcendentals=0
        ),
        name="input_grad",
    )(tok, gm, v1, gain, g, own_gain, qkv, *grads, wq, wr, wgate, wup, wq_all, wr_all)


def fast_local(
    n_dp, n_ctx, tokens, first_values, v1_accum, segment_ids, positions, cotangent,
    attn_gain, w_query, w_key, w_value, w_out, mlp_gain, w_gate, w_up, w_down,
):
    seq, model = tokens.shape[1:]
    width = model // n_ctx
    own_rows = w_query.shape[0]
    tok = tokens[0]
    mark = jnp.concatenate([segment_ids, positions, jnp.zeros((6, seq), jnp.int32)], axis=0)
    gains = jnp.stack([attn_gain, mlp_gain], axis=1)
    gains = jnp.tile(jnp.pad(gains, ((0, 0), (0, width - 2))), (1, n_ctx))
    pack = jnp.concatenate([w_query, w_key, w_value, gains], axis=0)
    pack = pack.reshape(4 * own_rows, n_ctx, width).transpose(1, 0, 2)
    freqs = 10000.0 ** (-jnp.arange(HEAD_DIM // 2).astype(F32) * (2.0 / HEAD_DIM))
    turn = jnp.ones((HEAD_DIM // 2,), F32)
    freq = jnp.stack([jnp.tile(freqs, 4), jnp.tile(jnp.concatenate([-turn, turn]), 2)])
    freq = jnp.pad(freq, ((0, 6), (0, 0)))
    (xn, q, k, v, out_full, log_total, cos, sin, seg_col, seg_row, gain_rows, attended,
     gate_all, up_all, out_all, down_all) = front_call(
        n_dp, n_ctx, tok, first_values[0], mark, pack, freq, w_gate, w_up, w_out, w_down
    )
    cut = model // 2
    wq = jnp.concatenate([w_query, w_key[:, :cut]], axis=1)
    wr = jnp.concatenate([w_key[:, cut:], w_value], axis=1)
    (output, grad_middle, head_grad, gate_keep, gate_came, up_keep, up_came, out_keep, out_came,
     down_keep, down_came, wq_all, wr_all) = mlp_call(
        n_ctx, tok, attended, cotangent[0], gain_rows[1:2], out_all, gate_all, up_all, down_all, wq, wr
    )
    sides = [
        x.reshape(x.shape[0], n_ctx, x.shape[1] // n_ctx, x.shape[2])
        for x in (gate_keep, gate_came, up_keep, up_came, out_keep, out_came, down_keep, down_came)
    ]
    home_grad, qkv_grad, *grads = back_call(
        n_ctx, head_grad, q, k, v, out_full, log_total, seg_col, seg_row, cos, sin, xn, sides
    )
    own_gain = jnp.stack([attn_gain.astype(F32)] + [mlp_gain.astype(F32)] * (LANES - 1), axis=1)
    (input_grad, v1_grad, query_grad, key_grad, value_grad, out_grad, gate_grad, up_grad, down_grad,
     gain_grads) = input_call(
        tok, grad_middle, v1_accum[0], gain_rows[0:1], home_grad, own_gain, qkv_grad, grads,
        wq, wr, w_gate, w_up, wq_all, wr_all
    )
    return (
        output[None], input_grad[None], v1_grad[None], gain_grads[:, 0], query_grad, key_grad, value_grad,
        out_grad, gain_grads[:, 1], gate_grad, up_grad, down_grad,
    )


def solution(mesh):
    placed = (
        P("dp", "ctx", None),
        P("dp", "ctx", None),
        P("dp", "ctx", None),
        P("dp", "ctx"),
        P("dp", "ctx"),
        P("dp", "ctx", None),
        P(("dp", "ctx")),
        P(("dp", "ctx"), None),
        P(("dp", "ctx"), None),
        P(("dp", "ctx"), None),
        P(("dp", "ctx"), None),
        P(("dp", "ctx")),
        P(("dp", "ctx"), None),
        P(("dp", "ctx"), None),
        P(("dp", "ctx"), None),
    )
    n_dp, n_ctx = mesh.shape["dp"], mesh.shape["ctx"]

    def local(*args):
        rows, seq, model = args[0].shape
        fits = (
            rows == 1
            and seq == TOKEN_BLOCK
            and model == n_dp * LANES
            and n_ctx == 4
            and model == 2 * LANES * n_ctx
            and args[12].shape[1] % FF_BLOCK == 0
        )
        return fast_local(n_dp, n_ctx, *args) if fits else plain_local(*args)

    return jax.shard_map(
        local,
        mesh=mesh,
        in_specs=placed,
        out_specs=(
            P("dp", "ctx", None),
            P("dp", "ctx", None),
            P("dp", "ctx", None),
            P(("dp", "ctx")),
            P(("dp", "ctx"), None),
            P(("dp", "ctx"), None),
            P(("dp", "ctx"), None),
            P(("dp", "ctx"), None),
            P(("dp", "ctx")),
            P(("dp", "ctx"), None),
            P(("dp", "ctx"), None),
            P(("dp", "ctx"), None),
        ),
        check_vma=False,
    )
```

```python
import functools

import jax
import jax.numpy as jnp
import numpy as np
from jax import lax
from jax.experimental import pallas as pl
from jax.experimental.pallas import tpu as pltpu
from jax.sharding import PartitionSpec as P

HEADS = 16
HEAD_DIM = 64
LANES = 128
TOKEN_BLOCK = 512
FF_BLOCK = 256
NEG = -1e30
MESH = pl.DeviceIdType.MESH
F32 = jnp.float32
LOW = jnp.bfloat16
BYTES = 63 * 2**20
epsilon = 1e-05


HEAD_BLOCK = 4


def rms_scale(values):
    return lax.rsqrt(jnp.mean(values * values, axis=-1, keepdims=True) + epsilon)


def angle_tables(position_rows):
    freqs = 10000.0 ** (-jnp.arange(HEAD_DIM // 2).astype(jnp.float32) * (2.0 / HEAD_DIM))
    angles = position_rows.astype(jnp.float32)[..., None] * freqs
    return (jnp.cos(angles)[..., None, :], jnp.sin(angles)[..., None, :])


def rotate(heads_in, cosine_table, sine_table):
    half_dim = heads_in.shape[-1] // 2
    first_half = heads_in[..., :half_dim]
    second_half = heads_in[..., half_dim:]
    return jnp.concatenate(
        [
            first_half * cosine_table - second_half * sine_table,
            second_half * cosine_table + first_half * sine_table,
        ],
        axis=-1,
    )


def norm_back(grad_normed, normed, inv_root, norm_gain):
    grad_scaled = grad_normed * norm_gain.astype(jnp.float32)
    grad_input = inv_root * (
        grad_scaled - normed * jnp.mean(grad_scaled * normed, axis=-1, keepdims=True)
    )
    return (grad_input, jnp.sum(grad_normed * normed, axis=0))


def attn_front(flat_tokens, first_flat, attn_set, cosine_table, sine_table, row_count, seq_piece):
    inv_root = rms_scale(flat_tokens)
    normed = flat_tokens * inv_root
    normed_in = (normed * attn_set[0].astype(jnp.float32)).astype(jnp.bfloat16)
    query_proj = jnp.dot(normed_in, attn_set[1], preferred_element_type=jnp.float32)
    key_proj = jnp.dot(normed_in, attn_set[2], preferred_element_type=jnp.float32)
    value_proj = jnp.dot(normed_in, attn_set[3], preferred_element_type=jnp.float32)
    query_rot = rotate(
        query_proj.reshape(row_count, seq_piece, HEADS, HEAD_DIM), cosine_table, sine_table
    )
    key_rot = rotate(
        key_proj.reshape(row_count, seq_piece, HEADS, HEAD_DIM), cosine_table, sine_table
    )
    query_rot = query_rot.astype(jnp.bfloat16).reshape(row_count, seq_piece, -1)
    key_rot = key_rot.astype(jnp.bfloat16).reshape(row_count, seq_piece, -1)
    value_mix = (
        (0.5 * value_proj + 0.5 * first_flat).astype(jnp.bfloat16).reshape(row_count, seq_piece, -1)
    )
    return (normed, inv_root, normed_in, query_rot, key_rot, value_mix)


def mlp_block(flat_tokens, attended_low, out_weight, mlp_set):
    middle = flat_tokens + jnp.dot(attended_low, out_weight, preferred_element_type=jnp.float32)
    inv_root_two = rms_scale(middle)
    normed_two = middle * inv_root_two
    mlp_in = (normed_two * mlp_set[0].astype(jnp.float32)).astype(jnp.bfloat16)
    gate_proj = jnp.dot(mlp_in, mlp_set[1], preferred_element_type=jnp.float32)
    up_proj = jnp.dot(mlp_in, mlp_set[2], preferred_element_type=jnp.float32)
    hidden = (gate_proj * jax.nn.sigmoid(gate_proj) * up_proj).astype(jnp.bfloat16)
    result = middle + jnp.dot(hidden, mlp_set[3], preferred_element_type=jnp.float32)
    return (normed_two, inv_root_two, mlp_in, gate_proj, up_proj, hidden, result)


def split_groups(row_block):
    tok_count = row_block.shape[0]
    return row_block.reshape(tok_count, HEADS // HEAD_BLOCK, HEAD_BLOCK * HEAD_DIM).transpose(
        1, 0, 2
    )


def join_groups(group_block):
    return group_block.transpose(1, 0, 2).reshape(group_block.shape[1], -1)


def as_heads(block):
    return block.reshape(block.shape[0], HEAD_BLOCK, HEAD_DIM)


def attend_row(members):
    query_row, key_row, value_row, allowed = members

    def per_group(pieces):
        query_block, key_block, value_block = pieces
        scores = (
            jnp.einsum(
                "qhd,khd->hqk",
                as_heads(query_block),
                as_heads(key_block),
                preferred_element_type=jnp.float32,
            )
            * 0.125
        )
        scores = jnp.where(allowed[None], scores, -1e30)
        highest = jnp.max(scores, axis=-1, keepdims=True)
        exp_scores = jnp.exp(scores - highest)
        denominator = jnp.sum(exp_scores, axis=-1, keepdims=True)
        soft_low = (exp_scores / denominator).astype(jnp.bfloat16)
        attended = jnp.einsum(
            "hqk,khd->qhd", soft_low, as_heads(value_block), preferred_element_type=jnp.float32
        )
        return (
            attended.reshape(query_block.shape[0], -1),
            (highest + jnp.log(denominator))[..., 0],
        )

    attended, log_total = lax.map(
        per_group, (split_groups(query_row), split_groups(key_row), split_groups(value_row))
    )
    return (join_groups(attended), log_total)


def attend_back(members):
    query_row, key_row, value_row, grad_row, log_total, allowed = members

    def per_group(pieces):
        query_block, key_block, value_block, grad_block, log_block = pieces
        query_heads = as_heads(query_block)
        key_heads = as_heads(key_block)
        grad_heads = as_heads(grad_block)
        scores = (
            jnp.einsum("qhd,khd->hqk", query_heads, key_heads, preferred_element_type=jnp.float32)
            * 0.125
        )
        soft_weights = jnp.where(allowed[None], jnp.exp(scores - log_block[..., None]), 0.0)
        soft_low = soft_weights.astype(jnp.bfloat16)
        grad_probs = jnp.einsum(
            "qhd,khd->hqk", grad_heads, as_heads(value_block), preferred_element_type=jnp.float32
        )
        row_delta = jnp.sum(soft_weights * grad_probs, axis=-1, keepdims=True)
        grad_scores = (soft_weights * (grad_probs - row_delta)).astype(jnp.bfloat16)
        grad_query = (
            jnp.einsum("hqk,khd->qhd", grad_scores, key_heads, preferred_element_type=jnp.float32)
            * 0.125
        )
        grad_key = (
            jnp.einsum("hqk,qhd->khd", grad_scores, query_heads, preferred_element_type=jnp.float32)
            * 0.125
        )
        grad_value = jnp.einsum(
            "hqk,qhd->khd", soft_low, grad_heads, preferred_element_type=jnp.float32
        )
        return (
            grad_query.reshape(query_block.shape[0], -1),
            grad_key.reshape(key_block.shape[0], -1),
            grad_value.reshape(key_block.shape[0], -1),
        )

    grad_query, grad_key, grad_value = lax.map(
        per_group,
        (
            split_groups(query_row),
            split_groups(key_row),
            split_groups(value_row),
            split_groups(grad_row),
            log_total,
        ),
    )
    return (join_groups(grad_query), join_groups(grad_key), join_groups(grad_value))


def plain_local(
    tokens,
    first_values,
    v1_accum,
    segment_ids,
    positions,
    cotangent,
    attn_gain,
    w_query,
    w_key,
    w_value,
    w_out,
    mlp_gain,
    w_gate,
    w_up,
    w_down,
):
    row_count, seq_piece, model_width = tokens.shape
    token_count = row_count * seq_piece
    flat_tokens = tokens.astype(jnp.float32).reshape(token_count, model_width)
    first_flat = first_values.astype(jnp.float32).reshape(token_count, model_width)
    cosine_table, sine_table = angle_tables(positions)
    segment_low = segment_ids.astype(jnp.bfloat16)
    attn_set = (
        lax.all_gather(attn_gain, ("dp", "ctx"), axis=0, tiled=True),
        lax.all_gather(w_query, ("dp", "ctx"), axis=0, tiled=True),
        lax.all_gather(w_key, ("dp", "ctx"), axis=0, tiled=True),
        lax.all_gather(w_value, ("dp", "ctx"), axis=0, tiled=True),
        lax.all_gather(w_out, ("dp", "ctx"), axis=0, tiled=True),
    )
    normed, inv_root, normed_in, query_rot, key_rot, value_mix = attn_front(
        flat_tokens, first_flat, attn_set, cosine_table, sine_table, row_count, seq_piece
    )
    key_full, value_full, segment_full = (
        lax.all_gather(key_rot, "ctx", axis=1, tiled=True),
        lax.all_gather(value_mix, "ctx", axis=1, tiled=True),
        lax.all_gather(segment_low, "ctx", axis=1, tiled=True),
    )
    query_order = lax.axis_index("ctx") * seq_piece + jnp.arange(seq_piece, dtype=jnp.int32)
    full_order = jnp.arange(key_full.shape[1], dtype=jnp.int32)
    segment_own = segment_ids.astype(jnp.float32)
    segment_all = segment_full.astype(jnp.float32)
    allowed = (segment_own[:, :, None] == segment_all[:, None, :]) & (
        query_order[None, :, None] >= full_order[None, None, :]
    )
    attended, log_total = lax.map(attend_row, (query_rot, key_full, value_full, allowed))
    attended_low = attended.reshape(token_count, model_width).astype(jnp.bfloat16)
    mlp_set = (
        lax.all_gather(mlp_gain, ("dp", "ctx"), axis=0, tiled=True),
        lax.all_gather(w_gate, ("dp", "ctx"), axis=0, tiled=True),
        lax.all_gather(w_up, ("dp", "ctx"), axis=0, tiled=True),
        lax.all_gather(w_down, ("dp", "ctx"), axis=0, tiled=True),
    )
    normed_two, inv_root_two, mlp_in, gate_proj, up_proj, hidden, output_flat = mlp_block(
        flat_tokens, attended_low, attn_set[4], mlp_set
    )
    output = output_flat.reshape(tokens.shape).astype(jnp.bfloat16)
    attn_set = (
        lax.all_gather(attn_gain, ("dp", "ctx"), axis=0, tiled=True),
        lax.all_gather(w_query, ("dp", "ctx"), axis=0, tiled=True),
        lax.all_gather(w_key, ("dp", "ctx"), axis=0, tiled=True),
        lax.all_gather(w_value, ("dp", "ctx"), axis=0, tiled=True),
        lax.all_gather(w_out, ("dp", "ctx"), axis=0, tiled=True),
    )
    mlp_set = (
        lax.all_gather(mlp_gain, ("dp", "ctx"), axis=0, tiled=True),
        lax.all_gather(w_gate, ("dp", "ctx"), axis=0, tiled=True),
        lax.all_gather(w_up, ("dp", "ctx"), axis=0, tiled=True),
        lax.all_gather(w_down, ("dp", "ctx"), axis=0, tiled=True),
    )
    normed, inv_root, normed_in, query_rot, key_rot, value_mix = attn_front(
        flat_tokens, first_flat, attn_set, cosine_table, sine_table, row_count, seq_piece
    )
    key_full, value_full = (
        lax.all_gather(key_rot, "ctx", axis=1, tiled=True),
        lax.all_gather(value_mix, "ctx", axis=1, tiled=True),
    )
    normed_two, inv_root_two, mlp_in, gate_proj, up_proj, hidden, output_flat = mlp_block(
        flat_tokens, attended_low, attn_set[4], mlp_set
    )
    cot_low = cotangent.reshape(token_count, model_width)
    cot_float = cot_low.astype(jnp.float32)
    grad_hidden = jnp.einsum("td,fd->tf", cot_low, mlp_set[3], preferred_element_type=jnp.float32)
    sigma = jax.nn.sigmoid(gate_proj)
    grad_gate_low = (grad_hidden * up_proj * sigma * (1.0 + gate_proj * (1.0 - sigma))).astype(
        jnp.bfloat16
    )
    grad_up_low = (grad_hidden * gate_proj * sigma).astype(jnp.bfloat16)
    grad_mlp_in = jnp.einsum(
        "tf,df->td", grad_gate_low, mlp_set[1], preferred_element_type=jnp.float32
    )
    grad_mlp_in = grad_mlp_in + jnp.einsum(
        "tf,df->td", grad_up_low, mlp_set[2], preferred_element_type=jnp.float32
    )
    grad_middle_norm, grad_gain_two = norm_back(grad_mlp_in, normed_two, inv_root_two, mlp_set[0])
    grad_middle = cot_float + grad_middle_norm
    grad_branch_low = grad_middle.astype(jnp.bfloat16)
    grad_attended = jnp.einsum(
        "te,de->td", grad_branch_low, attn_set[4], preferred_element_type=jnp.float32
    )
    grad_attended = grad_attended.astype(jnp.bfloat16).reshape(row_count, seq_piece, model_width)
    grad_query_rot, grad_key_full, grad_value_full = lax.map(
        attend_back, (query_rot, key_full, value_full, grad_attended, log_total, allowed)
    )
    grad_key_rot, grad_value_mix = (
        lax.psum_scatter(
            grad_key_full.astype(jnp.bfloat16), "ctx", scatter_dimension=1, tiled=True
        ).astype(jnp.float32),
        lax.psum_scatter(
            grad_value_full.astype(jnp.bfloat16), "ctx", scatter_dimension=1, tiled=True
        ).astype(jnp.float32),
    )
    v1_grad = v1_accum + 0.5 * grad_value_mix
    grad_query_low = rotate(
        grad_query_rot.reshape(row_count, seq_piece, HEADS, HEAD_DIM), cosine_table, -sine_table
    )
    grad_query_low = grad_query_low.astype(jnp.bfloat16).reshape(token_count, model_width)
    grad_key_low = rotate(
        grad_key_rot.reshape(row_count, seq_piece, HEADS, HEAD_DIM), cosine_table, -sine_table
    )
    grad_key_low = grad_key_low.astype(jnp.bfloat16).reshape(token_count, model_width)
    grad_value_low = (0.5 * grad_value_mix).astype(jnp.bfloat16).reshape(token_count, model_width)
    grad_normed_in = jnp.einsum(
        "te,de->td", grad_query_low, attn_set[1], preferred_element_type=jnp.float32
    )
    grad_normed_in = grad_normed_in + jnp.einsum(
        "te,de->td", grad_key_low, attn_set[2], preferred_element_type=jnp.float32
    )
    grad_normed_in = grad_normed_in + jnp.einsum(
        "te,de->td", grad_value_low, attn_set[3], preferred_element_type=jnp.float32
    )
    grad_input_norm, grad_gain_one = norm_back(grad_normed_in, normed, inv_root, attn_set[0])
    input_grad = (grad_middle + grad_input_norm).reshape(tokens.shape)
    attn_right = jnp.concatenate([grad_query_low, grad_key_low, grad_value_low], axis=1)
    left_in = normed_in
    projections = jnp.einsum("td,te->de", left_in, attn_right, preferred_element_type=jnp.float32)
    out_part = jnp.einsum(
        "td,te->de", attended_low, grad_branch_low, preferred_element_type=jnp.float32
    )
    attn_matrix = lax.psum_scatter(
        jnp.concatenate([projections, out_part], axis=1),
        ("dp", "ctx"),
        scatter_dimension=0,
        tiled=True,
    )
    mlp_right = jnp.concatenate([grad_gate_low, grad_up_low], axis=1)
    left_in = mlp_in
    gate_up_matrix = lax.psum_scatter(
        jnp.einsum("td,tf->df", left_in, mlp_right, preferred_element_type=jnp.float32),
        ("dp", "ctx"),
        scatter_dimension=0,
        tiled=True,
    )
    down_matrix = lax.psum_scatter(
        jnp.einsum("tf,td->fd", hidden, cot_low, preferred_element_type=jnp.float32),
        ("dp", "ctx"),
        scatter_dimension=0,
        tiled=True,
    )
    gain_one, gain_two = (
        lax.psum_scatter(grad_gain_one, ("dp", "ctx"), scatter_dimension=0, tiled=True),
        lax.psum_scatter(grad_gain_two, ("dp", "ctx"), scatter_dimension=0, tiled=True),
    )
    ff_width = w_gate.shape[1]
    return (
        output,
        input_grad,
        v1_grad,
        gain_one,
        attn_matrix[:, 0:model_width],
        attn_matrix[:, model_width : 2 * model_width],
        attn_matrix[:, 2 * model_width : 3 * model_width],
        attn_matrix[:, 3 * model_width : 4 * model_width],
        gain_two,
        gate_up_matrix[:, 0:ff_width],
        gate_up_matrix[:, ff_width : 2 * ff_width],
        down_matrix,
    )


def params(**kw):
    return pltpu.CompilerParams(vmem_limit_bytes=BYTES, **kw)


def dot(a, b, da, db):
    return lax.dot_general(a, b, (((da,), (db,)), ((), ())), preferred_element_type=F32)


def lane_block(index):
    return pl.ds(pl.multiple_of(index * LANES, LANES), LANES)


def half_swap(x):
    lane = lax.broadcasted_iota(jnp.int32, x.shape, 1)
    left = pltpu.roll(x, LANES - HEAD_DIM // 2, 1)
    right = pltpu.roll(x, HEAD_DIM // 2, 1)
    return jnp.where(lane % HEAD_DIM < HEAD_DIM // 2, left, right)


def head_lanes(x, head):
    lane = lax.broadcasted_iota(jnp.int32, x.shape, 1)
    return jnp.where(lane // HEAD_DIM == head, x, jnp.zeros_like(x))


def meet(n_ctx, bits):
    c, dp = lax.axis_index("ctx"), lax.axis_index("dp")
    barrier = pltpu.get_barrier_semaphore()
    for k in range(1, n_ctx):
        pl.semaphore_signal(barrier, inc=1, device_id={"ctx": lax.rem(c + k, n_ctx)}, device_id_type=MESH)
    for bit in bits:
        pl.semaphore_signal(barrier, inc=1, device_id={"dp": dp ^ bit}, device_id_type=MESH)
    pl.semaphore_wait(barrier, n_ctx - 1 + len(bits))


def ctx_copy(src, dst, send, recv, to):
    return pltpu.make_async_remote_copy(
        src_ref=src, dst_ref=dst, send_sem=send, recv_sem=recv, device_id={"ctx": to}, device_id_type=MESH
    )


def dp_copy(src, dst, send, recv, bit):
    to = lax.axis_index("dp") ^ bit
    return pltpu.make_async_remote_copy(
        src_ref=src, dst_ref=dst, send_sem=send, recv_sem=recv, device_id={"dp": to}, device_id_type=MESH
    )


def rows_of(index, size):
    return pl.ds(pl.multiple_of(index * size, size), size)


CORE, NEAR, FAR = 1, 2, 4


class Gather:
    def __init__(self, n_ctx, src, dst, send, recv, order):
        self.n, self.src, self.dst, self.send, self.recv = n_ctx, src, dst, send, recv
        self.first, self.second = order
        self.rows = src.shape[0]

    def place(self, c):
        return self.dst.at[0, pl.ds(c * self.rows, self.rows), :]

    def along(self, bit):
        c = lax.axis_index("ctx")
        return ctx_copy(self.src, self.place(c), self.send.at[bit - 1], self.recv.at[bit - 1], c ^ bit)

    def pass_on(self):
        c = lax.axis_index("ctx")
        return ctx_copy(self.place(c ^ 2), self.place(c ^ 2), self.send.at[2], self.recv.at[2], c ^ 1)

    def plane(self, slot, bit, at):
        return dp_copy(self.dst.at[slot], self.dst.at[slot ^ bit], self.send.at[at], self.recv.at[at], bit)

    def own(self):
        c = lax.axis_index("ctx")
        return pltpu.make_async_copy(self.src, self.dst.at[0, pl.ds(c * self.rows, self.rows), :], self.send.at[10])

    def hop(self, at):
        one, two = self.first, self.second
        slot, bit = [(0, one), (0, two), (one, two), (0, CORE), (one, CORE), (two, CORE), (one | two, CORE)][at]
        return self.plane(slot, bit, 3 + at)

    def start(self):
        self.own().start()
        self.along(2).start()
        self.along(1).start()

    def relay(self):
        self.along(2).wait_recv()
        self.pass_on().start()

    def spread(self):
        self.own().wait()
        self.along(1).wait_recv()
        self.pass_on().wait_recv()
        for at in (0, 1, 3):
            self.hop(at).start()

    def forward(self):
        self.hop(0).wait_recv()
        self.hop(2).start()
        self.hop(4).start()

    def cross(self):
        self.hop(1).wait_recv()
        self.hop(5).start()
        self.hop(2).wait_recv()
        self.hop(6).start()

    def finish(self):
        self.along(1).wait_send()
        self.along(2).wait_send()
        self.pass_on().wait_send()
        for at in range(7):
            self.hop(at).wait_send()
        for at in range(3, 7):
            self.hop(at).wait_recv()


def front_kernel(
    n_ctx, tok_ref, fv_ref, mark_ref, pack_ref, freq_ref, wg_ref, wu_ref, wo_ref, wd_ref,
    xn_ref, q_ref, k_ref, v_ref, of_ref, lse_ref, cos_ref, sin_ref, seg_ref, marks, gain_ref,
    att_ref, wg_all, wu_all, wo_all, wd_all,
    x_all, fvs, packs, whead, rel, o_ref, s_ref, m_ref, l_ref, acc_ref, p_all, total_ref,
    mark_send, mark_recv, pack_send, pack_recv, tok_send, tok_recv, fv_send, fv_recv, w_send, w_recv,
    o_send, o_recv, own, own_o,
):
    c, dp = lax.axis_index("ctx"), lax.axis_index("dp")
    tb = m_ref.shape[0]
    half = tb // 2
    model = tok_ref.shape[1]
    blocks = model // LANES
    width = q_ref.shape[1]
    own_rows = wg_ref.shape[0]
    lane = lax.broadcasted_iota(jnp.int32, (tb, LANES), 1)
    exact = lax.Precision.HIGHEST

    weights = []
    for i, (src, dst) in enumerate(((wg_ref, wg_all), (wo_ref, wo_all), (wu_ref, wu_all), (wd_ref, wd_all))):
        wide = src.shape[1] // 2
        weights.append([])
        for h, order in enumerate(((NEAR, FAR), (FAR, NEAR))):
            cols = pl.ds(h * wide, wide)
            unit = 2 * i + h
            weights[i].append(
                Gather(n_ctx, src.at[:, cols], dst.at[:, :, cols], w_send.at[unit], w_recv.at[unit], order)
            )
    gate, out, up, down = weights

    def each(what, *arrays):
        for array in arrays:
            for half_way in array:
                getattr(half_way, what)()

    def mark_copy(k):
        at = rows_of(c, tb)
        return ctx_copy(mark_ref, marks.at[:, at], mark_send.at[k - 1], mark_recv.at[k - 1], lax.rem(c + k, n_ctx))

    def pack_copy(k):
        to = lax.rem(c + k, n_ctx)
        return ctx_copy(pack_ref.at[to], packs.at[0, c], pack_send.at[k - 1], pack_recv.at[k - 1], to)

    def pack_hop(slot, bit, at):
        return dp_copy(packs.at[slot], packs.at[slot ^ bit], pack_send.at[at], pack_recv.at[at], bit)

    def fv_copy(k):
        to = lax.rem(c + k, n_ctx)
        return ctx_copy(fv_ref.at[:, rows_of(to, width)], fvs.at[rows_of(c, tb), :], fv_send.at[k - 1], fv_recv.at[k - 1], to)

    def tok_copy(bit):
        return ctx_copy(tok_ref, x_all.at[rows_of(c, tb), :], tok_send.at[bit - 1], tok_recv.at[bit - 1], c ^ bit)

    def tok_pass():
        at = rows_of(c ^ 2, tb)
        return ctx_copy(x_all.at[at, :], x_all.at[at, :], tok_send.at[2], tok_recv.at[2], c ^ 1)

    locals_ = [
        pltpu.make_async_copy(tok_ref, x_all.at[rows_of(c, tb), :], own.at[0]),
        pltpu.make_async_copy(fv_ref.at[:, rows_of(c, width)], fvs.at[rows_of(c, tb), :], own.at[1]),
        pltpu.make_async_copy(pack_ref.at[c], packs.at[0, c], own.at[2]),
        pltpu.make_async_copy(mark_ref, marks.at[:, rows_of(c, tb)], own.at[3]),
    ]

    meet(n_ctx, (CORE, NEAR, FAR))
    for k in range(1, n_ctx):
        mark_copy(k).start()
        pack_copy(k).start()
    each("start", gate, out)
    for m in locals_:
        m.start()

    locals_[3].wait()
    for k in range(1, n_ctx):
        mark_copy(k).wait_recv()
    row8 = lax.broadcasted_iota(jnp.int32, (8, LANES), 0)
    pick_seg = jnp.where(row8 == 0, 1.0, 0.0)
    pick_pos = jnp.where(row8 == 1, 1.0, 0.0)

    def table(b, carry):
        at = rows_of(b, tb)
        m = marks[:, at].astype(F32)
        dims = (((0,), (0,)), ((), ()))
        seg_ref[at, :] = lax.dot_general(m, pick_seg, dims, precision=exact, preferred_element_type=F32)
        pos = lax.dot_general(m, pick_pos, dims, precision=exact, preferred_element_type=F32)
        angle = pos * freq_ref[0:1, :]
        cos_ref[at, :] = jnp.cos(angle)
        sin_ref[at, :] = jnp.sin(angle) * freq_ref[1:2, :]
        return carry

    locals_[2].wait()
    for k in range(1, n_ctx):
        pack_copy(k).wait_recv()
    pack_hop(0, NEAR, 3).start()
    each("relay", gate, out)
    tok_copy(2).start()
    tok_copy(1).start()
    each("start", up)
    lax.fori_loop(0, n_ctx, table, 0)
    pack_hop(0, NEAR, 3).wait_recv()
    pack_hop(0, FAR, 4).start()
    pack_hop(NEAR, FAR, 5).start()
    pack_hop(0, CORE, 6).start()
    pack_hop(NEAR, CORE, 7).start()
    each("spread", gate, out)
    pack_hop(0, FAR, 4).wait_recv()
    pack_hop(FAR, CORE, 8).start()
    pack_hop(NEAR, FAR, 5).wait_recv()
    pack_hop(NEAR | FAR, CORE, 9).start()
    for at, (slot, bit) in enumerate([(0, CORE), (NEAR, CORE), (FAR, CORE), (NEAR | FAR, CORE)]):
        pack_hop(slot, bit, 6 + at).wait_recv()
    count = packs.shape[0]
    for t in range(3):
        block = packs[:, :, t * own_rows : (t + 1) * own_rows, :]
        whead[:, t * width : (t + 1) * width] = block.reshape(model, width)
    gains = packs[:, :, 3 * own_rows : 4 * own_rows, 0:LANES].reshape(model, LANES).astype(F32)
    gain_ref[...] = gains.T[0:8, :]
    locals_[0].wait()
    locals_[1].wait()

    def project(chunk, part):
        at = pl.ds(pl.multiple_of(chunk * tb + part * half, half), half)
        for d in range(blocks):
            rel[:, d * LANES : (d + 1) * LANES] = x_all[at, lane_block(dp ^ d)].astype(F32)
        x = rel[...]
        inv = lax.rsqrt(jnp.mean(x * x, axis=-1, keepdims=True) + epsilon)
        xn = (x * inv * gain_ref[0:1, :]).astype(LOW)
        xn_ref[at, :] = xn
        proj = dot(xn, whead[...], 1, 0)
        cos, sin = cos_ref[at, :], sin_ref[at, :]
        for b in range(width // LANES):
            cols = slice(b * LANES, (b + 1) * LANES)
            qb = proj[:, b * LANES : (b + 1) * LANES]
            q_ref[at, cols] = ((qb * cos + half_swap(qb) * sin) * 0.125).astype(LOW)
            kb = proj[:, width + b * LANES : width + (b + 1) * LANES]
            k_ref[at, cols] = (kb * cos + half_swap(kb) * sin).astype(LOW)
        of_ref[at, :] = 0.5 * proj[:, 2 * width :]

    def project_chunk(bit):
        def one(part, carry):
            project(c ^ bit, part)
            return carry

        lax.fori_loop(0, 2, one, 0)

    project_chunk(0)
    each("forward", gate, out)
    tok_copy(2).wait_recv()
    tok_pass().start()
    each("relay", up)
    each("start", down)
    each("cross", gate, out)
    tok_copy(1).wait_recv()
    project_chunk(1)
    project_chunk(2)
    each("spread", up)
    each("relay", down)
    for k in range(1, n_ctx):
        fv_copy(k).start()
    tok_pass().wait_recv()
    project_chunk(3)
    each("forward", up)
    each("spread", down)

    def fold(x, op):
        r = x[:, 0:LANES]
        for b in range(1, tb // LANES):
            r = op(r, x[:, b * LANES : (b + 1) * LANES])
        return r

    def home(pair):
        return att_ref.at[:, pl.ds(pl.multiple_of(c * width + pair * LANES, LANES), LANES)]

    def weigh(pair, i):
        cols = slice(pair * LANES, (pair + 1) * LANES)
        mine = rows_of(i, tb)
        q = q_ref[mine, cols]
        seg_q = seg_ref[mine, 0:1]
        base = i * (i + 1) // 2
        for head in range(2):
            qm = head_lanes(q, head)
            m_ref[...] = jnp.full_like(m_ref, NEG)

            def score(j, causal):
                at = rows_of(j, tb)
                s = dot(qm, k_ref[at, cols], 1, 1)
                ok = seg_q == marks[0:1, at].astype(F32)
                if causal:
                    r = lax.broadcasted_iota(jnp.int32, (tb, tb), 0)
                    t = lax.broadcasted_iota(jnp.int32, (tb, tb), 1)
                    ok = ok & (r >= t)
                s = jnp.where(ok, s, NEG)
                s_ref[:, at] = s
                m_ref[...] = jnp.maximum(m_ref[...], fold(s, jnp.maximum))

            def score_step(j, carry):
                score(j, False)
                return carry

            lax.fori_loop(0, i, score_step, 0)
            score(i, True)
            top = jnp.max(m_ref[...], axis=1, keepdims=True)
            l_ref[...] = jnp.zeros_like(l_ref)

            def weight_step(j, carry):
                p = jnp.exp(s_ref[:, rows_of(j, tb)] - top)
                l_ref[...] += fold(p, jnp.add)
                p_all[2 * pair + head, base + j] = p.astype(LOW)
                return carry

            lax.fori_loop(0, i + 1, weight_step, 0)
            total = jnp.sum(l_ref[...], axis=1, keepdims=True)
            total_ref[mine, :] = jnp.where(lane == 2 * pair + head, total, total_ref[mine, :])
            lse = jnp.broadcast_to(top + jnp.log(total), (tb, LANES))
            if head == 0:
                lse_ref[mine, cols] = lse
            else:
                lse_ref[mine, cols] = jnp.where(lane < HEAD_DIM, lse_ref[mine, cols], lse)

    def mix(pair, i):
        cols = slice(pair * LANES, (pair + 1) * LANES)
        mine = rows_of(i, tb)
        base = i * (i + 1) // 2
        for head in range(2):
            acc_ref[...] = jnp.zeros_like(acc_ref)

            def value_step(j, carry):
                acc_ref[...] += dot(p_all[2 * pair + head, base + j], v_ref[rows_of(j, tb), cols], 1, 0)
                return carry

            lax.fori_loop(0, i + 1, value_step, 0)
            out = acc_ref[...] / total_ref[mine, 2 * pair + head : 2 * pair + head + 1]
            if head == 0:
                of_ref[mine, cols] = out
            else:
                of_ref[mine, cols] = jnp.where(lane < HEAD_DIM, of_ref[mine, cols], out)
        o_ref[mine, cols] = of_ref[mine, cols].astype(LOW)

        @pl.when(i == c)
        def _():
            pltpu.make_async_copy(o_ref.at[mine, cols], home(pair), own_o.at[pair]).start()

        @pl.when(i != c)
        def _():
            k = lax.rem(i + n_ctx - c, n_ctx) - 1
            ctx_copy(o_ref.at[mine, cols], home(pair), o_send.at[k, pair], o_recv.at[k, pair], i).start()

    def over_queries(what, pair):
        def one(i, carry):
            what(pair, i)
            return carry

        lax.fori_loop(0, n_ctx, one, 0)

    total_ref[...] = jnp.ones_like(total_ref)
    over_queries(weigh, 0)
    each("cross", up)
    over_queries(weigh, 1)
    each("forward", down)
    for k in range(1, n_ctx):
        fv_copy(k).wait_recv()

    def values(b, carry):
        at = rows_of(b, tb)
        v_ref[at, :] = (of_ref[at, :] + 0.5 * fvs[at, :].astype(F32)).astype(LOW)
        return carry

    lax.fori_loop(0, n_ctx, values, 0)
    over_queries(mix, 0)
    each("cross", down)
    over_queries(mix, 1)
    for pair in range(width // LANES):
        cols = slice(pair * LANES, (pair + 1) * LANES)
        pltpu.make_async_copy(o_ref.at[0:tb, cols], home(pair), own_o.at[pair]).wait()
        for k in range(n_ctx - 1):
            ctx_copy(o_ref.at[0:tb, cols], home(pair), o_send.at[k, pair], o_recv.at[k, pair], c).wait()
    for k in range(1, n_ctx):
        mark_copy(k).wait_send()
        pack_copy(k).wait_send()
        fv_copy(k).wait_send()
    for at, (slot, bit) in enumerate(
        [(0, NEAR), (0, FAR), (NEAR, FAR), (0, CORE), (NEAR, CORE), (FAR, CORE), (NEAR | FAR, CORE)]
    ):
        pack_hop(slot, bit, 3 + at).wait_send()
    tok_copy(1).wait_send()
    tok_copy(2).wait_send()
    tok_pass().wait_send()
    each("finish", *weights)


def front_call(n_dp, n_ctx, tok, fv, mark, pack, freq, wg, wu, wo, wd):
    tb, model = tok.shape
    width = model // n_ctx
    length = n_ctx * tb
    pairs = width // LANES
    vmem = pl.BlockSpec(memory_space=pltpu.VMEM)
    anyspace = pl.BlockSpec(memory_space=pl.ANY)
    shape = jax.ShapeDtypeStruct
    dma = pltpu.SemaphoreType.DMA
    return pl.pallas_call(
        functools.partial(front_kernel, n_ctx),
        in_specs=[anyspace] * 4 + [vmem] + [anyspace] * 4,
        out_specs=[vmem] * 11 + [anyspace] * 5,
        out_shape=[shape((length, model), LOW)]
        + [shape((length, width), LOW)] * 3
        + [shape((length, width), F32)] * 2
        + [shape((length, LANES), F32)] * 3
        + [shape((8, length), jnp.int32), shape((8, model), F32)]
        + [shape((tb, model), LOW)]
        + [shape((n_dp, n_ctx * w.shape[0], w.shape[1]), LOW) for w in (wg, wu, wo, wd)],
        scratch_shapes=[
            pltpu.VMEM((length, model), LOW),
            pltpu.VMEM((length, width), LOW),
            pltpu.VMEM((n_dp,) + pack.shape, LOW),
            pltpu.VMEM((model, 3 * width), LOW),
            pltpu.VMEM((tb // 2, model), F32),
            pltpu.VMEM((length, width), LOW),
            pltpu.VMEM((tb, length), F32),
            pltpu.VMEM((tb, LANES), F32),
            pltpu.VMEM((tb, LANES), F32),
            pltpu.VMEM((tb, LANES), F32),
            pltpu.VMEM((2 * pairs, n_ctx * (n_ctx + 1) // 2, tb, tb), LOW),
            pltpu.VMEM((length, LANES), F32),
            dma((n_ctx - 1,)), dma((n_ctx - 1,)),
            dma((n_ctx + 6,)), dma((n_ctx + 6,)),
            dma((3,)), dma((3,)),
            dma((n_ctx - 1,)), dma((n_ctx - 1,)),
            dma((8, 11)), dma((8, 11)),
            dma((n_ctx - 1, pairs)), dma((n_ctx - 1, pairs)),
            dma((4,)), dma((pairs,)),
        ],
        compiler_params=params(collective_id=1, has_side_effects=True),
        cost_estimate=pl.CostEstimate(
            flops=24 * 10**9, bytes_accessed=60 * 2**20, transcendentals=2 * length * length
        ),
        name="front",
    )(tok, fv, mark, pack, freq, wg, wu, wo, wd)


class Reduce:
    def __init__(self, n_ctx, keep, came, acc, rc, rx, ry, rz, out, send, recv, order):
        self.n, self.keep, self.came, self.acc, self.rc, self.rx, self.ry, self.rz = n_ctx, keep, came, acc, rc, rx, ry, rz
        self.out, self.send, self.recv = out, send, recv
        self.one, self.two = order
        self.leave = (self.one >> 1, 3)
        self.stay = self.two >> 1

    def hop(self, at):
        src, dst, bit = [
            (self.acc.at[self.leave[0]], self.rx.at[0], self.one),
            (self.acc.at[self.leave[1]], self.rx.at[1], self.one),
            (self.acc.at[self.stay], self.ry, self.two),
        ][at - 1]
        return dp_copy(src, dst, self.send.at[at], self.recv.at[at], bit)

    def held(self):
        return pltpu.make_async_copy(self.keep, self.acc, self.send.at[7])

    def partner(self):
        return pltpu.make_async_copy(self.came, self.rc, self.send.at[0])

    def along(self, at):
        c = lax.axis_index("ctx")
        block, to = ((c ^ 1, c ^ 1), (c ^ 3, c ^ 1), (c ^ 2, c ^ 2))[at]
        return ctx_copy(self.acc.at[0, block], self.rz.at[at], self.send.at[4 + at], self.recv.at[4 + at], to)

    def begin(self):
        self.partner().start()
        self.held().start()

    def add(self, block, terms):
        def one(j, carry):
            total = self.acc[block, j].astype(F32)
            for t in terms:
                total = total + t(j).astype(F32)
            self.acc[block, j] = total.astype(LOW)
            return carry

        lax.fori_loop(0, self.acc.shape[1], one, 0)

    def step_one(self):
        self.held().wait()
        self.partner().wait()
        for at in (1, 0):
            block = self.leave[at]
            self.add(block, [lambda j, block=block: self.rc[block, j]])
            self.hop(1 + at).start()

    def step_two(self):
        self.hop(2).wait_recv()
        self.add(self.stay, [lambda j: self.rc[self.stay, j], lambda j: self.rx[1, j]])
        self.hop(3).start()

    def step_ctx(self):
        c = lax.axis_index("ctx")
        self.hop(1).wait_recv()
        self.hop(3).wait_recv()
        self.out[...] = (
            self.acc[0, c].astype(F32) + self.rc[0, c].astype(F32) + self.rx[0, c].astype(F32) + self.ry[c].astype(F32)
        )
        self.add(0, [lambda j: self.rc[0, j], lambda j: self.rx[0, j], lambda j: self.ry[j]])
        self.along(1).start()
        self.along(0).start()

    def step_far(self):
        block = lax.axis_index("ctx") ^ 2
        self.along(1).wait_recv()
        self.acc[0, block] = (self.acc[0, block].astype(F32) + self.rz[1].astype(F32)).astype(LOW)
        self.along(2).start()

    def finish(self):
        self.along(0).wait_recv()
        self.along(2).wait_recv()
        self.out[...] += self.rz[0].astype(F32) + self.rz[2].astype(F32)
        for at in range(1, 4):
            self.hop(at).wait_send()
        for at in range(3):
            self.along(at).wait_send()


def back_kernel(n_ctx, *refs):
    g_ref, q_ref, k_ref, v_ref, of_ref, lse_ref, sc_ref, sr_ref, cos_ref, sin_ref, xn_ref = refs[:11]
    sides = refs[11:19]
    home_ref, qkv_out = refs[19:21]
    outs = refs[21:25]
    (part_ref, lse_row, delta_row, dq_acc, dk_acc, dv_acc, prod) = refs[25:32]
    rest = refs[32:]
    buffers, rest = rest[:40], rest[40:]
    (pk, ps, prc, prx, pry, pz, qz) = rest[:7]
    (send, recv, own, r_send, r_recv, p_send, p_recv, z_send, z_recv) = rest[7:]
    c = lax.axis_index("ctx")
    tb = dk_acc.shape[0]
    length, width = q_ref.shape
    model = n_ctx * width
    pairs = width // LANES
    blocks = model // LANES
    orders = ((NEAR, FAR), (FAR, NEAR))
    groups = []
    for i in range(4):
        keep, came = sides[2 * i], sides[2 * i + 1]
        wide = keep.shape[3] // 2
        groups.append([])
        for h, order in enumerate(orders):
            cols = pl.ds(h * wide, wide)
            unit = 2 * i + h
            groups[i].append(
                Reduce(
                    n_ctx, keep.at[:, :, :, cols], came.at[:, :, :, cols], *buffers[5 * unit : 5 * unit + 5],
                    outs[i].at[:, cols], r_send.at[unit], r_recv.at[unit], order,
                )
            )

    def each(i, what):
        for unit in groups[i]:
            getattr(unit, what)()

    def home(pair, t):
        return home_ref.at[:, pl.ds(pl.multiple_of(t * model + c * width + pair * LANES, LANES), LANES)]

    def part(pair, t, chunk):
        return part_ref.at[pair, rows_of(chunk, tb), pl.ds(t * LANES, LANES)]

    def part_copy(pair, t, k, to):
        return ctx_copy(part(pair, t, to), home(pair, t), send.at[k - 1, pair, t], recv.at[k - 1, pair, t], to)

    def part_own(pair, t):
        return pltpu.make_async_copy(part(pair, t, c), home(pair, t), own.at[pair, t])

    meet(n_ctx, (CORE, NEAR, FAR))
    for i in range(4):
        each(i, "begin")
    each(0, "step_one")

    r8 = lax.broadcasted_iota(jnp.int32, (8, LANES), 0)
    l8 = lax.broadcasted_iota(jnp.int32, (8, LANES), 1)
    pick = jnp.where(l8 == r8 * HEAD_DIM, 1.0, 0.0)
    group = jnp.where(l8 // HEAD_DIM == r8, 1.0, 0.0)
    exact = lax.Precision.HIGHEST
    dims = (((1,), (1,)), ((), ()))

    def stats(pair):
        cols = slice(pair * LANES, (pair + 1) * LANES)

        def one(b, carry):
            at = rows_of(b, tb)
            lse_row[:, at] = lax.dot_general(pick, lse_ref[at, cols], dims, precision=exact, preferred_element_type=F32)
            mixed = g_ref[at, cols].astype(F32) * of_ref[at, cols]
            delta_row[:, at] = lax.dot_general(group, mixed, dims, precision=exact, preferred_element_type=F32)
            dq_acc[at, :] = jnp.zeros((tb, LANES), F32)
            return carry

        lax.fori_loop(0, n_ctx, one, 0)

    def key_blocks(pair, lo, hi):
        cols = slice(pair * LANES, (pair + 1) * LANES)

        def key_block(j, carry):
            dk_acc[...] = jnp.zeros_like(dk_acc)
            dv_acc[...] = jnp.zeros_like(dv_acc)
            mine = rows_of(j, tb)
            k = k_ref[mine, cols]
            v = v_ref[mine, cols]
            seg_k = sc_ref[mine, 0:1]

            def block(i, causal):
                at = rows_of(i, tb)
                q = q_ref[at, cols]
                g = g_ref[at, cols]
                ok = seg_k == sr_ref[0:1, at].astype(F32)
                if causal:
                    r = lax.broadcasted_iota(jnp.int32, (tb, tb), 0)
                    t = lax.broadcasted_iota(jnp.int32, (tb, tb), 1)
                    ok = ok & (r <= t)
                for head in range(2):
                    qm = head_lanes(q, head)
                    gm = head_lanes(g, head)
                    s = dot(k, qm, 1, 1)
                    p = jnp.where(ok, jnp.exp(s - lse_row[head : head + 1, at]), 0.0)
                    dp = dot(v, gm, 1, 1)
                    ds = (p * (dp - delta_row[head : head + 1, at])).astype(LOW)
                    dv_acc[...] += dot(p.astype(LOW), gm, 1, 0)
                    dk_acc[...] += dot(ds, qm, 1, 0)
                    dq_acc[at, :] += dot(ds, head_lanes(k, head), 0, 0)

            block(j, True)

            def step(i, carry):
                block(i, False)
                return carry

            lax.fori_loop(j + 1, n_ctx, step, 0)
            dk = dk_acc[...]
            dk = dk * cos_ref[mine, :] - half_swap(dk) * sin_ref[mine, :]
            part_ref[pair, mine, LANES : 2 * LANES] = dk.astype(LOW)
            part_ref[pair, mine, 2 * LANES : 3 * LANES] = dv_acc[...].astype(LOW)
            dq = dq_acc[mine, :] * 0.125
            dq = dq * cos_ref[mine, :] - half_swap(dq) * sin_ref[mine, :]
            part_ref[pair, mine, 0:LANES] = dq.astype(LOW)

            @pl.when(j == c)
            def _():
                for t in range(3):
                    part_own(pair, t).start()

            @pl.when(j != c)
            def _():
                for t in range(3):
                    part_copy(pair, t, lax.rem(j + n_ctx - c, n_ctx), j).start()

            return carry

        lax.fori_loop(lo, hi, key_block, 0)

    def pair_hop(pair, at):
        src, dst, bit = [
            (ps.at[pair], prc.at[pair], CORE),
            (pk.at[pair, 1], prx.at[pair, 0], NEAR),
            (pk.at[pair, 3], prx.at[pair, 1], NEAR),
            (pk.at[pair, 2], pry.at[pair], FAR),
        ][at]
        return dp_copy(src, dst, p_send.at[pair, at], p_recv.at[pair, at], bit)

    def pair_ctx(pair, k):
        to = lax.rem(c + k, n_ctx)
        return ctx_copy(pz.at[pair, to], qz.at[c, pair], z_send.at[pair, k - 1], z_recv.at[pair, k - 1], to)

    def pair_product(pair):
        prod[...] = jnp.zeros_like(prod)

        def one(b, carry):
            at = rows_of(b, tb)
            prod[...] += dot(part_ref[pair, at, :], xn_ref[at, :], 0, 0)
            return carry

        lax.fori_loop(0, n_ctx, one, 0)
        for d in range(blocks):
            (ps if d % 2 else pk)[pair, d // 2] = prod[:, d * LANES : (d + 1) * LANES].astype(LOW)
        pair_hop(pair, 0).start()

    def pair_one(pair):
        pair_hop(pair, 0).wait_recv()
        for i in (3, 1):
            pk[pair, i] = (pk[pair, i].astype(F32) + prc[pair, i].astype(F32)).astype(LOW)
            pair_hop(pair, 1 + i // 2).start()

    def pair_two(pair):
        pair_hop(pair, 2).wait_recv()
        total = pk[pair, 2].astype(F32) + prc[pair, 2].astype(F32) + prx[pair, 1].astype(F32)
        pk[pair, 2] = total.astype(LOW)
        pair_hop(pair, 3).start()

    def pair_three(pair):
        pair_hop(pair, 1).wait_recv()
        pair_hop(pair, 3).wait_recv()
        total = pk[pair, 0].astype(F32) + prc[pair, 0].astype(F32) + prx[pair, 0].astype(F32) + pry[pair].astype(F32)
        pz[pair] = total.T.reshape(pz.shape[1:]).astype(LOW)
        qz[c, pair] = pz[pair, c]
        for k in range(1, n_ctx):
            pair_ctx(pair, k).start()

    def pair_finish(pair):
        for k in range(1, n_ctx):
            pair_ctx(pair, k).wait()
        for at in range(4):
            pair_hop(pair, at).wait_send()

    middle = n_ctx // 2
    stats(0)
    key_blocks(0, 0, middle)
    each(0, "step_two")
    each(1, "step_one")
    key_blocks(0, middle, n_ctx)
    pair_product(0)
    each(0, "step_ctx")
    stats(1)
    key_blocks(1, 0, middle)
    each(1, "step_two")
    each(2, "step_one")
    pair_one(0)
    each(0, "step_far")
    key_blocks(1, middle, n_ctx)
    each(1, "step_ctx")
    pair_product(1)
    pair_two(0)
    each(2, "step_two")
    each(3, "step_one")
    pair_one(1)
    pair_three(0)
    each(1, "step_far")
    each(2, "step_ctx")
    pair_two(1)
    each(3, "step_two")
    each(2, "step_far")
    pair_three(1)
    each(3, "step_ctx")
    each(3, "step_far")
    for pair in range(pairs):
        pair_finish(pair)
        for s in range(n_ctx):
            for t in range(3):
                at = t * model + s * width + pair * LANES
                qkv_out[:, at : at + LANES] = qz[s, pair, :, t * LANES : (t + 1) * LANES].astype(F32)
    for i in range(4):
        each(i, "finish")
    for pair in range(pairs):
        for t in range(3):
            part_own(pair, t).wait()
            for k in range(1, n_ctx):
                part_copy(pair, t, k, lax.rem(c + k, n_ctx)).wait()


def back_call(n_ctx, g, q, k, v, of, lse, seg_col, seg_row, cos, sin, xn, sides):
    length, width = q.shape
    model = n_ctx * width
    tb = TOKEN_BLOCK
    pairs = width // LANES
    own_rows = model // (model // LANES) // n_ctx
    vmem = pl.BlockSpec(memory_space=pltpu.VMEM)
    anyspace = pl.BlockSpec(memory_space=pl.ANY)
    shape = jax.ShapeDtypeStruct
    dma = pltpu.SemaphoreType.DMA
    buffers = []
    for keep in sides[::2]:
        four, parts, rows, cols = keep.shape
        for lead in ((four, parts), (four, parts), (2, parts), (parts,), (3,)) * 2:
            buffers.append(pltpu.VMEM(lead + (rows, cols // 2), LOW))
    wide = 3 * LANES
    return pl.pallas_call(
        functools.partial(back_kernel, n_ctx),
        in_specs=[vmem] * 11 + [anyspace] * 8,
        out_specs=[anyspace] + [vmem] * 5,
        out_shape=[shape((tb, 3 * model), LOW), shape((own_rows, 3 * model), F32)]
        + [shape(keep.shape[2:], F32) for keep in sides[::2]],
        scratch_shapes=[
            pltpu.VMEM((pairs, length, wide), LOW),
            pltpu.VMEM((8, length), F32),
            pltpu.VMEM((8, length), F32),
            pltpu.VMEM((length, LANES), F32),
            pltpu.VMEM((tb, LANES), F32),
            pltpu.VMEM((tb, LANES), F32),
            pltpu.VMEM((wide, model), F32),
        ]
        + buffers
        + [
            pltpu.VMEM((pairs, 4, wide, LANES), LOW),
            pltpu.VMEM((pairs, 4, wide, LANES), LOW),
            pltpu.VMEM((pairs, 4, wide, LANES), LOW),
            pltpu.VMEM((pairs, 2, wide, LANES), LOW),
            pltpu.VMEM((pairs, wide, LANES), LOW),
            pltpu.VMEM((pairs, n_ctx, own_rows, wide), LOW),
            pltpu.VMEM((n_ctx, pairs, own_rows, wide), LOW),
            dma((n_ctx - 1, pairs, 3)), dma((n_ctx - 1, pairs, 3)),
            dma((pairs, 3)),
            dma((8, 8)), dma((8, 8)),
            dma((pairs, 4)), dma((pairs, 4)),
            dma((pairs, n_ctx - 1)), dma((pairs, n_ctx - 1)),
        ],
        compiler_params=params(collective_id=3, has_side_effects=True),
        cost_estimate=pl.CostEstimate(
            flops=40 * 10**9, bytes_accessed=60 * 2**20, transcendentals=2 * length * length
        ),
        name="back",
    )(g, q, k, v, of, lse, seg_col, seg_row, cos, sin, xn, *sides)


def mlp_kernel(
    blocks, n_ctx, tok_ref, att_ref, cot_ref, gain_ref, wo_in, wg_in, wu_in, wd_in, wq_ref, wr_ref,
    out_ref, gm_ref, gh_ref, gk, gc, uk, uc, ok, oc, dk, dc, wq_all, wr_all,
    wo, wg, wu, wd, att, nat, n2, mi, mit, oacc, dacc, hid_all, dg_all, du_all, stage, ostage,
    sem, hop_send, hop_recv, st_own, st_send, st_recv, o_sem, d_own, d_send, d_recv, g_send, g_recv,
):
    c, dp = lax.axis_index("ctx"), lax.axis_index("dp")
    tb, model = tok_ref.shape
    width = model // n_ctx
    ff = wu.shape[1]
    steps = ff // FF_BLOCK
    down = wd_in.shape[1]
    half = blocks // 2
    attn = [
        Gather(n_ctx, wq_ref, wq_all, hop_send.at[0], hop_recv.at[0], (NEAR, FAR)),
        Gather(n_ctx, wr_ref, wr_all, hop_send.at[1], hop_recv.at[1], (FAR, NEAR)),
    ]

    loads = []
    for d in range(blocks):
        at = pl.ds(d * LANES, LANES)
        loads.append(pltpu.make_async_copy(wo_in.at[d], wo.at[at, :], sem.at[0, d]))
    for d in range(blocks):
        at = pl.ds(d * LANES, LANES)
        rows = pl.ds(pl.multiple_of((dp ^ d) * down, 32), down)
        loads.append(pltpu.make_async_copy(wg_in.at[d], wg.at[at, :], sem.at[1, d]))
        loads.append(pltpu.make_async_copy(wu_in.at[d], wu.at[at, :], sem.at[2, d]))
        loads.append(pltpu.make_async_copy(wd_in.at[d], wd.at[rows, :], sem.at[3, d]))
    for m in loads:
        m.start()
    for d in range(blocks):
        att[:, d * LANES : (d + 1) * LANES] = att_ref[:, lane_block(dp ^ d)]
    meet(n_ctx, (CORE, NEAR, FAR))
    for w in attn:
        w.start()
    for m in loads[:blocks]:
        m.wait()
    mid = tok_ref[...].astype(F32) + dot(att[...], wo[...], 1, 0)
    inv = lax.rsqrt(jnp.mean(mid * mid, axis=-1, keepdims=True) + epsilon)
    oacc[...] = mid
    nat[...] = mid * inv
    for d in range(blocks):
        n2[:, d * LANES : (d + 1) * LANES] = nat[:, lane_block(dp ^ d)]
    mi[...] = (n2[...] * gain_ref[...]).astype(LOW)
    mit[...] = mi[...].T
    dacc[...] = jnp.zeros_like(dacc)
    for m in loads[blocks:]:
        m.wait()

    def columns(u):
        return pl.ds(pl.multiple_of(u * FF_BLOCK, FF_BLOCK), FF_BLOCK)

    def data_step(u, carry):
        cols = columns(u)
        x = mi[...]
        cot = cot_ref[...]
        wgu, wuu, wdu = wg[:, cols], wu[:, cols], wd[cols, :]
        gate = dot(x, wgu, 1, 0)
        up = dot(x, wuu, 1, 0)
        grad_hidden = dot(cot, wdu, 1, 1)
        sig = jax.nn.sigmoid(gate)
        hidden = (gate * sig * up).astype(LOW)
        dg = (grad_hidden * up * sig * (1.0 + gate * (1.0 - sig))).astype(LOW)
        du = (grad_hidden * gate * sig).astype(LOW)
        hid_all[:, cols] = hidden
        dg_all[:, cols] = dg
        du_all[:, cols] = du
        oacc[...] += dot(hidden, wdu, 1, 0)
        dacc[...] += dot(dg, wgu, 1, 1) + dot(du, wuu, 1, 1)
        return carry

    lax.fori_loop(0, 3, data_step, 0)
    for w in attn:
        w.relay()
    lax.fori_loop(3, 6, data_step, 0)
    for w in attn:
        w.spread()
    lax.fori_loop(6, steps, data_step, 0)

    out_ref[...] = oacc[...].astype(LOW)
    scaled = dacc[...] * gain_ref[...]
    norm = n2[...]
    mean = jnp.mean(scaled * norm, axis=-1, keepdims=True)
    n2[...] = inv * (scaled - norm * mean)
    for d in range(blocks):
        nat[:, lane_block(dp ^ d)] = n2[:, d * LANES : (d + 1) * LANES]
    gm = cot_ref[...].astype(F32) + nat[...]
    gm_ref[...] = gm
    gb = gm.astype(LOW)
    n2[...] = dot(gb, wo[...], 1, 1)
    for d in range(blocks):
        mi[:, lane_block(dp ^ d)] = n2[:, d * LANES : (d + 1) * LANES].astype(LOW)

    def grad_copy(k):
        to = lax.rem(c + k, n_ctx)
        return ctx_copy(mi.at[:, rows_of(to, width)], gh_ref.at[rows_of(c, tb), :], g_send.at[k - 1], g_recv.at[k - 1], to)

    grad_own = pltpu.make_async_copy(mi.at[:, rows_of(c, width)], gh_ref.at[rows_of(c, tb), :], o_sem.at[2])
    for k in range(1, n_ctx):
        grad_copy(k).start()
    grad_own.start()
    for w in attn:
        w.forward()

    def down_step(u, carry):
        cols = columns(u)
        wd[cols, :] = dot(hid_all[:, cols], cot_ref[...], 0, 0).astype(LOW)
        return carry

    lax.fori_loop(0, steps, down_step, 0)

    def down_copy(d):
        rows = pl.ds(pl.multiple_of((dp ^ d) * down, 32), down)
        if d % 2:
            return dp_copy(wd.at[rows, :], dc.at[d // 2], d_send.at[d // 2], d_recv.at[d // 2], CORE)
        return pltpu.make_async_copy(wd.at[rows, :], dk.at[d // 2], d_own.at[d // 2])

    for d in range(blocks):
        down_copy(d).start()

    dwo = dot(att[...], gb, 0, 0).astype(LOW)
    for d in range(blocks):
        ostage[d % 2, d // 2] = dwo[d * LANES : (d + 1) * LANES]
    out_own = pltpu.make_async_copy(ostage.at[0], ok, o_sem.at[0])
    out_gone = dp_copy(ostage.at[1], oc, o_sem.at[1], o_sem.at[3], CORE)
    out_own.start()
    out_gone.start()

    def side(u, t, which):
        slot = lax.rem(u, 2)
        cols = columns(u)
        keep, came = ((gk, gc), (uk, uc))[t]
        if which == 0:
            return pltpu.make_async_copy(stage.at[slot, t, 0], keep.at[:, :, cols], st_own.at[slot, t])
        return dp_copy(stage.at[slot, t, 1], came.at[:, :, cols], st_send.at[slot, t], st_recv.at[t, u], CORE)

    def weight_step(u, carry):
        cols = columns(u)

        @pl.when(u >= 2)
        def _():
            for t in range(2):
                side(u - 2, t, 0).wait()
                side(u - 2, t, 1).wait_send()

        slot = lax.rem(u, 2)
        for t, grad in enumerate((dg_all, du_all)):
            dw = dot(mit[...], grad[:, cols], 1, 0).astype(LOW)
            for d in range(blocks):
                stage[slot, t, d % 2, d // 2] = dw[d * LANES : (d + 1) * LANES]
            side(u, t, 0).start()
            side(u, t, 1).start()
        return carry

    lax.fori_loop(0, 5, weight_step, 0)
    for w in attn:
        w.cross()
    lax.fori_loop(5, steps, weight_step, 0)

    for u in (steps - 2, steps - 1):
        for t in range(2):
            side(u, t, 0).wait()
            side(u, t, 1).wait_send()

    def arrived(u, carry):
        for t in range(2):
            side(u, t, 1).wait_recv()
        return carry

    lax.fori_loop(0, steps, arrived, 0)
    out_own.wait()
    out_gone.wait()
    for d in range(blocks):
        down_copy(d).wait()
    grad_own.wait()
    for k in range(1, n_ctx):
        grad_copy(k).wait()
    for w in attn:
        w.finish()


def mlp_call(n_ctx, tok, att, cot, gain, wo, wg, wu, wd, wq, wr):
    tb, model = tok.shape
    blocks, _, ff = wg.shape
    half = blocks // 2
    down = wd.shape[1]
    width = model // n_ctx
    vmem = pl.BlockSpec(memory_space=pltpu.VMEM)
    anyspace = pl.BlockSpec(memory_space=pl.ANY)
    shape = jax.ShapeDtypeStruct
    dma = pltpu.SemaphoreType.DMA
    return pl.pallas_call(
        functools.partial(mlp_kernel, blocks, n_ctx),
        in_specs=[vmem] * 4 + [anyspace] * 6,
        out_specs=[vmem] * 2 + [anyspace] * 11,
        out_shape=[shape((tb, model), LOW), shape((tb, model), F32), shape((n_ctx * tb, width), LOW)]
        + [shape((half, LANES, ff), LOW)] * 4
        + [shape((half, LANES, model), LOW)] * 2
        + [shape((half, down, model), LOW)] * 2
        + [shape((blocks, n_ctx * w.shape[0], w.shape[1]), LOW) for w in (wq, wr)],
        scratch_shapes=[
            pltpu.VMEM((model, model), LOW),
            pltpu.VMEM((model, ff), LOW),
            pltpu.VMEM((model, ff), LOW),
            pltpu.VMEM((ff, model), LOW),
            pltpu.VMEM((tb, model), LOW),
            pltpu.VMEM((tb, model), F32),
            pltpu.VMEM((tb, model), F32),
            pltpu.VMEM((tb, model), LOW),
            pltpu.VMEM((model, tb), LOW),
            pltpu.VMEM((tb, model), F32),
            pltpu.VMEM((tb, model), F32),
            pltpu.VMEM((tb, ff), LOW),
            pltpu.VMEM((tb, ff), LOW),
            pltpu.VMEM((tb, ff), LOW),
            pltpu.VMEM((2, 2, 2, half, LANES, FF_BLOCK), LOW),
            pltpu.VMEM((2, half, LANES, model), LOW),
            dma((4, blocks)),
            dma((2, 11)), dma((2, 11)),
            dma((2, 2)), dma((2, 2)), dma((2, ff // FF_BLOCK)),
            dma((4,)),
            dma((half,)), dma((half,)), dma((half,)),
            dma((n_ctx - 1,)), dma((n_ctx - 1,)),
        ],
        compiler_params=params(collective_id=2, has_side_effects=True),
        cost_estimate=pl.CostEstimate(
            flops=2 * tb * model * (8 * ff + 3 * model), bytes_accessed=50 * 2**20, transcendentals=0
        ),
        name="mlp",
    )(tok, att, cot, gain, wo, wg, wu, wd, wq, wr)


def input_kernel(
    blocks, tok_ref, gm_ref, v1_ref, y_ref, g, gain_ref, own_gain, qkv_ref, gate_ref, up_ref, out_ref, down_ref,
    wq_ref, wr_ref, wgate_ref, wup_ref, wq_all, wr_all,
    ig_ref, vg_ref, yo_ref, gq_ref, gk_ref, gv_ref, go_ref, gg_ref, gu_ref, gd_ref, gains_ref, w, rel, nat, sem,
):
    dp = lax.axis_index("dp")
    model = tok_ref.shape[1]
    cut = wq_ref.shape[1]
    made = []
    for d in range(blocks):
        at = pl.ds(d * LANES, LANES)
        made.append(pltpu.make_async_copy(wq_all.at[d], w.at[at, pl.ds(0, cut)], sem.at[0, d]))
        made.append(pltpu.make_async_copy(wr_all.at[d], w.at[at, pl.ds(cut, 3 * model - cut)], sem.at[1, d]))

    def row_dot(a, b):
        return jnp.sum(a * b.astype(F32), axis=1, keepdims=True)

    @pl.when(pl.program_id(0) == 0)
    def _():
        for m in made:
            m.start()
        gq_ref[...] = qkv_ref[:, :model]
        gk_ref[...] = qkv_ref[:, model : 2 * model]
        gv_ref[...] = 0.5 * qkv_ref[:, 2 * model :]
        go_ref[...] = out_ref[...]
        gg_ref[...] = gate_ref[...]
        gu_ref[...] = up_ref[...]
        gd_ref[...] = down_ref[...]
        both = 2 * model - cut
        one = row_dot(qkv_ref[:, :cut], wq_ref[...]) + row_dot(qkv_ref[:, cut : 2 * model], wr_ref[:, :both])
        one = one + row_dot(gv_ref[...], wr_ref[:, both:])
        two = row_dot(gate_ref[...], wgate_ref[...]) + row_dot(up_ref[...], wup_ref[...])
        lane = lax.broadcasted_iota(jnp.int32, gains_ref.shape, 1)
        gains_ref[...] = jnp.where(lane == 0, one, two) / own_gain[...]

    yo_ref[...] = y_ref[...]
    for d in range(blocks):
        rel[:, d * LANES : (d + 1) * LANES] = tok_ref[:, lane_block(dp ^ d)].astype(F32)
    gv = g[:, 2 * model :].astype(F32)
    vg_ref[...] = v1_ref[...] + 0.5 * gv

    x = rel[...]
    inv = lax.rsqrt(jnp.mean(x * x, axis=-1, keepdims=True) + epsilon)
    norm = x * inv

    @pl.when(pl.program_id(0) == 0)
    def _():
        for m in made:
            m.wait()

    grad = dot(g[:, : 2 * model], w[:, : 2 * model], 1, 1)
    grad = grad + 0.5 * dot(g[:, 2 * model :], w[:, 2 * model :], 1, 1)
    scaled = grad * gain_ref[...]
    mean = jnp.mean(scaled * norm, axis=-1, keepdims=True)
    rel[...] = inv * (scaled - norm * mean)
    for d in range(blocks):
        nat[:, lane_block(dp ^ d)] = rel[:, d * LANES : (d + 1) * LANES]
    ig_ref[...] = gm_ref[...] + nat[...]


def input_call(tok, gm, v1, y, g, gain, own_gain, qkv, grads, wq, wr, wgate, wup, wq_all, wr_all):
    tb, model = tok.shape
    blocks = wq_all.shape[0]
    rows = qkv.shape[0]
    part = tb // 2
    shape = jax.ShapeDtypeStruct
    token = lambda cols: pl.BlockSpec((part, cols), lambda i: (i, 0))
    whole = lambda a: pl.BlockSpec(a.shape, lambda i: (0, 0))
    small = [gain, own_gain, qkv, *grads, wq, wr, wgate, wup]
    ends = [shape((rows, model), F32)] * 4 + [shape(x.shape, F32) for x in (grads[0], grads[1], grads[3])]
    ends.append(shape((rows, LANES), F32))
    return pl.pallas_call(
        functools.partial(input_kernel, blocks),
        grid=(tb // part,),
        in_specs=[token(model)] * 4 + [token(3 * model)] + [whole(x) for x in small] + [pl.BlockSpec(memory_space=pl.ANY)] * 2,
        out_specs=[token(model)] * 3 + [whole(x) for x in ends],
        out_shape=[shape((tb, model), F32)] * 2 + [shape((tb, model), LOW)] + ends,
        scratch_shapes=[
            pltpu.VMEM((model, 3 * model), LOW),
            pltpu.VMEM((part, model), F32),
            pltpu.VMEM((part, model), F32),
            pltpu.SemaphoreType.DMA((2, blocks)),
        ],
        compiler_params=params(),
        cost_estimate=pl.CostEstimate(
            flops=2 * tb * model * 3 * model, bytes_accessed=20 * 2**20, transcendentals=0
        ),
        name="input_grad",
    )(tok, gm, v1, y, g, *small, wq_all, wr_all)


def fast_local(
    n_dp, n_ctx, tokens, first_values, v1_accum, segment_ids, positions, cotangent,
    attn_gain, w_query, w_key, w_value, w_out, mlp_gain, w_gate, w_up, w_down,
):
    seq, model = tokens.shape[1:]
    width = model // n_ctx
    own_rows = w_query.shape[0]
    tok = tokens[0]
    mark = jnp.concatenate([segment_ids, positions, jnp.zeros((6, seq), jnp.int32)], axis=0)
    gains = jnp.stack([attn_gain, mlp_gain], axis=1)
    gains = jnp.tile(jnp.pad(gains, ((0, 0), (0, width - 2))), (1, n_ctx))
    pack = jnp.concatenate([w_query, w_key, w_value, gains], axis=0)
    pack = pack.reshape(4 * own_rows, n_ctx, width).transpose(1, 0, 2)
    freqs = 10000.0 ** (-np.arange(HEAD_DIM // 2).astype(np.float32) * np.float32(2.0 / HEAD_DIM))
    freq = np.zeros((8, LANES), np.float32)
    freq[0] = np.tile(freqs.astype(np.float32), LANES // (HEAD_DIM // 2))
    freq[1] = np.where(np.arange(LANES) % HEAD_DIM < HEAD_DIM // 2, -1.0, 1.0)
    freq = jnp.asarray(freq)
    (xn, q, k, v, out_full, log_total, cos, sin, seg_col, seg_row, gain_rows, attended,
     gate_all, up_all, out_all, down_all) = front_call(
        n_dp, n_ctx, tok, first_values[0], mark, pack, freq, w_gate, w_up, w_out, w_down
    )
    cut = model // 2
    wq = jnp.concatenate([w_query, w_key[:, :cut]], axis=1)
    wr = jnp.concatenate([w_key[:, cut:], w_value], axis=1)
    (output, grad_middle, head_grad, gate_keep, gate_came, up_keep, up_came, out_keep, out_came,
     down_keep, down_came, wq_all, wr_all) = mlp_call(
        n_ctx, tok, attended, cotangent[0], gain_rows[1:2], out_all, gate_all, up_all, down_all, wq, wr
    )
    sides = [
        x.reshape(x.shape[0], n_ctx, x.shape[1] // n_ctx, x.shape[2])
        for x in (gate_keep, gate_came, up_keep, up_came, out_keep, out_came, down_keep, down_came)
    ]
    home_grad, qkv_grad, *grads = back_call(
        n_ctx, head_grad, q, k, v, out_full, log_total, seg_col, seg_row, cos, sin, xn, sides
    )
    own_gain = jnp.stack([attn_gain.astype(F32)] + [mlp_gain.astype(F32)] * (LANES - 1), axis=1)
    (input_grad, v1_grad, output, query_grad, key_grad, value_grad, out_grad, gate_grad, up_grad, down_grad,
     gain_grads) = input_call(
        tok, grad_middle, v1_accum[0], output, home_grad, gain_rows[0:1], own_gain, qkv_grad, grads,
        wq, wr, w_gate, w_up, wq_all, wr_all
    )
    return (
        output[None], input_grad[None], v1_grad[None], gain_grads[:, 0], query_grad, key_grad, value_grad,
        out_grad, gain_grads[:, 1], gate_grad, up_grad, down_grad,
    )


def solution(mesh):
    placed = (
        P("dp", "ctx", None),
        P("dp", "ctx", None),
        P("dp", "ctx", None),
        P("dp", "ctx"),
        P("dp", "ctx"),
        P("dp", "ctx", None),
        P(("dp", "ctx")),
        P(("dp", "ctx"), None),
        P(("dp", "ctx"), None),
        P(("dp", "ctx"), None),
        P(("dp", "ctx"), None),
        P(("dp", "ctx")),
        P(("dp", "ctx"), None),
        P(("dp", "ctx"), None),
        P(("dp", "ctx"), None),
    )
    n_dp, n_ctx = mesh.shape["dp"], mesh.shape["ctx"]

    def local(*args):
        rows, seq, model = args[0].shape
        fits = (
            rows == 1
            and seq == TOKEN_BLOCK
            and model == n_dp * LANES
            and n_ctx == 4
            and model == 2 * LANES * n_ctx
            and args[12].shape[1] % FF_BLOCK == 0
        )
        return fast_local(n_dp, n_ctx, *args) if fits else plain_local(*args)

    return jax.shard_map(
        local,
        mesh=mesh,
        in_specs=placed,
        out_specs=(
            P("dp", "ctx", None),
            P("dp", "ctx", None),
            P("dp", "ctx", None),
            P(("dp", "ctx")),
            P(("dp", "ctx"), None),
            P(("dp", "ctx"), None),
            P(("dp", "ctx"), None),
            P(("dp", "ctx"), None),
            P(("dp", "ctx")),
            P(("dp", "ctx"), None),
            P(("dp", "ctx"), None),
            P(("dp", "ctx"), None),
        ),
        check_vma=False,
    )
```

```python
import functools

import jax
import jax.numpy as jnp
import numpy as np
from jax import lax
from jax.experimental import pallas as pl
from jax.experimental.pallas import tpu as pltpu
from jax.sharding import PartitionSpec as P

HEADS = 16
HEAD_DIM = 64
LANES = 128
TOKEN_BLOCK = 512
FF_BLOCK = 256
NEG = -1e30
MESH = pl.DeviceIdType.MESH
F32 = jnp.float32
LOW = jnp.bfloat16
BYTES = 63 * 2**20
epsilon = 1e-05


HEAD_BLOCK = 4


def rms_scale(values):
    return lax.rsqrt(jnp.mean(values * values, axis=-1, keepdims=True) + epsilon)


def angle_tables(position_rows):
    freqs = 10000.0 ** (-jnp.arange(HEAD_DIM // 2).astype(jnp.float32) * (2.0 / HEAD_DIM))
    angles = position_rows.astype(jnp.float32)[..., None] * freqs
    return (jnp.cos(angles)[..., None, :], jnp.sin(angles)[..., None, :])


def rotate(heads_in, cosine_table, sine_table):
    half_dim = heads_in.shape[-1] // 2
    first_half = heads_in[..., :half_dim]
    second_half = heads_in[..., half_dim:]
    return jnp.concatenate(
        [
            first_half * cosine_table - second_half * sine_table,
            second_half * cosine_table + first_half * sine_table,
        ],
        axis=-1,
    )


def norm_back(grad_normed, normed, inv_root, norm_gain):
    grad_scaled = grad_normed * norm_gain.astype(jnp.float32)
    grad_input = inv_root * (
        grad_scaled - normed * jnp.mean(grad_scaled * normed, axis=-1, keepdims=True)
    )
    return (grad_input, jnp.sum(grad_normed * normed, axis=0))


def attn_front(flat_tokens, first_flat, attn_set, cosine_table, sine_table, row_count, seq_piece):
    inv_root = rms_scale(flat_tokens)
    normed = flat_tokens * inv_root
    normed_in = (normed * attn_set[0].astype(jnp.float32)).astype(jnp.bfloat16)
    query_proj = jnp.dot(normed_in, attn_set[1], preferred_element_type=jnp.float32)
    key_proj = jnp.dot(normed_in, attn_set[2], preferred_element_type=jnp.float32)
    value_proj = jnp.dot(normed_in, attn_set[3], preferred_element_type=jnp.float32)
    query_rot = rotate(
        query_proj.reshape(row_count, seq_piece, HEADS, HEAD_DIM), cosine_table, sine_table
    )
    key_rot = rotate(
        key_proj.reshape(row_count, seq_piece, HEADS, HEAD_DIM), cosine_table, sine_table
    )
    query_rot = query_rot.astype(jnp.bfloat16).reshape(row_count, seq_piece, -1)
    key_rot = key_rot.astype(jnp.bfloat16).reshape(row_count, seq_piece, -1)
    value_mix = (
        (0.5 * value_proj + 0.5 * first_flat).astype(jnp.bfloat16).reshape(row_count, seq_piece, -1)
    )
    return (normed, inv_root, normed_in, query_rot, key_rot, value_mix)


def mlp_block(flat_tokens, attended_low, out_weight, mlp_set):
    middle = flat_tokens + jnp.dot(attended_low, out_weight, preferred_element_type=jnp.float32)
    inv_root_two = rms_scale(middle)
    normed_two = middle * inv_root_two
    mlp_in = (normed_two * mlp_set[0].astype(jnp.float32)).astype(jnp.bfloat16)
    gate_proj = jnp.dot(mlp_in, mlp_set[1], preferred_element_type=jnp.float32)
    up_proj = jnp.dot(mlp_in, mlp_set[2], preferred_element_type=jnp.float32)
    hidden = (gate_proj * jax.nn.sigmoid(gate_proj) * up_proj).astype(jnp.bfloat16)
    result = middle + jnp.dot(hidden, mlp_set[3], preferred_element_type=jnp.float32)
    return (normed_two, inv_root_two, mlp_in, gate_proj, up_proj, hidden, result)


def split_groups(row_block):
    tok_count = row_block.shape[0]
    return row_block.reshape(tok_count, HEADS // HEAD_BLOCK, HEAD_BLOCK * HEAD_DIM).transpose(
        1, 0, 2
    )


def join_groups(group_block):
    return group_block.transpose(1, 0, 2).reshape(group_block.shape[1], -1)


def as_heads(block):
    return block.reshape(block.shape[0], HEAD_BLOCK, HEAD_DIM)


def attend_row(members):
    query_row, key_row, value_row, allowed = members

    def per_group(pieces):
        query_block, key_block, value_block = pieces
        scores = (
            jnp.einsum(
                "qhd,khd->hqk",
                as_heads(query_block),
                as_heads(key_block),
                preferred_element_type=jnp.float32,
            )
            * 0.125
        )
        scores = jnp.where(allowed[None], scores, -1e30)
        highest = jnp.max(scores, axis=-1, keepdims=True)
        exp_scores = jnp.exp(scores - highest)
        denominator = jnp.sum(exp_scores, axis=-1, keepdims=True)
        soft_low = (exp_scores / denominator).astype(jnp.bfloat16)
        attended = jnp.einsum(
            "hqk,khd->qhd", soft_low, as_heads(value_block), preferred_element_type=jnp.float32
        )
        return (
            attended.reshape(query_block.shape[0], -1),
            (highest + jnp.log(denominator))[..., 0],
        )

    attended, log_total = lax.map(
        per_group, (split_groups(query_row), split_groups(key_row), split_groups(value_row))
    )
    return (join_groups(attended), log_total)


def attend_back(members):
    query_row, key_row, value_row, grad_row, log_total, allowed = members

    def per_group(pieces):
        query_block, key_block, value_block, grad_block, log_block = pieces
        query_heads = as_heads(query_block)
        key_heads = as_heads(key_block)
        grad_heads = as_heads(grad_block)
        scores = (
            jnp.einsum("qhd,khd->hqk", query_heads, key_heads, preferred_element_type=jnp.float32)
            * 0.125
        )
        soft_weights = jnp.where(allowed[None], jnp.exp(scores - log_block[..., None]), 0.0)
        soft_low = soft_weights.astype(jnp.bfloat16)
        grad_probs = jnp.einsum(
            "qhd,khd->hqk", grad_heads, as_heads(value_block), preferred_element_type=jnp.float32
        )
        row_delta = jnp.sum(soft_weights * grad_probs, axis=-1, keepdims=True)
        grad_scores = (soft_weights * (grad_probs - row_delta)).astype(jnp.bfloat16)
        grad_query = (
            jnp.einsum("hqk,khd->qhd", grad_scores, key_heads, preferred_element_type=jnp.float32)
            * 0.125
        )
        grad_key = (
            jnp.einsum("hqk,qhd->khd", grad_scores, query_heads, preferred_element_type=jnp.float32)
            * 0.125
        )
        grad_value = jnp.einsum(
            "hqk,qhd->khd", soft_low, grad_heads, preferred_element_type=jnp.float32
        )
        return (
            grad_query.reshape(query_block.shape[0], -1),
            grad_key.reshape(key_block.shape[0], -1),
            grad_value.reshape(key_block.shape[0], -1),
        )

    grad_query, grad_key, grad_value = lax.map(
        per_group,
        (
            split_groups(query_row),
            split_groups(key_row),
            split_groups(value_row),
            split_groups(grad_row),
            log_total,
        ),
    )
    return (join_groups(grad_query), join_groups(grad_key), join_groups(grad_value))


def plain_local(
    tokens,
    first_values,
    v1_accum,
    segment_ids,
    positions,
    cotangent,
    attn_gain,
    w_query,
    w_key,
    w_value,
    w_out,
    mlp_gain,
    w_gate,
    w_up,
    w_down,
):
    row_count, seq_piece, model_width = tokens.shape
    token_count = row_count * seq_piece
    flat_tokens = tokens.astype(jnp.float32).reshape(token_count, model_width)
    first_flat = first_values.astype(jnp.float32).reshape(token_count, model_width)
    cosine_table, sine_table = angle_tables(positions)
    segment_low = segment_ids.astype(jnp.bfloat16)
    attn_set = (
        lax.all_gather(attn_gain, ("dp", "ctx"), axis=0, tiled=True),
        lax.all_gather(w_query, ("dp", "ctx"), axis=0, tiled=True),
        lax.all_gather(w_key, ("dp", "ctx"), axis=0, tiled=True),
        lax.all_gather(w_value, ("dp", "ctx"), axis=0, tiled=True),
        lax.all_gather(w_out, ("dp", "ctx"), axis=0, tiled=True),
    )
    normed, inv_root, normed_in, query_rot, key_rot, value_mix = attn_front(
        flat_tokens, first_flat, attn_set, cosine_table, sine_table, row_count, seq_piece
    )
    key_full, value_full, segment_full = (
        lax.all_gather(key_rot, "ctx", axis=1, tiled=True),
        lax.all_gather(value_mix, "ctx", axis=1, tiled=True),
        lax.all_gather(segment_low, "ctx", axis=1, tiled=True),
    )
    query_order = lax.axis_index("ctx") * seq_piece + jnp.arange(seq_piece, dtype=jnp.int32)
    full_order = jnp.arange(key_full.shape[1], dtype=jnp.int32)
    segment_own = segment_ids.astype(jnp.float32)
    segment_all = segment_full.astype(jnp.float32)
    allowed = (segment_own[:, :, None] == segment_all[:, None, :]) & (
        query_order[None, :, None] >= full_order[None, None, :]
    )
    attended, log_total = lax.map(attend_row, (query_rot, key_full, value_full, allowed))
    attended_low = attended.reshape(token_count, model_width).astype(jnp.bfloat16)
    mlp_set = (
        lax.all_gather(mlp_gain, ("dp", "ctx"), axis=0, tiled=True),
        lax.all_gather(w_gate, ("dp", "ctx"), axis=0, tiled=True),
        lax.all_gather(w_up, ("dp", "ctx"), axis=0, tiled=True),
        lax.all_gather(w_down, ("dp", "ctx"), axis=0, tiled=True),
    )
    normed_two, inv_root_two, mlp_in, gate_proj, up_proj, hidden, output_flat = mlp_block(
        flat_tokens, attended_low, attn_set[4], mlp_set
    )
    output = output_flat.reshape(tokens.shape).astype(jnp.bfloat16)
    attn_set = (
        lax.all_gather(attn_gain, ("dp", "ctx"), axis=0, tiled=True),
        lax.all_gather(w_query, ("dp", "ctx"), axis=0, tiled=True),
        lax.all_gather(w_key, ("dp", "ctx"), axis=0, tiled=True),
        lax.all_gather(w_value, ("dp", "ctx"), axis=0, tiled=True),
        lax.all_gather(w_out, ("dp", "ctx"), axis=0, tiled=True),
    )
    mlp_set = (
        lax.all_gather(mlp_gain, ("dp", "ctx"), axis=0, tiled=True),
        lax.all_gather(w_gate, ("dp", "ctx"), axis=0, tiled=True),
        lax.all_gather(w_up, ("dp", "ctx"), axis=0, tiled=True),
        lax.all_gather(w_down, ("dp", "ctx"), axis=0, tiled=True),
    )
    normed, inv_root, normed_in, query_rot, key_rot, value_mix = attn_front(
        flat_tokens, first_flat, attn_set, cosine_table, sine_table, row_count, seq_piece
    )
    key_full, value_full = (
        lax.all_gather(key_rot, "ctx", axis=1, tiled=True),
        lax.all_gather(value_mix, "ctx", axis=1, tiled=True),
    )
    normed_two, inv_root_two, mlp_in, gate_proj, up_proj, hidden, output_flat = mlp_block(
        flat_tokens, attended_low, attn_set[4], mlp_set
    )
    cot_low = cotangent.reshape(token_count, model_width)
    cot_float = cot_low.astype(jnp.float32)
    grad_hidden = jnp.einsum("td,fd->tf", cot_low, mlp_set[3], preferred_element_type=jnp.float32)
    sigma = jax.nn.sigmoid(gate_proj)
    grad_gate_low = (grad_hidden * up_proj * sigma * (1.0 + gate_proj * (1.0 - sigma))).astype(
        jnp.bfloat16
    )
    grad_up_low = (grad_hidden * gate_proj * sigma).astype(jnp.bfloat16)
    grad_mlp_in = jnp.einsum(
        "tf,df->td", grad_gate_low, mlp_set[1], preferred_element_type=jnp.float32
    )
    grad_mlp_in = grad_mlp_in + jnp.einsum(
        "tf,df->td", grad_up_low, mlp_set[2], preferred_element_type=jnp.float32
    )
    grad_middle_norm, grad_gain_two = norm_back(grad_mlp_in, normed_two, inv_root_two, mlp_set[0])
    grad_middle = cot_float + grad_middle_norm
    grad_branch_low = grad_middle.astype(jnp.bfloat16)
    grad_attended = jnp.einsum(
        "te,de->td", grad_branch_low, attn_set[4], preferred_element_type=jnp.float32
    )
    grad_attended = grad_attended.astype(jnp.bfloat16).reshape(row_count, seq_piece, model_width)
    grad_query_rot, grad_key_full, grad_value_full = lax.map(
        attend_back, (query_rot, key_full, value_full, grad_attended, log_total, allowed)
    )
    grad_key_rot, grad_value_mix = (
        lax.psum_scatter(
            grad_key_full.astype(jnp.bfloat16), "ctx", scatter_dimension=1, tiled=True
        ).astype(jnp.float32),
        lax.psum_scatter(
            grad_value_full.astype(jnp.bfloat16), "ctx", scatter_dimension=1, tiled=True
        ).astype(jnp.float32),
    )
    v1_grad = v1_accum + 0.5 * grad_value_mix
    grad_query_low = rotate(
        grad_query_rot.reshape(row_count, seq_piece, HEADS, HEAD_DIM), cosine_table, -sine_table
    )
    grad_query_low = grad_query_low.astype(jnp.bfloat16).reshape(token_count, model_width)
    grad_key_low = rotate(
        grad_key_rot.reshape(row_count, seq_piece, HEADS, HEAD_DIM), cosine_table, -sine_table
    )
    grad_key_low = grad_key_low.astype(jnp.bfloat16).reshape(token_count, model_width)
    grad_value_low = (0.5 * grad_value_mix).astype(jnp.bfloat16).reshape(token_count, model_width)
    grad_normed_in = jnp.einsum(
        "te,de->td", grad_query_low, attn_set[1], preferred_element_type=jnp.float32
    )
    grad_normed_in = grad_normed_in + jnp.einsum(
        "te,de->td", grad_key_low, attn_set[2], preferred_element_type=jnp.float32
    )
    grad_normed_in = grad_normed_in + jnp.einsum(
        "te,de->td", grad_value_low, attn_set[3], preferred_element_type=jnp.float32
    )
    grad_input_norm, grad_gain_one = norm_back(grad_normed_in, normed, inv_root, attn_set[0])
    input_grad = (grad_middle + grad_input_norm).reshape(tokens.shape)
    attn_right = jnp.concatenate([grad_query_low, grad_key_low, grad_value_low], axis=1)
    left_in = normed_in
    projections = jnp.einsum("td,te->de", left_in, attn_right, preferred_element_type=jnp.float32)
    out_part = jnp.einsum(
        "td,te->de", attended_low, grad_branch_low, preferred_element_type=jnp.float32
    )
    attn_matrix = lax.psum_scatter(
        jnp.concatenate([projections, out_part], axis=1),
        ("dp", "ctx"),
        scatter_dimension=0,
        tiled=True,
    )
    mlp_right = jnp.concatenate([grad_gate_low, grad_up_low], axis=1)
    left_in = mlp_in
    gate_up_matrix = lax.psum_scatter(
        jnp.einsum("td,tf->df", left_in, mlp_right, preferred_element_type=jnp.float32),
        ("dp", "ctx"),
        scatter_dimension=0,
        tiled=True,
    )
    down_matrix = lax.psum_scatter(
        jnp.einsum("tf,td->fd", hidden, cot_low, preferred_element_type=jnp.float32),
        ("dp", "ctx"),
        scatter_dimension=0,
        tiled=True,
    )
    gain_one, gain_two = (
        lax.psum_scatter(grad_gain_one, ("dp", "ctx"), scatter_dimension=0, tiled=True),
        lax.psum_scatter(grad_gain_two, ("dp", "ctx"), scatter_dimension=0, tiled=True),
    )
    ff_width = w_gate.shape[1]
    return (
        output,
        input_grad,
        v1_grad,
        gain_one,
        attn_matrix[:, 0:model_width],
        attn_matrix[:, model_width : 2 * model_width],
        attn_matrix[:, 2 * model_width : 3 * model_width],
        attn_matrix[:, 3 * model_width : 4 * model_width],
        gain_two,
        gate_up_matrix[:, 0:ff_width],
        gate_up_matrix[:, ff_width : 2 * ff_width],
        down_matrix,
    )


def params(**kw):
    return pltpu.CompilerParams(vmem_limit_bytes=BYTES, **kw)


def dot(a, b, da, db):
    return lax.dot_general(a, b, (((da,), (db,)), ((), ())), preferred_element_type=F32)


def lane_block(index):
    return pl.ds(pl.multiple_of(index * LANES, LANES), LANES)


def half_swap(x):
    lane = lax.broadcasted_iota(jnp.int32, x.shape, 1)
    left = pltpu.roll(x, LANES - HEAD_DIM // 2, 1)
    right = pltpu.roll(x, HEAD_DIM // 2, 1)
    return jnp.where(lane % HEAD_DIM < HEAD_DIM // 2, left, right)


def head_lanes(x, head):
    lane = lax.broadcasted_iota(jnp.int32, x.shape, 1)
    return jnp.where(lane // HEAD_DIM == head, x, jnp.zeros_like(x))


def meet(n_ctx, bits):
    c, dp = lax.axis_index("ctx"), lax.axis_index("dp")
    barrier = pltpu.get_barrier_semaphore()
    for k in range(1, n_ctx):
        pl.semaphore_signal(barrier, inc=1, device_id={"ctx": lax.rem(c + k, n_ctx)}, device_id_type=MESH)
    for bit in bits:
        pl.semaphore_signal(barrier, inc=1, device_id={"dp": dp ^ bit}, device_id_type=MESH)
    pl.semaphore_wait(barrier, n_ctx - 1 + len(bits))


def ctx_copy(src, dst, send, recv, to):
    return pltpu.make_async_remote_copy(
        src_ref=src, dst_ref=dst, send_sem=send, recv_sem=recv, device_id={"ctx": to}, device_id_type=MESH
    )


def dp_copy(src, dst, send, recv, bit):
    to = lax.axis_index("dp") ^ bit
    return pltpu.make_async_remote_copy(
        src_ref=src, dst_ref=dst, send_sem=send, recv_sem=recv, device_id={"dp": to}, device_id_type=MESH
    )


def rows_of(index, size):
    return pl.ds(pl.multiple_of(index * size, size), size)


CORE, NEAR, FAR = 1, 2, 4


class Gather:
    def __init__(self, n_ctx, src, dst, send, recv, order):
        self.n, self.src, self.dst, self.send, self.recv = n_ctx, src, dst, send, recv
        self.first, self.second = order
        self.rows = src.shape[0]

    def place(self, c):
        return self.dst.at[0, pl.ds(c * self.rows, self.rows), :]

    def along(self, bit):
        c = lax.axis_index("ctx")
        return ctx_copy(self.src, self.place(c), self.send.at[bit - 1], self.recv.at[bit - 1], c ^ bit)

    def pass_on(self):
        c = lax.axis_index("ctx")
        return ctx_copy(self.place(c ^ 2), self.place(c ^ 2), self.send.at[2], self.recv.at[2], c ^ 1)

    def plane(self, slot, bit, at):
        return dp_copy(self.dst.at[slot], self.dst.at[slot ^ bit], self.send.at[at], self.recv.at[at], bit)

    def own(self):
        c = lax.axis_index("ctx")
        return pltpu.make_async_copy(self.src, self.dst.at[0, pl.ds(c * self.rows, self.rows), :], self.send.at[10])

    def hop(self, at):
        one, two = self.first, self.second
        slot, bit = [(0, one), (0, two), (one, two), (0, CORE), (one, CORE), (two, CORE), (one | two, CORE)][at]
        return self.plane(slot, bit, 3 + at)

    def start(self):
        self.own().start()
        self.along(2).start()
        self.along(1).start()

    def relay(self):
        self.along(2).wait_recv()
        self.pass_on().start()

    def spread(self):
        self.own().wait()
        self.along(1).wait_recv()
        self.pass_on().wait_recv()
        for at in (0, 1, 3):
            self.hop(at).start()

    def forward(self):
        self.hop(0).wait_recv()
        self.hop(2).start()
        self.hop(4).start()

    def cross(self):
        self.hop(1).wait_recv()
        self.hop(5).start()
        self.hop(2).wait_recv()
        self.hop(6).start()

    def finish(self):
        self.along(1).wait_send()
        self.along(2).wait_send()
        self.pass_on().wait_send()
        for at in range(7):
            self.hop(at).wait_send()
        for at in range(3, 7):
            self.hop(at).wait_recv()


def front_kernel(
    n_ctx, tok_ref, fv_ref, mark_ref, pack_ref, freq_ref, wg_ref, wu_ref, wo_ref, wd_ref,
    xn_ref, q_ref, k_ref, v_ref, of_ref, lse_ref, cos_ref, sin_ref, seg_ref, marks, gain_ref,
    att_ref, wg_all, wu_all, wo_all, wd_all,
    x_all, fvs, packs, whead, rel, o_ref, s_ref, m_ref, l_ref, acc_ref, p_all, total_ref,
    mark_send, mark_recv, pack_send, pack_recv, tok_send, tok_recv, fv_send, fv_recv, w_send, w_recv,
    o_send, o_recv, own, own_o,
):
    c, dp = lax.axis_index("ctx"), lax.axis_index("dp")
    tb = m_ref.shape[0]
    half = tb // 2
    model = tok_ref.shape[1]
    blocks = model // LANES
    width = q_ref.shape[1]
    own_rows = wg_ref.shape[0]
    lane = lax.broadcasted_iota(jnp.int32, (tb, LANES), 1)
    exact = lax.Precision.HIGHEST

    weights = []
    for i, (src, dst) in enumerate(((wg_ref, wg_all), (wo_ref, wo_all), (wu_ref, wu_all), (wd_ref, wd_all))):
        wide = src.shape[1] // 2
        weights.append([])
        for h, order in enumerate(((NEAR, FAR), (FAR, NEAR))):
            cols = pl.ds(h * wide, wide)
            unit = 2 * i + h
            weights[i].append(
                Gather(n_ctx, src.at[:, cols], dst.at[:, :, cols], w_send.at[unit], w_recv.at[unit], order)
            )
    gate, out, up, down = weights

    def each(what, *arrays):
        for array in arrays:
            for half_way in array:
                getattr(half_way, what)()

    def mark_copy(k):
        at = rows_of(c, tb)
        return ctx_copy(mark_ref, marks.at[:, at], mark_send.at[k - 1], mark_recv.at[k - 1], lax.rem(c + k, n_ctx))

    def pack_copy(k):
        to = lax.rem(c + k, n_ctx)
        return ctx_copy(pack_ref.at[to], packs.at[0, c], pack_send.at[k - 1], pack_recv.at[k - 1], to)

    def pack_hop(slot, bit, at):
        return dp_copy(packs.at[slot], packs.at[slot ^ bit], pack_send.at[at], pack_recv.at[at], bit)

    def fv_copy(k):
        to = lax.rem(c + k, n_ctx)
        return ctx_copy(fv_ref.at[:, rows_of(to, width)], fvs.at[rows_of(c, tb), :], fv_send.at[k - 1], fv_recv.at[k - 1], to)

    def tok_copy(bit):
        return ctx_copy(tok_ref, x_all.at[rows_of(c, tb), :], tok_send.at[bit - 1], tok_recv.at[bit - 1], c ^ bit)

    def tok_pass():
        at = rows_of(c ^ 2, tb)
        return ctx_copy(x_all.at[at, :], x_all.at[at, :], tok_send.at[2], tok_recv.at[2], c ^ 1)

    locals_ = [
        pltpu.make_async_copy(tok_ref, x_all.at[rows_of(c, tb), :], own.at[0]),
        pltpu.make_async_copy(fv_ref.at[:, rows_of(c, width)], fvs.at[rows_of(c, tb), :], own.at[1]),
        pltpu.make_async_copy(pack_ref.at[c], packs.at[0, c], own.at[2]),
        pltpu.make_async_copy(mark_ref, marks.at[:, rows_of(c, tb)], own.at[3]),
    ]

    meet(n_ctx, (CORE, NEAR, FAR))
    for k in range(1, n_ctx):
        mark_copy(k).start()
        pack_copy(k).start()
    each("start", gate, out, up)
    for m in locals_:
        m.start()

    locals_[3].wait()
    for k in range(1, n_ctx):
        mark_copy(k).wait_recv()
    row8 = lax.broadcasted_iota(jnp.int32, (8, LANES), 0)
    pick_seg = jnp.where(row8 == 0, 1.0, 0.0)
    pick_pos = jnp.where(row8 == 1, 1.0, 0.0)

    def table(b, carry):
        at = rows_of(b, tb)
        m = marks[:, at].astype(F32)
        dims = (((0,), (0,)), ((), ()))
        seg_ref[at, :] = lax.dot_general(m, pick_seg, dims, precision=exact, preferred_element_type=F32)
        pos = lax.dot_general(m, pick_pos, dims, precision=exact, preferred_element_type=F32)
        angle = pos * freq_ref[0:1, :]
        cos_ref[at, :] = jnp.cos(angle)
        sin_ref[at, :] = jnp.sin(angle) * freq_ref[1:2, :]
        return carry

    locals_[2].wait()
    for k in range(1, n_ctx):
        pack_copy(k).wait_recv()
    pack_hop(0, NEAR, 3).start()
    each("relay", gate, out, up)
    tok_copy(2).start()
    tok_copy(1).start()
    lax.fori_loop(0, n_ctx, table, 0)
    pack_hop(0, NEAR, 3).wait_recv()
    pack_hop(0, FAR, 4).start()
    pack_hop(NEAR, FAR, 5).start()
    pack_hop(0, CORE, 6).start()
    pack_hop(NEAR, CORE, 7).start()
    each("spread", gate, out, up)
    pack_hop(0, FAR, 4).wait_recv()
    pack_hop(FAR, CORE, 8).start()
    pack_hop(NEAR, FAR, 5).wait_recv()
    pack_hop(NEAR | FAR, CORE, 9).start()
    for at, (slot, bit) in enumerate([(0, CORE), (NEAR, CORE), (FAR, CORE), (NEAR | FAR, CORE)]):
        pack_hop(slot, bit, 6 + at).wait_recv()
    count = packs.shape[0]
    for t in range(3):
        block = packs[:, :, t * own_rows : (t + 1) * own_rows, :]
        whead[:, t * width : (t + 1) * width] = block.reshape(model, width)
    gains = packs[:, :, 3 * own_rows : 4 * own_rows, 0:LANES].reshape(model, LANES).astype(F32)
    gain_ref[...] = gains.T[0:8, :]
    locals_[0].wait()
    locals_[1].wait()

    def project(chunk, part):
        at = pl.ds(pl.multiple_of(chunk * tb + part * half, half), half)
        for d in range(blocks):
            rel[:, d * LANES : (d + 1) * LANES] = x_all[at, lane_block(dp ^ d)].astype(F32)
        x = rel[...]
        inv = lax.rsqrt(jnp.mean(x * x, axis=-1, keepdims=True) + epsilon)
        xn = (x * inv * gain_ref[0:1, :]).astype(LOW)
        xn_ref[at, :] = xn
        proj = dot(xn, whead[...], 1, 0)
        cos, sin = cos_ref[at, :], sin_ref[at, :]
        for b in range(width // LANES):
            cols = slice(b * LANES, (b + 1) * LANES)
            qb = proj[:, b * LANES : (b + 1) * LANES]
            q_ref[at, cols] = ((qb * cos + half_swap(qb) * sin) * 0.125).astype(LOW)
            kb = proj[:, width + b * LANES : width + (b + 1) * LANES]
            k_ref[at, cols] = (kb * cos + half_swap(kb) * sin).astype(LOW)
        of_ref[at, :] = 0.5 * proj[:, 2 * width :]

    def project_chunk(bit):
        def one(part, carry):
            project(c ^ bit, part)
            return carry

        lax.fori_loop(0, 2, one, 0)

    project_chunk(0)
    each("forward", gate, out, up)
    tok_copy(2).wait_recv()
    tok_pass().start()
    tok_copy(1).wait_recv()
    project_chunk(1)
    project_chunk(2)
    each("cross", gate, out, up)
    tok_pass().wait_recv()
    each("start", down)
    for k in range(1, n_ctx):
        fv_copy(k).start()
    project_chunk(3)

    def fold(x, op):
        r = x[:, 0:LANES]
        for b in range(1, tb // LANES):
            r = op(r, x[:, b * LANES : (b + 1) * LANES])
        return r

    def home(pair):
        return att_ref.at[:, pl.ds(pl.multiple_of(c * width + pair * LANES, LANES), LANES)]

    def weigh(pair, i):
        cols = slice(pair * LANES, (pair + 1) * LANES)
        mine = rows_of(i, tb)
        q = q_ref[mine, cols]
        seg_q = seg_ref[mine, 0:1]
        base = i * (i + 1) // 2
        for head in range(2):
            qm = head_lanes(q, head)
            m_ref[...] = jnp.full_like(m_ref, NEG)

            def score(j, causal):
                at = rows_of(j, tb)
                s = dot(qm, k_ref[at, cols], 1, 1)
                ok = seg_q == marks[0:1, at].astype(F32)
                if causal:
                    r = lax.broadcasted_iota(jnp.int32, (tb, tb), 0)
                    t = lax.broadcasted_iota(jnp.int32, (tb, tb), 1)
                    ok = ok & (r >= t)
                s = jnp.where(ok, s, NEG)
                s_ref[:, at] = s
                m_ref[...] = jnp.maximum(m_ref[...], fold(s, jnp.maximum))

            def score_step(j, carry):
                score(j, False)
                return carry

            lax.fori_loop(0, i, score_step, 0)
            score(i, True)
            top = jnp.max(m_ref[...], axis=1, keepdims=True)
            l_ref[...] = jnp.zeros_like(l_ref)

            def weight_step(j, carry):
                p = jnp.exp(s_ref[:, rows_of(j, tb)] - top)
                l_ref[...] += fold(p, jnp.add)
                p_all[2 * pair + head, base + j] = p.astype(LOW)
                return carry

            lax.fori_loop(0, i + 1, weight_step, 0)
            total = jnp.sum(l_ref[...], axis=1, keepdims=True)
            total_ref[mine, :] = jnp.where(lane == 2 * pair + head, total, total_ref[mine, :])
            lse = jnp.broadcast_to(top + jnp.log(total), (tb, LANES))
            if head == 0:
                lse_ref[mine, cols] = lse
            else:
                lse_ref[mine, cols] = jnp.where(lane < HEAD_DIM, lse_ref[mine, cols], lse)

    def mix(pair, i):
        cols = slice(pair * LANES, (pair + 1) * LANES)
        mine = rows_of(i, tb)
        base = i * (i + 1) // 2
        for head in range(2):
            acc_ref[...] = jnp.zeros_like(acc_ref)

            def value_step(j, carry):
                acc_ref[...] += dot(p_all[2 * pair + head, base + j], v_ref[rows_of(j, tb), cols], 1, 0)
                return carry

            lax.fori_loop(0, i + 1, value_step, 0)
            out = acc_ref[...] / total_ref[mine, 2 * pair + head : 2 * pair + head + 1]
            if head == 0:
                of_ref[mine, cols] = out
            else:
                of_ref[mine, cols] = jnp.where(lane < HEAD_DIM, of_ref[mine, cols], out)
        o_ref[mine, cols] = of_ref[mine, cols].astype(LOW)

        @pl.when(i == c)
        def _():
            pltpu.make_async_copy(o_ref.at[mine, cols], home(pair), own_o.at[pair]).start()

        @pl.when(i != c)
        def _():
            k = lax.rem(i + n_ctx - c, n_ctx) - 1
            ctx_copy(o_ref.at[mine, cols], home(pair), o_send.at[k, pair], o_recv.at[k, pair], i).start()

    def over_queries(what, pair, lo, hi):
        def one(i, carry):
            what(pair, i)
            return carry

        lax.fori_loop(lo, hi, one, 0)

    total_ref[...] = jnp.ones_like(total_ref)
    over_queries(weigh, 0, 0, n_ctx)
    each("relay", down)
    over_queries(weigh, 1, 0, 3)
    each("spread", down)
    over_queries(weigh, 1, 3, n_ctx)
    for k in range(1, n_ctx):
        fv_copy(k).wait_recv()

    def values(b, carry):
        at = rows_of(b, tb)
        v_ref[at, :] = (of_ref[at, :] + 0.5 * fvs[at, :].astype(F32)).astype(LOW)
        return carry

    lax.fori_loop(0, n_ctx, values, 0)
    over_queries(mix, 0, 0, n_ctx)
    each("forward", down)
    over_queries(mix, 1, 0, n_ctx)
    each("cross", down)
    for pair in range(width // LANES):
        cols = slice(pair * LANES, (pair + 1) * LANES)
        pltpu.make_async_copy(o_ref.at[0:tb, cols], home(pair), own_o.at[pair]).wait()
        for k in range(n_ctx - 1):
            ctx_copy(o_ref.at[0:tb, cols], home(pair), o_send.at[k, pair], o_recv.at[k, pair], c).wait()
    for k in range(1, n_ctx):
        mark_copy(k).wait_send()
        pack_copy(k).wait_send()
        fv_copy(k).wait_send()
    for at, (slot, bit) in enumerate(
        [(0, NEAR), (0, FAR), (NEAR, FAR), (0, CORE), (NEAR, CORE), (FAR, CORE), (NEAR | FAR, CORE)]
    ):
        pack_hop(slot, bit, 3 + at).wait_send()
    tok_copy(1).wait_send()
    tok_copy(2).wait_send()
    tok_pass().wait_send()
    each("finish", *weights)


def front_call(n_dp, n_ctx, tok, fv, mark, pack, freq, wg, wu, wo, wd):
    tb, model = tok.shape
    width = model // n_ctx
    length = n_ctx * tb
    pairs = width // LANES
    vmem = pl.BlockSpec(memory_space=pltpu.VMEM)
    anyspace = pl.BlockSpec(memory_space=pl.ANY)
    shape = jax.ShapeDtypeStruct
    dma = pltpu.SemaphoreType.DMA
    return pl.pallas_call(
        functools.partial(front_kernel, n_ctx),
        in_specs=[anyspace] * 4 + [vmem] + [anyspace] * 4,
        out_specs=[vmem] * 11 + [anyspace] * 5,
        out_shape=[shape((length, model), LOW)]
        + [shape((length, width), LOW)] * 3
        + [shape((length, width), F32)] * 2
        + [shape((length, LANES), F32)] * 3
        + [shape((8, length), jnp.int32), shape((8, model), F32)]
        + [shape((tb, model), LOW)]
        + [shape((n_dp, n_ctx * w.shape[0], w.shape[1]), LOW) for w in (wg, wu, wo, wd)],
        scratch_shapes=[
            pltpu.VMEM((length, model), LOW),
            pltpu.VMEM((length, width), LOW),
            pltpu.VMEM((n_dp,) + pack.shape, LOW),
            pltpu.VMEM((model, 3 * width), LOW),
            pltpu.VMEM((tb // 2, model), F32),
            pltpu.VMEM((length, width), LOW),
            pltpu.VMEM((tb, length), F32),
            pltpu.VMEM((tb, LANES), F32),
            pltpu.VMEM((tb, LANES), F32),
            pltpu.VMEM((tb, LANES), F32),
            pltpu.VMEM((2 * pairs, n_ctx * (n_ctx + 1) // 2, tb, tb), LOW),
            pltpu.VMEM((length, LANES), F32),
            dma((n_ctx - 1,)), dma((n_ctx - 1,)),
            dma((n_ctx + 6,)), dma((n_ctx + 6,)),
            dma((3,)), dma((3,)),
            dma((n_ctx - 1,)), dma((n_ctx - 1,)),
            dma((8, 11)), dma((8, 11)),
            dma((n_ctx - 1, pairs)), dma((n_ctx - 1, pairs)),
            dma((4,)), dma((pairs,)),
        ],
        compiler_params=params(collective_id=1, has_side_effects=True),
        cost_estimate=pl.CostEstimate(
            flops=24 * 10**9, bytes_accessed=60 * 2**20, transcendentals=2 * length * length
        ),
        name="front",
    )(tok, fv, mark, pack, freq, wg, wu, wo, wd)


class Reduce:
    def __init__(self, n_ctx, keep, came, acc, rc, rx, ry, rz, out, send, recv, order):
        self.n, self.keep, self.came, self.acc, self.rc, self.rx, self.ry, self.rz = n_ctx, keep, came, acc, rc, rx, ry, rz
        self.out, self.send, self.recv = out, send, recv
        self.one, self.two = order
        self.leave = (self.one >> 1, 3)
        self.stay = self.two >> 1

    def hop(self, at):
        src, dst, bit = [
            (self.acc.at[self.leave[0]], self.rx.at[0], self.one),
            (self.acc.at[self.leave[1]], self.rx.at[1], self.one),
            (self.acc.at[self.stay], self.ry, self.two),
        ][at - 1]
        return dp_copy(src, dst, self.send.at[at], self.recv.at[at], bit)

    def held(self):
        return pltpu.make_async_copy(self.keep, self.acc, self.send.at[7])

    def partner(self):
        return pltpu.make_async_copy(self.came, self.rc, self.send.at[0])

    def along(self, at):
        c = lax.axis_index("ctx")
        block, to = ((c ^ 1, c ^ 1), (c ^ 3, c ^ 1), (c ^ 2, c ^ 2))[at]
        return ctx_copy(self.acc.at[0, block], self.rz.at[at], self.send.at[4 + at], self.recv.at[4 + at], to)

    def begin(self):
        self.partner().start()
        self.held().start()

    def add(self, block, terms):
        def one(j, carry):
            total = self.acc[block, j].astype(F32)
            for t in terms:
                total = total + t(j).astype(F32)
            self.acc[block, j] = total.astype(LOW)
            return carry

        lax.fori_loop(0, self.acc.shape[1], one, 0)

    def step_one(self):
        self.held().wait()
        self.partner().wait()
        for at in (1, 0):
            block = self.leave[at]
            self.add(block, [lambda j, block=block: self.rc[block, j]])
            self.hop(1 + at).start()

    def step_two(self):
        self.hop(2).wait_recv()
        self.add(self.stay, [lambda j: self.rc[self.stay, j], lambda j: self.rx[1, j]])
        self.hop(3).start()

    def step_ctx(self):
        c = lax.axis_index("ctx")
        self.hop(1).wait_recv()
        self.hop(3).wait_recv()
        self.out[...] = (
            self.acc[0, c].astype(F32) + self.rc[0, c].astype(F32) + self.rx[0, c].astype(F32) + self.ry[c].astype(F32)
        )
        self.add(0, [lambda j: self.rc[0, j], lambda j: self.rx[0, j], lambda j: self.ry[j]])
        self.along(1).start()
        self.along(0).start()

    def step_far(self):
        block = lax.axis_index("ctx") ^ 2
        self.along(1).wait_recv()
        self.acc[0, block] = (self.acc[0, block].astype(F32) + self.rz[1].astype(F32)).astype(LOW)
        self.along(2).start()

    def finish(self):
        self.along(0).wait_recv()
        self.along(2).wait_recv()
        self.out[...] += self.rz[0].astype(F32) + self.rz[2].astype(F32)
        for at in range(1, 4):
            self.hop(at).wait_send()
        for at in range(3):
            self.along(at).wait_send()


def back_kernel(n_ctx, *refs):
    g_ref, q_ref, k_ref, v_ref, of_ref, lse_ref, sc_ref, sr_ref, cos_ref, sin_ref, xn_ref = refs[:11]
    sides = refs[11:19]
    home_ref, qkv_out = refs[19:21]
    outs = refs[21:25]
    (part_ref, lse_row, delta_row, dq_acc, dk_acc, dv_acc, prod) = refs[25:32]
    rest = refs[32:]
    buffers, rest = rest[:40], rest[40:]
    (pk, ps, prc, prx, pry, pz, qz) = rest[:7]
    (send, recv, own, r_send, r_recv, p_send, p_recv, z_send, z_recv) = rest[7:]
    c = lax.axis_index("ctx")
    tb = dk_acc.shape[0]
    length, width = q_ref.shape
    model = n_ctx * width
    pairs = width // LANES
    blocks = model // LANES
    orders = ((NEAR, FAR), (FAR, NEAR))
    groups = []
    for i in range(4):
        keep, came = sides[2 * i], sides[2 * i + 1]
        wide = keep.shape[3] // 2
        groups.append([])
        for h, order in enumerate(orders):
            cols = pl.ds(h * wide, wide)
            unit = 2 * i + h
            groups[i].append(
                Reduce(
                    n_ctx, keep.at[:, :, :, cols], came.at[:, :, :, cols], *buffers[5 * unit : 5 * unit + 5],
                    outs[i].at[:, cols], r_send.at[unit], r_recv.at[unit], order,
                )
            )

    def each(i, what):
        for unit in groups[i]:
            getattr(unit, what)()

    def home(pair, t):
        return home_ref.at[:, pl.ds(pl.multiple_of(t * model + c * width + pair * LANES, LANES), LANES)]

    def part(pair, t, chunk):
        return part_ref.at[pair, rows_of(chunk, tb), pl.ds(t * LANES, LANES)]

    def part_copy(pair, t, k, to):
        return ctx_copy(part(pair, t, to), home(pair, t), send.at[k - 1, pair, t], recv.at[k - 1, pair, t], to)

    def part_own(pair, t):
        return pltpu.make_async_copy(part(pair, t, c), home(pair, t), own.at[pair, t])

    meet(n_ctx, (CORE, NEAR, FAR))
    for i in range(4):
        each(i, "begin")
    each(0, "step_one")

    r8 = lax.broadcasted_iota(jnp.int32, (8, LANES), 0)
    l8 = lax.broadcasted_iota(jnp.int32, (8, LANES), 1)
    pick = jnp.where(l8 == r8 * HEAD_DIM, 1.0, 0.0)
    group = jnp.where(l8 // HEAD_DIM == r8, 1.0, 0.0)
    exact = lax.Precision.HIGHEST
    dims = (((1,), (1,)), ((), ()))

    def stats(pair):
        cols = slice(pair * LANES, (pair + 1) * LANES)

        def one(b, carry):
            at = rows_of(b, tb)
            lse_row[:, at] = lax.dot_general(pick, lse_ref[at, cols], dims, precision=exact, preferred_element_type=F32)
            mixed = g_ref[at, cols].astype(F32) * of_ref[at, cols]
            delta_row[:, at] = lax.dot_general(group, mixed, dims, precision=exact, preferred_element_type=F32)
            dq_acc[at, :] = jnp.zeros((tb, LANES), F32)
            return carry

        lax.fori_loop(0, n_ctx, one, 0)

    def key_blocks(pair, lo, hi):
        cols = slice(pair * LANES, (pair + 1) * LANES)

        def key_block(j, carry):
            dk_acc[...] = jnp.zeros_like(dk_acc)
            dv_acc[...] = jnp.zeros_like(dv_acc)
            mine = rows_of(j, tb)
            k = k_ref[mine, cols]
            v = v_ref[mine, cols]
            seg_k = sc_ref[mine, 0:1]

            def block(i, causal):
                at = rows_of(i, tb)
                q = q_ref[at, cols]
                g = g_ref[at, cols]
                ok = seg_k == sr_ref[0:1, at].astype(F32)
                if causal:
                    r = lax.broadcasted_iota(jnp.int32, (tb, tb), 0)
                    t = lax.broadcasted_iota(jnp.int32, (tb, tb), 1)
                    ok = ok & (r <= t)
                for head in range(2):
                    qm = head_lanes(q, head)
                    gm = head_lanes(g, head)
                    s = dot(k, qm, 1, 1)
                    p = jnp.where(ok, jnp.exp(s - lse_row[head : head + 1, at]), 0.0)
                    dp = dot(v, gm, 1, 1)
                    ds = (p * (dp - delta_row[head : head + 1, at])).astype(LOW)
                    dv_acc[...] += dot(p.astype(LOW), gm, 1, 0)
                    dk_acc[...] += dot(ds, qm, 1, 0)
                    dq_acc[at, :] += dot(ds, head_lanes(k, head), 0, 0)

            block(j, True)

            def step(i, carry):
                block(i, False)
                return carry

            lax.fori_loop(j + 1, n_ctx, step, 0)
            dk = dk_acc[...]
            dk = dk * cos_ref[mine, :] - half_swap(dk) * sin_ref[mine, :]
            part_ref[pair, mine, LANES : 2 * LANES] = dk.astype(LOW)
            part_ref[pair, mine, 2 * LANES : 3 * LANES] = dv_acc[...].astype(LOW)
            dq = dq_acc[mine, :] * 0.125
            dq = dq * cos_ref[mine, :] - half_swap(dq) * sin_ref[mine, :]
            part_ref[pair, mine, 0:LANES] = dq.astype(LOW)

            @pl.when(j == c)
            def _():
                for t in range(3):
                    part_own(pair, t).start()

            @pl.when(j != c)
            def _():
                for t in range(3):
                    part_copy(pair, t, lax.rem(j + n_ctx - c, n_ctx), j).start()

            return carry

        lax.fori_loop(lo, hi, key_block, 0)

    def pair_hop(pair, at):
        src, dst, bit = [
            (ps.at[pair], prc.at[pair], CORE),
            (pk.at[pair, 1], prx.at[pair, 0], NEAR),
            (pk.at[pair, 3], prx.at[pair, 1], NEAR),
            (pk.at[pair, 2], pry.at[pair], FAR),
        ][at]
        return dp_copy(src, dst, p_send.at[pair, at], p_recv.at[pair, at], bit)

    def pair_ctx(pair, k):
        to = lax.rem(c + k, n_ctx)
        return ctx_copy(pz.at[pair, to], qz.at[c, pair], z_send.at[pair, k - 1], z_recv.at[pair, k - 1], to)

    def pair_product(pair):
        prod[...] = jnp.zeros_like(prod)

        def one(b, carry):
            at = rows_of(b, tb)
            prod[...] += dot(part_ref[pair, at, :], xn_ref[at, :], 0, 0)
            return carry

        lax.fori_loop(0, n_ctx, one, 0)
        for d in range(blocks):
            (ps if d % 2 else pk)[pair, d // 2] = prod[:, d * LANES : (d + 1) * LANES].astype(LOW)
        pair_hop(pair, 0).start()

    def pair_one(pair):
        pair_hop(pair, 0).wait_recv()
        for i in (3, 1):
            pk[pair, i] = (pk[pair, i].astype(F32) + prc[pair, i].astype(F32)).astype(LOW)
            pair_hop(pair, 1 + i // 2).start()

    def pair_two(pair):
        pair_hop(pair, 2).wait_recv()
        total = pk[pair, 2].astype(F32) + prc[pair, 2].astype(F32) + prx[pair, 1].astype(F32)
        pk[pair, 2] = total.astype(LOW)
        pair_hop(pair, 3).start()

    def pair_three(pair):
        pair_hop(pair, 1).wait_recv()
        pair_hop(pair, 3).wait_recv()
        total = pk[pair, 0].astype(F32) + prc[pair, 0].astype(F32) + prx[pair, 0].astype(F32) + pry[pair].astype(F32)
        pz[pair] = total.T.reshape(pz.shape[1:]).astype(LOW)
        qz[c, pair] = pz[pair, c]
        for k in range(1, n_ctx):
            pair_ctx(pair, k).start()

    def pair_finish(pair):
        for k in range(1, n_ctx):
            pair_ctx(pair, k).wait()
        for at in range(4):
            pair_hop(pair, at).wait_send()

    middle = n_ctx // 2
    stats(0)
    key_blocks(0, 0, middle)
    each(0, "step_two")
    each(1, "step_one")
    key_blocks(0, middle, n_ctx)
    pair_product(0)
    each(0, "step_ctx")
    stats(1)
    key_blocks(1, 0, middle)
    each(1, "step_two")
    each(2, "step_one")
    pair_one(0)
    key_blocks(1, middle, n_ctx)
    each(0, "step_far")
    each(1, "step_ctx")
    pair_product(1)
    pair_two(0)
    each(2, "step_two")
    each(3, "step_one")
    pair_one(1)
    pair_three(0)
    each(1, "step_far")
    each(2, "step_ctx")
    pair_two(1)
    each(3, "step_two")
    each(2, "step_far")
    pair_three(1)
    each(3, "step_ctx")
    each(3, "step_far")
    for pair in range(pairs):
        pair_finish(pair)
        for s in range(n_ctx):
            for t in range(3):
                at = t * model + s * width + pair * LANES
                qkv_out[:, at : at + LANES] = qz[s, pair, :, t * LANES : (t + 1) * LANES].astype(F32)
    for i in range(4):
        each(i, "finish")
    for pair in range(pairs):
        for t in range(3):
            part_own(pair, t).wait()
            for k in range(1, n_ctx):
                part_copy(pair, t, k, lax.rem(c + k, n_ctx)).wait()


def back_call(n_ctx, g, q, k, v, of, lse, seg_col, seg_row, cos, sin, xn, sides):
    length, width = q.shape
    model = n_ctx * width
    tb = TOKEN_BLOCK
    pairs = width // LANES
    own_rows = model // (model // LANES) // n_ctx
    vmem = pl.BlockSpec(memory_space=pltpu.VMEM)
    anyspace = pl.BlockSpec(memory_space=pl.ANY)
    shape = jax.ShapeDtypeStruct
    dma = pltpu.SemaphoreType.DMA
    buffers = []
    for keep in sides[::2]:
        four, parts, rows, cols = keep.shape
        for lead in ((four, parts), (four, parts), (2, parts), (parts,), (3,)) * 2:
            buffers.append(pltpu.VMEM(lead + (rows, cols // 2), LOW))
    wide = 3 * LANES
    return pl.pallas_call(
        functools.partial(back_kernel, n_ctx),
        in_specs=[vmem] * 11 + [anyspace] * 8,
        out_specs=[anyspace] + [vmem] * 5,
        out_shape=[shape((tb, 3 * model), LOW), shape((own_rows, 3 * model), F32)]
        + [shape(keep.shape[2:], F32) for keep in sides[::2]],
        scratch_shapes=[
            pltpu.VMEM((pairs, length, wide), LOW),
            pltpu.VMEM((8, length), F32),
            pltpu.VMEM((8, length), F32),
            pltpu.VMEM((length, LANES), F32),
            pltpu.VMEM((tb, LANES), F32),
            pltpu.VMEM((tb, LANES), F32),
            pltpu.VMEM((wide, model), F32),
        ]
        + buffers
        + [
            pltpu.VMEM((pairs, 4, wide, LANES), LOW),
            pltpu.VMEM((pairs, 4, wide, LANES), LOW),
            pltpu.VMEM((pairs, 4, wide, LANES), LOW),
            pltpu.VMEM((pairs, 2, wide, LANES), LOW),
            pltpu.VMEM((pairs, wide, LANES), LOW),
            pltpu.VMEM((pairs, n_ctx, own_rows, wide), LOW),
            pltpu.VMEM((n_ctx, pairs, own_rows, wide), LOW),
            dma((n_ctx - 1, pairs, 3)), dma((n_ctx - 1, pairs, 3)),
            dma((pairs, 3)),
            dma((8, 8)), dma((8, 8)),
            dma((pairs, 4)), dma((pairs, 4)),
            dma((pairs, n_ctx - 1)), dma((pairs, n_ctx - 1)),
        ],
        compiler_params=params(collective_id=3, has_side_effects=True),
        cost_estimate=pl.CostEstimate(
            flops=40 * 10**9, bytes_accessed=60 * 2**20, transcendentals=2 * length * length
        ),
        name="back",
    )(g, q, k, v, of, lse, seg_col, seg_row, cos, sin, xn, *sides)


def mlp_kernel(
    blocks, n_ctx, tok_ref, att_ref, cot_ref, gain_ref, wo_in, wg_in, wu_in, wd_in, wq_ref, wr_ref,
    out_ref, gm_ref, gh_ref, gk, gc, uk, uc, ok, oc, dk, dc, wq_all, wr_all,
    wo, wg, wu, wd, att, nat, n2, mi, mit, oacc, dacc, hid_all, dg_all, du_all, stage, ostage,
    sem, hop_send, hop_recv, st_own, st_send, st_recv, o_sem, d_own, d_send, d_recv, g_send, g_recv,
):
    c, dp = lax.axis_index("ctx"), lax.axis_index("dp")
    tb, model = tok_ref.shape
    width = model // n_ctx
    ff = wu.shape[1]
    steps = ff // FF_BLOCK
    down = wd_in.shape[1]
    half = blocks // 2
    attn = [
        Gather(n_ctx, wq_ref, wq_all, hop_send.at[0], hop_recv.at[0], (NEAR, FAR)),
        Gather(n_ctx, wr_ref, wr_all, hop_send.at[1], hop_recv.at[1], (FAR, NEAR)),
    ]

    loads = []
    for d in range(blocks):
        at = pl.ds(d * LANES, LANES)
        loads.append(pltpu.make_async_copy(wo_in.at[d], wo.at[at, :], sem.at[0, d]))
    for d in range(blocks):
        at = pl.ds(d * LANES, LANES)
        rows = pl.ds(pl.multiple_of((dp ^ d) * down, 32), down)
        loads.append(pltpu.make_async_copy(wg_in.at[d], wg.at[at, :], sem.at[1, d]))
        loads.append(pltpu.make_async_copy(wu_in.at[d], wu.at[at, :], sem.at[2, d]))
        loads.append(pltpu.make_async_copy(wd_in.at[d], wd.at[rows, :], sem.at[3, d]))
    for m in loads:
        m.start()
    for d in range(blocks):
        att[:, d * LANES : (d + 1) * LANES] = att_ref[:, lane_block(dp ^ d)]
    meet(n_ctx, (CORE, NEAR, FAR))
    for w in attn:
        w.start()
    for m in loads[:blocks]:
        m.wait()
    mid = tok_ref[...].astype(F32) + dot(att[...], wo[...], 1, 0)
    inv = lax.rsqrt(jnp.mean(mid * mid, axis=-1, keepdims=True) + epsilon)
    oacc[...] = mid
    nat[...] = mid * inv
    for d in range(blocks):
        n2[:, d * LANES : (d + 1) * LANES] = nat[:, lane_block(dp ^ d)]
    mi[...] = (n2[...] * gain_ref[1:2, :]).astype(LOW)
    mit[...] = mi[...].T
    dacc[...] = jnp.zeros_like(dacc)
    for m in loads[blocks:]:
        m.wait()

    def columns(u):
        return pl.ds(pl.multiple_of(u * FF_BLOCK, FF_BLOCK), FF_BLOCK)

    def data_step(u, carry):
        cols = columns(u)
        x = mi[...]
        cot = cot_ref[...]
        wgu, wuu, wdu = wg[:, cols], wu[:, cols], wd[cols, :]
        gate = dot(x, wgu, 1, 0)
        up = dot(x, wuu, 1, 0)
        grad_hidden = dot(cot, wdu, 1, 1)
        sig = jax.nn.sigmoid(gate)
        hidden = (gate * sig * up).astype(LOW)
        dg = (grad_hidden * up * sig * (1.0 + gate * (1.0 - sig))).astype(LOW)
        du = (grad_hidden * gate * sig).astype(LOW)
        hid_all[:, cols] = hidden
        dg_all[:, cols] = dg
        du_all[:, cols] = du
        oacc[...] += dot(hidden, wdu, 1, 0)
        dacc[...] += dot(dg, wgu, 1, 1) + dot(du, wuu, 1, 1)
        return carry

    lax.fori_loop(0, 2, data_step, 0)
    for w in attn:
        w.relay()
    lax.fori_loop(2, 5, data_step, 0)
    for w in attn:
        w.spread()
    lax.fori_loop(5, steps, data_step, 0)

    out_ref[...] = oacc[...].astype(LOW)
    scaled = dacc[...] * gain_ref[1:2, :]
    norm = n2[...]
    mean = jnp.mean(scaled * norm, axis=-1, keepdims=True)
    n2[...] = inv * (scaled - norm * mean)
    for d in range(blocks):
        nat[:, lane_block(dp ^ d)] = n2[:, d * LANES : (d + 1) * LANES]
    gm = cot_ref[...].astype(F32) + nat[...]
    gm_ref[...] = gm
    gb = gm.astype(LOW)
    n2[...] = dot(gb, wo[...], 1, 1)
    for d in range(blocks):
        mi[:, lane_block(dp ^ d)] = n2[:, d * LANES : (d + 1) * LANES].astype(LOW)

    def grad_copy(k):
        to = lax.rem(c + k, n_ctx)
        return ctx_copy(mi.at[:, rows_of(to, width)], gh_ref.at[rows_of(c, tb), :], g_send.at[k - 1], g_recv.at[k - 1], to)

    grad_own = pltpu.make_async_copy(mi.at[:, rows_of(c, width)], gh_ref.at[rows_of(c, tb), :], o_sem.at[2])
    for k in range(1, n_ctx):
        grad_copy(k).start()
    grad_own.start()
    for w in attn:
        w.forward()

    def down_step(u, carry):
        cols = columns(u)
        wd[cols, :] = dot(hid_all[:, cols], cot_ref[...], 0, 0).astype(LOW)
        return carry

    lax.fori_loop(0, steps, down_step, 0)

    def down_copy(d):
        rows = pl.ds(pl.multiple_of((dp ^ d) * down, 32), down)
        if d % 2:
            return dp_copy(wd.at[rows, :], dc.at[d // 2], d_send.at[d // 2], d_recv.at[d // 2], CORE)
        return pltpu.make_async_copy(wd.at[rows, :], dk.at[d // 2], d_own.at[d // 2])

    for d in range(blocks):
        down_copy(d).start()

    dwo = dot(att[...], gb, 0, 0).astype(LOW)
    for d in range(blocks):
        ostage[d % 2, d // 2] = dwo[d * LANES : (d + 1) * LANES]
    out_own = pltpu.make_async_copy(ostage.at[0], ok, o_sem.at[0])
    out_gone = dp_copy(ostage.at[1], oc, o_sem.at[1], o_sem.at[3], CORE)
    out_own.start()
    out_gone.start()

    def side(u, t, which):
        slot = lax.rem(u, 2)
        cols = columns(u)
        keep, came = ((gk, gc), (uk, uc))[t]
        if which == 0:
            return pltpu.make_async_copy(stage.at[slot, t, 0], keep.at[:, :, cols], st_own.at[slot, t])
        return dp_copy(stage.at[slot, t, 1], came.at[:, :, cols], st_send.at[slot, t], st_recv.at[t, u], CORE)

    def weight_step(u, carry):
        cols = columns(u)

        @pl.when(u >= 2)
        def _():
            for t in range(2):
                side(u - 2, t, 0).wait()
                side(u - 2, t, 1).wait_send()

        slot = lax.rem(u, 2)
        for t, grad in enumerate((dg_all, du_all)):
            dw = dot(mit[...], grad[:, cols], 1, 0).astype(LOW)
            for d in range(blocks):
                stage[slot, t, d % 2, d // 2] = dw[d * LANES : (d + 1) * LANES]
            side(u, t, 0).start()
            side(u, t, 1).start()
        return carry

    lax.fori_loop(0, 3, weight_step, 0)
    for w in attn:
        w.cross()
    lax.fori_loop(3, steps, weight_step, 0)

    for u in (steps - 2, steps - 1):
        for t in range(2):
            side(u, t, 0).wait()
            side(u, t, 1).wait_send()

    def arrived(u, carry):
        for t in range(2):
            side(u, t, 1).wait_recv()
        return carry

    lax.fori_loop(0, steps, arrived, 0)
    out_own.wait()
    out_gone.wait()
    for d in range(blocks):
        down_copy(d).wait()
    grad_own.wait()
    for k in range(1, n_ctx):
        grad_copy(k).wait()
    for w in attn:
        w.finish()


def mlp_call(n_ctx, tok, att, cot, gain, wo, wg, wu, wd, wq, wr):
    tb, model = tok.shape
    blocks, _, ff = wg.shape
    half = blocks // 2
    down = wd.shape[1]
    width = model // n_ctx
    vmem = pl.BlockSpec(memory_space=pltpu.VMEM)
    anyspace = pl.BlockSpec(memory_space=pl.ANY)
    shape = jax.ShapeDtypeStruct
    dma = pltpu.SemaphoreType.DMA
    return pl.pallas_call(
        functools.partial(mlp_kernel, blocks, n_ctx),
        in_specs=[vmem] * 4 + [anyspace] * 6,
        out_specs=[vmem] * 2 + [anyspace] * 11,
        out_shape=[shape((tb, model), LOW), shape((tb, model), F32), shape((n_ctx * tb, width), LOW)]
        + [shape((half, LANES, ff), LOW)] * 4
        + [shape((half, LANES, model), LOW)] * 2
        + [shape((half, down, model), LOW)] * 2
        + [shape((blocks, n_ctx * w.shape[0], w.shape[1]), LOW) for w in (wq, wr)],
        scratch_shapes=[
            pltpu.VMEM((model, model), LOW),
            pltpu.VMEM((model, ff), LOW),
            pltpu.VMEM((model, ff), LOW),
            pltpu.VMEM((ff, model), LOW),
            pltpu.VMEM((tb, model), LOW),
            pltpu.VMEM((tb, model), F32),
            pltpu.VMEM((tb, model), F32),
            pltpu.VMEM((tb, model), LOW),
            pltpu.VMEM((model, tb), LOW),
            pltpu.VMEM((tb, model), F32),
            pltpu.VMEM((tb, model), F32),
            pltpu.VMEM((tb, ff), LOW),
            pltpu.VMEM((tb, ff), LOW),
            pltpu.VMEM((tb, ff), LOW),
            pltpu.VMEM((2, 2, 2, half, LANES, FF_BLOCK), LOW),
            pltpu.VMEM((2, half, LANES, model), LOW),
            dma((4, blocks)),
            dma((2, 11)), dma((2, 11)),
            dma((2, 2)), dma((2, 2)), dma((2, ff // FF_BLOCK)),
            dma((4,)),
            dma((half,)), dma((half,)), dma((half,)),
            dma((n_ctx - 1,)), dma((n_ctx - 1,)),
        ],
        compiler_params=params(collective_id=2, has_side_effects=True),
        cost_estimate=pl.CostEstimate(
            flops=2 * tb * model * (8 * ff + 3 * model), bytes_accessed=50 * 2**20, transcendentals=0
        ),
        name="mlp",
    )(tok, att, cot, gain, wo, wg, wu, wd, wq, wr)


def input_kernel(
    blocks, tok_ref, gm_ref, v1_ref, y_ref, g, gain_ref, own_gain, qkv_ref, gate_ref, up_ref, out_ref, down_ref,
    wq_ref, wr_ref, wgate_ref, wup_ref, wq_all, wr_all,
    ig_ref, vg_ref, yo_ref, gq_ref, gk_ref, gv_ref, go_ref, gg_ref, gu_ref, gd_ref, gains_ref, w, rel, nat, sem,
):
    dp = lax.axis_index("dp")
    model = tok_ref.shape[1]
    cut = wq_ref.shape[1]
    made = []
    for d in range(blocks):
        at = pl.ds(d * LANES, LANES)
        made.append(pltpu.make_async_copy(wq_all.at[d], w.at[at, pl.ds(0, cut)], sem.at[0, d]))
        made.append(pltpu.make_async_copy(wr_all.at[d], w.at[at, pl.ds(cut, 3 * model - cut)], sem.at[1, d]))

    def row_dot(a, b):
        return jnp.sum(a * b.astype(F32), axis=1, keepdims=True)

    @pl.when(pl.program_id(0) == 0)
    def _():
        for m in made:
            m.start()
        gq_ref[...] = qkv_ref[:, :model]
        gk_ref[...] = qkv_ref[:, model : 2 * model]
        gv_ref[...] = 0.5 * qkv_ref[:, 2 * model :]
        go_ref[...] = out_ref[...]
        gg_ref[...] = gate_ref[...]
        gu_ref[...] = up_ref[...]
        gd_ref[...] = down_ref[...]
        both = 2 * model - cut
        one = row_dot(qkv_ref[:, :cut], wq_ref[...]) + row_dot(qkv_ref[:, cut : 2 * model], wr_ref[:, :both])
        one = one + row_dot(gv_ref[...], wr_ref[:, both:])
        two = row_dot(gate_ref[...], wgate_ref[...]) + row_dot(up_ref[...], wup_ref[...])
        lane = lax.broadcasted_iota(jnp.int32, gains_ref.shape, 1)
        own = own_gain[...].astype(F32)
        gains_ref[...] = jnp.where(lane == 0, one / own[:, 0:1], two / own[:, 1:2])

    yo_ref[...] = y_ref[...]
    for d in range(blocks):
        rel[:, d * LANES : (d + 1) * LANES] = tok_ref[:, lane_block(dp ^ d)].astype(F32)
    gv = g[:, 2 * model :].astype(F32)
    vg_ref[...] = v1_ref[...] + 0.5 * gv

    x = rel[...]
    inv = lax.rsqrt(jnp.mean(x * x, axis=-1, keepdims=True) + epsilon)
    norm = x * inv

    @pl.when(pl.program_id(0) == 0)
    def _():
        for m in made:
            m.wait()

    grad = dot(g[:, : 2 * model], w[:, : 2 * model], 1, 1)
    grad = grad + 0.5 * dot(g[:, 2 * model :], w[:, 2 * model :], 1, 1)
    scaled = grad * gain_ref[0:1, :]
    mean = jnp.mean(scaled * norm, axis=-1, keepdims=True)
    rel[...] = inv * (scaled - norm * mean)
    for d in range(blocks):
        nat[:, lane_block(dp ^ d)] = rel[:, d * LANES : (d + 1) * LANES]
    ig_ref[...] = gm_ref[...] + nat[...]


def input_call(tok, gm, v1, y, g, gain, own_gain, qkv, grads, wq, wr, wgate, wup, wq_all, wr_all):
    tb, model = tok.shape
    blocks = wq_all.shape[0]
    rows = qkv.shape[0]
    part = tb // 2
    shape = jax.ShapeDtypeStruct
    token = lambda cols: pl.BlockSpec((part, cols), lambda i: (i, 0))
    whole = lambda a: pl.BlockSpec(a.shape, lambda i: (0, 0))
    small = [gain, own_gain, qkv, *grads, wq, wr, wgate, wup]
    ends = [shape((rows, model), F32)] * 4 + [shape(x.shape, F32) for x in (grads[0], grads[1], grads[3])]
    ends.append(shape((rows, LANES), F32))
    return pl.pallas_call(
        functools.partial(input_kernel, blocks),
        grid=(tb // part,),
        in_specs=[token(model)] * 4 + [token(3 * model)] + [whole(x) for x in small] + [pl.BlockSpec(memory_space=pl.ANY)] * 2,
        out_specs=[token(model)] * 3 + [whole(x) for x in ends],
        out_shape=[shape((tb, model), F32)] * 2 + [shape((tb, model), LOW)] + ends,
        scratch_shapes=[
            pltpu.VMEM((model, 3 * model), LOW),
            pltpu.VMEM((part, model), F32),
            pltpu.VMEM((part, model), F32),
            pltpu.SemaphoreType.DMA((2, blocks)),
        ],
        compiler_params=params(),
        cost_estimate=pl.CostEstimate(
            flops=2 * tb * model * 3 * model, bytes_accessed=20 * 2**20, transcendentals=0
        ),
        name="input_grad",
    )(tok, gm, v1, y, g, *small, wq_all, wr_all)


def fast_local(
    n_dp, n_ctx, tokens, first_values, v1_accum, segment_ids, positions, cotangent,
    attn_gain, w_query, w_key, w_value, w_out, mlp_gain, w_gate, w_up, w_down,
):
    seq, model = tokens.shape[1:]
    width = model // n_ctx
    own_rows = w_query.shape[0]
    tok = tokens[0]
    mark = jnp.concatenate([segment_ids, positions, jnp.zeros((6, seq), jnp.int32)], axis=0)
    gains = jnp.stack([attn_gain, mlp_gain], axis=1)
    gains = jnp.tile(jnp.pad(gains, ((0, 0), (0, width - 2))), (1, n_ctx))
    pack = jnp.concatenate([w_query, w_key, w_value, gains], axis=0)
    pack = pack.reshape(4 * own_rows, n_ctx, width).transpose(1, 0, 2)
    freqs = 10000.0 ** (-np.arange(HEAD_DIM // 2).astype(np.float32) * np.float32(2.0 / HEAD_DIM))
    freq = np.zeros((8, LANES), np.float32)
    freq[0] = np.tile(freqs.astype(np.float32), LANES // (HEAD_DIM // 2))
    freq[1] = np.where(np.arange(LANES) % HEAD_DIM < HEAD_DIM // 2, -1.0, 1.0)
    freq = jnp.asarray(freq)
    (xn, q, k, v, out_full, log_total, cos, sin, seg_col, seg_row, gain_rows, attended,
     gate_all, up_all, out_all, down_all) = front_call(
        n_dp, n_ctx, tok, first_values[0], mark, pack, freq, w_gate, w_up, w_out, w_down
    )
    cut = model // 2
    wq = jnp.concatenate([w_query, w_key[:, :cut]], axis=1)
    wr = jnp.concatenate([w_key[:, cut:], w_value], axis=1)
    (output, grad_middle, head_grad, gate_keep, gate_came, up_keep, up_came, out_keep, out_came,
     down_keep, down_came, wq_all, wr_all) = mlp_call(
        n_ctx, tok, attended, cotangent[0], gain_rows, out_all, gate_all, up_all, down_all, wq, wr
    )
    sides = [
        x.reshape(x.shape[0], n_ctx, x.shape[1] // n_ctx, x.shape[2])
        for x in (gate_keep, gate_came, up_keep, up_came, out_keep, out_came, down_keep, down_came)
    ]
    home_grad, qkv_grad, *grads = back_call(
        n_ctx, head_grad, q, k, v, out_full, log_total, seg_col, seg_row, cos, sin, xn, sides
    )
    (input_grad, v1_grad, output, query_grad, key_grad, value_grad, out_grad, gate_grad, up_grad, down_grad,
     gain_grads) = input_call(
        tok, grad_middle, v1_accum[0], output, home_grad, gain_rows, gains, qkv_grad, grads,
        wq, wr, w_gate, w_up, wq_all, wr_all
    )
    return (
        output[None], input_grad[None], v1_grad[None], gain_grads[:, 0], query_grad, key_grad, value_grad,
        out_grad, gain_grads[:, 1], gate_grad, up_grad, down_grad,
    )


def solution(mesh):
    placed = (
        P("dp", "ctx", None),
        P("dp", "ctx", None),
        P("dp", "ctx", None),
        P("dp", "ctx"),
        P("dp", "ctx"),
        P("dp", "ctx", None),
        P(("dp", "ctx")),
        P(("dp", "ctx"), None),
        P(("dp", "ctx"), None),
        P(("dp", "ctx"), None),
        P(("dp", "ctx"), None),
        P(("dp", "ctx")),
        P(("dp", "ctx"), None),
        P(("dp", "ctx"), None),
        P(("dp", "ctx"), None),
    )
    n_dp, n_ctx = mesh.shape["dp"], mesh.shape["ctx"]

    def local(*args):
        rows, seq, model = args[0].shape
        fits = (
            rows == 1
            and seq == TOKEN_BLOCK
            and model == n_dp * LANES
            and n_ctx == 4
            and model == 2 * LANES * n_ctx
            and args[12].shape[1] % FF_BLOCK == 0
        )
        return fast_local(n_dp, n_ctx, *args) if fits else plain_local(*args)

    return jax.shard_map(
        local,
        mesh=mesh,
        in_specs=placed,
        out_specs=(
            P("dp", "ctx", None),
            P("dp", "ctx", None),
            P("dp", "ctx", None),
            P(("dp", "ctx")),
            P(("dp", "ctx"), None),
            P(("dp", "ctx"), None),
            P(("dp", "ctx"), None),
            P(("dp", "ctx"), None),
            P(("dp", "ctx")),
            P(("dp", "ctx"), None),
            P(("dp", "ctx"), None),
            P(("dp", "ctx"), None),
        ),
        check_vma=False,
    )
```

```python
import functools

import jax
import jax.numpy as jnp
import numpy as np
from jax import lax
from jax.experimental import pallas as pl
from jax.experimental.pallas import tpu as pltpu
from jax.sharding import PartitionSpec as P

HEADS = 16
HEAD_DIM = 64
LANES = 128
TOKEN_BLOCK = 512
FF_BLOCK = 256
NEG = -1e30
MESH = pl.DeviceIdType.MESH
F32 = jnp.float32
LOW = jnp.bfloat16
BYTES = 63 * 2**20
epsilon = 1e-05


HEAD_BLOCK = 4


def rms_scale(values):
    return lax.rsqrt(jnp.mean(values * values, axis=-1, keepdims=True) + epsilon)


def angle_tables(position_rows):
    freqs = 10000.0 ** (-jnp.arange(HEAD_DIM // 2).astype(jnp.float32) * (2.0 / HEAD_DIM))
    angles = position_rows.astype(jnp.float32)[..., None] * freqs
    return (jnp.cos(angles)[..., None, :], jnp.sin(angles)[..., None, :])


def rotate(heads_in, cosine_table, sine_table):
    half_dim = heads_in.shape[-1] // 2
    first_half = heads_in[..., :half_dim]
    second_half = heads_in[..., half_dim:]
    return jnp.concatenate(
        [
            first_half * cosine_table - second_half * sine_table,
            second_half * cosine_table + first_half * sine_table,
        ],
        axis=-1,
    )


def norm_back(grad_normed, normed, inv_root, norm_gain):
    grad_scaled = grad_normed * norm_gain.astype(jnp.float32)
    grad_input = inv_root * (
        grad_scaled - normed * jnp.mean(grad_scaled * normed, axis=-1, keepdims=True)
    )
    return (grad_input, jnp.sum(grad_normed * normed, axis=0))


def attn_front(flat_tokens, first_flat, attn_set, cosine_table, sine_table, row_count, seq_piece):
    inv_root = rms_scale(flat_tokens)
    normed = flat_tokens * inv_root
    normed_in = (normed * attn_set[0].astype(jnp.float32)).astype(jnp.bfloat16)
    query_proj = jnp.dot(normed_in, attn_set[1], preferred_element_type=jnp.float32)
    key_proj = jnp.dot(normed_in, attn_set[2], preferred_element_type=jnp.float32)
    value_proj = jnp.dot(normed_in, attn_set[3], preferred_element_type=jnp.float32)
    query_rot = rotate(
        query_proj.reshape(row_count, seq_piece, HEADS, HEAD_DIM), cosine_table, sine_table
    )
    key_rot = rotate(
        key_proj.reshape(row_count, seq_piece, HEADS, HEAD_DIM), cosine_table, sine_table
    )
    query_rot = query_rot.astype(jnp.bfloat16).reshape(row_count, seq_piece, -1)
    key_rot = key_rot.astype(jnp.bfloat16).reshape(row_count, seq_piece, -1)
    value_mix = (
        (0.5 * value_proj + 0.5 * first_flat).astype(jnp.bfloat16).reshape(row_count, seq_piece, -1)
    )
    return (normed, inv_root, normed_in, query_rot, key_rot, value_mix)


def mlp_block(flat_tokens, attended_low, out_weight, mlp_set):
    middle = flat_tokens + jnp.dot(attended_low, out_weight, preferred_element_type=jnp.float32)
    inv_root_two = rms_scale(middle)
    normed_two = middle * inv_root_two
    mlp_in = (normed_two * mlp_set[0].astype(jnp.float32)).astype(jnp.bfloat16)
    gate_proj = jnp.dot(mlp_in, mlp_set[1], preferred_element_type=jnp.float32)
    up_proj = jnp.dot(mlp_in, mlp_set[2], preferred_element_type=jnp.float32)
    hidden = (gate_proj * jax.nn.sigmoid(gate_proj) * up_proj).astype(jnp.bfloat16)
    result = middle + jnp.dot(hidden, mlp_set[3], preferred_element_type=jnp.float32)
    return (normed_two, inv_root_two, mlp_in, gate_proj, up_proj, hidden, result)


def split_groups(row_block):
    tok_count = row_block.shape[0]
    return row_block.reshape(tok_count, HEADS // HEAD_BLOCK, HEAD_BLOCK * HEAD_DIM).transpose(
        1, 0, 2
    )


def join_groups(group_block):
    return group_block.transpose(1, 0, 2).reshape(group_block.shape[1], -1)


def as_heads(block):
    return block.reshape(block.shape[0], HEAD_BLOCK, HEAD_DIM)


def attend_row(members):
    query_row, key_row, value_row, allowed = members

    def per_group(pieces):
        query_block, key_block, value_block = pieces
        scores = (
            jnp.einsum(
                "qhd,khd->hqk",
                as_heads(query_block),
                as_heads(key_block),
                preferred_element_type=jnp.float32,
            )
            * 0.125
        )
        scores = jnp.where(allowed[None], scores, -1e30)
        highest = jnp.max(scores, axis=-1, keepdims=True)
        exp_scores = jnp.exp(scores - highest)
        denominator = jnp.sum(exp_scores, axis=-1, keepdims=True)
        soft_low = (exp_scores / denominator).astype(jnp.bfloat16)
        attended = jnp.einsum(
            "hqk,khd->qhd", soft_low, as_heads(value_block), preferred_element_type=jnp.float32
        )
        return (
            attended.reshape(query_block.shape[0], -1),
            (highest + jnp.log(denominator))[..., 0],
        )

    attended, log_total = lax.map(
        per_group, (split_groups(query_row), split_groups(key_row), split_groups(value_row))
    )
    return (join_groups(attended), log_total)


def attend_back(members):
    query_row, key_row, value_row, grad_row, log_total, allowed = members

    def per_group(pieces):
        query_block, key_block, value_block, grad_block, log_block = pieces
        query_heads = as_heads(query_block)
        key_heads = as_heads(key_block)
        grad_heads = as_heads(grad_block)
        scores = (
            jnp.einsum("qhd,khd->hqk", query_heads, key_heads, preferred_element_type=jnp.float32)
            * 0.125
        )
        soft_weights = jnp.where(allowed[None], jnp.exp(scores - log_block[..., None]), 0.0)
        soft_low = soft_weights.astype(jnp.bfloat16)
        grad_probs = jnp.einsum(
            "qhd,khd->hqk", grad_heads, as_heads(value_block), preferred_element_type=jnp.float32
        )
        row_delta = jnp.sum(soft_weights * grad_probs, axis=-1, keepdims=True)
        grad_scores = (soft_weights * (grad_probs - row_delta)).astype(jnp.bfloat16)
        grad_query = (
            jnp.einsum("hqk,khd->qhd", grad_scores, key_heads, preferred_element_type=jnp.float32)
            * 0.125
        )
        grad_key = (
            jnp.einsum("hqk,qhd->khd", grad_scores, query_heads, preferred_element_type=jnp.float32)
            * 0.125
        )
        grad_value = jnp.einsum(
            "hqk,qhd->khd", soft_low, grad_heads, preferred_element_type=jnp.float32
        )
        return (
            grad_query.reshape(query_block.shape[0], -1),
            grad_key.reshape(key_block.shape[0], -1),
            grad_value.reshape(key_block.shape[0], -1),
        )

    grad_query, grad_key, grad_value = lax.map(
        per_group,
        (
            split_groups(query_row),
            split_groups(key_row),
            split_groups(value_row),
            split_groups(grad_row),
            log_total,
        ),
    )
    return (join_groups(grad_query), join_groups(grad_key), join_groups(grad_value))


def plain_local(
    tokens,
    first_values,
    v1_accum,
    segment_ids,
    positions,
    cotangent,
    attn_gain,
    w_query,
    w_key,
    w_value,
    w_out,
    mlp_gain,
    w_gate,
    w_up,
    w_down,
):
    row_count, seq_piece, model_width = tokens.shape
    token_count = row_count * seq_piece
    flat_tokens = tokens.astype(jnp.float32).reshape(token_count, model_width)
    first_flat = first_values.astype(jnp.float32).reshape(token_count, model_width)
    cosine_table, sine_table = angle_tables(positions)
    segment_low = segment_ids.astype(jnp.bfloat16)
    attn_set = (
        lax.all_gather(attn_gain, ("dp", "ctx"), axis=0, tiled=True),
        lax.all_gather(w_query, ("dp", "ctx"), axis=0, tiled=True),
        lax.all_gather(w_key, ("dp", "ctx"), axis=0, tiled=True),
        lax.all_gather(w_value, ("dp", "ctx"), axis=0, tiled=True),
        lax.all_gather(w_out, ("dp", "ctx"), axis=0, tiled=True),
    )
    normed, inv_root, normed_in, query_rot, key_rot, value_mix = attn_front(
        flat_tokens, first_flat, attn_set, cosine_table, sine_table, row_count, seq_piece
    )
    key_full, value_full, segment_full = (
        lax.all_gather(key_rot, "ctx", axis=1, tiled=True),
        lax.all_gather(value_mix, "ctx", axis=1, tiled=True),
        lax.all_gather(segment_low, "ctx", axis=1, tiled=True),
    )
    query_order = lax.axis_index("ctx") * seq_piece + jnp.arange(seq_piece, dtype=jnp.int32)
    full_order = jnp.arange(key_full.shape[1], dtype=jnp.int32)
    segment_own = segment_ids.astype(jnp.float32)
    segment_all = segment_full.astype(jnp.float32)
    allowed = (segment_own[:, :, None] == segment_all[:, None, :]) & (
        query_order[None, :, None] >= full_order[None, None, :]
    )
    attended, log_total = lax.map(attend_row, (query_rot, key_full, value_full, allowed))
    attended_low = attended.reshape(token_count, model_width).astype(jnp.bfloat16)
    mlp_set = (
        lax.all_gather(mlp_gain, ("dp", "ctx"), axis=0, tiled=True),
        lax.all_gather(w_gate, ("dp", "ctx"), axis=0, tiled=True),
        lax.all_gather(w_up, ("dp", "ctx"), axis=0, tiled=True),
        lax.all_gather(w_down, ("dp", "ctx"), axis=0, tiled=True),
    )
    normed_two, inv_root_two, mlp_in, gate_proj, up_proj, hidden, output_flat = mlp_block(
        flat_tokens, attended_low, attn_set[4], mlp_set
    )
    output = output_flat.reshape(tokens.shape).astype(jnp.bfloat16)
    attn_set = (
        lax.all_gather(attn_gain, ("dp", "ctx"), axis=0, tiled=True),
        lax.all_gather(w_query, ("dp", "ctx"), axis=0, tiled=True),
        lax.all_gather(w_key, ("dp", "ctx"), axis=0, tiled=True),
        lax.all_gather(w_value, ("dp", "ctx"), axis=0, tiled=True),
        lax.all_gather(w_out, ("dp", "ctx"), axis=0, tiled=True),
    )
    mlp_set = (
        lax.all_gather(mlp_gain, ("dp", "ctx"), axis=0, tiled=True),
        lax.all_gather(w_gate, ("dp", "ctx"), axis=0, tiled=True),
        lax.all_gather(w_up, ("dp", "ctx"), axis=0, tiled=True),
        lax.all_gather(w_down, ("dp", "ctx"), axis=0, tiled=True),
    )
    normed, inv_root, normed_in, query_rot, key_rot, value_mix = attn_front(
        flat_tokens, first_flat, attn_set, cosine_table, sine_table, row_count, seq_piece
    )
    key_full, value_full = (
        lax.all_gather(key_rot, "ctx", axis=1, tiled=True),
        lax.all_gather(value_mix, "ctx", axis=1, tiled=True),
    )
    normed_two, inv_root_two, mlp_in, gate_proj, up_proj, hidden, output_flat = mlp_block(
        flat_tokens, attended_low, attn_set[4], mlp_set
    )
    cot_low = cotangent.reshape(token_count, model_width)
    cot_float = cot_low.astype(jnp.float32)
    grad_hidden = jnp.einsum("td,fd->tf", cot_low, mlp_set[3], preferred_element_type=jnp.float32)
    sigma = jax.nn.sigmoid(gate_proj)
    grad_gate_low = (grad_hidden * up_proj * sigma * (1.0 + gate_proj * (1.0 - sigma))).astype(
        jnp.bfloat16
    )
    grad_up_low = (grad_hidden * gate_proj * sigma).astype(jnp.bfloat16)
    grad_mlp_in = jnp.einsum(
        "tf,df->td", grad_gate_low, mlp_set[1], preferred_element_type=jnp.float32
    )
    grad_mlp_in = grad_mlp_in + jnp.einsum(
        "tf,df->td", grad_up_low, mlp_set[2], preferred_element_type=jnp.float32
    )
    grad_middle_norm, grad_gain_two = norm_back(grad_mlp_in, normed_two, inv_root_two, mlp_set[0])
    grad_middle = cot_float + grad_middle_norm
    grad_branch_low = grad_middle.astype(jnp.bfloat16)
    grad_attended = jnp.einsum(
        "te,de->td", grad_branch_low, attn_set[4], preferred_element_type=jnp.float32
    )
    grad_attended = grad_attended.astype(jnp.bfloat16).reshape(row_count, seq_piece, model_width)
    grad_query_rot, grad_key_full, grad_value_full = lax.map(
        attend_back, (query_rot, key_full, value_full, grad_attended, log_total, allowed)
    )
    grad_key_rot, grad_value_mix = (
        lax.psum_scatter(
            grad_key_full.astype(jnp.bfloat16), "ctx", scatter_dimension=1, tiled=True
        ).astype(jnp.float32),
        lax.psum_scatter(
            grad_value_full.astype(jnp.bfloat16), "ctx", scatter_dimension=1, tiled=True
        ).astype(jnp.float32),
    )
    v1_grad = v1_accum + 0.5 * grad_value_mix
    grad_query_low = rotate(
        grad_query_rot.reshape(row_count, seq_piece, HEADS, HEAD_DIM), cosine_table, -sine_table
    )
    grad_query_low = grad_query_low.astype(jnp.bfloat16).reshape(token_count, model_width)
    grad_key_low = rotate(
        grad_key_rot.reshape(row_count, seq_piece, HEADS, HEAD_DIM), cosine_table, -sine_table
    )
    grad_key_low = grad_key_low.astype(jnp.bfloat16).reshape(token_count, model_width)
    grad_value_low = (0.5 * grad_value_mix).astype(jnp.bfloat16).reshape(token_count, model_width)
    grad_normed_in = jnp.einsum(
        "te,de->td", grad_query_low, attn_set[1], preferred_element_type=jnp.float32
    )
    grad_normed_in = grad_normed_in + jnp.einsum(
        "te,de->td", grad_key_low, attn_set[2], preferred_element_type=jnp.float32
    )
    grad_normed_in = grad_normed_in + jnp.einsum(
        "te,de->td", grad_value_low, attn_set[3], preferred_element_type=jnp.float32
    )
    grad_input_norm, grad_gain_one = norm_back(grad_normed_in, normed, inv_root, attn_set[0])
    input_grad = (grad_middle + grad_input_norm).reshape(tokens.shape)
    attn_right = jnp.concatenate([grad_query_low, grad_key_low, grad_value_low], axis=1)
    left_in = normed_in
    projections = jnp.einsum("td,te->de", left_in, attn_right, preferred_element_type=jnp.float32)
    out_part = jnp.einsum(
        "td,te->de", attended_low, grad_branch_low, preferred_element_type=jnp.float32
    )
    attn_matrix = lax.psum_scatter(
        jnp.concatenate([projections, out_part], axis=1),
        ("dp", "ctx"),
        scatter_dimension=0,
        tiled=True,
    )
    mlp_right = jnp.concatenate([grad_gate_low, grad_up_low], axis=1)
    left_in = mlp_in
    gate_up_matrix = lax.psum_scatter(
        jnp.einsum("td,tf->df", left_in, mlp_right, preferred_element_type=jnp.float32),
        ("dp", "ctx"),
        scatter_dimension=0,
        tiled=True,
    )
    down_matrix = lax.psum_scatter(
        jnp.einsum("tf,td->fd", hidden, cot_low, preferred_element_type=jnp.float32),
        ("dp", "ctx"),
        scatter_dimension=0,
        tiled=True,
    )
    gain_one, gain_two = (
        lax.psum_scatter(grad_gain_one, ("dp", "ctx"), scatter_dimension=0, tiled=True),
        lax.psum_scatter(grad_gain_two, ("dp", "ctx"), scatter_dimension=0, tiled=True),
    )
    ff_width = w_gate.shape[1]
    return (
        output,
        input_grad,
        v1_grad,
        gain_one,
        attn_matrix[:, 0:model_width],
        attn_matrix[:, model_width : 2 * model_width],
        attn_matrix[:, 2 * model_width : 3 * model_width],
        attn_matrix[:, 3 * model_width : 4 * model_width],
        gain_two,
        gate_up_matrix[:, 0:ff_width],
        gate_up_matrix[:, ff_width : 2 * ff_width],
        down_matrix,
    )


def params(**kw):
    return pltpu.CompilerParams(vmem_limit_bytes=BYTES, **kw)


def dot(a, b, da, db):
    return lax.dot_general(a, b, (((da,), (db,)), ((), ())), preferred_element_type=F32)


def lane_block(index):
    return pl.ds(pl.multiple_of(index * LANES, LANES), LANES)


def half_swap(x):
    lane = lax.broadcasted_iota(jnp.int32, x.shape, 1)
    left = pltpu.roll(x, LANES - HEAD_DIM // 2, 1)
    right = pltpu.roll(x, HEAD_DIM // 2, 1)
    return jnp.where(lane % HEAD_DIM < HEAD_DIM // 2, left, right)


def head_lanes(x, head):
    lane = lax.broadcasted_iota(jnp.int32, x.shape, 1)
    return jnp.where(lane // HEAD_DIM == head, x, jnp.zeros_like(x))


def meet(n_ctx, bits):
    c, dp = lax.axis_index("ctx"), lax.axis_index("dp")
    barrier = pltpu.get_barrier_semaphore()
    for k in range(1, n_ctx):
        pl.semaphore_signal(barrier, inc=1, device_id={"ctx": lax.rem(c + k, n_ctx)}, device_id_type=MESH)
    for bit in bits:
        pl.semaphore_signal(barrier, inc=1, device_id={"dp": dp ^ bit}, device_id_type=MESH)
    pl.semaphore_wait(barrier, n_ctx - 1 + len(bits))


def ctx_copy(src, dst, send, recv, to):
    return pltpu.make_async_remote_copy(
        src_ref=src, dst_ref=dst, send_sem=send, recv_sem=recv, device_id={"ctx": to}, device_id_type=MESH
    )


def dp_copy(src, dst, send, recv, bit):
    to = lax.axis_index("dp") ^ bit
    return pltpu.make_async_remote_copy(
        src_ref=src, dst_ref=dst, send_sem=send, recv_sem=recv, device_id={"dp": to}, device_id_type=MESH
    )


def rows_of(index, size):
    return pl.ds(pl.multiple_of(index * size, size), size)


CORE, NEAR, FAR = 1, 2, 4


class Gather:
    def __init__(self, n_ctx, src, dst, send, recv, order):
        self.n, self.src, self.dst, self.send, self.recv = n_ctx, src, dst, send, recv
        self.first, self.second = order
        self.rows = src.shape[0]

    def place(self, c):
        return self.dst.at[0, pl.ds(c * self.rows, self.rows), :]

    def along(self, bit):
        c = lax.axis_index("ctx")
        return ctx_copy(self.src, self.place(c), self.send.at[bit - 1], self.recv.at[bit - 1], c ^ bit)

    def pass_on(self):
        c = lax.axis_index("ctx")
        return ctx_copy(self.place(c ^ 2), self.place(c ^ 2), self.send.at[2], self.recv.at[2], c ^ 1)

    def plane(self, slot, bit, at):
        return dp_copy(self.dst.at[slot], self.dst.at[slot ^ bit], self.send.at[at], self.recv.at[at], bit)

    def own(self):
        c = lax.axis_index("ctx")
        return pltpu.make_async_copy(self.src, self.dst.at[0, pl.ds(c * self.rows, self.rows), :], self.send.at[10])

    def hop(self, at):
        one, two = self.first, self.second
        slot, bit = [(0, one), (0, two), (one, two), (0, CORE), (one, CORE), (two, CORE), (one | two, CORE)][at]
        return self.plane(slot, bit, 3 + at)

    def start(self):
        self.own().start()
        self.along(2).start()
        self.along(1).start()

    def relay(self):
        self.along(2).wait_recv()
        self.pass_on().start()

    def spread(self):
        self.own().wait()
        self.along(1).wait_recv()
        self.pass_on().wait_recv()
        for at in (0, 1, 3):
            self.hop(at).start()

    def forward(self):
        self.hop(0).wait_recv()
        self.hop(2).start()
        self.hop(4).start()

    def cross(self):
        self.hop(1).wait_recv()
        self.hop(5).start()
        self.hop(2).wait_recv()
        self.hop(6).start()

    def finish(self):
        self.along(1).wait_send()
        self.along(2).wait_send()
        self.pass_on().wait_send()
        for at in range(7):
            self.hop(at).wait_send()
        for at in range(3, 7):
            self.hop(at).wait_recv()


def front_kernel(
    n_ctx, tok_ref, fv_ref, seg_in, pos_in, wq_ref, wk_ref, wv_ref, gains_ref, freq_ref, wg_ref, wu_ref, wo_ref, wd_ref,
    xn_ref, q_ref, k_ref, v_ref, of_ref, lse_ref, cos_ref, sin_ref, seg_ref, marks, gain_ref,
    att_ref, wg_all, wu_all, wo_all, wd_all,
    x_all, fvs, packs, whead, rel, o_ref, s_ref, m_ref, l_ref, acc_ref, p_all, total_ref,
    mark_send, mark_recv, piece_send, piece_recv, pack_send, pack_recv, tok_send, tok_recv, fv_send, fv_recv, w_send, w_recv,
    o_send, o_recv, own, own_o,
):
    c, dp = lax.axis_index("ctx"), lax.axis_index("dp")
    tb = m_ref.shape[0]
    half = tb // 2
    model = tok_ref.shape[1]
    blocks = model // LANES
    width = q_ref.shape[1]
    own_rows = wg_ref.shape[0]
    lane = lax.broadcasted_iota(jnp.int32, (tb, LANES), 1)
    exact = lax.Precision.HIGHEST

    weights = []
    for i, (src, dst) in enumerate(((wg_ref, wg_all), (wo_ref, wo_all), (wu_ref, wu_all), (wd_ref, wd_all))):
        wide = src.shape[1] // 2
        weights.append([])
        for h, order in enumerate(((NEAR, FAR), (FAR, NEAR))):
            cols = pl.ds(h * wide, wide)
            unit = 2 * i + h
            weights[i].append(
                Gather(n_ctx, src.at[:, cols], dst.at[:, :, cols], w_send.at[unit], w_recv.at[unit], order)
            )
    gate, out, up, down = weights

    def each(what, *arrays):
        for array in arrays:
            for half_way in array:
                getattr(half_way, what)()

    def mark_copies(k):
        at, to = rows_of(c, tb), lax.rem(c + k, n_ctx)
        return [
            ctx_copy(src, marks.at[pl.ds(r, 1), at], mark_send.at[k - 1, r], mark_recv.at[k - 1, r], to)
            for r, src in enumerate((seg_in, pos_in))
        ]

    def pieces(to):
        cols = rows_of(to, width)
        return [wq_ref.at[:, cols], wk_ref.at[:, cols], wv_ref.at[:, cols], gains_ref]

    def pack_copies(k):
        to = lax.rem(c + k, n_ctx)
        return [
            ctx_copy(src, packs.at[0, c, pl.ds(t * own_rows, own_rows), :], piece_send.at[k - 1, t], piece_recv.at[k - 1, t], to)
            for t, src in enumerate(pieces(to))
        ]

    def pack_hop(slot, bit, at):
        return dp_copy(packs.at[slot], packs.at[slot ^ bit], pack_send.at[at], pack_recv.at[at], bit)

    def fv_copy(k):
        to = lax.rem(c + k, n_ctx)
        return ctx_copy(fv_ref.at[:, rows_of(to, width)], fvs.at[rows_of(c, tb), :], fv_send.at[k - 1], fv_recv.at[k - 1], to)

    def tok_copy(bit):
        return ctx_copy(tok_ref, x_all.at[rows_of(c, tb), :], tok_send.at[bit - 1], tok_recv.at[bit - 1], c ^ bit)

    def tok_pass():
        at = rows_of(c ^ 2, tb)
        return ctx_copy(x_all.at[at, :], x_all.at[at, :], tok_send.at[2], tok_recv.at[2], c ^ 1)

    locals_ = [
        pltpu.make_async_copy(tok_ref, x_all.at[rows_of(c, tb), :], own.at[0]),
        pltpu.make_async_copy(fv_ref.at[:, rows_of(c, width)], fvs.at[rows_of(c, tb), :], own.at[1]),
    ] + [
        pltpu.make_async_copy(src, packs.at[0, c, pl.ds(t * own_rows, own_rows), :], own.at[4 + t])
        for t, src in enumerate(pieces(c))
    ] + [
        pltpu.make_async_copy(src, marks.at[pl.ds(r, 1), rows_of(c, tb)], own.at[2 + r])
        for r, src in enumerate((seg_in, pos_in))
    ]

    meet(n_ctx, (CORE, NEAR, FAR))
    for k in range(1, n_ctx):
        for m in mark_copies(k) + pack_copies(k):
            m.start()
    each("start", gate, out, up)
    for m in locals_:
        m.start()

    for m in locals_[6:]:
        m.wait()
    for k in range(1, n_ctx):
        for m in mark_copies(k):
            m.wait_recv()
    row8 = lax.broadcasted_iota(jnp.int32, (2, LANES), 0)
    pick_seg = jnp.where(row8 == 0, 1.0, 0.0)
    pick_pos = jnp.where(row8 == 1, 1.0, 0.0)

    def table(b, carry):
        at = rows_of(b, tb)
        m = marks[0:2, at].astype(F32)
        dims = (((0,), (0,)), ((), ()))
        seg_ref[at, :] = lax.dot_general(m, pick_seg, dims, precision=exact, preferred_element_type=F32)
        pos = lax.dot_general(m, pick_pos, dims, precision=exact, preferred_element_type=F32)
        angle = pos * freq_ref[0:1, :]
        cos_ref[at, :] = jnp.cos(angle)
        sin_ref[at, :] = jnp.sin(angle) * freq_ref[1:2, :]
        return carry

    for m in locals_[2:6]:
        m.wait()
    for k in range(1, n_ctx):
        for m in pack_copies(k):
            m.wait_recv()
    pack_hop(0, NEAR, 3).start()
    each("relay", gate, out, up)
    tok_copy(2).start()
    tok_copy(1).start()
    lax.fori_loop(0, n_ctx, table, 0)
    pack_hop(0, NEAR, 3).wait_recv()
    pack_hop(0, FAR, 4).start()
    pack_hop(NEAR, FAR, 5).start()
    pack_hop(0, CORE, 6).start()
    pack_hop(NEAR, CORE, 7).start()
    each("spread", gate, out, up)
    pack_hop(0, FAR, 4).wait_recv()
    pack_hop(FAR, CORE, 8).start()
    pack_hop(NEAR, FAR, 5).wait_recv()
    pack_hop(NEAR | FAR, CORE, 9).start()
    for at, (slot, bit) in enumerate([(0, CORE), (NEAR, CORE), (FAR, CORE), (NEAR | FAR, CORE)]):
        pack_hop(slot, bit, 6 + at).wait_recv()
    count = packs.shape[0]
    for t in range(3):
        block = packs[:, :, t * own_rows : (t + 1) * own_rows, :]
        whead[:, t * width : (t + 1) * width] = block.reshape(model, width)
    gains = packs[:, :, 3 * own_rows : 4 * own_rows, 0:LANES].reshape(model, LANES).astype(F32)
    gain_ref[...] = gains.T[0:8, :]
    locals_[0].wait()
    locals_[1].wait()

    def project(chunk, part):
        at = pl.ds(pl.multiple_of(chunk * tb + part * half, half), half)
        for d in range(blocks):
            rel[:, d * LANES : (d + 1) * LANES] = x_all[at, lane_block(dp ^ d)].astype(F32)
        x = rel[...]
        inv = lax.rsqrt(jnp.mean(x * x, axis=-1, keepdims=True) + epsilon)
        xn = (x * inv * gain_ref[0:1, :]).astype(LOW)
        xn_ref[at, :] = xn
        proj = dot(xn, whead[...], 1, 0)
        cos, sin = cos_ref[at, :], sin_ref[at, :]
        for b in range(width // LANES):
            cols = slice(b * LANES, (b + 1) * LANES)
            qb = proj[:, b * LANES : (b + 1) * LANES]
            q_ref[at, cols] = ((qb * cos + half_swap(qb) * sin) * 0.125).astype(LOW)
            kb = proj[:, width + b * LANES : width + (b + 1) * LANES]
            k_ref[at, cols] = (kb * cos + half_swap(kb) * sin).astype(LOW)
        of_ref[at, :] = 0.5 * proj[:, 2 * width :]

    def project_chunk(bit):
        def one(part, carry):
            project(c ^ bit, part)
            return carry

        lax.fori_loop(0, 2, one, 0)

    project_chunk(0)
    each("forward", gate, out, up)
    tok_copy(2).wait_recv()
    tok_pass().start()
    tok_copy(1).wait_recv()
    project_chunk(1)
    project_chunk(2)
    each("cross", gate, out, up)
    tok_pass().wait_recv()
    each("start", down)
    for k in range(1, n_ctx):
        fv_copy(k).start()
    project_chunk(3)

    def fold(x, op):
        r = x[:, 0:LANES]
        for b in range(1, tb // LANES):
            r = op(r, x[:, b * LANES : (b + 1) * LANES])
        return r

    def home(pair):
        return att_ref.at[:, pl.ds(pl.multiple_of(c * width + pair * LANES, LANES), LANES)]

    def weigh(pair, i):
        cols = slice(pair * LANES, (pair + 1) * LANES)
        mine = rows_of(i, tb)
        q = q_ref[mine, cols]
        seg_q = seg_ref[mine, 0:1]
        base = i * (i + 1) // 2
        for head in range(2):
            qm = head_lanes(q, head)
            m_ref[...] = jnp.full_like(m_ref, NEG)

            def score(j, causal):
                at = rows_of(j, tb)
                s = dot(qm, k_ref[at, cols], 1, 1)
                ok = seg_q == marks[0:1, at].astype(F32)
                if causal:
                    r = lax.broadcasted_iota(jnp.int32, (tb, tb), 0)
                    t = lax.broadcasted_iota(jnp.int32, (tb, tb), 1)
                    ok = ok & (r >= t)
                s = jnp.where(ok, s, NEG)
                s_ref[:, at] = s
                m_ref[...] = jnp.maximum(m_ref[...], fold(s, jnp.maximum))

            def score_step(j, carry):
                score(j, False)
                return carry

            lax.fori_loop(0, i, score_step, 0)
            score(i, True)
            top = jnp.max(m_ref[...], axis=1, keepdims=True)
            l_ref[...] = jnp.zeros_like(l_ref)

            def weight_step(j, carry):
                p = jnp.exp(s_ref[:, rows_of(j, tb)] - top)
                l_ref[...] += fold(p, jnp.add)
                p_all[2 * pair + head, base + j] = p.astype(LOW)
                return carry

            lax.fori_loop(0, i + 1, weight_step, 0)
            total = jnp.sum(l_ref[...], axis=1, keepdims=True)
            total_ref[mine, :] = jnp.where(lane == 2 * pair + head, total, total_ref[mine, :])
            lse = jnp.broadcast_to(top + jnp.log(total), (tb, LANES))
            if head == 0:
                lse_ref[mine, cols] = lse
            else:
                lse_ref[mine, cols] = jnp.where(lane < HEAD_DIM, lse_ref[mine, cols], lse)

    def mix(pair, i):
        cols = slice(pair * LANES, (pair + 1) * LANES)
        mine = rows_of(i, tb)
        base = i * (i + 1) // 2
        for head in range(2):
            acc_ref[...] = jnp.zeros_like(acc_ref)

            def value_step(j, carry):
                acc_ref[...] += dot(p_all[2 * pair + head, base + j], v_ref[rows_of(j, tb), cols], 1, 0)
                return carry

            lax.fori_loop(0, i + 1, value_step, 0)
            out = acc_ref[...] / total_ref[mine, 2 * pair + head : 2 * pair + head + 1]
            if head == 0:
                of_ref[mine, cols] = out
            else:
                of_ref[mine, cols] = jnp.where(lane < HEAD_DIM, of_ref[mine, cols], out)
        o_ref[mine, cols] = of_ref[mine, cols].astype(LOW)

        @pl.when(i == c)
        def _():
            pltpu.make_async_copy(o_ref.at[mine, cols], home(pair), own_o.at[pair]).start()

        @pl.when(i != c)
        def _():
            k = lax.rem(i + n_ctx - c, n_ctx) - 1
            ctx_copy(o_ref.at[mine, cols], home(pair), o_send.at[k, pair], o_recv.at[k, pair], i).start()

    def over_queries(what, pair, lo, hi):
        def one(i, carry):
            what(pair, i)
            return carry

        lax.fori_loop(lo, hi, one, 0)

    total_ref[...] = jnp.ones_like(total_ref)
    over_queries(weigh, 0, 0, n_ctx)
    each("relay", down)
    over_queries(weigh, 1, 0, 3)
    each("spread", down)
    over_queries(weigh, 1, 3, n_ctx)
    for k in range(1, n_ctx):
        fv_copy(k).wait_recv()

    def values(b, carry):
        at = rows_of(b, tb)
        v_ref[at, :] = (of_ref[at, :] + 0.5 * fvs[at, :].astype(F32)).astype(LOW)
        return carry

    lax.fori_loop(0, n_ctx, values, 0)
    over_queries(mix, 0, 0, n_ctx)
    each("forward", down)
    over_queries(mix, 1, 0, n_ctx)
    each("cross", down)
    for pair in range(width // LANES):
        cols = slice(pair * LANES, (pair + 1) * LANES)
        pltpu.make_async_copy(o_ref.at[0:tb, cols], home(pair), own_o.at[pair]).wait()
        for k in range(n_ctx - 1):
            ctx_copy(o_ref.at[0:tb, cols], home(pair), o_send.at[k, pair], o_recv.at[k, pair], c).wait()
    for k in range(1, n_ctx):
        for m in mark_copies(k) + pack_copies(k):
            m.wait_send()
        fv_copy(k).wait_send()
    for at, (slot, bit) in enumerate(
        [(0, NEAR), (0, FAR), (NEAR, FAR), (0, CORE), (NEAR, CORE), (FAR, CORE), (NEAR | FAR, CORE)]
    ):
        pack_hop(slot, bit, 3 + at).wait_send()
    tok_copy(1).wait_send()
    tok_copy(2).wait_send()
    tok_pass().wait_send()
    each("finish", *weights)


def front_call(n_dp, n_ctx, tok, fv, seg, pos, wq, wk, wv, gains, freq, wg, wu, wo, wd):
    tb, model = tok.shape
    width = model // n_ctx
    length = n_ctx * tb
    pairs = width // LANES
    vmem = pl.BlockSpec(memory_space=pltpu.VMEM)
    anyspace = pl.BlockSpec(memory_space=pl.ANY)
    shape = jax.ShapeDtypeStruct
    dma = pltpu.SemaphoreType.DMA
    return pl.pallas_call(
        functools.partial(front_kernel, n_ctx),
        in_specs=[anyspace] * 8 + [vmem] + [anyspace] * 4,
        out_specs=[vmem] * 11 + [anyspace] * 5,
        out_shape=[shape((length, model), LOW)]
        + [shape((length, width), LOW)] * 3
        + [shape((length, width), F32)] * 2
        + [shape((length, LANES), F32)] * 3
        + [shape((2, length), jnp.int32), shape((8, model), F32)]
        + [shape((tb, model), LOW)]
        + [shape((n_dp, n_ctx * w.shape[0], w.shape[1]), LOW) for w in (wg, wu, wo, wd)],
        scratch_shapes=[
            pltpu.VMEM((length, model), LOW),
            pltpu.VMEM((length, width), LOW),
            pltpu.VMEM((n_dp, n_ctx, 4 * wq.shape[0], width), LOW),
            pltpu.VMEM((model, 3 * width), LOW),
            pltpu.VMEM((tb // 2, model), F32),
            pltpu.VMEM((length, width), LOW),
            pltpu.VMEM((tb, length), F32),
            pltpu.VMEM((tb, LANES), F32),
            pltpu.VMEM((tb, LANES), F32),
            pltpu.VMEM((tb, LANES), F32),
            pltpu.VMEM((2 * pairs, n_ctx * (n_ctx + 1) // 2, tb, tb), LOW),
            pltpu.VMEM((length, LANES), F32),
            dma((n_ctx - 1, 2)), dma((n_ctx - 1, 2)),
            dma((n_ctx - 1, 4)), dma((n_ctx - 1, 4)),
            dma((n_ctx + 6,)), dma((n_ctx + 6,)),
            dma((3,)), dma((3,)),
            dma((n_ctx - 1,)), dma((n_ctx - 1,)),
            dma((8, 11)), dma((8, 11)),
            dma((n_ctx - 1, pairs)), dma((n_ctx - 1, pairs)),
            dma((8,)), dma((pairs,)),
        ],
        compiler_params=params(collective_id=1, has_side_effects=True),
        cost_estimate=pl.CostEstimate(
            flops=24 * 10**9, bytes_accessed=60 * 2**20, transcendentals=2 * length * length
        ),
        name="front",
    )(tok, fv, seg, pos, wq, wk, wv, gains, freq, wg, wu, wo, wd)


class Reduce:
    def __init__(self, n_ctx, keep, came, acc, rc, rx, ry, rz, out, send, recv, order):
        self.n, self.keep, self.came, self.acc, self.rc, self.rx, self.ry, self.rz = n_ctx, keep, came, acc, rc, rx, ry, rz
        self.out, self.send, self.recv = out, send, recv
        self.one, self.two = order
        self.leave = (self.one >> 1, 3)
        self.stay = self.two >> 1

    def hop(self, at):
        src, dst, bit = [
            (self.acc.at[self.leave[0]], self.rx.at[0], self.one),
            (self.acc.at[self.leave[1]], self.rx.at[1], self.one),
            (self.acc.at[self.stay], self.ry, self.two),
        ][at - 1]
        return dp_copy(src, dst, self.send.at[at], self.recv.at[at], bit)

    def held(self):
        return pltpu.make_async_copy(self.keep, self.acc, self.send.at[7])

    def partner(self):
        return pltpu.make_async_copy(self.came, self.rc, self.send.at[0])

    def along(self, at):
        c = lax.axis_index("ctx")
        block, to = ((c ^ 1, c ^ 1), (c ^ 3, c ^ 1), (c ^ 2, c ^ 2))[at]
        return ctx_copy(self.acc.at[0, block], self.rz.at[at], self.send.at[4 + at], self.recv.at[4 + at], to)

    def begin(self):
        self.partner().start()
        self.held().start()

    def add(self, block, terms):
        def one(j, carry):
            total = self.acc[block, j].astype(F32)
            for t in terms:
                total = total + t(j).astype(F32)
            self.acc[block, j] = total.astype(LOW)
            return carry

        lax.fori_loop(0, self.acc.shape[1], one, 0)

    def step_one(self):
        self.held().wait()
        self.partner().wait()
        for at in (1, 0):
            block = self.leave[at]
            self.add(block, [lambda j, block=block: self.rc[block, j]])
            self.hop(1 + at).start()

    def step_two(self):
        self.hop(2).wait_recv()
        self.add(self.stay, [lambda j: self.rc[self.stay, j], lambda j: self.rx[1, j]])
        self.hop(3).start()

    def step_ctx(self):
        c = lax.axis_index("ctx")
        self.hop(1).wait_recv()
        self.hop(3).wait_recv()
        self.out[...] = (
            self.acc[0, c].astype(F32) + self.rc[0, c].astype(F32) + self.rx[0, c].astype(F32) + self.ry[c].astype(F32)
        )
        self.add(0, [lambda j: self.rc[0, j], lambda j: self.rx[0, j], lambda j: self.ry[j]])
        self.along(1).start()
        self.along(0).start()

    def step_far(self):
        block = lax.axis_index("ctx") ^ 2
        self.along(1).wait_recv()
        self.acc[0, block] = (self.acc[0, block].astype(F32) + self.rz[1].astype(F32)).astype(LOW)
        self.along(2).start()

    def finish(self):
        self.along(0).wait_recv()
        self.along(2).wait_recv()
        self.out[...] += self.rz[0].astype(F32) + self.rz[2].astype(F32)
        for at in range(1, 4):
            self.hop(at).wait_send()
        for at in range(3):
            self.along(at).wait_send()


def back_kernel(n_ctx, *refs):
    g_ref, q_ref, k_ref, v_ref, of_ref, lse_ref, sc_ref, sr_ref, cos_ref, sin_ref, xn_ref = refs[:11]
    sides = refs[11:19]
    home_ref, qkv_out = refs[19:21]
    outs = refs[21:25]
    (part_ref, lse_row, delta_row, dq_acc, dk_acc, dv_acc, prod) = refs[25:32]
    rest = refs[32:]
    buffers, rest = rest[:40], rest[40:]
    (pk, ps, prc, prx, pry, pz, qz) = rest[:7]
    (send, recv, own, r_send, r_recv, p_send, p_recv, z_send, z_recv) = rest[7:]
    c = lax.axis_index("ctx")
    tb = dk_acc.shape[0]
    length, width = q_ref.shape
    model = n_ctx * width
    pairs = width // LANES
    blocks = model // LANES
    orders = ((NEAR, FAR), (FAR, NEAR))
    groups = []
    for i in range(4):
        keep, came = sides[2 * i], sides[2 * i + 1]
        wide = keep.shape[3] // 2
        groups.append([])
        for h, order in enumerate(orders):
            cols = pl.ds(h * wide, wide)
            unit = 2 * i + h
            groups[i].append(
                Reduce(
                    n_ctx, keep.at[:, :, :, cols], came.at[:, :, :, cols], *buffers[5 * unit : 5 * unit + 5],
                    outs[i].at[:, cols], r_send.at[unit], r_recv.at[unit], order,
                )
            )

    def each(i, what):
        for unit in groups[i]:
            getattr(unit, what)()

    def home(pair, t):
        return home_ref.at[:, pl.ds(pl.multiple_of(t * model + c * width + pair * LANES, LANES), LANES)]

    def part(pair, t, chunk):
        return part_ref.at[pair, rows_of(chunk, tb), pl.ds(t * LANES, LANES)]

    def part_copy(pair, t, k, to):
        return ctx_copy(part(pair, t, to), home(pair, t), send.at[k - 1, pair, t], recv.at[k - 1, pair, t], to)

    def part_own(pair, t):
        return pltpu.make_async_copy(part(pair, t, c), home(pair, t), own.at[pair, t])

    meet(n_ctx, (CORE, NEAR, FAR))
    for i in range(4):
        each(i, "begin")
    each(0, "step_one")

    r8 = lax.broadcasted_iota(jnp.int32, (8, LANES), 0)
    l8 = lax.broadcasted_iota(jnp.int32, (8, LANES), 1)
    pick = jnp.where(l8 == r8 * HEAD_DIM, 1.0, 0.0)
    group = jnp.where(l8 // HEAD_DIM == r8, 1.0, 0.0)
    exact = lax.Precision.HIGHEST
    dims = (((1,), (1,)), ((), ()))

    def stats(pair):
        cols = slice(pair * LANES, (pair + 1) * LANES)

        def one(b, carry):
            at = rows_of(b, tb)
            lse_row[:, at] = lax.dot_general(pick, lse_ref[at, cols], dims, precision=exact, preferred_element_type=F32)
            mixed = g_ref[at, cols].astype(F32) * of_ref[at, cols]
            delta_row[:, at] = lax.dot_general(group, mixed, dims, precision=exact, preferred_element_type=F32)
            dq_acc[at, :] = jnp.zeros((tb, LANES), F32)
            return carry

        lax.fori_loop(0, n_ctx, one, 0)

    def key_blocks(pair, lo, hi):
        cols = slice(pair * LANES, (pair + 1) * LANES)

        def key_block(j, carry):
            dk_acc[...] = jnp.zeros_like(dk_acc)
            dv_acc[...] = jnp.zeros_like(dv_acc)
            mine = rows_of(j, tb)
            k = k_ref[mine, cols]
            v = v_ref[mine, cols]
            seg_k = sc_ref[mine, 0:1]

            def block(i, causal):
                at = rows_of(i, tb)
                q = q_ref[at, cols]
                g = g_ref[at, cols]
                ok = seg_k == sr_ref[0:1, at].astype(F32)
                if causal:
                    r = lax.broadcasted_iota(jnp.int32, (tb, tb), 0)
                    t = lax.broadcasted_iota(jnp.int32, (tb, tb), 1)
                    ok = ok & (r <= t)
                for head in range(2):
                    qm = head_lanes(q, head)
                    gm = head_lanes(g, head)
                    s = dot(k, qm, 1, 1)
                    p = jnp.where(ok, jnp.exp(s - lse_row[head : head + 1, at]), 0.0)
                    dp = dot(v, gm, 1, 1)
                    ds = (p * (dp - delta_row[head : head + 1, at])).astype(LOW)
                    dv_acc[...] += dot(p.astype(LOW), gm, 1, 0)
                    dk_acc[...] += dot(ds, qm, 1, 0)
                    dq_acc[at, :] += dot(ds, head_lanes(k, head), 0, 0)

            block(j, True)

            def step(i, carry):
                block(i, False)
                return carry

            lax.fori_loop(j + 1, n_ctx, step, 0)
            dk = dk_acc[...]
            dk = dk * cos_ref[mine, :] - half_swap(dk) * sin_ref[mine, :]
            part_ref[pair, mine, LANES : 2 * LANES] = dk.astype(LOW)
            part_ref[pair, mine, 2 * LANES : 3 * LANES] = dv_acc[...].astype(LOW)
            dq = dq_acc[mine, :] * 0.125
            dq = dq * cos_ref[mine, :] - half_swap(dq) * sin_ref[mine, :]
            part_ref[pair, mine, 0:LANES] = dq.astype(LOW)

            @pl.when(j == c)
            def _():
                for t in range(3):
                    part_own(pair, t).start()

            @pl.when(j != c)
            def _():
                for t in range(3):
                    part_copy(pair, t, lax.rem(j + n_ctx - c, n_ctx), j).start()

            return carry

        lax.fori_loop(lo, hi, key_block, 0)

    def pair_hop(pair, at):
        src, dst, bit = [
            (ps.at[pair], prc.at[pair], CORE),
            (pk.at[pair, 1], prx.at[pair, 0], NEAR),
            (pk.at[pair, 3], prx.at[pair, 1], NEAR),
            (pk.at[pair, 2], pry.at[pair], FAR),
        ][at]
        return dp_copy(src, dst, p_send.at[pair, at], p_recv.at[pair, at], bit)

    def pair_ctx(pair, k):
        to = lax.rem(c + k, n_ctx)
        return ctx_copy(pz.at[pair, to], qz.at[c, pair], z_send.at[pair, k - 1], z_recv.at[pair, k - 1], to)

    def pair_product(pair):
        prod[...] = jnp.zeros_like(prod)

        def one(b, carry):
            at = rows_of(b, tb)
            prod[...] += dot(part_ref[pair, at, :], xn_ref[at, :], 0, 0)
            return carry

        lax.fori_loop(0, n_ctx, one, 0)
        for d in range(blocks):
            (ps if d % 2 else pk)[pair, d // 2] = prod[:, d * LANES : (d + 1) * LANES].astype(LOW)
        pair_hop(pair, 0).start()

    def pair_one(pair):
        pair_hop(pair, 0).wait_recv()
        for i in (3, 1):
            pk[pair, i] = (pk[pair, i].astype(F32) + prc[pair, i].astype(F32)).astype(LOW)
            pair_hop(pair, 1 + i // 2).start()

    def pair_two(pair):
        pair_hop(pair, 2).wait_recv()
        total = pk[pair, 2].astype(F32) + prc[pair, 2].astype(F32) + prx[pair, 1].astype(F32)
        pk[pair, 2] = total.astype(LOW)
        pair_hop(pair, 3).start()

    def pair_three(pair):
        pair_hop(pair, 1).wait_recv()
        pair_hop(pair, 3).wait_recv()
        total = pk[pair, 0].astype(F32) + prc[pair, 0].astype(F32) + prx[pair, 0].astype(F32) + pry[pair].astype(F32)
        pz[pair] = total.T.reshape(pz.shape[1:]).astype(LOW)
        qz[c, pair] = pz[pair, c]
        for k in range(1, n_ctx):
            pair_ctx(pair, k).start()

    def pair_finish(pair):
        for k in range(1, n_ctx):
            pair_ctx(pair, k).wait()
        for at in range(4):
            pair_hop(pair, at).wait_send()

    middle = n_ctx // 2
    stats(0)
    key_blocks(0, 0, middle)
    each(0, "step_two")
    each(1, "step_one")
    key_blocks(0, middle, n_ctx)
    each(0, "step_ctx")
    stats(1)
    key_blocks(1, 0, middle)
    each(1, "step_two")
    each(2, "step_one")
    key_blocks(1, middle, n_ctx)
    pair_product(1)
    each(1, "step_ctx")
    pair_product(0)
    each(0, "step_far")
    pair_one(1)
    each(2, "step_two")
    each(3, "step_one")
    pair_one(0)
    pair_two(1)
    each(1, "step_far")
    pair_two(0)
    pair_three(1)
    each(2, "step_ctx")
    each(3, "step_two")
    pair_three(0)
    each(2, "step_far")
    each(3, "step_ctx")
    each(3, "step_far")
    for pair in range(pairs):
        pair_finish(pair)
        for s in range(n_ctx):
            for t in range(3):
                at = t * model + s * width + pair * LANES
                qkv_out[:, at : at + LANES] = qz[s, pair, :, t * LANES : (t + 1) * LANES].astype(F32)
    for i in range(4):
        each(i, "finish")
    for pair in range(pairs):
        for t in range(3):
            part_own(pair, t).wait()
            for k in range(1, n_ctx):
                part_copy(pair, t, k, lax.rem(c + k, n_ctx)).wait()


def back_call(n_ctx, g, q, k, v, of, lse, seg_col, seg_row, cos, sin, xn, sides):
    length, width = q.shape
    model = n_ctx * width
    tb = TOKEN_BLOCK
    pairs = width // LANES
    own_rows = model // (model // LANES) // n_ctx
    vmem = pl.BlockSpec(memory_space=pltpu.VMEM)
    anyspace = pl.BlockSpec(memory_space=pl.ANY)
    shape = jax.ShapeDtypeStruct
    dma = pltpu.SemaphoreType.DMA
    buffers = []
    for keep in sides[::2]:
        four, parts, rows, cols = keep.shape
        for lead in ((four, parts), (four, parts), (2, parts), (parts,), (3,)) * 2:
            buffers.append(pltpu.VMEM(lead + (rows, cols // 2), LOW))
    wide = 3 * LANES
    return pl.pallas_call(
        functools.partial(back_kernel, n_ctx),
        in_specs=[vmem] * 11 + [anyspace] * 8,
        out_specs=[anyspace] + [vmem] * 5,
        out_shape=[shape((tb, 3 * model), LOW), shape((own_rows, 3 * model), F32)]
        + [shape(keep.shape[2:], F32) for keep in sides[::2]],
        scratch_shapes=[
            pltpu.VMEM((pairs, length, wide), LOW),
            pltpu.VMEM((8, length), F32),
            pltpu.VMEM((8, length), F32),
            pltpu.VMEM((length, LANES), F32),
            pltpu.VMEM((tb, LANES), F32),
            pltpu.VMEM((tb, LANES), F32),
            pltpu.VMEM((wide, model), F32),
        ]
        + buffers
        + [
            pltpu.VMEM((pairs, 4, wide, LANES), LOW),
            pltpu.VMEM((pairs, 4, wide, LANES), LOW),
            pltpu.VMEM((pairs, 4, wide, LANES), LOW),
            pltpu.VMEM((pairs, 2, wide, LANES), LOW),
            pltpu.VMEM((pairs, wide, LANES), LOW),
            pltpu.VMEM((pairs, n_ctx, own_rows, wide), LOW),
            pltpu.VMEM((n_ctx, pairs, own_rows, wide), LOW),
            dma((n_ctx - 1, pairs, 3)), dma((n_ctx - 1, pairs, 3)),
            dma((pairs, 3)),
            dma((8, 8)), dma((8, 8)),
            dma((pairs, 4)), dma((pairs, 4)),
            dma((pairs, n_ctx - 1)), dma((pairs, n_ctx - 1)),
        ],
        compiler_params=params(collective_id=3, has_side_effects=True),
        cost_estimate=pl.CostEstimate(
            flops=40 * 10**9, bytes_accessed=60 * 2**20, transcendentals=2 * length * length
        ),
        name="back",
    )(g, q, k, v, of, lse, seg_col, seg_row, cos, sin, xn, *sides)


def mlp_kernel(
    blocks, n_ctx, tok_ref, att_ref, cot_ref, gain_ref, wo_in, wg_in, wu_in, wd_in, wq_ref, wr_ref,
    out_ref, gm_ref, gh_ref, gk, gc, uk, uc, ok, oc, dk, dc, wq_all, wr_all,
    wo, wg, wu, wd, att, nat, n2, mi, mit, oacc, dacc, hid_all, dg_all, du_all, stage, ostage,
    sem, hop_send, hop_recv, st_own, st_send, st_recv, o_sem, d_own, d_send, d_recv, g_send, g_recv,
):
    c, dp = lax.axis_index("ctx"), lax.axis_index("dp")
    tb, model = tok_ref.shape
    width = model // n_ctx
    ff = wu.shape[1]
    steps = ff // FF_BLOCK
    down = wd_in.shape[1]
    half = blocks // 2
    attn = [
        Gather(n_ctx, wq_ref, wq_all, hop_send.at[0], hop_recv.at[0], (NEAR, FAR)),
        Gather(n_ctx, wr_ref, wr_all, hop_send.at[1], hop_recv.at[1], (FAR, NEAR)),
    ]

    loads = []
    for d in range(blocks):
        at = pl.ds(d * LANES, LANES)
        loads.append(pltpu.make_async_copy(wo_in.at[d], wo.at[at, :], sem.at[0, d]))
    for d in range(blocks):
        at = pl.ds(d * LANES, LANES)
        rows = pl.ds(pl.multiple_of((dp ^ d) * down, 32), down)
        loads.append(pltpu.make_async_copy(wg_in.at[d], wg.at[at, :], sem.at[1, d]))
        loads.append(pltpu.make_async_copy(wu_in.at[d], wu.at[at, :], sem.at[2, d]))
        loads.append(pltpu.make_async_copy(wd_in.at[d], wd.at[rows, :], sem.at[3, d]))
    for m in loads:
        m.start()
    for d in range(blocks):
        att[:, d * LANES : (d + 1) * LANES] = att_ref[:, lane_block(dp ^ d)]
    meet(n_ctx, (CORE, NEAR, FAR))
    for w in attn:
        w.start()
    for m in loads[:blocks]:
        m.wait()
    mid = tok_ref[...].astype(F32) + dot(att[...], wo[...], 1, 0)
    inv = lax.rsqrt(jnp.mean(mid * mid, axis=-1, keepdims=True) + epsilon)
    oacc[...] = mid
    nat[...] = mid * inv
    for d in range(blocks):
        n2[:, d * LANES : (d + 1) * LANES] = nat[:, lane_block(dp ^ d)]
    mi[...] = (n2[...] * gain_ref[1:2, :]).astype(LOW)
    mit[...] = mi[...].T
    dacc[...] = jnp.zeros_like(dacc)
    for m in loads[blocks:]:
        m.wait()

    def columns(u):
        return pl.ds(pl.multiple_of(u * FF_BLOCK, FF_BLOCK), FF_BLOCK)

    def data_step(u, carry):
        cols = columns(u)
        x = mi[...]
        cot = cot_ref[...]
        wgu, wuu, wdu = wg[:, cols], wu[:, cols], wd[cols, :]
        gate = dot(x, wgu, 1, 0)
        up = dot(x, wuu, 1, 0)
        grad_hidden = dot(cot, wdu, 1, 1)
        sig = jax.nn.sigmoid(gate)
        hidden = (gate * sig * up).astype(LOW)
        dg = (grad_hidden * up * sig * (1.0 + gate * (1.0 - sig))).astype(LOW)
        du = (grad_hidden * gate * sig).astype(LOW)
        hid_all[:, cols] = hidden
        dg_all[:, cols] = dg
        du_all[:, cols] = du
        oacc[...] += dot(hidden, wdu, 1, 0)
        dacc[...] += dot(dg, wgu, 1, 1) + dot(du, wuu, 1, 1)
        return carry

    lax.fori_loop(0, 2, data_step, 0)
    for w in attn:
        w.relay()
    lax.fori_loop(2, 5, data_step, 0)
    for w in attn:
        w.spread()
    lax.fori_loop(5, steps, data_step, 0)

    out_ref[...] = oacc[...].astype(LOW)
    scaled = dacc[...] * gain_ref[1:2, :]
    norm = n2[...]
    mean = jnp.mean(scaled * norm, axis=-1, keepdims=True)
    n2[...] = inv * (scaled - norm * mean)
    for d in range(blocks):
        nat[:, lane_block(dp ^ d)] = n2[:, d * LANES : (d + 1) * LANES]
    gm = cot_ref[...].astype(F32) + nat[...]
    gm_ref[...] = gm
    gb = gm.astype(LOW)
    n2[...] = dot(gb, wo[...], 1, 1)
    for d in range(blocks):
        mi[:, lane_block(dp ^ d)] = n2[:, d * LANES : (d + 1) * LANES].astype(LOW)

    def grad_copy(k):
        to = lax.rem(c + k, n_ctx)
        return ctx_copy(mi.at[:, rows_of(to, width)], gh_ref.at[rows_of(c, tb), :], g_send.at[k - 1], g_recv.at[k - 1], to)

    grad_own = pltpu.make_async_copy(mi.at[:, rows_of(c, width)], gh_ref.at[rows_of(c, tb), :], o_sem.at[2])
    for k in range(1, n_ctx):
        grad_copy(k).start()
    grad_own.start()
    for w in attn:
        w.forward()

    def down_step(u, carry):
        cols = columns(u)
        wd[cols, :] = dot(hid_all[:, cols], cot_ref[...], 0, 0).astype(LOW)
        return carry

    lax.fori_loop(0, steps, down_step, 0)

    def down_copy(d):
        rows = pl.ds(pl.multiple_of((dp ^ d) * down, 32), down)
        if d % 2:
            return dp_copy(wd.at[rows, :], dc.at[d // 2], d_send.at[d // 2], d_recv.at[d // 2], CORE)
        return pltpu.make_async_copy(wd.at[rows, :], dk.at[d // 2], d_own.at[d // 2])

    for d in range(blocks):
        down_copy(d).start()

    dwo = dot(att[...], gb, 0, 0).astype(LOW)
    for d in range(blocks):
        ostage[d % 2, d // 2] = dwo[d * LANES : (d + 1) * LANES]
    out_own = pltpu.make_async_copy(ostage.at[0], ok, o_sem.at[0])
    out_gone = dp_copy(ostage.at[1], oc, o_sem.at[1], o_sem.at[3], CORE)
    out_own.start()
    out_gone.start()

    def side(u, t, which):
        slot = lax.rem(u, 2)
        cols = columns(u)
        keep, came = ((gk, gc), (uk, uc))[t]
        if which == 0:
            return pltpu.make_async_copy(stage.at[slot, t, 0], keep.at[:, :, cols], st_own.at[slot, t])
        return dp_copy(stage.at[slot, t, 1], came.at[:, :, cols], st_send.at[slot, t], st_recv.at[t, u], CORE)

    def weight_step(u, carry):
        cols = columns(u)

        @pl.when(u >= 2)
        def _():
            for t in range(2):
                side(u - 2, t, 0).wait()
                side(u - 2, t, 1).wait_send()

        slot = lax.rem(u, 2)
        for t, grad in enumerate((dg_all, du_all)):
            dw = dot(mit[...], grad[:, cols], 1, 0).astype(LOW)
            for d in range(blocks):
                stage[slot, t, d % 2, d // 2] = dw[d * LANES : (d + 1) * LANES]
            side(u, t, 0).start()
            side(u, t, 1).start()
        return carry

    lax.fori_loop(0, 3, weight_step, 0)
    for w in attn:
        w.cross()
    lax.fori_loop(3, steps, weight_step, 0)

    for u in (steps - 2, steps - 1):
        for t in range(2):
            side(u, t, 0).wait()
            side(u, t, 1).wait_send()

    def arrived(u, carry):
        for t in range(2):
            side(u, t, 1).wait_recv()
        return carry

    lax.fori_loop(0, steps, arrived, 0)
    out_own.wait()
    out_gone.wait()
    for d in range(blocks):
        down_copy(d).wait()
    grad_own.wait()
    for k in range(1, n_ctx):
        grad_copy(k).wait()
    for w in attn:
        w.finish()


def mlp_call(n_ctx, tok, att, cot, gain, wo, wg, wu, wd, wq, wr):
    tb, model = tok.shape
    blocks, _, ff = wg.shape
    half = blocks // 2
    down = wd.shape[1]
    width = model // n_ctx
    vmem = pl.BlockSpec(memory_space=pltpu.VMEM)
    anyspace = pl.BlockSpec(memory_space=pl.ANY)
    shape = jax.ShapeDtypeStruct
    dma = pltpu.SemaphoreType.DMA
    return pl.pallas_call(
        functools.partial(mlp_kernel, blocks, n_ctx),
        in_specs=[vmem] * 4 + [anyspace] * 6,
        out_specs=[vmem] * 2 + [anyspace] * 11,
        out_shape=[shape((tb, model), LOW), shape((tb, model), F32), shape((n_ctx * tb, width), LOW)]
        + [shape((half, LANES, ff), LOW)] * 4
        + [shape((half, LANES, model), LOW)] * 2
        + [shape((half, down, model), LOW)] * 2
        + [shape((blocks, n_ctx * w.shape[0], w.shape[1]), LOW) for w in (wq, wr)],
        scratch_shapes=[
            pltpu.VMEM((model, model), LOW),
            pltpu.VMEM((model, ff), LOW),
            pltpu.VMEM((model, ff), LOW),
            pltpu.VMEM((ff, model), LOW),
            pltpu.VMEM((tb, model), LOW),
            pltpu.VMEM((tb, model), F32),
            pltpu.VMEM((tb, model), F32),
            pltpu.VMEM((tb, model), LOW),
            pltpu.VMEM((model, tb), LOW),
            pltpu.VMEM((tb, model), F32),
            pltpu.VMEM((tb, model), F32),
            pltpu.VMEM((tb, ff), LOW),
            pltpu.VMEM((tb, ff), LOW),
            pltpu.VMEM((tb, ff), LOW),
            pltpu.VMEM((2, 2, 2, half, LANES, FF_BLOCK), LOW),
            pltpu.VMEM((2, half, LANES, model), LOW),
            dma((4, blocks)),
            dma((2, 11)), dma((2, 11)),
            dma((2, 2)), dma((2, 2)), dma((2, ff // FF_BLOCK)),
            dma((4,)),
            dma((half,)), dma((half,)), dma((half,)),
            dma((n_ctx - 1,)), dma((n_ctx - 1,)),
        ],
        compiler_params=params(collective_id=2, has_side_effects=True),
        cost_estimate=pl.CostEstimate(
            flops=2 * tb * model * (8 * ff + 3 * model), bytes_accessed=50 * 2**20, transcendentals=0
        ),
        name="mlp",
    )(tok, att, cot, gain, wo, wg, wu, wd, wq, wr)


def input_kernel(
    blocks, tok_ref, gm_ref, v1_ref, y_ref, g, gain_ref, own_gain, qkv_ref, gate_ref, up_ref, out_ref, down_ref,
    wq_ref, wr_ref, wgate_ref, wup_ref, wq_all, wr_all,
    ig_ref, vg_ref, yo_ref, gq_ref, gk_ref, gv_ref, go_ref, gg_ref, gu_ref, gd_ref, gains_ref, w, rel, nat, sem,
):
    dp = lax.axis_index("dp")
    model = tok_ref.shape[1]
    cut = wq_ref.shape[1]
    made = []
    for d in range(blocks):
        at = pl.ds(d * LANES, LANES)
        made.append(pltpu.make_async_copy(wq_all.at[d], w.at[at, pl.ds(0, cut)], sem.at[0, d]))
        made.append(pltpu.make_async_copy(wr_all.at[d], w.at[at, pl.ds(cut, 3 * model - cut)], sem.at[1, d]))

    def row_dot(a, b):
        return jnp.sum(a * b.astype(F32), axis=1, keepdims=True)

    @pl.when(pl.program_id(0) == 0)
    def _():
        for m in made:
            m.start()
        gq_ref[...] = qkv_ref[:, :model]
        gk_ref[...] = qkv_ref[:, model : 2 * model]
        gv_ref[...] = 0.5 * qkv_ref[:, 2 * model :]
        go_ref[...] = out_ref[...]
        gg_ref[...] = gate_ref[...]
        gu_ref[...] = up_ref[...]
        gd_ref[...] = down_ref[...]
        both = 2 * model - cut
        one = row_dot(qkv_ref[:, :cut], wq_ref[...]) + row_dot(qkv_ref[:, cut : 2 * model], wr_ref[:, :both])
        one = one + row_dot(gv_ref[...], wr_ref[:, both:])
        two = row_dot(gate_ref[...], wgate_ref[...]) + row_dot(up_ref[...], wup_ref[...])
        lane = lax.broadcasted_iota(jnp.int32, gains_ref.shape, 1)
        own = own_gain[...].astype(F32)
        gains_ref[...] = jnp.where(lane == 0, one / own[:, 0:1], two / own[:, 1:2])

    yo_ref[...] = y_ref[...]
    for d in range(blocks):
        rel[:, d * LANES : (d + 1) * LANES] = tok_ref[:, lane_block(dp ^ d)].astype(F32)
    gv = g[:, 2 * model :].astype(F32)
    vg_ref[...] = v1_ref[...] + 0.5 * gv

    x = rel[...]
    inv = lax.rsqrt(jnp.mean(x * x, axis=-1, keepdims=True) + epsilon)
    norm = x * inv

    @pl.when(pl.program_id(0) == 0)
    def _():
        for m in made:
            m.wait()

    grad = dot(g[:, : 2 * model], w[:, : 2 * model], 1, 1)
    grad = grad + 0.5 * dot(g[:, 2 * model :], w[:, 2 * model :], 1, 1)
    scaled = grad * gain_ref[0:1, :]
    mean = jnp.mean(scaled * norm, axis=-1, keepdims=True)
    rel[...] = inv * (scaled - norm * mean)
    for d in range(blocks):
        nat[:, lane_block(dp ^ d)] = rel[:, d * LANES : (d + 1) * LANES]
    ig_ref[...] = gm_ref[...] + nat[...]


def input_call(tok, gm, v1, y, g, gain, own_gain, qkv, grads, wq, wr, wgate, wup, wq_all, wr_all):
    tb, model = tok.shape
    blocks = wq_all.shape[0]
    rows = qkv.shape[0]
    part = tb // 2
    shape = jax.ShapeDtypeStruct
    token = lambda cols: pl.BlockSpec((part, cols), lambda i: (i, 0))
    whole = lambda a: pl.BlockSpec(a.shape, lambda i: (0, 0))
    small = [gain, own_gain, qkv, *grads, wq, wr, wgate, wup]
    ends = [shape((rows, model), F32)] * 4 + [shape(x.shape, F32) for x in (grads[0], grads[1], grads[3])]
    ends.append(shape((rows, LANES), F32))
    return pl.pallas_call(
        functools.partial(input_kernel, blocks),
        grid=(tb // part,),
        in_specs=[token(model)] * 4 + [token(3 * model)] + [whole(x) for x in small] + [pl.BlockSpec(memory_space=pl.ANY)] * 2,
        out_specs=[token(model)] * 3 + [whole(x) for x in ends],
        out_shape=[shape((tb, model), F32)] * 2 + [shape((tb, model), LOW)] + ends,
        scratch_shapes=[
            pltpu.VMEM((model, 3 * model), LOW),
            pltpu.VMEM((part, model), F32),
            pltpu.VMEM((part, model), F32),
            pltpu.SemaphoreType.DMA((2, blocks)),
        ],
        compiler_params=params(),
        cost_estimate=pl.CostEstimate(
            flops=2 * tb * model * 3 * model, bytes_accessed=20 * 2**20, transcendentals=0
        ),
        name="input_grad",
    )(tok, gm, v1, y, g, *small, wq_all, wr_all)


def fast_local(
    n_dp, n_ctx, tokens, first_values, v1_accum, segment_ids, positions, cotangent,
    attn_gain, w_query, w_key, w_value, w_out, mlp_gain, w_gate, w_up, w_down,
):
    seq, model = tokens.shape[1:]
    width = model // n_ctx
    tok = tokens[0]
    gains = jnp.pad(jnp.stack([attn_gain, mlp_gain], axis=1), ((0, 0), (0, width - 2)))
    freqs = 10000.0 ** (-np.arange(HEAD_DIM // 2).astype(np.float32) * np.float32(2.0 / HEAD_DIM))
    freq = np.zeros((8, LANES), np.float32)
    freq[0] = np.tile(freqs.astype(np.float32), LANES // (HEAD_DIM // 2))
    freq[1] = np.where(np.arange(LANES) % HEAD_DIM < HEAD_DIM // 2, -1.0, 1.0)
    freq = jnp.asarray(freq)
    (xn, q, k, v, out_full, log_total, cos, sin, seg_col, seg_row, gain_rows, attended,
     gate_all, up_all, out_all, down_all) = front_call(
        n_dp, n_ctx, tok, first_values[0], segment_ids, positions, w_query, w_key, w_value, gains, freq,
        w_gate, w_up, w_out, w_down,
    )
    cut = model // 2
    wq = jnp.concatenate([w_query, w_key[:, :cut]], axis=1)
    wr = jnp.concatenate([w_key[:, cut:], w_value], axis=1)
    (output, grad_middle, head_grad, gate_keep, gate_came, up_keep, up_came, out_keep, out_came,
     down_keep, down_came, wq_all, wr_all) = mlp_call(
        n_ctx, tok, attended, cotangent[0], gain_rows, out_all, gate_all, up_all, down_all, wq, wr
    )
    sides = [
        x.reshape(x.shape[0], n_ctx, x.shape[1] // n_ctx, x.shape[2])
        for x in (gate_keep, gate_came, up_keep, up_came, out_keep, out_came, down_keep, down_came)
    ]
    home_grad, qkv_grad, *grads = back_call(
        n_ctx, head_grad, q, k, v, out_full, log_total, seg_col, seg_row, cos, sin, xn, sides
    )
    (input_grad, v1_grad, output, query_grad, key_grad, value_grad, out_grad, gate_grad, up_grad, down_grad,
     gain_grads) = input_call(
        tok, grad_middle, v1_accum[0], output, home_grad, gain_rows, gains, qkv_grad, grads,
        wq, wr, w_gate, w_up, wq_all, wr_all
    )
    return (
        output[None], input_grad[None], v1_grad[None], gain_grads[:, 0], query_grad, key_grad, value_grad,
        out_grad, gain_grads[:, 1], gate_grad, up_grad, down_grad,
    )


def solution(mesh):
    placed = (
        P("dp", "ctx", None),
        P("dp", "ctx", None),
        P("dp", "ctx", None),
        P("dp", "ctx"),
        P("dp", "ctx"),
        P("dp", "ctx", None),
        P(("dp", "ctx")),
        P(("dp", "ctx"), None),
        P(("dp", "ctx"), None),
        P(("dp", "ctx"), None),
        P(("dp", "ctx"), None),
        P(("dp", "ctx")),
        P(("dp", "ctx"), None),
        P(("dp", "ctx"), None),
        P(("dp", "ctx"), None),
    )
    n_dp, n_ctx = mesh.shape["dp"], mesh.shape["ctx"]

    def local(*args):
        rows, seq, model = args[0].shape
        fits = (
            rows == 1
            and seq == TOKEN_BLOCK
            and model == n_dp * LANES
            and n_ctx == 4
            and model == 2 * LANES * n_ctx
            and args[12].shape[1] % FF_BLOCK == 0
        )
        return fast_local(n_dp, n_ctx, *args) if fits else plain_local(*args)

    return jax.shard_map(
        local,
        mesh=mesh,
        in_specs=placed,
        out_specs=(
            P("dp", "ctx", None),
            P("dp", "ctx", None),
            P("dp", "ctx", None),
            P(("dp", "ctx")),
            P(("dp", "ctx"), None),
            P(("dp", "ctx"), None),
            P(("dp", "ctx"), None),
            P(("dp", "ctx"), None),
            P(("dp", "ctx")),
            P(("dp", "ctx"), None),
            P(("dp", "ctx"), None),
            P(("dp", "ctx"), None),
        ),
        check_vma=False,
    )
```

```python
import functools

import jax
import jax.numpy as jnp
import numpy as np
from jax import lax
from jax.experimental import pallas as pl
from jax.experimental.pallas import tpu as pltpu
from jax.sharding import PartitionSpec as P

HEADS = 16
HEAD_DIM = 64
LANES = 128
TOKEN_BLOCK = 512
FF_BLOCK = 256
NEG = -1e30
MESH = pl.DeviceIdType.MESH
F32 = jnp.float32
LOW = jnp.bfloat16
BYTES = 63 * 2**20
epsilon = 1e-05


HEAD_BLOCK = 4


def rms_scale(values):
    return lax.rsqrt(jnp.mean(values * values, axis=-1, keepdims=True) + epsilon)


def angle_tables(position_rows):
    freqs = 10000.0 ** (-jnp.arange(HEAD_DIM // 2).astype(jnp.float32) * (2.0 / HEAD_DIM))
    angles = position_rows.astype(jnp.float32)[..., None] * freqs
    return (jnp.cos(angles)[..., None, :], jnp.sin(angles)[..., None, :])


def rotate(heads_in, cosine_table, sine_table):
    half_dim = heads_in.shape[-1] // 2
    first_half = heads_in[..., :half_dim]
    second_half = heads_in[..., half_dim:]
    return jnp.concatenate(
        [
            first_half * cosine_table - second_half * sine_table,
            second_half * cosine_table + first_half * sine_table,
        ],
        axis=-1,
    )


def norm_back(grad_normed, normed, inv_root, norm_gain):
    grad_scaled = grad_normed * norm_gain.astype(jnp.float32)
    grad_input = inv_root * (
        grad_scaled - normed * jnp.mean(grad_scaled * normed, axis=-1, keepdims=True)
    )
    return (grad_input, jnp.sum(grad_normed * normed, axis=0))


def attn_front(flat_tokens, first_flat, attn_set, cosine_table, sine_table, row_count, seq_piece):
    inv_root = rms_scale(flat_tokens)
    normed = flat_tokens * inv_root
    normed_in = (normed * attn_set[0].astype(jnp.float32)).astype(jnp.bfloat16)
    query_proj = jnp.dot(normed_in, attn_set[1], preferred_element_type=jnp.float32)
    key_proj = jnp.dot(normed_in, attn_set[2], preferred_element_type=jnp.float32)
    value_proj = jnp.dot(normed_in, attn_set[3], preferred_element_type=jnp.float32)
    query_rot = rotate(
        query_proj.reshape(row_count, seq_piece, HEADS, HEAD_DIM), cosine_table, sine_table
    )
    key_rot = rotate(
        key_proj.reshape(row_count, seq_piece, HEADS, HEAD_DIM), cosine_table, sine_table
    )
    query_rot = query_rot.astype(jnp.bfloat16).reshape(row_count, seq_piece, -1)
    key_rot = key_rot.astype(jnp.bfloat16).reshape(row_count, seq_piece, -1)
    value_mix = (
        (0.5 * value_proj + 0.5 * first_flat).astype(jnp.bfloat16).reshape(row_count, seq_piece, -1)
    )
    return (normed, inv_root, normed_in, query_rot, key_rot, value_mix)


def mlp_block(flat_tokens, attended_low, out_weight, mlp_set):
    middle = flat_tokens + jnp.dot(attended_low, out_weight, preferred_element_type=jnp.float32)
    inv_root_two = rms_scale(middle)
    normed_two = middle * inv_root_two
    mlp_in = (normed_two * mlp_set[0].astype(jnp.float32)).astype(jnp.bfloat16)
    gate_proj = jnp.dot(mlp_in, mlp_set[1], preferred_element_type=jnp.float32)
    up_proj = jnp.dot(mlp_in, mlp_set[2], preferred_element_type=jnp.float32)
    hidden = (gate_proj * jax.nn.sigmoid(gate_proj) * up_proj).astype(jnp.bfloat16)
    result = middle + jnp.dot(hidden, mlp_set[3], preferred_element_type=jnp.float32)
    return (normed_two, inv_root_two, mlp_in, gate_proj, up_proj, hidden, result)


def split_groups(row_block):
    tok_count = row_block.shape[0]
    return row_block.reshape(tok_count, HEADS // HEAD_BLOCK, HEAD_BLOCK * HEAD_DIM).transpose(
        1, 0, 2
    )


def join_groups(group_block):
    return group_block.transpose(1, 0, 2).reshape(group_block.shape[1], -1)


def as_heads(block):
    return block.reshape(block.shape[0], HEAD_BLOCK, HEAD_DIM)


def attend_row(members):
    query_row, key_row, value_row, allowed = members

    def per_group(pieces):
        query_block, key_block, value_block = pieces
        scores = (
            jnp.einsum(
                "qhd,khd->hqk",
                as_heads(query_block),
                as_heads(key_block),
                preferred_element_type=jnp.float32,
            )
            * 0.125
        )
        scores = jnp.where(allowed[None], scores, -1e30)
        highest = jnp.max(scores, axis=-1, keepdims=True)
        exp_scores = jnp.exp(scores - highest)
        denominator = jnp.sum(exp_scores, axis=-1, keepdims=True)
        soft_low = (exp_scores / denominator).astype(jnp.bfloat16)
        attended = jnp.einsum(
            "hqk,khd->qhd", soft_low, as_heads(value_block), preferred_element_type=jnp.float32
        )
        return (
            attended.reshape(query_block.shape[0], -1),
            (highest + jnp.log(denominator))[..., 0],
        )

    attended, log_total = lax.map(
        per_group, (split_groups(query_row), split_groups(key_row), split_groups(value_row))
    )
    return (join_groups(attended), log_total)


def attend_back(members):
    query_row, key_row, value_row, grad_row, log_total, allowed = members

    def per_group(pieces):
        query_block, key_block, value_block, grad_block, log_block = pieces
        query_heads = as_heads(query_block)
        key_heads = as_heads(key_block)
        grad_heads = as_heads(grad_block)
        scores = (
            jnp.einsum("qhd,khd->hqk", query_heads, key_heads, preferred_element_type=jnp.float32)
            * 0.125
        )
        soft_weights = jnp.where(allowed[None], jnp.exp(scores - log_block[..., None]), 0.0)
        soft_low = soft_weights.astype(jnp.bfloat16)
        grad_probs = jnp.einsum(
            "qhd,khd->hqk", grad_heads, as_heads(value_block), preferred_element_type=jnp.float32
        )
        row_delta = jnp.sum(soft_weights * grad_probs, axis=-1, keepdims=True)
        grad_scores = (soft_weights * (grad_probs - row_delta)).astype(jnp.bfloat16)
        grad_query = (
            jnp.einsum("hqk,khd->qhd", grad_scores, key_heads, preferred_element_type=jnp.float32)
            * 0.125
        )
        grad_key = (
            jnp.einsum("hqk,qhd->khd", grad_scores, query_heads, preferred_element_type=jnp.float32)
            * 0.125
        )
        grad_value = jnp.einsum(
            "hqk,qhd->khd", soft_low, grad_heads, preferred_element_type=jnp.float32
        )
        return (
            grad_query.reshape(query_block.shape[0], -1),
            grad_key.reshape(key_block.shape[0], -1),
            grad_value.reshape(key_block.shape[0], -1),
        )

    grad_query, grad_key, grad_value = lax.map(
        per_group,
        (
            split_groups(query_row),
            split_groups(key_row),
            split_groups(value_row),
            split_groups(grad_row),
            log_total,
        ),
    )
    return (join_groups(grad_query), join_groups(grad_key), join_groups(grad_value))


def plain_local(
    tokens,
    first_values,
    v1_accum,
    segment_ids,
    positions,
    cotangent,
    attn_gain,
    w_query,
    w_key,
    w_value,
    w_out,
    mlp_gain,
    w_gate,
    w_up,
    w_down,
):
    row_count, seq_piece, model_width = tokens.shape
    token_count = row_count * seq_piece
    flat_tokens = tokens.astype(jnp.float32).reshape(token_count, model_width)
    first_flat = first_values.astype(jnp.float32).reshape(token_count, model_width)
    cosine_table, sine_table = angle_tables(positions)
    segment_low = segment_ids.astype(jnp.bfloat16)
    attn_set = (
        lax.all_gather(attn_gain, ("dp", "ctx"), axis=0, tiled=True),
        lax.all_gather(w_query, ("dp", "ctx"), axis=0, tiled=True),
        lax.all_gather(w_key, ("dp", "ctx"), axis=0, tiled=True),
        lax.all_gather(w_value, ("dp", "ctx"), axis=0, tiled=True),
        lax.all_gather(w_out, ("dp", "ctx"), axis=0, tiled=True),
    )
    normed, inv_root, normed_in, query_rot, key_rot, value_mix = attn_front(
        flat_tokens, first_flat, attn_set, cosine_table, sine_table, row_count, seq_piece
    )
    key_full, value_full, segment_full = (
        lax.all_gather(key_rot, "ctx", axis=1, tiled=True),
        lax.all_gather(value_mix, "ctx", axis=1, tiled=True),
        lax.all_gather(segment_low, "ctx", axis=1, tiled=True),
    )
    query_order = lax.axis_index("ctx") * seq_piece + jnp.arange(seq_piece, dtype=jnp.int32)
    full_order = jnp.arange(key_full.shape[1], dtype=jnp.int32)
    segment_own = segment_ids.astype(jnp.float32)
    segment_all = segment_full.astype(jnp.float32)
    allowed = (segment_own[:, :, None] == segment_all[:, None, :]) & (
        query_order[None, :, None] >= full_order[None, None, :]
    )
    attended, log_total = lax.map(attend_row, (query_rot, key_full, value_full, allowed))
    attended_low = attended.reshape(token_count, model_width).astype(jnp.bfloat16)
    mlp_set = (
        lax.all_gather(mlp_gain, ("dp", "ctx"), axis=0, tiled=True),
        lax.all_gather(w_gate, ("dp", "ctx"), axis=0, tiled=True),
        lax.all_gather(w_up, ("dp", "ctx"), axis=0, tiled=True),
        lax.all_gather(w_down, ("dp", "ctx"), axis=0, tiled=True),
    )
    normed_two, inv_root_two, mlp_in, gate_proj, up_proj, hidden, output_flat = mlp_block(
        flat_tokens, attended_low, attn_set[4], mlp_set
    )
    output = output_flat.reshape(tokens.shape).astype(jnp.bfloat16)
    attn_set = (
        lax.all_gather(attn_gain, ("dp", "ctx"), axis=0, tiled=True),
        lax.all_gather(w_query, ("dp", "ctx"), axis=0, tiled=True),
        lax.all_gather(w_key, ("dp", "ctx"), axis=0, tiled=True),
        lax.all_gather(w_value, ("dp", "ctx"), axis=0, tiled=True),
        lax.all_gather(w_out, ("dp", "ctx"), axis=0, tiled=True),
    )
    mlp_set = (
        lax.all_gather(mlp_gain, ("dp", "ctx"), axis=0, tiled=True),
        lax.all_gather(w_gate, ("dp", "ctx"), axis=0, tiled=True),
        lax.all_gather(w_up, ("dp", "ctx"), axis=0, tiled=True),
        lax.all_gather(w_down, ("dp", "ctx"), axis=0, tiled=True),
    )
    normed, inv_root, normed_in, query_rot, key_rot, value_mix = attn_front(
        flat_tokens, first_flat, attn_set, cosine_table, sine_table, row_count, seq_piece
    )
    key_full, value_full = (
        lax.all_gather(key_rot, "ctx", axis=1, tiled=True),
        lax.all_gather(value_mix, "ctx", axis=1, tiled=True),
    )
    normed_two, inv_root_two, mlp_in, gate_proj, up_proj, hidden, output_flat = mlp_block(
        flat_tokens, attended_low, attn_set[4], mlp_set
    )
    cot_low = cotangent.reshape(token_count, model_width)
    cot_float = cot_low.astype(jnp.float32)
    grad_hidden = jnp.einsum("td,fd->tf", cot_low, mlp_set[3], preferred_element_type=jnp.float32)
    sigma = jax.nn.sigmoid(gate_proj)
    grad_gate_low = (grad_hidden * up_proj * sigma * (1.0 + gate_proj * (1.0 - sigma))).astype(
        jnp.bfloat16
    )
    grad_up_low = (grad_hidden * gate_proj * sigma).astype(jnp.bfloat16)
    grad_mlp_in = jnp.einsum(
        "tf,df->td", grad_gate_low, mlp_set[1], preferred_element_type=jnp.float32
    )
    grad_mlp_in = grad_mlp_in + jnp.einsum(
        "tf,df->td", grad_up_low, mlp_set[2], preferred_element_type=jnp.float32
    )
    grad_middle_norm, grad_gain_two = norm_back(grad_mlp_in, normed_two, inv_root_two, mlp_set[0])
    grad_middle = cot_float + grad_middle_norm
    grad_branch_low = grad_middle.astype(jnp.bfloat16)
    grad_attended = jnp.einsum(
        "te,de->td", grad_branch_low, attn_set[4], preferred_element_type=jnp.float32
    )
    grad_attended = grad_attended.astype(jnp.bfloat16).reshape(row_count, seq_piece, model_width)
    grad_query_rot, grad_key_full, grad_value_full = lax.map(
        attend_back, (query_rot, key_full, value_full, grad_attended, log_total, allowed)
    )
    grad_key_rot, grad_value_mix = (
        lax.psum_scatter(
            grad_key_full.astype(jnp.bfloat16), "ctx", scatter_dimension=1, tiled=True
        ).astype(jnp.float32),
        lax.psum_scatter(
            grad_value_full.astype(jnp.bfloat16), "ctx", scatter_dimension=1, tiled=True
        ).astype(jnp.float32),
    )
    v1_grad = v1_accum + 0.5 * grad_value_mix
    grad_query_low = rotate(
        grad_query_rot.reshape(row_count, seq_piece, HEADS, HEAD_DIM), cosine_table, -sine_table
    )
    grad_query_low = grad_query_low.astype(jnp.bfloat16).reshape(token_count, model_width)
    grad_key_low = rotate(
        grad_key_rot.reshape(row_count, seq_piece, HEADS, HEAD_DIM), cosine_table, -sine_table
    )
    grad_key_low = grad_key_low.astype(jnp.bfloat16).reshape(token_count, model_width)
    grad_value_low = (0.5 * grad_value_mix).astype(jnp.bfloat16).reshape(token_count, model_width)
    grad_normed_in = jnp.einsum(
        "te,de->td", grad_query_low, attn_set[1], preferred_element_type=jnp.float32
    )
    grad_normed_in = grad_normed_in + jnp.einsum(
        "te,de->td", grad_key_low, attn_set[2], preferred_element_type=jnp.float32
    )
    grad_normed_in = grad_normed_in + jnp.einsum(
        "te,de->td", grad_value_low, attn_set[3], preferred_element_type=jnp.float32
    )
    grad_input_norm, grad_gain_one = norm_back(grad_normed_in, normed, inv_root, attn_set[0])
    input_grad = (grad_middle + grad_input_norm).reshape(tokens.shape)
    attn_right = jnp.concatenate([grad_query_low, grad_key_low, grad_value_low], axis=1)
    left_in = normed_in
    projections = jnp.einsum("td,te->de", left_in, attn_right, preferred_element_type=jnp.float32)
    out_part = jnp.einsum(
        "td,te->de", attended_low, grad_branch_low, preferred_element_type=jnp.float32
    )
    attn_matrix = lax.psum_scatter(
        jnp.concatenate([projections, out_part], axis=1),
        ("dp", "ctx"),
        scatter_dimension=0,
        tiled=True,
    )
    mlp_right = jnp.concatenate([grad_gate_low, grad_up_low], axis=1)
    left_in = mlp_in
    gate_up_matrix = lax.psum_scatter(
        jnp.einsum("td,tf->df", left_in, mlp_right, preferred_element_type=jnp.float32),
        ("dp", "ctx"),
        scatter_dimension=0,
        tiled=True,
    )
    down_matrix = lax.psum_scatter(
        jnp.einsum("tf,td->fd", hidden, cot_low, preferred_element_type=jnp.float32),
        ("dp", "ctx"),
        scatter_dimension=0,
        tiled=True,
    )
    gain_one, gain_two = (
        lax.psum_scatter(grad_gain_one, ("dp", "ctx"), scatter_dimension=0, tiled=True),
        lax.psum_scatter(grad_gain_two, ("dp", "ctx"), scatter_dimension=0, tiled=True),
    )
    ff_width = w_gate.shape[1]
    return (
        output,
        input_grad,
        v1_grad,
        gain_one,
        attn_matrix[:, 0:model_width],
        attn_matrix[:, model_width : 2 * model_width],
        attn_matrix[:, 2 * model_width : 3 * model_width],
        attn_matrix[:, 3 * model_width : 4 * model_width],
        gain_two,
        gate_up_matrix[:, 0:ff_width],
        gate_up_matrix[:, ff_width : 2 * ff_width],
        down_matrix,
    )


def params(**kw):
    return pltpu.CompilerParams(vmem_limit_bytes=BYTES, **kw)


def dot(a, b, da, db):
    return lax.dot_general(a, b, (((da,), (db,)), ((), ())), preferred_element_type=F32)


def lane_block(index):
    return pl.ds(pl.multiple_of(index * LANES, LANES), LANES)


def half_swap(x):
    lane = lax.broadcasted_iota(jnp.int32, x.shape, 1)
    left = pltpu.roll(x, LANES - HEAD_DIM // 2, 1)
    right = pltpu.roll(x, HEAD_DIM // 2, 1)
    return jnp.where(lane % HEAD_DIM < HEAD_DIM // 2, left, right)


def head_lanes(x, head):
    lane = lax.broadcasted_iota(jnp.int32, x.shape, 1)
    return jnp.where(lane // HEAD_DIM == head, x, jnp.zeros_like(x))


def meet(n_ctx, bits):
    c, dp = lax.axis_index("ctx"), lax.axis_index("dp")
    barrier = pltpu.get_barrier_semaphore()
    for k in range(1, n_ctx):
        pl.semaphore_signal(barrier, inc=1, device_id={"ctx": lax.rem(c + k, n_ctx)}, device_id_type=MESH)
    for bit in bits:
        pl.semaphore_signal(barrier, inc=1, device_id={"dp": dp ^ bit}, device_id_type=MESH)
    pl.semaphore_wait(barrier, n_ctx - 1 + len(bits))


def ctx_copy(src, dst, send, recv, to):
    return pltpu.make_async_remote_copy(
        src_ref=src, dst_ref=dst, send_sem=send, recv_sem=recv, device_id={"ctx": to}, device_id_type=MESH
    )


def dp_copy(src, dst, send, recv, bit):
    to = lax.axis_index("dp") ^ bit
    return pltpu.make_async_remote_copy(
        src_ref=src, dst_ref=dst, send_sem=send, recv_sem=recv, device_id={"dp": to}, device_id_type=MESH
    )


def rows_of(index, size):
    return pl.ds(pl.multiple_of(index * size, size), size)


CORE, NEAR, FAR = 1, 2, 4


class Gather:
    def __init__(self, n_ctx, src, dst, send, recv, order):
        self.n, self.src, self.dst, self.send, self.recv = n_ctx, src, dst, send, recv
        self.first, self.second = order
        self.rows = src.shape[0]

    def place(self, c):
        return self.dst.at[0, pl.ds(c * self.rows, self.rows), :]

    def along(self, bit):
        c = lax.axis_index("ctx")
        return ctx_copy(self.src, self.place(c), self.send.at[bit - 1], self.recv.at[bit - 1], c ^ bit)

    def pass_on(self):
        c = lax.axis_index("ctx")
        return ctx_copy(self.place(c ^ 2), self.place(c ^ 2), self.send.at[2], self.recv.at[2], c ^ 1)

    def plane(self, slot, bit, at):
        return dp_copy(self.dst.at[slot], self.dst.at[slot ^ bit], self.send.at[at], self.recv.at[at], bit)

    def own(self):
        c = lax.axis_index("ctx")
        return pltpu.make_async_copy(self.src, self.dst.at[0, pl.ds(c * self.rows, self.rows), :], self.send.at[10])

    def hop(self, at):
        one, two = self.first, self.second
        slot, bit = [(0, one), (0, two), (one, two), (0, CORE), (one, CORE), (two, CORE), (one | two, CORE)][at]
        return self.plane(slot, bit, 3 + at)

    def start(self):
        self.own().start()
        self.along(2).start()
        self.along(1).start()

    def relay(self):
        self.along(2).wait_recv()
        self.pass_on().start()

    def spread(self):
        self.own().wait()
        self.along(1).wait_recv()
        self.pass_on().wait_recv()
        for at in (0, 1, 3):
            self.hop(at).start()

    def forward(self):
        self.hop(0).wait_recv()
        self.hop(2).start()
        self.hop(4).start()

    def cross(self):
        self.hop(1).wait_recv()
        self.hop(5).start()
        self.hop(2).wait_recv()
        self.hop(6).start()

    def finish(self):
        self.along(1).wait_send()
        self.along(2).wait_send()
        self.pass_on().wait_send()
        for at in range(7):
            self.hop(at).wait_send()
        for at in range(3, 7):
            self.hop(at).wait_recv()


def front_kernel(
    n_ctx, tok_ref, fv_ref, seg_in, pos_in, wq_ref, wk_ref, wv_ref, gains_ref, freq_ref, wg_ref, wu_ref, wo_ref, wd_ref,
    xn_ref, q_ref, k_ref, v_ref, of_ref, lse_ref, cos_ref, sin_ref, seg_ref, marks, gain_ref,
    att_ref, wg_all, wu_all, wo_all, wd_all,
    x_all, fvs, packs, whead, rel, o_ref, s_ref, m_ref, l_ref, acc_ref, p_all, total_ref,
    mark_send, mark_recv, piece_send, piece_recv, pack_send, pack_recv, tok_send, tok_recv, fv_send, fv_recv, w_send, w_recv,
    o_send, o_recv, own, own_o,
):
    c, dp = lax.axis_index("ctx"), lax.axis_index("dp")
    tb = m_ref.shape[0]
    half = tb // 2
    model = tok_ref.shape[1]
    blocks = model // LANES
    width = q_ref.shape[1]
    own_rows = wg_ref.shape[0]
    lane = lax.broadcasted_iota(jnp.int32, (tb, LANES), 1)
    exact = lax.Precision.HIGHEST

    weights = []
    for i, (src, dst) in enumerate(((wg_ref, wg_all), (wo_ref, wo_all), (wu_ref, wu_all), (wd_ref, wd_all))):
        wide = src.shape[1] // 2
        weights.append([])
        for h, order in enumerate(((NEAR, FAR), (FAR, NEAR))):
            cols = pl.ds(h * wide, wide)
            unit = 2 * i + h
            weights[i].append(
                Gather(n_ctx, src.at[:, cols], dst.at[:, :, cols], w_send.at[unit], w_recv.at[unit], order)
            )
    gate, out, up, down = weights

    def each(what, *arrays):
        for array in arrays:
            for half_way in array:
                getattr(half_way, what)()

    def mark_copies(k):
        at, to = rows_of(c, tb), lax.rem(c + k, n_ctx)
        return [
            ctx_copy(src, marks.at[pl.ds(r, 1), at], mark_send.at[k - 1, r], mark_recv.at[k - 1, r], to)
            for r, src in enumerate((seg_in, pos_in))
        ]

    def pieces(to):
        cols = rows_of(to, width)
        return [wq_ref.at[:, cols], wk_ref.at[:, cols], wv_ref.at[:, cols], gains_ref]

    def pack_copies(k):
        to = lax.rem(c + k, n_ctx)
        return [
            ctx_copy(src, packs.at[0, c, pl.ds(t * own_rows, own_rows), :], piece_send.at[k - 1, t], piece_recv.at[k - 1, t], to)
            for t, src in enumerate(pieces(to))
        ]

    def pack_hop(slot, bit, at):
        return dp_copy(packs.at[slot], packs.at[slot ^ bit], pack_send.at[at], pack_recv.at[at], bit)

    def fv_copy(k):
        to = lax.rem(c + k, n_ctx)
        return ctx_copy(fv_ref.at[:, rows_of(to, width)], fvs.at[rows_of(c, tb), :], fv_send.at[k - 1], fv_recv.at[k - 1], to)

    def tok_copy(bit):
        return ctx_copy(tok_ref, x_all.at[rows_of(c, tb), :], tok_send.at[bit - 1], tok_recv.at[bit - 1], c ^ bit)

    def tok_pass():
        at = rows_of(c ^ 2, tb)
        return ctx_copy(x_all.at[at, :], x_all.at[at, :], tok_send.at[2], tok_recv.at[2], c ^ 1)

    locals_ = [
        pltpu.make_async_copy(tok_ref, x_all.at[rows_of(c, tb), :], own.at[0]),
        pltpu.make_async_copy(fv_ref.at[:, rows_of(c, width)], fvs.at[rows_of(c, tb), :], own.at[1]),
    ] + [
        pltpu.make_async_copy(src, packs.at[0, c, pl.ds(t * own_rows, own_rows), :], own.at[4 + t])
        for t, src in enumerate(pieces(c))
    ] + [
        pltpu.make_async_copy(src, marks.at[pl.ds(r, 1), rows_of(c, tb)], own.at[2 + r])
        for r, src in enumerate((seg_in, pos_in))
    ]

    meet(n_ctx, (CORE, NEAR, FAR))
    for k in range(1, n_ctx):
        for m in mark_copies(k) + pack_copies(k):
            m.start()
    each("start", gate, out, up)
    for m in locals_:
        m.start()

    for m in locals_[6:]:
        m.wait()
    for k in range(1, n_ctx):
        for m in mark_copies(k):
            m.wait_recv()
    row8 = lax.broadcasted_iota(jnp.int32, (2, LANES), 0)
    pick_seg = jnp.where(row8 == 0, 1.0, 0.0)
    pick_pos = jnp.where(row8 == 1, 1.0, 0.0)

    def table(b, carry):
        at = rows_of(b, tb)
        m = marks[0:2, at].astype(F32)
        dims = (((0,), (0,)), ((), ()))
        seg_ref[at, :] = lax.dot_general(m, pick_seg, dims, precision=exact, preferred_element_type=F32)
        pos = lax.dot_general(m, pick_pos, dims, precision=exact, preferred_element_type=F32)
        angle = pos * freq_ref[0:1, :]
        cos_ref[at, :] = jnp.cos(angle)
        sin_ref[at, :] = jnp.sin(angle) * freq_ref[1:2, :]
        return carry

    for m in locals_[2:6]:
        m.wait()
    for k in range(1, n_ctx):
        for m in pack_copies(k):
            m.wait_recv()
    pack_hop(0, NEAR, 3).start()
    each("relay", gate, out, up)
    tok_copy(2).start()
    tok_copy(1).start()
    lax.fori_loop(0, n_ctx, table, 0)
    pack_hop(0, NEAR, 3).wait_recv()
    pack_hop(0, FAR, 4).start()
    pack_hop(NEAR, FAR, 5).start()
    pack_hop(0, CORE, 6).start()
    pack_hop(NEAR, CORE, 7).start()
    each("spread", gate, out, up)
    pack_hop(0, FAR, 4).wait_recv()
    pack_hop(FAR, CORE, 8).start()
    pack_hop(NEAR, FAR, 5).wait_recv()
    pack_hop(NEAR | FAR, CORE, 9).start()
    for at, (slot, bit) in enumerate([(0, CORE), (NEAR, CORE), (FAR, CORE), (NEAR | FAR, CORE)]):
        pack_hop(slot, bit, 6 + at).wait_recv()
    count = packs.shape[0]
    for t in range(3):
        block = packs[:, :, t * own_rows : (t + 1) * own_rows, :]
        whead[:, t * width : (t + 1) * width] = block.reshape(model, width)
    gains = packs[:, :, 3 * own_rows : 4 * own_rows, 0:LANES].reshape(model, LANES).astype(F32)
    gain_ref[...] = gains.T[0:8, :]
    locals_[0].wait()
    locals_[1].wait()

    def project(chunk, part):
        at = pl.ds(pl.multiple_of(chunk * tb + part * half, half), half)
        for d in range(blocks):
            rel[:, d * LANES : (d + 1) * LANES] = x_all[at, lane_block(dp ^ d)].astype(F32)
        x = rel[...]
        inv = lax.rsqrt(jnp.mean(x * x, axis=-1, keepdims=True) + epsilon)
        xn = (x * inv * gain_ref[0:1, :]).astype(LOW)
        xn_ref[at, :] = xn
        proj = dot(xn, whead[...], 1, 0)
        cos, sin = cos_ref[at, :], sin_ref[at, :]
        for b in range(width // LANES):
            cols = slice(b * LANES, (b + 1) * LANES)
            qb = proj[:, b * LANES : (b + 1) * LANES]
            q_ref[at, cols] = ((qb * cos + half_swap(qb) * sin) * 0.125).astype(LOW)
            kb = proj[:, width + b * LANES : width + (b + 1) * LANES]
            k_ref[at, cols] = (kb * cos + half_swap(kb) * sin).astype(LOW)
        of_ref[at, :] = 0.5 * proj[:, 2 * width :]

    def project_chunk(bit):
        def one(part, carry):
            project(c ^ bit, part)
            return carry

        lax.fori_loop(0, 2, one, 0)

    project_chunk(0)
    each("forward", gate, out, up)
    tok_copy(2).wait_recv()
    tok_pass().start()
    tok_copy(1).wait_recv()
    project_chunk(1)
    project_chunk(2)
    each("cross", gate, out, up)
    tok_pass().wait_recv()
    each("start", down)
    for k in range(1, n_ctx):
        fv_copy(k).start()
    project_chunk(3)

    def fold(x, op):
        r = x[:, 0:LANES]
        for b in range(1, tb // LANES):
            r = op(r, x[:, b * LANES : (b + 1) * LANES])
        return r

    def home(pair):
        return att_ref.at[:, pl.ds(pl.multiple_of(c * width + pair * LANES, LANES), LANES)]

    def weigh(pair, i):
        cols = slice(pair * LANES, (pair + 1) * LANES)
        mine = rows_of(i, tb)
        q = q_ref[mine, cols]
        seg_q = seg_ref[mine, 0:1]
        base = i * (i + 1) // 2
        for head in range(2):
            qm = head_lanes(q, head)
            m_ref[...] = jnp.full_like(m_ref, NEG)

            def score(j, causal):
                at = rows_of(j, tb)
                s = dot(qm, k_ref[at, cols], 1, 1)
                ok = seg_q == marks[0:1, at].astype(F32)
                if causal:
                    r = lax.broadcasted_iota(jnp.int32, (tb, tb), 0)
                    t = lax.broadcasted_iota(jnp.int32, (tb, tb), 1)
                    ok = ok & (r >= t)
                s = jnp.where(ok, s, NEG)
                s_ref[:, at] = s
                m_ref[...] = jnp.maximum(m_ref[...], fold(s, jnp.maximum))

            def score_step(j, carry):
                score(j, False)
                return carry

            lax.fori_loop(0, i, score_step, 0)
            score(i, True)
            top = jnp.max(m_ref[...], axis=1, keepdims=True)
            l_ref[...] = jnp.zeros_like(l_ref)

            def weight_step(j, carry):
                p = jnp.exp(s_ref[:, rows_of(j, tb)] - top)
                l_ref[...] += fold(p, jnp.add)
                p_all[2 * pair + head, base + j] = p.astype(LOW)
                return carry

            lax.fori_loop(0, i + 1, weight_step, 0)
            total = jnp.sum(l_ref[...], axis=1, keepdims=True)
            total_ref[mine, :] = jnp.where(lane == 2 * pair + head, total, total_ref[mine, :])
            lse = jnp.broadcast_to(top + jnp.log(total), (tb, LANES))
            if head == 0:
                lse_ref[mine, cols] = lse
            else:
                lse_ref[mine, cols] = jnp.where(lane < HEAD_DIM, lse_ref[mine, cols], lse)

    def mix(pair, i):
        cols = slice(pair * LANES, (pair + 1) * LANES)
        mine = rows_of(i, tb)
        base = i * (i + 1) // 2
        for head in range(2):
            acc_ref[...] = jnp.zeros_like(acc_ref)

            def value_step(j, carry):
                acc_ref[...] += dot(p_all[2 * pair + head, base + j], v_ref[rows_of(j, tb), cols], 1, 0)
                return carry

            lax.fori_loop(0, i + 1, value_step, 0)
            out = acc_ref[...] / total_ref[mine, 2 * pair + head : 2 * pair + head + 1]
            if head == 0:
                of_ref[mine, cols] = out
            else:
                of_ref[mine, cols] = jnp.where(lane < HEAD_DIM, of_ref[mine, cols], out)
        o_ref[mine, cols] = of_ref[mine, cols].astype(LOW)

        @pl.when(i == c)
        def _():
            pltpu.make_async_copy(o_ref.at[mine, cols], home(pair), own_o.at[pair]).start()

        @pl.when(i != c)
        def _():
            k = lax.rem(i + n_ctx - c, n_ctx) - 1
            ctx_copy(o_ref.at[mine, cols], home(pair), o_send.at[k, pair], o_recv.at[k, pair], i).start()

    def over_queries(what, pair, lo, hi):
        def one(i, carry):
            what(pair, i)
            return carry

        lax.fori_loop(lo, hi, one, 0)

    total_ref[...] = jnp.ones_like(total_ref)
    over_queries(weigh, 0, 0, n_ctx)
    each("relay", down)
    over_queries(weigh, 1, 0, 3)
    each("spread", down)
    over_queries(weigh, 1, 3, n_ctx)
    for k in range(1, n_ctx):
        fv_copy(k).wait_recv()

    def values(b, carry):
        at = rows_of(b, tb)
        v_ref[at, :] = (of_ref[at, :] + 0.5 * fvs[at, :].astype(F32)).astype(LOW)
        return carry

    lax.fori_loop(0, n_ctx, values, 0)
    over_queries(mix, 0, 0, n_ctx)
    each("forward", down)
    over_queries(mix, 1, 0, n_ctx)
    each("cross", down)
    for pair in range(width // LANES):
        cols = slice(pair * LANES, (pair + 1) * LANES)
        pltpu.make_async_copy(o_ref.at[0:tb, cols], home(pair), own_o.at[pair]).wait()
        for k in range(n_ctx - 1):
            ctx_copy(o_ref.at[0:tb, cols], home(pair), o_send.at[k, pair], o_recv.at[k, pair], c).wait()
    for k in range(1, n_ctx):
        for m in mark_copies(k) + pack_copies(k):
            m.wait_send()
        fv_copy(k).wait_send()
    for at, (slot, bit) in enumerate(
        [(0, NEAR), (0, FAR), (NEAR, FAR), (0, CORE), (NEAR, CORE), (FAR, CORE), (NEAR | FAR, CORE)]
    ):
        pack_hop(slot, bit, 3 + at).wait_send()
    tok_copy(1).wait_send()
    tok_copy(2).wait_send()
    tok_pass().wait_send()
    each("finish", *weights)


def front_call(n_dp, n_ctx, tok, fv, seg, pos, wq, wk, wv, gains, freq, wg, wu, wo, wd):
    tb, model = tok.shape
    width = model // n_ctx
    length = n_ctx * tb
    pairs = width // LANES
    vmem = pl.BlockSpec(memory_space=pltpu.VMEM)
    anyspace = pl.BlockSpec(memory_space=pl.ANY)
    shape = jax.ShapeDtypeStruct
    dma = pltpu.SemaphoreType.DMA
    return pl.pallas_call(
        functools.partial(front_kernel, n_ctx),
        in_specs=[anyspace] * 8 + [vmem] + [anyspace] * 4,
        out_specs=[vmem] * 11 + [anyspace] * 5,
        out_shape=[shape((length, model), LOW)]
        + [shape((length, width), LOW)] * 3
        + [shape((length, width), F32)] * 2
        + [shape((length, LANES), F32)] * 3
        + [shape((2, length), jnp.int32), shape((8, model), F32)]
        + [shape((tb, model), LOW)]
        + [shape((n_dp, n_ctx * w.shape[0], w.shape[1]), LOW) for w in (wg, wu, wo, wd)],
        scratch_shapes=[
            pltpu.VMEM((length, model), LOW),
            pltpu.VMEM((length, width), LOW),
            pltpu.VMEM((n_dp, n_ctx, 4 * wq.shape[0], width), LOW),
            pltpu.VMEM((model, 3 * width), LOW),
            pltpu.VMEM((tb // 2, model), F32),
            pltpu.VMEM((length, width), LOW),
            pltpu.VMEM((tb, length), F32),
            pltpu.VMEM((tb, LANES), F32),
            pltpu.VMEM((tb, LANES), F32),
            pltpu.VMEM((tb, LANES), F32),
            pltpu.VMEM((2 * pairs, n_ctx * (n_ctx + 1) // 2, tb, tb), LOW),
            pltpu.VMEM((length, LANES), F32),
            dma((n_ctx - 1, 2)), dma((n_ctx - 1, 2)),
            dma((n_ctx - 1, 4)), dma((n_ctx - 1, 4)),
            dma((n_ctx + 6,)), dma((n_ctx + 6,)),
            dma((3,)), dma((3,)),
            dma((n_ctx - 1,)), dma((n_ctx - 1,)),
            dma((8, 11)), dma((8, 11)),
            dma((n_ctx - 1, pairs)), dma((n_ctx - 1, pairs)),
            dma((8,)), dma((pairs,)),
        ],
        compiler_params=params(collective_id=1, has_side_effects=True),
        cost_estimate=pl.CostEstimate(
            flops=24 * 10**9, bytes_accessed=60 * 2**20, transcendentals=2 * length * length
        ),
        name="front",
    )(tok, fv, seg, pos, wq, wk, wv, gains, freq, wg, wu, wo, wd)


class Reduce:
    def __init__(self, n_ctx, keep, came, acc, rc, rx, ry, rz, out, send, recv, order):
        self.n, self.keep, self.came, self.acc, self.rc, self.rx, self.ry, self.rz = n_ctx, keep, came, acc, rc, rx, ry, rz
        self.out, self.send, self.recv = out, send, recv
        self.one, self.two = order
        self.leave = (self.one >> 1, 3)
        self.stay = self.two >> 1

    def hop(self, at):
        src, dst, bit = [
            (self.acc.at[self.leave[0]], self.rx.at[0], self.one),
            (self.acc.at[self.leave[1]], self.rx.at[1], self.one),
            (self.acc.at[self.stay], self.ry, self.two),
        ][at - 1]
        return dp_copy(src, dst, self.send.at[at], self.recv.at[at], bit)

    def held(self):
        return pltpu.make_async_copy(self.keep, self.acc, self.send.at[7])

    def partner(self):
        return pltpu.make_async_copy(self.came, self.rc, self.send.at[0])

    def along(self, at):
        c = lax.axis_index("ctx")
        block, to = ((c ^ 1, c ^ 1), (c ^ 3, c ^ 1), (c ^ 2, c ^ 2))[at]
        return ctx_copy(self.acc.at[0, block], self.rz.at[at], self.send.at[4 + at], self.recv.at[4 + at], to)

    def begin(self):
        self.partner().start()
        self.held().start()

    def add(self, block, terms):
        def one(j, carry):
            total = self.acc[block, j].astype(F32)
            for t in terms:
                total = total + t(j).astype(F32)
            self.acc[block, j] = total.astype(LOW)
            return carry

        lax.fori_loop(0, self.acc.shape[1], one, 0)

    def step_one(self):
        self.held().wait()
        self.partner().wait()
        for at in (1, 0):
            block = self.leave[at]
            self.add(block, [lambda j, block=block: self.rc[block, j]])
            self.hop(1 + at).start()

    def step_two(self):
        self.hop(2).wait_recv()
        self.add(self.stay, [lambda j: self.rc[self.stay, j], lambda j: self.rx[1, j]])
        self.hop(3).start()

    def step_ctx(self):
        c = lax.axis_index("ctx")
        self.hop(1).wait_recv()
        self.hop(3).wait_recv()
        self.out[...] = (
            self.acc[0, c].astype(F32) + self.rc[0, c].astype(F32) + self.rx[0, c].astype(F32) + self.ry[c].astype(F32)
        )
        self.add(0, [lambda j: self.rc[0, j], lambda j: self.rx[0, j], lambda j: self.ry[j]])
        self.along(1).start()
        self.along(0).start()

    def step_far(self):
        block = lax.axis_index("ctx") ^ 2
        self.along(1).wait_recv()
        self.acc[0, block] = (self.acc[0, block].astype(F32) + self.rz[1].astype(F32)).astype(LOW)
        self.along(2).start()

    def finish(self):
        self.along(0).wait_recv()
        self.along(2).wait_recv()
        self.out[...] += self.rz[0].astype(F32) + self.rz[2].astype(F32)
        for at in range(1, 4):
            self.hop(at).wait_send()
        for at in range(3):
            self.along(at).wait_send()


def back_kernel(n_ctx, *refs):
    g_ref, q_ref, k_ref, v_ref, of_ref, lse_ref, sc_ref, sr_ref, cos_ref, sin_ref, xn_ref = refs[:11]
    sides = refs[11:19]
    home_ref, qkv_out = refs[19:21]
    outs = refs[21:25]
    (part_ref, lse_row, delta_row, dq_acc, dk_acc, dv_acc, prod) = refs[25:32]
    rest = refs[32:]
    buffers, rest = rest[:40], rest[40:]
    (pk, ps, prc, prx, pry, pz, qz) = rest[:7]
    (send, recv, own, r_send, r_recv, p_send, p_recv, z_send, z_recv) = rest[7:]
    c = lax.axis_index("ctx")
    tb = dk_acc.shape[0]
    length, width = q_ref.shape
    model = n_ctx * width
    pairs = width // LANES
    blocks = model // LANES
    orders = ((NEAR, FAR), (FAR, NEAR))
    groups = []
    for i in range(4):
        keep, came = sides[2 * i], sides[2 * i + 1]
        wide = keep.shape[3] // 2
        groups.append([])
        for h, order in enumerate(orders):
            cols = pl.ds(h * wide, wide)
            unit = 2 * i + h
            groups[i].append(
                Reduce(
                    n_ctx, keep.at[:, :, :, cols], came.at[:, :, :, cols], *buffers[5 * unit : 5 * unit + 5],
                    outs[i].at[:, cols], r_send.at[unit], r_recv.at[unit], order,
                )
            )

    def each(i, what):
        for unit in groups[i]:
            getattr(unit, what)()

    def home(pair, t):
        return home_ref.at[:, pl.ds(pl.multiple_of(t * model + c * width + pair * LANES, LANES), LANES)]

    def part(pair, t, chunk):
        return part_ref.at[pair, rows_of(chunk, tb), pl.ds(t * LANES, LANES)]

    def part_copy(pair, t, k, to):
        return ctx_copy(part(pair, t, to), home(pair, t), send.at[k - 1, pair, t], recv.at[k - 1, pair, t], to)

    def part_own(pair, t):
        return pltpu.make_async_copy(part(pair, t, c), home(pair, t), own.at[pair, t])

    meet(n_ctx, (CORE, NEAR, FAR))
    for i in range(4):
        each(i, "begin")
    each(0, "step_one")

    r8 = lax.broadcasted_iota(jnp.int32, (8, LANES), 0)
    l8 = lax.broadcasted_iota(jnp.int32, (8, LANES), 1)
    pick = jnp.where(l8 == r8 * HEAD_DIM, 1.0, 0.0)
    group = jnp.where(l8 // HEAD_DIM == r8, 1.0, 0.0)
    exact = lax.Precision.HIGHEST
    dims = (((1,), (1,)), ((), ()))

    def stats(pair):
        cols = slice(pair * LANES, (pair + 1) * LANES)

        def one(b, carry):
            at = rows_of(b, tb)
            lse_row[:, at] = lax.dot_general(pick, lse_ref[at, cols], dims, precision=exact, preferred_element_type=F32)
            mixed = g_ref[at, cols].astype(F32) * of_ref[at, cols]
            delta_row[:, at] = lax.dot_general(group, mixed, dims, precision=exact, preferred_element_type=F32)
            dq_acc[at, :] = jnp.zeros((tb, LANES), F32)
            return carry

        lax.fori_loop(0, n_ctx, one, 0)

    def key_blocks(pair, lo, hi):
        cols = slice(pair * LANES, (pair + 1) * LANES)

        def key_block(j, carry):
            dk_acc[...] = jnp.zeros_like(dk_acc)
            dv_acc[...] = jnp.zeros_like(dv_acc)
            mine = rows_of(j, tb)
            k = k_ref[mine, cols]
            v = v_ref[mine, cols]
            seg_k = sc_ref[mine, 0:1]

            def block(i, causal):
                at = rows_of(i, tb)
                q = q_ref[at, cols]
                g = g_ref[at, cols]
                ok = seg_k == sr_ref[0:1, at].astype(F32)
                if causal:
                    r = lax.broadcasted_iota(jnp.int32, (tb, tb), 0)
                    t = lax.broadcasted_iota(jnp.int32, (tb, tb), 1)
                    ok = ok & (r <= t)
                for head in range(2):
                    qm = head_lanes(q, head)
                    gm = head_lanes(g, head)
                    s = dot(k, qm, 1, 1)
                    p = jnp.where(ok, jnp.exp(s - lse_row[head : head + 1, at]), 0.0)
                    dp = dot(v, gm, 1, 1)
                    ds = (p * (dp - delta_row[head : head + 1, at])).astype(LOW)
                    dv_acc[...] += dot(p.astype(LOW), gm, 1, 0)
                    dk_acc[...] += dot(ds, qm, 1, 0)
                    dq_acc[at, :] += dot(ds, head_lanes(k, head), 0, 0)

            block(j, True)

            def step(i, carry):
                block(i, False)
                return carry

            lax.fori_loop(j + 1, n_ctx, step, 0)
            dk = dk_acc[...]
            dk = dk * cos_ref[mine, :] - half_swap(dk) * sin_ref[mine, :]
            part_ref[pair, mine, LANES : 2 * LANES] = dk.astype(LOW)
            part_ref[pair, mine, 2 * LANES : 3 * LANES] = dv_acc[...].astype(LOW)
            dq = dq_acc[mine, :] * 0.125
            dq = dq * cos_ref[mine, :] - half_swap(dq) * sin_ref[mine, :]
            part_ref[pair, mine, 0:LANES] = dq.astype(LOW)

            @pl.when(j == c)
            def _():
                for t in range(3):
                    part_own(pair, t).start()

            @pl.when(j != c)
            def _():
                for t in range(3):
                    part_copy(pair, t, lax.rem(j + n_ctx - c, n_ctx), j).start()

            return carry

        lax.fori_loop(lo, hi, key_block, 0)

    def pair_hop(pair, at):
        src, dst, bit = [
            (ps.at[pair], prc.at[pair], CORE),
            (pk.at[pair, 1], prx.at[pair, 0], NEAR),
            (pk.at[pair, 3], prx.at[pair, 1], NEAR),
            (pk.at[pair, 2], pry.at[pair], FAR),
        ][at]
        return dp_copy(src, dst, p_send.at[pair, at], p_recv.at[pair, at], bit)

    def pair_ctx(pair, k):
        to = lax.rem(c + k, n_ctx)
        return ctx_copy(pz.at[pair, to], qz.at[c, pair], z_send.at[pair, k - 1], z_recv.at[pair, k - 1], to)

    def pair_product(pair):
        prod[...] = jnp.zeros_like(prod)

        def one(b, carry):
            at = rows_of(b, tb)
            prod[...] += dot(part_ref[pair, at, :], xn_ref[at, :], 0, 0)
            return carry

        lax.fori_loop(0, n_ctx, one, 0)
        for d in range(blocks):
            (ps if d % 2 else pk)[pair, d // 2] = prod[:, d * LANES : (d + 1) * LANES].astype(LOW)
        pair_hop(pair, 0).start()

    def pair_one(pair):
        pair_hop(pair, 0).wait_recv()
        for i in (3, 1):
            pk[pair, i] = (pk[pair, i].astype(F32) + prc[pair, i].astype(F32)).astype(LOW)
            pair_hop(pair, 1 + i // 2).start()

    def pair_two(pair):
        pair_hop(pair, 2).wait_recv()
        total = pk[pair, 2].astype(F32) + prc[pair, 2].astype(F32) + prx[pair, 1].astype(F32)
        pk[pair, 2] = total.astype(LOW)
        pair_hop(pair, 3).start()

    def pair_three(pair):
        pair_hop(pair, 1).wait_recv()
        pair_hop(pair, 3).wait_recv()
        total = pk[pair, 0].astype(F32) + prc[pair, 0].astype(F32) + prx[pair, 0].astype(F32) + pry[pair].astype(F32)
        pz[pair] = total.T.reshape(pz.shape[1:]).astype(LOW)
        qz[c, pair] = pz[pair, c]
        for k in range(1, n_ctx):
            pair_ctx(pair, k).start()

    def pair_finish(pair):
        for k in range(1, n_ctx):
            pair_ctx(pair, k).wait()
        for at in range(4):
            pair_hop(pair, at).wait_send()

    middle = n_ctx // 2
    stats(0)
    key_blocks(0, 0, middle)
    each(0, "step_two")
    each(1, "step_one")
    key_blocks(0, middle, n_ctx)
    each(0, "step_ctx")
    stats(1)
    key_blocks(1, 0, middle)
    each(1, "step_two")
    each(2, "step_one")
    key_blocks(1, middle, n_ctx)
    pair_product(1)
    each(1, "step_ctx")
    pair_product(0)
    each(0, "step_far")
    pair_one(1)
    each(2, "step_two")
    each(3, "step_one")
    pair_one(0)
    pair_two(1)
    each(1, "step_far")
    pair_two(0)
    pair_three(1)
    each(2, "step_ctx")
    each(3, "step_two")
    pair_three(0)
    each(2, "step_far")
    each(3, "step_ctx")
    each(3, "step_far")
    for pair in range(pairs):
        pair_finish(pair)
        for s in range(n_ctx):
            for t in range(3):
                at = t * model + s * width + pair * LANES
                qkv_out[:, at : at + LANES] = qz[s, pair, :, t * LANES : (t + 1) * LANES].astype(F32)
    for i in range(4):
        each(i, "finish")
    for pair in range(pairs):
        for t in range(3):
            part_own(pair, t).wait()
            for k in range(1, n_ctx):
                part_copy(pair, t, k, lax.rem(c + k, n_ctx)).wait()


def back_call(n_ctx, g, q, k, v, of, lse, seg_col, seg_row, cos, sin, xn, sides):
    length, width = q.shape
    model = n_ctx * width
    tb = TOKEN_BLOCK
    pairs = width // LANES
    own_rows = model // (model // LANES) // n_ctx
    vmem = pl.BlockSpec(memory_space=pltpu.VMEM)
    anyspace = pl.BlockSpec(memory_space=pl.ANY)
    shape = jax.ShapeDtypeStruct
    dma = pltpu.SemaphoreType.DMA
    buffers = []
    for keep in sides[::2]:
        four, parts, rows, cols = keep.shape
        for lead in ((four, parts), (four, parts), (2, parts), (parts,), (3,)) * 2:
            buffers.append(pltpu.VMEM(lead + (rows, cols // 2), LOW))
    wide = 3 * LANES
    return pl.pallas_call(
        functools.partial(back_kernel, n_ctx),
        in_specs=[vmem] * 11 + [anyspace] * 8,
        out_specs=[anyspace] + [vmem] * 5,
        out_shape=[shape((tb, 3 * model), LOW), shape((own_rows, 3 * model), F32)]
        + [shape(keep.shape[2:], F32) for keep in sides[::2]],
        scratch_shapes=[
            pltpu.VMEM((pairs, length, wide), LOW),
            pltpu.VMEM((8, length), F32),
            pltpu.VMEM((8, length), F32),
            pltpu.VMEM((length, LANES), F32),
            pltpu.VMEM((tb, LANES), F32),
            pltpu.VMEM((tb, LANES), F32),
            pltpu.VMEM((wide, model), F32),
        ]
        + buffers
        + [
            pltpu.VMEM((pairs, 4, wide, LANES), LOW),
            pltpu.VMEM((pairs, 4, wide, LANES), LOW),
            pltpu.VMEM((pairs, 4, wide, LANES), LOW),
            pltpu.VMEM((pairs, 2, wide, LANES), LOW),
            pltpu.VMEM((pairs, wide, LANES), LOW),
            pltpu.VMEM((pairs, n_ctx, own_rows, wide), LOW),
            pltpu.VMEM((n_ctx, pairs, own_rows, wide), LOW),
            dma((n_ctx - 1, pairs, 3)), dma((n_ctx - 1, pairs, 3)),
            dma((pairs, 3)),
            dma((8, 8)), dma((8, 8)),
            dma((pairs, 4)), dma((pairs, 4)),
            dma((pairs, n_ctx - 1)), dma((pairs, n_ctx - 1)),
        ],
        compiler_params=params(collective_id=3, has_side_effects=True),
        cost_estimate=pl.CostEstimate(
            flops=40 * 10**9, bytes_accessed=60 * 2**20, transcendentals=2 * length * length
        ),
        name="back",
    )(g, q, k, v, of, lse, seg_col, seg_row, cos, sin, xn, *sides)


def mlp_kernel(
    blocks, n_ctx, tok_ref, att_ref, cot_ref, gain_ref, wo_in, wg_in, wu_in, wd_in, wq_ref, wk_ref, wv_ref,
    out_ref, gm_ref, gh_ref, gk, gc, uk, uc, ok, oc, dk, dc, wq_all, wk_all, wv_all,
    wo, wg, wu, wd, att, nat, n2, mi, mit, oacc, dacc, hid_all, dg_all, du_all, stage, ostage,
    sem, hop_send, hop_recv, st_own, st_send, st_recv, o_sem, d_own, d_send, d_recv, g_send, g_recv,
):
    c, dp = lax.axis_index("ctx"), lax.axis_index("dp")
    tb, model = tok_ref.shape
    width = model // n_ctx
    ff = wu.shape[1]
    steps = ff // FF_BLOCK
    down = wd_in.shape[1]
    half = blocks // 2
    attn = [
        Gather(n_ctx, wq_ref, wq_all, hop_send.at[0], hop_recv.at[0], (NEAR, FAR)),
        Gather(n_ctx, wk_ref, wk_all, hop_send.at[1], hop_recv.at[1], (FAR, NEAR)),
    ]
    for h, order in enumerate(((NEAR, FAR), (FAR, NEAR))):
        cols = pl.ds(h * (model // 2), model // 2)
        attn.append(
            Gather(n_ctx, wv_ref.at[:, cols], wv_all.at[:, :, cols], hop_send.at[2 + h], hop_recv.at[2 + h], order)
        )

    loads = []
    for d in range(blocks):
        at = pl.ds(d * LANES, LANES)
        loads.append(pltpu.make_async_copy(wo_in.at[d], wo.at[at, :], sem.at[0, d]))
    for d in range(blocks):
        at = pl.ds(d * LANES, LANES)
        rows = pl.ds(pl.multiple_of((dp ^ d) * down, 32), down)
        loads.append(pltpu.make_async_copy(wg_in.at[d], wg.at[at, :], sem.at[1, d]))
        loads.append(pltpu.make_async_copy(wu_in.at[d], wu.at[at, :], sem.at[2, d]))
        loads.append(pltpu.make_async_copy(wd_in.at[d], wd.at[rows, :], sem.at[3, d]))
    for m in loads:
        m.start()
    for d in range(blocks):
        att[:, d * LANES : (d + 1) * LANES] = att_ref[:, lane_block(dp ^ d)]
    meet(n_ctx, (CORE, NEAR, FAR))
    for w in attn:
        w.start()
    for m in loads[:blocks]:
        m.wait()
    mid = tok_ref[...].astype(F32) + dot(att[...], wo[...], 1, 0)
    inv = lax.rsqrt(jnp.mean(mid * mid, axis=-1, keepdims=True) + epsilon)
    oacc[...] = mid
    nat[...] = mid * inv
    for d in range(blocks):
        n2[:, d * LANES : (d + 1) * LANES] = nat[:, lane_block(dp ^ d)]
    mi[...] = (n2[...] * gain_ref[1:2, :]).astype(LOW)
    mit[...] = mi[...].T
    dacc[...] = jnp.zeros_like(dacc)
    for m in loads[blocks:]:
        m.wait()

    def columns(u):
        return pl.ds(pl.multiple_of(u * FF_BLOCK, FF_BLOCK), FF_BLOCK)

    def data_step(u, carry):
        cols = columns(u)
        x = mi[...]
        cot = cot_ref[...]
        wgu, wuu, wdu = wg[:, cols], wu[:, cols], wd[cols, :]
        gate = dot(x, wgu, 1, 0)
        up = dot(x, wuu, 1, 0)
        grad_hidden = dot(cot, wdu, 1, 1)
        sig = jax.nn.sigmoid(gate)
        hidden = (gate * sig * up).astype(LOW)
        dg = (grad_hidden * up * sig * (1.0 + gate * (1.0 - sig))).astype(LOW)
        du = (grad_hidden * gate * sig).astype(LOW)
        hid_all[:, cols] = hidden
        dg_all[:, cols] = dg
        du_all[:, cols] = du
        oacc[...] += dot(hidden, wdu, 1, 0)
        dacc[...] += dot(dg, wgu, 1, 1) + dot(du, wuu, 1, 1)
        return carry

    lax.fori_loop(0, 2, data_step, 0)
    for w in attn:
        w.relay()
    lax.fori_loop(2, 5, data_step, 0)
    for w in attn:
        w.spread()
    lax.fori_loop(5, steps, data_step, 0)

    out_ref[...] = oacc[...].astype(LOW)
    scaled = dacc[...] * gain_ref[1:2, :]
    norm = n2[...]
    mean = jnp.mean(scaled * norm, axis=-1, keepdims=True)
    n2[...] = inv * (scaled - norm * mean)
    for d in range(blocks):
        nat[:, lane_block(dp ^ d)] = n2[:, d * LANES : (d + 1) * LANES]
    gm = cot_ref[...].astype(F32) + nat[...]
    gm_ref[...] = gm
    gb = gm.astype(LOW)
    n2[...] = dot(gb, wo[...], 1, 1)
    for d in range(blocks):
        mi[:, lane_block(dp ^ d)] = n2[:, d * LANES : (d + 1) * LANES].astype(LOW)

    def grad_copy(k):
        to = lax.rem(c + k, n_ctx)
        return ctx_copy(mi.at[:, rows_of(to, width)], gh_ref.at[rows_of(c, tb), :], g_send.at[k - 1], g_recv.at[k - 1], to)

    grad_own = pltpu.make_async_copy(mi.at[:, rows_of(c, width)], gh_ref.at[rows_of(c, tb), :], o_sem.at[2])
    for k in range(1, n_ctx):
        grad_copy(k).start()
    grad_own.start()
    for w in attn:
        w.forward()

    def down_step(u, carry):
        cols = columns(u)
        wd[cols, :] = dot(hid_all[:, cols], cot_ref[...], 0, 0).astype(LOW)
        return carry

    lax.fori_loop(0, steps, down_step, 0)

    def down_copy(d):
        rows = pl.ds(pl.multiple_of((dp ^ d) * down, 32), down)
        if d % 2:
            return dp_copy(wd.at[rows, :], dc.at[d // 2], d_send.at[d // 2], d_recv.at[d // 2], CORE)
        return pltpu.make_async_copy(wd.at[rows, :], dk.at[d // 2], d_own.at[d // 2])

    for d in range(blocks):
        down_copy(d).start()

    dwo = dot(att[...], gb, 0, 0).astype(LOW)
    for d in range(blocks):
        ostage[d % 2, d // 2] = dwo[d * LANES : (d + 1) * LANES]
    out_own = pltpu.make_async_copy(ostage.at[0], ok, o_sem.at[0])
    out_gone = dp_copy(ostage.at[1], oc, o_sem.at[1], o_sem.at[3], CORE)
    out_own.start()
    out_gone.start()

    def side(u, t, which):
        slot = lax.rem(u, 2)
        cols = columns(u)
        keep, came = ((gk, gc), (uk, uc))[t]
        if which == 0:
            return pltpu.make_async_copy(stage.at[slot, t, 0], keep.at[:, :, cols], st_own.at[slot, t])
        return dp_copy(stage.at[slot, t, 1], came.at[:, :, cols], st_send.at[slot, t], st_recv.at[t, u], CORE)

    def weight_step(u, carry):
        cols = columns(u)

        @pl.when(u >= 2)
        def _():
            for t in range(2):
                side(u - 2, t, 0).wait()
                side(u - 2, t, 1).wait_send()

        slot = lax.rem(u, 2)
        for t, grad in enumerate((dg_all, du_all)):
            dw = dot(mit[...], grad[:, cols], 1, 0).astype(LOW)
            for d in range(blocks):
                stage[slot, t, d % 2, d // 2] = dw[d * LANES : (d + 1) * LANES]
            side(u, t, 0).start()
            side(u, t, 1).start()
        return carry

    lax.fori_loop(0, 3, weight_step, 0)
    for w in attn:
        w.cross()
    lax.fori_loop(3, steps, weight_step, 0)

    for u in (steps - 2, steps - 1):
        for t in range(2):
            side(u, t, 0).wait()
            side(u, t, 1).wait_send()

    def arrived(u, carry):
        for t in range(2):
            side(u, t, 1).wait_recv()
        return carry

    lax.fori_loop(0, steps, arrived, 0)
    out_own.wait()
    out_gone.wait()
    for d in range(blocks):
        down_copy(d).wait()
    grad_own.wait()
    for k in range(1, n_ctx):
        grad_copy(k).wait()
    for w in attn:
        w.finish()


def mlp_call(n_ctx, tok, att, cot, gain, wo, wg, wu, wd, wq, wk, wv):
    tb, model = tok.shape
    blocks, _, ff = wg.shape
    half = blocks // 2
    down = wd.shape[1]
    width = model // n_ctx
    vmem = pl.BlockSpec(memory_space=pltpu.VMEM)
    anyspace = pl.BlockSpec(memory_space=pl.ANY)
    shape = jax.ShapeDtypeStruct
    dma = pltpu.SemaphoreType.DMA
    return pl.pallas_call(
        functools.partial(mlp_kernel, blocks, n_ctx),
        in_specs=[vmem] * 4 + [anyspace] * 7,
        out_specs=[vmem] * 2 + [anyspace] * 12,
        out_shape=[shape((tb, model), LOW), shape((tb, model), F32), shape((n_ctx * tb, width), LOW)]
        + [shape((half, LANES, ff), LOW)] * 4
        + [shape((half, LANES, model), LOW)] * 2
        + [shape((half, down, model), LOW)] * 2
        + [shape((blocks, n_ctx * w.shape[0], w.shape[1]), LOW) for w in (wq, wk, wv)],
        scratch_shapes=[
            pltpu.VMEM((model, model), LOW),
            pltpu.VMEM((model, ff), LOW),
            pltpu.VMEM((model, ff), LOW),
            pltpu.VMEM((ff, model), LOW),
            pltpu.VMEM((tb, model), LOW),
            pltpu.VMEM((tb, model), F32),
            pltpu.VMEM((tb, model), F32),
            pltpu.VMEM((tb, model), LOW),
            pltpu.VMEM((model, tb), LOW),
            pltpu.VMEM((tb, model), F32),
            pltpu.VMEM((tb, model), F32),
            pltpu.VMEM((tb, ff), LOW),
            pltpu.VMEM((tb, ff), LOW),
            pltpu.VMEM((tb, ff), LOW),
            pltpu.VMEM((2, 2, 2, half, LANES, FF_BLOCK), LOW),
            pltpu.VMEM((2, half, LANES, model), LOW),
            dma((4, blocks)),
            dma((4, 11)), dma((4, 11)),
            dma((2, 2)), dma((2, 2)), dma((2, ff // FF_BLOCK)),
            dma((4,)),
            dma((half,)), dma((half,)), dma((half,)),
            dma((n_ctx - 1,)), dma((n_ctx - 1,)),
        ],
        compiler_params=params(collective_id=2, has_side_effects=True),
        cost_estimate=pl.CostEstimate(
            flops=2 * tb * model * (8 * ff + 3 * model), bytes_accessed=50 * 2**20, transcendentals=0
        ),
        name="mlp",
    )(tok, att, cot, gain, wo, wg, wu, wd, wq, wk, wv)


def input_kernel(
    blocks, tok_ref, gm_ref, v1_ref, y_ref, g, gain_ref, own_gain, qkv_ref, gate_ref, up_ref, out_ref, down_ref,
    wq_ref, wk_ref, wv_ref, wgate_ref, wup_ref, wq_all, wk_all, wv_all,
    ig_ref, vg_ref, yo_ref, gq_ref, gk_ref, gv_ref, go_ref, gg_ref, gu_ref, gd_ref, gains_ref, w, rel, nat, sem,
):
    dp = lax.axis_index("dp")
    model = tok_ref.shape[1]
    made = []
    for d in range(blocks):
        at = pl.ds(d * LANES, LANES)
        for t, part in enumerate((wq_all, wk_all, wv_all)):
            made.append(pltpu.make_async_copy(part.at[d], w.at[at, pl.ds(t * model, model)], sem.at[t, d]))

    def row_dot(a, b):
        return jnp.sum(a * b.astype(F32), axis=1, keepdims=True)

    @pl.when(pl.program_id(0) == 0)
    def _():
        for m in made:
            m.start()
        gq_ref[...] = qkv_ref[:, :model]
        gk_ref[...] = qkv_ref[:, model : 2 * model]
        gv_ref[...] = 0.5 * qkv_ref[:, 2 * model :]
        go_ref[...] = out_ref[...]
        gg_ref[...] = gate_ref[...]
        gu_ref[...] = up_ref[...]
        gd_ref[...] = down_ref[...]
        one = row_dot(gq_ref[...], wq_ref[...]) + row_dot(gk_ref[...], wk_ref[...]) + row_dot(gv_ref[...], wv_ref[...])
        two = row_dot(gate_ref[...], wgate_ref[...]) + row_dot(up_ref[...], wup_ref[...])
        lane = lax.broadcasted_iota(jnp.int32, gains_ref.shape, 1)
        own = own_gain[...].astype(F32)
        gains_ref[...] = jnp.where(lane == 0, one / own[:, 0:1], two / own[:, 1:2])

    yo_ref[...] = y_ref[...]
    for d in range(blocks):
        rel[:, d * LANES : (d + 1) * LANES] = tok_ref[:, lane_block(dp ^ d)].astype(F32)
    gv = g[:, 2 * model :].astype(F32)
    vg_ref[...] = v1_ref[...] + 0.5 * gv

    x = rel[...]
    inv = lax.rsqrt(jnp.mean(x * x, axis=-1, keepdims=True) + epsilon)
    norm = x * inv

    @pl.when(pl.program_id(0) == 0)
    def _():
        for m in made:
            m.wait()

    grad = dot(g[:, : 2 * model], w[:, : 2 * model], 1, 1)
    grad = grad + 0.5 * dot(g[:, 2 * model :], w[:, 2 * model :], 1, 1)
    scaled = grad * gain_ref[0:1, :]
    mean = jnp.mean(scaled * norm, axis=-1, keepdims=True)
    rel[...] = inv * (scaled - norm * mean)
    for d in range(blocks):
        nat[:, lane_block(dp ^ d)] = rel[:, d * LANES : (d + 1) * LANES]
    ig_ref[...] = gm_ref[...] + nat[...]


def input_call(tok, gm, v1, y, g, gain, own_gain, qkv, grads, wq, wk, wv, wgate, wup, wq_all, wk_all, wv_all):
    tb, model = tok.shape
    blocks = wq_all.shape[0]
    rows = qkv.shape[0]
    part = tb // 2
    shape = jax.ShapeDtypeStruct
    token = lambda cols: pl.BlockSpec((part, cols), lambda i: (i, 0))
    whole = lambda a: pl.BlockSpec(a.shape, lambda i: (0, 0))
    small = [gain, own_gain, qkv, *grads, wq, wk, wv, wgate, wup]
    ends = [shape((rows, model), F32)] * 4 + [shape(x.shape, F32) for x in (grads[0], grads[1], grads[3])]
    ends.append(shape((rows, LANES), F32))
    return pl.pallas_call(
        functools.partial(input_kernel, blocks),
        grid=(tb // part,),
        in_specs=[token(model)] * 4 + [token(3 * model)] + [whole(x) for x in small] + [pl.BlockSpec(memory_space=pl.ANY)] * 3,
        out_specs=[token(model)] * 3 + [whole(x) for x in ends],
        out_shape=[shape((tb, model), F32)] * 2 + [shape((tb, model), LOW)] + ends,
        scratch_shapes=[
            pltpu.VMEM((model, 3 * model), LOW),
            pltpu.VMEM((part, model), F32),
            pltpu.VMEM((part, model), F32),
            pltpu.SemaphoreType.DMA((3, blocks)),
        ],
        compiler_params=params(),
        cost_estimate=pl.CostEstimate(
            flops=2 * tb * model * 3 * model, bytes_accessed=20 * 2**20, transcendentals=0
        ),
        name="input_grad",
    )(tok, gm, v1, y, g, *small, wq_all, wk_all, wv_all)


def fast_local(
    n_dp, n_ctx, tokens, first_values, v1_accum, segment_ids, positions, cotangent,
    attn_gain, w_query, w_key, w_value, w_out, mlp_gain, w_gate, w_up, w_down,
):
    seq, model = tokens.shape[1:]
    width = model // n_ctx
    tok = tokens[0]
    gains = jnp.pad(jnp.stack([attn_gain, mlp_gain], axis=1), ((0, 0), (0, width - 2)))
    freqs = 10000.0 ** (-np.arange(HEAD_DIM // 2).astype(np.float32) * np.float32(2.0 / HEAD_DIM))
    freq = np.zeros((8, LANES), np.float32)
    freq[0] = np.tile(freqs.astype(np.float32), LANES // (HEAD_DIM // 2))
    freq[1] = np.where(np.arange(LANES) % HEAD_DIM < HEAD_DIM // 2, -1.0, 1.0)
    freq = jnp.asarray(freq)
    (xn, q, k, v, out_full, log_total, cos, sin, seg_col, seg_row, gain_rows, attended,
     gate_all, up_all, out_all, down_all) = front_call(
        n_dp, n_ctx, tok, first_values[0], segment_ids, positions, w_query, w_key, w_value, gains, freq,
        w_gate, w_up, w_out, w_down,
    )
    (output, grad_middle, head_grad, gate_keep, gate_came, up_keep, up_came, out_keep, out_came,
     down_keep, down_came, *attn_all) = mlp_call(
        n_ctx, tok, attended, cotangent[0], gain_rows, out_all, gate_all, up_all, down_all,
        w_query, w_key, w_value,
    )
    sides = [
        x.reshape(x.shape[0], n_ctx, x.shape[1] // n_ctx, x.shape[2])
        for x in (gate_keep, gate_came, up_keep, up_came, out_keep, out_came, down_keep, down_came)
    ]
    home_grad, qkv_grad, *grads = back_call(
        n_ctx, head_grad, q, k, v, out_full, log_total, seg_col, seg_row, cos, sin, xn, sides
    )
    (input_grad, v1_grad, output, query_grad, key_grad, value_grad, out_grad, gate_grad, up_grad, down_grad,
     gain_grads) = input_call(
        tok, grad_middle, v1_accum[0], output, home_grad, gain_rows, gains, qkv_grad, grads,
        w_query, w_key, w_value, w_gate, w_up, *attn_all,
    )
    return (
        output[None], input_grad[None], v1_grad[None], gain_grads[:, 0], query_grad, key_grad, value_grad,
        out_grad, gain_grads[:, 1], gate_grad, up_grad, down_grad,
    )


def solution(mesh):
    placed = (
        P("dp", "ctx", None),
        P("dp", "ctx", None),
        P("dp", "ctx", None),
        P("dp", "ctx"),
        P("dp", "ctx"),
        P("dp", "ctx", None),
        P(("dp", "ctx")),
        P(("dp", "ctx"), None),
        P(("dp", "ctx"), None),
        P(("dp", "ctx"), None),
        P(("dp", "ctx"), None),
        P(("dp", "ctx")),
        P(("dp", "ctx"), None),
        P(("dp", "ctx"), None),
        P(("dp", "ctx"), None),
    )
    n_dp, n_ctx = mesh.shape["dp"], mesh.shape["ctx"]

    def local(*args):
        rows, seq, model = args[0].shape
        fits = (
            rows == 1
            and seq == TOKEN_BLOCK
            and model == n_dp * LANES
            and n_ctx == 4
            and model == 2 * LANES * n_ctx
            and args[12].shape[1] % FF_BLOCK == 0
        )
        return fast_local(n_dp, n_ctx, *args) if fits else plain_local(*args)

    return jax.shard_map(
        local,
        mesh=mesh,
        in_specs=placed,
        out_specs=(
            P("dp", "ctx", None),
            P("dp", "ctx", None),
            P("dp", "ctx", None),
            P(("dp", "ctx")),
            P(("dp", "ctx"), None),
            P(("dp", "ctx"), None),
            P(("dp", "ctx"), None),
            P(("dp", "ctx"), None),
            P(("dp", "ctx")),
            P(("dp", "ctx"), None),
            P(("dp", "ctx"), None),
            P(("dp", "ctx"), None),
        ),
        check_vma=False,
    )
```
